32 devices in a mesh: dp: 8 (over y, x, core), tensor: 4 (over z).
Axes of the slice: x: 2, y: 2, z: 4, core: 2. Of those that a mesh axis runs over, the one named last changes fastest.
Arguments:
- tokens: bfloat16 [5120, 2048], P('dp'), may hold values from -6 to 6
- cotangent: bfloat16 [5120, 2048], P('dp'), may hold values from -6 to 6
- token_slots: int32 [5120], replicated, may hold values from 0 to 8191, as said below
- lengths: int32 [8, 3], P('dp'), may hold values from 0 to 1024, as said below
- mixer_gain: bfloat16 [2048], replicated, may hold values from 0.5 to 1.5
- query_weight: bfloat16 [2048, 1024], P(None, 'tensor'), may hold values from -0.125 to 0.125
- key_weight: bfloat16 [2048, 1024], P(None, 'tensor'), may hold values from -0.125 to 0.125
- value_weight: bfloat16 [2048, 2048], P(None, 'tensor'), may hold values from -0.125 to 0.125
- gate_weight: bfloat16 [2048, 2048], P(None, 'tensor'), may hold values from -0.125 to 0.125
- decay_down: bfloat16 [2048, 16], replicated, may hold values from -0.125 to 0.125
- decay_up: bfloat16 [1024, 16], P('tensor'), may hold values from -1.5 to 1.5
- decay_bias: bfloat16 [1024], P('tensor'), may hold values from -3 to 5
- head_gain: bfloat16 [512], replicated, may hold values from 0.5 to 1.5
- out_weight: bfloat16 [2048, 2048], P('tensor'), may hold values from -0.125 to 0.125
- feed_gain: bfloat16 [2048], replicated, may hold values from 0.5 to 1.5
- feed_gate: bfloat16 [2048, 5632], P(None, 'tensor'), may hold values from -0.125 to 0.125
- feed_up: bfloat16 [2048, 5632], P(None, 'tensor'), may hold values from -0.125 to 0.125
- feed_down: bfloat16 [5632, 2048], P('tensor'), may hold values from -0.078125 to 0.078125
Outputs:
- layer_out: bfloat16 [5120, 2048], P('dp')
- token_grad: bfloat16 [5120, 2048], P('dp')
- grad_mixer_gain: float32 [2048], P('dp')
- grad_query: float32 [2048, 1024], P('dp', 'tensor')
- grad_key: float32 [2048, 1024], P('dp', 'tensor')
- grad_value: float32 [2048, 2048], P('dp', 'tensor')
- grad_gate: float32 [2048, 2048], P('dp', 'tensor')
- grad_decay_down: float32 [2048, 16], P('dp')
- grad_decay_up: float32 [4, 256, 16], P('tensor', 'dp')
- grad_decay_bias: float32 [4, 256], P('tensor', 'dp')
- grad_head_gain: float32 [512], P('dp')
- grad_out: float32 [4, 512, 2048], P('tensor', 'dp')
- grad_feed_gain: float32 [2048], P('dp')
- grad_feed_gate: float32 [2048, 5632], P('dp', 'tensor')
- grad_feed_up: float32 [2048, 5632], P('dp', 'tensor')
- grad_feed_down: float32 [4, 1408, 2048], P('tensor', 'dp')
The draws below stay inside these ranges and needn't reach their ends.
Inputs may be any that keep to these rules, and one draw needn't show every extreme that they name: `token_slots`: the tokens of one sequence fill consecutive positions of one owner, starting at the sum of the lengths before it; every position below the sum of its owner's lengths receives exactly one token and no position above it; the last owner's positions are all filled; of the 640 tokens of one data device's block at most 128 go to one owner, and some owner receives exactly 128 from every block. The lengths of one owner sum to at most 1024, all lengths together to 5120; a length may be 0; some owner holds one sequence of 1024 tokens.
All inputs are finite; a program needn't handle non-finite values.
Results may differ from the reference program's by a relative error of at most 0.019.
Values may be sent and summed in bfloat16 or wider, within the bound.
A program may use at most 256 MiB of HBM per device.

```python
import jax
import jax.numpy as jnp
from jax import lax

D = 2048
HEADS = 4
DK = 256
DV = 512
RANK = 16
FF = 5632
SPAN = 64
OWN_CAP = 1024
TOK_DEV = 640
OWNERS = 8
TOKENS = 5120


def owner_plan(key):
    base_key = jax.random.fold_in(key, 4711)
    keys_list = jax.random.split(base_key, 6)
    half_count = OWNERS // 2
    spread = OWN_CAP - TOK_DEV
    offsets = jax.random.randint(keys_list[0], (half_count,), 0, spread + 1).astype(jnp.int32)
    offsets = offsets.at[0].set(spread)
    paired = jnp.stack([TOK_DEV + offsets, TOK_DEV - offsets], axis=1).reshape(OWNERS)
    shuffled_loads = paired[jax.random.permutation(keys_list[1], OWNERS)].astype(jnp.int32)
    full_place = jnp.argmax((shuffled_loads == OWN_CAP).astype(jnp.int32)).astype(jnp.int32)
    owner_loads = shuffled_loads.at[full_place].set(shuffled_loads[OWNERS - 1]).at[OWNERS - 1].set(OWN_CAP)
    owner_loads = owner_loads.astype(jnp.int32)
    first_len = jax.random.randint(keys_list[2], (OWNERS,), 0, owner_loads // 2 + 1).astype(jnp.int32)
    remain = owner_loads - first_len
    second_len = jax.random.randint(keys_list[3], (OWNERS,), 0, remain // 2 + 1).astype(jnp.int32)
    is_full = owner_loads == OWN_CAP
    lengths = jnp.stack([jnp.where(is_full, owner_loads, first_len), jnp.where(is_full, 0, second_len), jnp.where(is_full, 0, remain - second_len)], axis=1).astype(jnp.int32)
    load_ends = jnp.cumsum(owner_loads).astype(jnp.int32)
    starts = load_ends - owner_loads
    positions = jnp.arange(TOKENS, dtype=jnp.int32)
    owner_of = jnp.sum((positions[:, None] >= load_ends[None, :]).astype(jnp.int32), axis=1)
    slot_index = owner_of * OWN_CAP + positions - starts[owner_of]
    rotation = jax.random.randint(keys_list[4], (), 0, OWNERS).astype(jnp.int32)
    source = (positions + rotation) % OWNERS
    column = positions // OWNERS

    def shuffled(sub_key):
        return jax.random.permutation(sub_key, TOK_DEV).astype(jnp.int32)
    orders = jax.vmap(shuffled)(jax.random.split(keys_list[5], OWNERS))
    arrival = source * TOK_DEV + orders[source, column]
    token_slots = jnp.zeros((TOKENS,), jnp.int32).at[arrival].set(slot_index.astype(jnp.int32))
    return (lengths, token_slots)


def draw_token_slots(key, part):
    return owner_plan(key)[1]


def draw_lengths(key, part):
    return owner_plan(key)[0]


def block_levels(key, dims, cuts, least, high):
    gain, own = 1.0, jax.random.fold_in(key, 6)
    for dim, parts in cuts:
        draws = jnp.exp(jax.random.uniform(jax.random.fold_in(own, dim), (parts,), jnp.float32, least / len(cuts), high / len(cuts)))
        gain = gain * jnp.repeat(draws, dims[dim] // parts).reshape([-1 if axis == dim else 1 for axis in range(len(dims))])
    return gain


def noise(key, dims, scale, most, cuts=(), held_as=jnp.bfloat16):
    level = block_levels(key, dims, cuts, -0.22, 0.18) if cuts else 1.0
    result = jax.random.normal(key, dims, jnp.float32) * scale * level
    return jnp.minimum(jnp.maximum(result, -most), most).astype(held_as)


def setup_inputs(seed: int = 0) -> dict:
    keys = jax.random.split(jax.random.key(seed), 19)
    return {
        "tokens": noise(keys[0], (TOKENS, D), 1.0, 6.0, ((0, 8),)),
        "cotangent": noise(keys[1], (TOKENS, D), 1.0, 6.0, ((0, 8),)),
        "token_slots": draw_token_slots(jax.random.fold_in(keys[18], 71), 0),
        "lengths": draw_lengths(jax.random.fold_in(keys[18], 71), 0),
        "mixer_gain": jnp.clip(1.0 + 0.1 * jax.random.normal(keys[4], (D,), jnp.float32), 0.5, 1.5).astype(jnp.bfloat16),
        "query_weight": noise(keys[5], (D, HEADS * DK), D ** -0.5, 0.125, ((1, 4),)),
        "key_weight": noise(keys[6], (D, HEADS * DK), D ** -0.5, 0.125, ((1, 4),)),
        "value_weight": noise(keys[7], (D, HEADS * DV), D ** -0.5, 0.125, ((1, 4),)),
        "gate_weight": noise(keys[8], (D, HEADS * DV), D ** -0.5, 0.125, ((1, 4),)),
        "decay_down": noise(keys[9], (D, RANK), D ** -0.5, 0.125),
        "decay_up": noise(keys[10], (HEADS * DK, RANK), RANK ** -0.5, 1.5, ((0, 4),)),
        "decay_bias": jnp.clip(-3.0 + 8.0 * jax.random.uniform(keys[11], (HEADS * DK,), jnp.float32) ** block_levels(keys[11], (HEADS * DK,), ((0, 4),), -0.2, 0.2), -3.0, 5.0).astype(jnp.bfloat16),
        "head_gain": jnp.clip(1.0 + 0.1 * jax.random.normal(keys[12], (DV,), jnp.float32), 0.5, 1.5).astype(jnp.bfloat16),
        "out_weight": noise(keys[13], (HEADS * DV, D), (HEADS * DV) ** -0.5, 0.125, ((0, 4),)),
        "feed_gain": jnp.clip(1.0 + 0.1 * jax.random.normal(keys[14], (D,), jnp.float32), 0.5, 1.5).astype(jnp.bfloat16),
        "feed_gate": noise(keys[15], (D, FF), D ** -0.5, 0.125, ((1, 4),)),
        "feed_up": noise(keys[16], (D, FF), D ** -0.5, 0.125, ((1, 4),)),
        "feed_down": noise(keys[17], (FF, D), FF ** -0.5, 0.078125, ((0, 4),)),
    }


epsilon = 1e-06
head_floor = 1.0
highest_precision = lax.Precision.HIGHEST

@jax.custom_vjp
def low(v):
    return lax.optimization_barrier(v.astype(jnp.bfloat16)).astype(jnp.float32)

@jax.custom_vjp
def low_back(v):
    return v

def low_keep(v):
    return (low(v), None)

def low_pass(kept, grad):
    return (grad,)

def back_keep(v):
    return (v, None)

def back_low(kept, grad):
    return (low(grad),)
low.defvjp(low_keep, low_pass)
low_back.defvjp(back_keep, back_low)

def segment_ids(lengths_row, row_count):
    boundary = jnp.cumsum(lengths_row).astype(jnp.int32)
    position = jnp.arange(row_count, dtype=jnp.int32)
    return lax.optimization_barrier(jnp.sum((position[:, None] >= boundary[None, :]).astype(jnp.int32), axis=1)).astype(jnp.int32)

def norm_rows(row_block, gain_row):
    return row_block * lax.rsqrt(lax.optimization_barrier(jnp.mean(row_block * row_block, axis=-1, keepdims=True)) + epsilon) * gain_row

def gla_head(query_rows, key_rows, value_rows, gate_logits, out_gate, head_gain, segments):
    row_count = query_rows.shape[0]
    key_width = query_rows.shape[1]
    value_width = value_rows.shape[1]
    blocks = row_count // SPAN
    log_decay = (jax.nn.log_sigmoid(gate_logits) / 16.0).reshape(blocks, SPAN, key_width)
    cumulative = jnp.cumsum(log_decay, axis=1)
    span_total = cumulative[:, SPAN - 1, :]
    queries = (query_rows * float(key_width) ** (-0.5)).reshape(blocks, SPAN, key_width)
    key_block = key_rows.reshape(blocks, SPAN, key_width)
    value_vectors = value_rows.reshape(blocks, SPAN, value_width)
    labels = segments.reshape(blocks, SPAN)
    before = jnp.concatenate([jnp.full((1,), -1, jnp.int32), labels[:-1, SPAN - 1]])
    state_carried_in = (labels == before[:, None]).astype(jnp.float32)
    tail_mask = (labels == labels[:, SPAN - 1:]).astype(jnp.float32)
    position = jnp.arange(SPAN, dtype=jnp.int32)
    allowed = (position[None, :, None] >= position[None, None, :]) & (labels[:, :, None] == labels[:, None, :])
    query_decay_scaled = queries * jnp.exp(cumulative)
    key_grown = key_block * jnp.exp(-cumulative)
    key_final = key_block * jnp.exp(span_total[:, None, :] - cumulative) * tail_mask[:, :, None]
    score_matrix = jnp.einsum('nid,njd->nij', query_decay_scaled, key_grown, precision=highest_precision)
    score_matrix = jnp.where(allowed, score_matrix, 0.0)
    inside_span_part = jnp.einsum('kgp,kpc->kgc', score_matrix, value_vectors, precision=highest_precision)
    updates = jnp.einsum('njd,nje->nde', key_final, value_vectors, precision=highest_precision)

    def advance(carry_state, inputs):
        update, decay_total, keep_flag = inputs
        return (keep_flag * jnp.exp(decay_total)[:, None] * carry_state + update, carry_state)
    _, state_entering_span = lax.scan(advance, jnp.zeros((key_width, value_width), jnp.float32), (updates, span_total, state_carried_in[:, SPAN - 1]))
    cross_span_part = jnp.einsum('rsm,rmh->rsh', query_decay_scaled * state_carried_in[:, :, None], state_entering_span, precision=highest_precision)
    output = (inside_span_part + cross_span_part).reshape(row_count, value_width)
    scaling = lax.rsqrt(lax.optimization_barrier(jnp.mean(output * output, axis=-1, keepdims=True)) + head_floor)
    return output * scaling * head_gain * jax.nn.silu(out_gate)

def owner_layer(params, owner_rows, labels):
    mixer_gain, query_weight, key_weight, value_weight, gate_weight, decay_down, decay_up, decay_bias, head_gain, out_weight, feed_gain, feed_gate, feed_up, feed_down = params
    row_count = owner_rows.shape[0]
    normed = low(norm_rows(owner_rows, mixer_gain))

    def project(weight):
        return jnp.dot(normed, weight, precision=highest_precision)
    queries = low(low_back(project(query_weight)))
    keys_all = low(low_back(project(key_weight)))
    value_vectors = low(low_back(project(value_weight)))
    gate_pre = low_back(project(gate_weight))
    latent = project(decay_down)
    logits = lax.dot_general(latent, decay_up, (((1,), (1,)), ((), ())), precision=highest_precision) + decay_bias

    def split_heads(matrix):
        return matrix.reshape(row_count, HEADS, -1).transpose(1, 0, 2)
    gated = jax.vmap(gla_head, in_axes=(0, 0, 0, 0, 0, None, None))(split_heads(queries), split_heads(keys_all), split_heads(value_vectors), split_heads(logits), split_heads(gate_pre), head_gain, labels)
    gated = low(gated.transpose(1, 0, 2).reshape(row_count, -1))
    hidden = owner_rows + low_back(jnp.dot(gated, out_weight, precision=highest_precision))
    feed_normed = low(norm_rows(hidden, feed_gain))
    gate_hidden = low_back(jnp.dot(feed_normed, feed_gate, precision=highest_precision))
    up_hidden = low_back(jnp.dot(feed_normed, feed_up, precision=highest_precision))
    active = low(jax.nn.silu(gate_hidden) * up_hidden)
    return hidden + low_back(jnp.dot(active, feed_down, precision=highest_precision))

def reference(tokens, cotangent, token_slots, lengths, mixer_gain, query_weight, key_weight, value_weight, gate_weight, decay_down, decay_up, decay_bias, head_gain, out_weight, feed_gain, feed_gate, feed_up, feed_down):
    weights = tuple((weight_arg.astype(jnp.float32) for weight_arg in (mixer_gain, query_weight, key_weight, value_weight, gate_weight, decay_down, decay_up, decay_bias, head_gain, out_weight, feed_gain, feed_gate, feed_up, feed_down)))

    def labels_of(lengths_row):
        return segment_ids(lengths_row, OWN_CAP)
    all_labels = jax.vmap(labels_of)(lengths)

    def forward(token_rows, weight_set):
        flat_rows = jnp.zeros((OWNERS * OWN_CAP, D), jnp.float32).at[token_slots].set(token_rows)
        owner_grid = flat_rows.reshape(OWNERS, OWN_CAP, D)

        def per_owner(carry_value, owner_pair):
            return (carry_value, jax.checkpoint(owner_layer)(weight_set, owner_pair[0], owner_pair[1]))
        _, results = lax.scan(per_owner, jnp.zeros((), jnp.float32), (owner_grid, all_labels))
        return results.reshape(OWNERS * OWN_CAP, D)[token_slots]
    layer_out, pullback = jax.vjp(forward, tokens.astype(jnp.float32), weights)
    token_grad, grads = pullback(cotangent.astype(jnp.float32))
    return (layer_out.astype(jnp.bfloat16), token_grad.astype(jnp.bfloat16), grads[0], grads[1], grads[2], grads[3], grads[4], grads[5], grads[6].reshape(HEADS, DK, RANK), grads[7].reshape(HEADS, DK), grads[8], grads[9].reshape(HEADS, DV, D), grads[10], grads[11], grads[12], grads[13].reshape(HEADS, FF // HEADS, D))
```

```python
import functools

import jax
import jax.numpy as jnp
from jax import lax
from jax.experimental import pallas as pl
from jax.experimental.pallas import tpu as pltpu
from jax.sharding import PartitionSpec as P

OWN_CAP = 1024
SPAN = 128
LANES = 128
epsilon = 1e-06
head_floor = 1.0

f32 = jnp.float32
bf16 = jnp.bfloat16
MESH = pl.DeviceIdType.MESH


def rows_dot(left, right):
    return lax.dot_general(left, right, (((0,), (0,)), ((), ())), preferred_element_type=f32)


def dot_t(left, right):
    return lax.dot_general(left, right, (((1,), (1,)), ((), ())), preferred_element_type=f32)


def dot(left, right):
    return jnp.dot(left, right, preferred_element_type=f32)


def span_terms(first, ends, logits):
    rows = logits.shape[0]

    def label(position):
        count = jnp.zeros_like(position)
        for end in ends:
            count = count + (position >= end).astype(jnp.int32)
        return count

    log_decay = jax.nn.log_sigmoid(logits) * (1.0 / 16.0)
    row = lax.broadcasted_iota(jnp.int32, (rows, rows), 0)
    column = lax.broadcasted_iota(jnp.int32, (rows, rows), 1)
    lower = (row >= column).astype(f32)
    cumulative = jnp.dot(
        lower, log_decay, precision=lax.Precision.HIGHEST, preferred_element_type=f32
    )
    total = cumulative[rows - 1 :, :]
    middle = cumulative[rows // 2 - 1 : rows // 2, :]
    label_column = label(first + lax.broadcasted_iota(jnp.int32, (rows, 1), 0))
    label_row = label(first + lax.broadcasted_iota(jnp.int32, (1, rows), 1))
    before = jnp.where(first > 0, label(first - 1), -1)
    last = label(first + rows - 1)
    carried = (label_column == before).astype(f32)
    tail = (label_column == last).astype(f32)
    keep = (before == last).astype(f32)
    allowed = (row >= column) & (label_column == label_row)
    return log_decay, cumulative, total, middle, carried, tail, keep, allowed


def recur_forward_kernel(
    dk, dv, slot_row_ref, slot_column_ref, lengths_ref, up_ref, bias_ref, arrived_ref,
    out_ref, held_ref, states_ref, state, result,
):
    step = pl.program_id(0)
    first = step * SPAN
    end0 = lengths_ref[0, 0]
    end1 = end0 + lengths_ref[0, 1]
    end2 = end1 + lengths_ref[0, 2]
    slots = slot_row_ref.shape[1]

    @pl.when(step == 0)
    def _():
        state[...] = jnp.zeros_like(state)

    position = first + lax.broadcasted_iota(jnp.int32, (SPAN, slots), 0)
    place = (slot_row_ref[...] == position).astype(f32).astype(bf16)
    held = dot(place, arrived_ref[...]).astype(bf16)
    held_ref[...] = held
    queries = held[:, :dk].astype(f32) * (float(dk) ** -0.5)
    keys = held[:, dk : 2 * dk].astype(f32)
    values = held[:, 2 * dk : 2 * dk + dv]
    logits = dot(held[:, 2 * dk + dv :], up_ref[...]) + bias_ref[...]
    _, cumulative, total, middle, carried, tail, keep, allowed = span_terms(
        first, (end0, end1, end2), logits
    )
    query_mid = (queries * jnp.exp(cumulative - middle)).astype(bf16)
    key_mid = (keys * jnp.exp(middle - cumulative)).astype(bf16)
    query_start = (queries * jnp.exp(cumulative) * carried).astype(bf16)
    key_end = (keys * jnp.exp(total - cumulative) * tail).astype(bf16)
    scores = jnp.where(allowed, dot_t(query_mid, key_mid), 0.0).astype(bf16)
    entering = state[...]
    entering_low = entering.astype(bf16)
    states_ref[0] = entering_low
    attended = dot(scores, values) + dot(query_start, entering_low)
    result[pl.ds(pl.multiple_of(first, SPAN), SPAN), :] = attended.astype(bf16)
    decay_column = jnp.transpose(jnp.broadcast_to(keep * jnp.exp(total), (8, dk)))[:, :1]
    state[...] = decay_column * entering + rows_dot(key_end, values)

    @pl.when(step == pl.num_programs(0) - 1)
    def _():
        return_rows(slot_column_ref, result, out_ref)


def return_rows(slot_column_ref, source, out_ref):
    positions = source.shape[0]
    block = 256

    def body(i, carry):
        at = pl.ds(pl.multiple_of(i * block, block), block)
        column = lax.broadcasted_iota(jnp.int32, (block, positions), 1)
        pick = (slot_column_ref[at, :] == column).astype(f32).astype(bf16)
        out_ref[at, :] = dot(pick, source[...]).astype(out_ref.dtype)
        return carry

    lax.fori_loop(0, out_ref.shape[0] // block, body, 0)


def recur_backward_kernel(
    dk, dv, slot_row_ref, slot_column_ref, lengths_ref, up_ref, bias_ref, down_ref, arrived_ref,
    held_ref, states_ref, out_ref, grad_up_ref, grad_bias_ref, d_state, result,
):
    step = pl.num_programs(0) - 1 - pl.program_id(0)
    first = step * SPAN
    end0 = lengths_ref[0, 0]
    end1 = end0 + lengths_ref[0, 1]
    end2 = end1 + lengths_ref[0, 2]
    slots = slot_row_ref.shape[1]

    @pl.when(pl.program_id(0) == 0)
    def _():
        d_state[...] = jnp.zeros_like(d_state)
        grad_up_ref[...] = jnp.zeros_like(grad_up_ref)
        grad_bias_ref[...] = jnp.zeros_like(grad_bias_ref)

    position = first + lax.broadcasted_iota(jnp.int32, (SPAN, slots), 0)
    place = (slot_row_ref[...] == position).astype(f32).astype(bf16)
    d_out = dot(place, arrived_ref[...]).astype(bf16)
    scale = float(dk) ** -0.5
    queries = held_ref[:, :dk].astype(f32) * scale
    keys = held_ref[:, dk : 2 * dk].astype(f32)
    values = held_ref[:, 2 * dk : 2 * dk + dv]
    latent = held_ref[:, 2 * dk + dv :]
    logits = dot(latent, up_ref[...]) + bias_ref[...]
    _, cumulative, total, middle, carried, tail, keep, allowed = span_terms(
        first, (end0, end1, end2), logits
    )
    grow_query = jnp.exp(cumulative - middle)
    grow_key = jnp.exp(middle - cumulative)
    start_decay = jnp.exp(cumulative) * carried
    end_decay = jnp.exp(total - cumulative) * tail
    query_mid = (queries * grow_query).astype(bf16)
    key_mid = (keys * grow_key).astype(bf16)
    query_start = (queries * start_decay).astype(bf16)
    key_end = (keys * end_decay).astype(bf16)
    scores = jnp.where(allowed, dot_t(query_mid, key_mid), 0.0).astype(bf16)
    d_scores = jnp.where(allowed, dot_t(d_out, values), 0.0).astype(bf16)
    leaving = d_state[...]
    leaving_low = leaving.astype(bf16)
    entering = states_ref[0]
    d_values = rows_dot(scores, d_out) + dot(key_end, leaving_low)
    d_queries = dot(d_scores, key_mid) * grow_query + dot_t(d_out, entering) * start_decay
    d_key_end = dot_t(values, leaving_low) * end_decay
    d_keys = rows_dot(d_scores, query_mid) * grow_key + d_key_end
    kept = keep * jnp.exp(total)
    state_pair = jnp.sum(entering.astype(f32) * leaving, axis=1, keepdims=True)
    state_row = jnp.transpose(jnp.broadcast_to(state_pair, (dk, LANES)))[:1, :]
    d_total = jnp.sum(keys * d_key_end, axis=0, keepdims=True) + kept * state_row
    d_cumulative = queries * d_queries - keys * d_keys
    row = lax.broadcasted_iota(jnp.int32, (SPAN, SPAN), 0)
    column = lax.broadcasted_iota(jnp.int32, (SPAN, SPAN), 1)
    upper = (row <= column).astype(f32)
    d_log_decay = (
        jnp.dot(upper, d_cumulative, precision=lax.Precision.HIGHEST, preferred_element_type=f32)
        + d_total
    )
    d_logits = d_log_decay * (1.0 / 16.0) * jax.nn.sigmoid(-logits)
    grad_bias_ref[...] += jnp.broadcast_to(jnp.sum(d_logits, axis=0, keepdims=True), (8, dk))
    d_logits_high = d_logits.astype(bf16)
    d_logits_low = (d_logits - d_logits_high.astype(f32)).astype(bf16)
    grad_up_ref[...] += rows_dot(d_logits_high, latent) + rows_dot(d_logits_low, latent)
    d_latent = dot(d_logits_high, down_ref[...]) + dot(d_logits_low, down_ref[...])
    high = d_latent.astype(bf16).astype(f32)
    lane = lax.broadcasted_iota(jnp.int32, d_latent.shape, 1)
    d_latent_packed = jnp.where(lane < LANES // 4, high, d_latent - high)
    at = pl.ds(pl.multiple_of(first, SPAN), SPAN)
    result[at, :dk] = (d_queries * scale).astype(bf16)
    result[at, dk : 2 * dk] = d_keys.astype(bf16)
    result[at, 2 * dk : 2 * dk + dv] = d_values.astype(bf16)
    result[at, 2 * dk + dv :] = d_latent_packed.astype(bf16)
    kept_column = jnp.transpose(jnp.broadcast_to(kept, (8, dk)))[:, :1]
    d_state[...] = kept_column * leaving + rows_dot(query_start, d_out)

    @pl.when(step == 0)
    def _():
        return_rows(slot_column_ref, result, out_ref)


def whole(shape):
    return pl.BlockSpec(shape, lambda i: (0,) * len(shape))


def recur_forward(slot_map, lengths, up_wide, bias, arrived, dk, dv):
    slots, width = arrived.shape
    steps = OWN_CAP // SPAN
    return pl.pallas_call(
        functools.partial(recur_forward_kernel, dk, dv),
        grid=(steps,),
        in_specs=[
            whole((1, slots)),
            whole((slots, 1)),
            pl.BlockSpec(memory_space=pltpu.SMEM),
            whole((LANES, dk)),
            whole((1, dk)),
            whole((slots, width)),
        ],
        out_specs=[
            whole((slots, dv)),
            pl.BlockSpec((SPAN, width), lambda i: (i, 0)),
            pl.BlockSpec((1, dk, dv), lambda i: (i, 0, 0)),
        ],
        out_shape=[
            jax.ShapeDtypeStruct((slots, dv), bf16),
            jax.ShapeDtypeStruct((OWN_CAP, width), bf16),
            jax.ShapeDtypeStruct((steps, dk, dv), bf16),
        ],
        scratch_shapes=[pltpu.VMEM((dk, dv), f32), pltpu.VMEM((OWN_CAP, dv), bf16)],
        compiler_params=pltpu.CompilerParams(vmem_limit_bytes=40 << 20),
        cost_estimate=pl.CostEstimate(
            flops=6_000_000_000, bytes_accessed=10_000_000, transcendentals=2_000_000
        ),
        name="recur_forward",
    )(slot_map.reshape(1, -1), slot_map.reshape(-1, 1), lengths, up_wide, bias, arrived)


def recur_backward(slot_map, lengths, up_wide, bias, down_wide, arrived, held, states, dk, dv):
    slots = arrived.shape[0]
    width = held.shape[1]
    steps = OWN_CAP // SPAN
    return pl.pallas_call(
        functools.partial(recur_backward_kernel, dk, dv),
        grid=(steps,),
        in_specs=[
            whole((1, slots)),
            whole((slots, 1)),
            pl.BlockSpec(memory_space=pltpu.SMEM),
            whole((LANES, dk)),
            whole((1, dk)),
            whole((dk, LANES)),
            whole((slots, dv)),
            pl.BlockSpec((SPAN, width), lambda i: (steps - 1 - i, 0)),
            pl.BlockSpec((1, dk, dv), lambda i: (steps - 1 - i, 0, 0)),
        ],
        out_specs=[whole((slots, width)), whole((dk, LANES)), whole((8, dk))],
        out_shape=[
            jax.ShapeDtypeStruct((slots, width), bf16),
            jax.ShapeDtypeStruct((dk, LANES), f32),
            jax.ShapeDtypeStruct((8, dk), f32),
        ],
        scratch_shapes=[pltpu.VMEM((dk, dv), f32), pltpu.VMEM((OWN_CAP, width), bf16)],
        compiler_params=pltpu.CompilerParams(vmem_limit_bytes=40 << 20),
        cost_estimate=pl.CostEstimate(
            flops=12_000_000_000, bytes_accessed=12_000_000, transcendentals=4_000_000
        ),
        name="recur_backward",
    )(
        slot_map.reshape(1, -1), slot_map.reshape(-1, 1), lengths, up_wide, bias, down_wide,
        arrived, held, states,
    )


CHUNK = 32


def line_kernel(mode, n, *refs):
    share_ref, x_ref, base_ref, gain_ref = refs[:4]
    if mode == "norm":
        out_ref, kept_ref = refs[4:6]
        scratch = refs[6:]
    elif mode == "back":
        out_ref, kept_ref, gain_grad_ref = refs[4:7]
        scratch = refs[7:]
    else:
        out_ref = refs[4]
        kept_ref = None
        scratch = refs[5:]
    up_in, up_out, down_in, down_out, sems = scratch
    me = lax.axis_index("tensor")
    half = up_in.shape[0]
    count = half // CHUNK

    barrier = pltpu.get_barrier_semaphore()

    @pl.when(me > 0)
    def _():
        pl.semaphore_signal(barrier, inc=1, device_id={"tensor": me - 1}, device_id_type=MESH)

    @pl.when(me < n - 1)
    def _():
        pl.semaphore_signal(barrier, inc=1, device_id={"tensor": me + 1}, device_id_type=MESH)

    inside = (me > 0) & (me < n - 1)

    @pl.when(inside)
    def _():
        pl.semaphore_wait(barrier, 2)

    @pl.when(jnp.logical_not(inside))
    def _():
        pl.semaphore_wait(barrier, 1)

    def at(g):
        return pl.ds(pl.multiple_of(g * CHUNK, CHUNK), CHUNK)

    def low(g):
        return pl.ds(pl.multiple_of(half + g * CHUNK, CHUNK), CHUNK)

    def right(source, target, lane, g):
        return pltpu.make_async_remote_copy(
            source, target, sems.at[2 * lane, g], sems.at[2 * lane + 1, g],
            device_id={"tensor": jnp.minimum(me + 1, n - 1)}, device_id_type=MESH,
        )

    def left(source, target, lane, g):
        return pltpu.make_async_remote_copy(
            source, target, sems.at[2 * lane, g], sems.at[2 * lane + 1, g],
            device_id={"tensor": jnp.maximum(me - 1, 0)}, device_id_type=MESH,
        )

    def up_copy(g):
        return right(up_out.at[at(g), :], up_in.at[at(g), :], 0, g)

    def down_copy(g):
        return left(down_out.at[at(g), :], down_in.at[at(g), :], 1, g)

    def first_up_copy(g):
        return right(share_ref.at[at(g), :], up_in.at[at(g), :], 0, g)

    def first_down_copy(g):
        return left(share_ref.at[low(g), :], down_in.at[at(g), :], 1, g)

    def up_back_copy(g):
        return left(out_ref.at[at(g), :], out_ref.at[at(g), :], 2, g)

    def down_back_copy(g):
        return right(out_ref.at[low(g), :], out_ref.at[low(g), :], 3, g)

    if mode == "back":
        gain_grad_ref[...] = jnp.zeros_like(gain_grad_ref)

    def finish(total, g, place):
        base = base_ref[at(g), :].astype(f32)
        if mode == "sum":
            out_ref[place, :] = (base + total).astype(out_ref.dtype)
            return
        if mode == "norm":
            hidden = base + total
            kept_ref[at(g), :] = hidden
            scaling = lax.rsqrt(jnp.mean(hidden * hidden, axis=1, keepdims=True) + epsilon)
            out_ref[place, :] = (hidden * scaling * gain_ref[...]).astype(out_ref.dtype)
            return
        rows = x_ref[at(g), :].astype(f32)
        scaling = lax.rsqrt(jnp.mean(rows * rows, axis=1, keepdims=True) + epsilon)
        unit = rows * scaling
        gained = gain_ref[...] * total
        grad = base + scaling * (gained - unit * jnp.mean(gained * unit, axis=1, keepdims=True))
        kept_ref[at(g), :] = grad
        out_ref[place, :] = grad.astype(out_ref.dtype)
        term = total * unit
        part = term[0:8, :]
        for i in range(1, CHUNK // 8):
            part = part + term[8 * i : 8 * i + 8, :]
        gain_grad_ref[...] += part

    @pl.when(me == 0)
    def _():
        @pl.loop(0, count)
        def _(g):
            first_up_copy(g).start()

    @pl.when(me == n - 1)
    def _():
        @pl.loop(0, count)
        def _(g):
            first_down_copy(g).start()

    @pl.loop(0, count + n - 2)
    def _(step):
        g_up = step - (me - 1)

        @pl.when((me > 0) & (g_up >= 0) & (g_up < count))
        def _():
            up_copy(g_up).wait_recv()
            total = up_in[at(g_up), :].astype(f32) + share_ref[at(g_up), :].astype(f32)

            @pl.when(me < n - 1)
            def _():
                up_out[at(g_up), :] = total.astype(bf16)
                up_copy(g_up).start()

            @pl.when(me == n - 1)
            def _():
                finish(total, g_up, at(g_up))
                up_back_copy(g_up).start()

        g_down = step - (n - 2 - me)

        @pl.when((me < n - 1) & (g_down >= 0) & (g_down < count))
        def _():
            down_copy(g_down).wait_recv()
            total = down_in[at(g_down), :].astype(f32) + share_ref[low(g_down), :].astype(f32)

            @pl.when(me > 0)
            def _():
                down_out[at(g_down), :] = total.astype(bf16)
                down_copy(g_down).start()

            @pl.when(me == 0)
            def _():
                finish(total, g_down, low(g_down))
                down_back_copy(g_down).start()

    @pl.loop(0, count + n - 2)
    def _(step):
        g_up = step - (n - 2 - me)

        @pl.when((me < n - 1) & (g_up >= 0) & (g_up < count))
        def _():
            up_back_copy(g_up).wait_recv()

            @pl.when(me > 0)
            def _():
                up_back_copy(g_up).start()

        g_down = step - (me - 1)

        @pl.when((me > 0) & (g_down >= 0) & (g_down < count))
        def _():
            down_back_copy(g_down).wait_recv()

            @pl.when(me < n - 1)
            def _():
                down_back_copy(g_down).start()

    @pl.loop(0, count)
    def _(g):
        @pl.when(me < n - 1)
        def _():
            up_copy(g).wait_send()
            down_back_copy(g).wait_send()

        @pl.when(me > 0)
        def _():
            down_copy(g).wait_send()
            up_back_copy(g).wait_send()


def line_sum(mode, call, n, share, x_own, base_own, gain):
    rows, width = share.shape
    half = rows // 2
    vmem = pl.BlockSpec(memory_space=pltpu.VMEM)
    outs = [jax.ShapeDtypeStruct((rows, width), bf16)]
    if mode != "sum":
        outs.append(jax.ShapeDtypeStruct((half, width), f32))
    if mode == "back":
        outs.append(jax.ShapeDtypeStruct((8, width), f32))
    return pl.pallas_call(
        functools.partial(line_kernel, mode, n),
        in_specs=[vmem] * 4,
        out_specs=[vmem] * len(outs),
        out_shape=outs,
        scratch_shapes=[
            pltpu.VMEM((half, width), bf16),
            pltpu.VMEM((half, width), bf16),
            pltpu.VMEM((half, width), bf16),
            pltpu.VMEM((half, width), bf16),
            pltpu.SemaphoreType.DMA((8, half // CHUNK)),
        ],
        compiler_params=pltpu.CompilerParams(
            collective_id=call, has_side_effects=True, vmem_limit_bytes=40 << 20
        ),
        cost_estimate=pl.CostEstimate(
            flops=10_000_000, bytes_accessed=200_000_000, transcendentals=0
        ),
        name="line_" + mode,
    )(share, x_own, base_own, gain)


def per_device(
    tokens,
    cotangent,
    token_slots,
    lengths,
    mixer_gain,
    query_weight,
    key_weight,
    value_weight,
    gate_weight,
    decay_down,
    decay_up,
    decay_bias,
    head_gain,
    out_weight,
    feed_gain,
    feed_gate,
    feed_up,
    feed_down,
):
    groups = lax.axis_size("dp")
    lines = lax.axis_size("tensor")
    member = lax.axis_index("dp")
    place = lax.axis_index("tensor")
    count, width = tokens.shape
    cap = OWN_CAP // groups
    slots = groups * cap
    dk = query_weight.shape[1]
    dv = value_weight.shape[1]
    rank = decay_up.shape[1]
    parity = lax.rem(member, 2)
    pairs = [(i, i ^ 1) for i in range(groups)]
    same_parity = [[i for i in range(groups) if i % 2 == b] for b in range(2)]

    owners = (token_slots // OWN_CAP).reshape(groups, count)
    mine = (owners == member).astype(bf16)
    my_slots = lax.dynamic_slice_in_dim(token_slots, member * count, count)
    my_owner = my_slots // OWN_CAP
    chosen = (my_owner[None, :] == jnp.arange(groups, dtype=jnp.int32)[:, None]).astype(bf16)
    index = jnp.arange(count, dtype=jnp.int32)
    before = (index[:, None] < index[None, :]).astype(bf16)
    ranks = dot(jnp.concatenate([mine, chosen], axis=0), before).astype(jnp.int32)
    recv_rank, send_rank = ranks[:groups], ranks[groups:]
    hit = (recv_rank[:, None, :] == jnp.arange(cap, dtype=jnp.int32)[None, :, None]) & (
        owners == member
    )[:, None, :]
    local = (token_slots % OWN_CAP).reshape(groups, count)
    slot_map = (
        jnp.sum(jnp.where(hit, local[:, None, :] - OWN_CAP, 0), axis=2) + OWN_CAP
    ).reshape(slots)
    send_pos = my_owner * cap + jnp.sum(
        jnp.where(chosen > 0, send_rank, 0), axis=0, dtype=jnp.int32
    )
    slot_ids = jnp.arange(slots, dtype=jnp.int32)
    pack = (slot_ids[:, None] == send_pos[None, :]).astype(bf16)
    unpack = (send_pos[:, None] == slot_ids[None, :]).astype(bf16)

    def exchange(row_block):
        blocks = row_block.reshape(groups, cap, row_block.shape[1])
        moved = lax.all_to_all(blocks, "dp", split_axis=0, concat_axis=0, tiled=True)
        return moved.reshape(slots, row_block.shape[1])

    half = count // 2
    own_at = jnp.where(place == 0, half, 0)
    tokens_own = lax.dynamic_slice_in_dim(tokens, own_at, half)
    cotangent_own = lax.dynamic_slice_in_dim(cotangent, own_at, half)

    tokens_wide = tokens.astype(f32)
    mixer_gain_wide = mixer_gain.astype(f32)
    feed_gain_wide = feed_gain.astype(f32)
    normed = (
        tokens_wide
        * lax.rsqrt(jnp.mean(tokens_wide * tokens_wide, axis=-1, keepdims=True) + epsilon)
        * mixer_gain_wide
    ).astype(bf16)
    queries = dot(normed, query_weight).astype(bf16)
    keys_low = dot(normed, key_weight).astype(bf16)
    value_rows = dot(normed, value_weight).astype(bf16)
    gate_pre = dot(normed, gate_weight)
    third = LANES // 4
    down_pad = jnp.pad(decay_down, ((0, 0), (0, third - rank)))
    latent = dot(
        normed,
        jnp.concatenate([down_pad, down_pad, down_pad, jnp.zeros_like(down_pad)], axis=1),
    )
    latent_high = latent.astype(bf16)
    latent_rest = latent - latent_high.astype(f32)
    latent_mid = latent_rest.astype(bf16)
    latent_low = (latent_rest - latent_mid.astype(f32)).astype(bf16)
    lane = jnp.arange(LANES, dtype=jnp.int32)[None, :]
    latent_packed = jnp.where(
        lane < third, latent_high, jnp.where(lane < 2 * third, latent_mid, latent_low)
    )
    rows_out = jnp.concatenate([queries, keys_low, value_rows, latent_packed], axis=1)
    arrived = exchange(dot(pack, rows_out).astype(bf16))
    up_pad = jnp.pad(decay_up, ((0, 0), (0, third - rank)))
    up_wide = jnp.concatenate([up_pad, up_pad, up_pad, jnp.zeros_like(up_pad)], axis=1).T
    down_wide = jnp.concatenate(
        [up_pad, up_pad, jnp.zeros_like(up_pad), jnp.zeros_like(up_pad)], axis=1
    )
    bias = decay_bias.astype(f32).reshape(1, dk)
    attended_slots, held, states = recur_forward(
        slot_map, lengths, up_wide, bias, arrived, dk, dv
    )
    attended = dot(unpack, exchange(attended_slots))

    head_gain_wide = head_gain.astype(f32)

    def head_output(rows, gate_rows, gain_row):
        scaling = lax.rsqrt(jnp.mean(rows * rows, axis=-1, keepdims=True) + head_floor)
        return rows * scaling * gain_row * jax.nn.silu(gate_rows)

    gated_wide, head_back = jax.vjp(head_output, attended, gate_pre, head_gain_wide)
    gated = gated_wide.astype(bf16)
    mixer_share = dot(gated, out_weight).astype(bf16)
    feed_normed, hidden_own = line_sum(
        "norm", 1, lines, mixer_share, tokens_own, tokens_own, feed_gain_wide.reshape(1, -1)
    )

    gate_hidden = dot(feed_normed, feed_gate)
    up_hidden = dot(feed_normed, feed_up)
    d_active = dot_t(cotangent, feed_down)
    sigmoid_gate = jax.nn.sigmoid(gate_hidden)
    swish_gate = gate_hidden * sigmoid_gate
    active = (swish_gate * up_hidden).astype(bf16)
    d_gate_hidden = (
        d_active * up_hidden * sigmoid_gate * (1.0 + gate_hidden * (1.0 - sigmoid_gate))
    ).astype(bf16)
    d_up_hidden = (d_active * swish_gate).astype(bf16)
    feed_share = (dot_t(d_gate_hidden, feed_gate) + dot_t(d_up_hidden, feed_up)).astype(bf16)
    d_mixed, d_hidden_own, feed_gain_part = line_sum(
        "back", 2, lines, feed_share, hidden_own, cotangent_own, feed_gain_wide.reshape(1, -1)
    )

    d_gated = dot_t(d_mixed, out_weight)
    d_attended, d_gate_pre, head_gain_part = head_back(d_gated)
    d_gate_low = d_gate_pre.astype(bf16)
    d_arrived = exchange(dot(pack, d_attended.astype(bf16)).astype(bf16))
    d_slots, up_part, bias_part = recur_backward(
        slot_map, lengths, up_wide, bias, down_wide, d_arrived, held, states, dk, dv
    )
    d_rows = dot(unpack, exchange(d_slots)).astype(bf16)
    d_query_low = d_rows[:, :dk]
    d_key_low = d_rows[:, dk : 2 * dk]
    d_value_low = d_rows[:, 2 * dk : 2 * dk + dv]
    d_latent_low = d_rows[:, 2 * dk + dv :]
    down_both = jnp.concatenate(
        [down_pad, down_pad, jnp.zeros_like(down_pad), jnp.zeros_like(down_pad)], axis=1
    )
    normed_share = (
        dot_t(d_query_low, query_weight)
        + dot_t(d_key_low, key_weight)
        + dot_t(d_value_low, value_weight)
        + dot_t(d_gate_low, gate_weight)
        + dot_t(d_latent_low, down_both)
    ).astype(bf16)
    token_grad, _, mixer_gain_part = line_sum(
        "back", 3, lines, normed_share, tokens_own, d_hidden_own, mixer_gain_wide.reshape(1, -1)
    )
    layer_share = dot(active, feed_down).astype(bf16)
    (layer_out,) = line_sum(
        "sum", 4, lines, layer_share, tokens_own, hidden_own, feed_gain_wide.reshape(1, -1)
    )

    def halves(row_block, dims):
        split = row_block.reshape(row_block.shape[0], groups // 2, 2, dims // groups)
        keep = lax.dynamic_index_in_dim(split, parity, 2, keepdims=False)
        send = lax.dynamic_index_in_dim(split, 1 - parity, 2, keepdims=False)
        got = lax.ppermute(send, "dp", pairs)
        shape = (row_block.shape[0], dims // 2)
        return keep.reshape(shape), got.reshape(shape)

    def partner(row_block):
        return row_block, lax.ppermute(row_block, "dp", pairs)

    def summed_share(left, right):
        share = (rows_dot(left[0], right[0]) + rows_dot(left[1], right[1])).astype(bf16)
        rows = share.shape[0] // (groups // 2)
        blocks = share.reshape(groups // 2, rows, share.shape[1])
        moved = lax.all_to_all(
            blocks, "dp", split_axis=0, concat_axis=0, tiled=True, axis_index_groups=same_parity
        )
        return jnp.sum(moved.astype(f32), axis=0)

    feed_halves = halves(feed_normed, width)
    normed_halves = halves(normed, width)
    grad_feed_down = summed_share(halves(active, active.shape[1]), partner(cotangent))
    grad_feed_gate = summed_share(feed_halves, partner(d_gate_hidden))
    grad_feed_up = summed_share(feed_halves, partner(d_up_hidden))
    grad_out = summed_share(halves(gated, dv), partner(d_mixed))
    grad_query = summed_share(normed_halves, partner(d_query_low))
    grad_key = summed_share(normed_halves, partner(d_key_low))
    grad_value = summed_share(normed_halves, partner(d_value_low))
    grad_gate = summed_share(normed_halves, partner(d_gate_low))

    down_part = rows_dot(normed, d_latent_low)
    down_part = down_part[:, :rank] + down_part[:, third : third + rank]
    up_part = up_part[:, :rank] + up_part[:, third : third + rank] + (
        up_part[:, 2 * third : 2 * third + rank]
    )

    def by_owner(vector):
        return vector.reshape(groups, -1)

    over_all = jnp.concatenate(
        [
            by_owner(jnp.sum(mixer_gain_part, axis=0)),
            by_owner(jnp.sum(feed_gain_part, axis=0)),
            by_owner(head_gain_part),
            by_owner(down_part),
        ],
        axis=1,
    )
    over_owners = jnp.concatenate([by_owner(up_part), by_owner(bias_part[0])], axis=1)
    wide = over_all.shape[1]
    small = lax.psum_scatter(
        jnp.concatenate([over_all, over_owners], axis=1), "dp", scatter_dimension=0, tiled=True
    )[0]
    summed = lax.psum(small[:wide], "tensor")
    per = width // groups
    head_per = dv // groups
    return (
        layer_out,
        token_grad,
        summed[:per],
        grad_query,
        grad_key,
        grad_value,
        grad_gate,
        summed[2 * per + head_per :].reshape(per, rank),
        small[wide : wide + dk // groups * rank].reshape(1, dk // groups, rank),
        small[wide + dk // groups * rank :].reshape(1, dk // groups),
        summed[2 * per : 2 * per + head_per],
        grad_out[None],
        summed[per : 2 * per],
        grad_feed_gate,
        grad_feed_up,
        grad_feed_down[None],
    )


def solution(mesh):
    placed = (
        P("dp", None),
        P("dp", None),
        P(),
        P("dp", None),
        P(),
        P(None, "tensor"),
        P(None, "tensor"),
        P(None, "tensor"),
        P(None, "tensor"),
        P(),
        P("tensor", None),
        P("tensor"),
        P(),
        P("tensor", None),
        P(),
        P(None, "tensor"),
        P(None, "tensor"),
        P("tensor", None),
    )
    return jax.shard_map(
        per_device,
        mesh=mesh,
        in_specs=placed,
        out_specs=(
            P("dp", None),
            P("dp", None),
            P("dp"),
            P("dp", "tensor"),
            P("dp", "tensor"),
            P("dp", "tensor"),
            P("dp", "tensor"),
            P("dp", None),
            P("tensor", "dp", None),
            P("tensor", "dp"),
            P("dp"),
            P("tensor", "dp", None),
            P("dp"),
            P("dp", "tensor"),
            P("dp", "tensor"),
            P("tensor", "dp", None),
        ),
        check_vma=False,
    )
```

```python
import functools

import jax
import jax.numpy as jnp
from jax import lax
from jax.experimental import pallas as pl
from jax.experimental.pallas import tpu as pltpu
from jax.sharding import PartitionSpec as P

OWN_CAP = 1024
SPAN = 128
LANES = 128
epsilon = 1e-06
head_floor = 1.0

f32 = jnp.float32
bf16 = jnp.bfloat16
MESH = pl.DeviceIdType.MESH


def rows_dot(left, right):
    return lax.dot_general(left, right, (((0,), (0,)), ((), ())), preferred_element_type=f32)


def dot_t(left, right):
    return lax.dot_general(left, right, (((1,), (1,)), ((), ())), preferred_element_type=f32)


def dot(left, right):
    return jnp.dot(left, right, preferred_element_type=f32)


def span_terms(first, ends, logits):
    rows = logits.shape[0]

    def label(position):
        count = jnp.zeros_like(position)
        for end in ends:
            count = count + (position >= end).astype(jnp.int32)
        return count

    log_decay = jax.nn.log_sigmoid(logits) * (1.0 / 16.0)
    row = lax.broadcasted_iota(jnp.int32, (rows, rows), 0)
    column = lax.broadcasted_iota(jnp.int32, (rows, rows), 1)
    lower = (row >= column).astype(f32)
    cumulative = jnp.dot(
        lower, log_decay, precision=lax.Precision.HIGHEST, preferred_element_type=f32
    )
    total = cumulative[rows - 1 :, :]
    middle = cumulative[rows // 2 - 1 : rows // 2, :]
    label_column = label(first + lax.broadcasted_iota(jnp.int32, (rows, 1), 0))
    label_row = label(first + lax.broadcasted_iota(jnp.int32, (1, rows), 1))
    before = jnp.where(first > 0, label(first - 1), -1)
    last = label(first + rows - 1)
    carried = (label_column == before).astype(f32)
    tail = (label_column == last).astype(f32)
    keep = (before == last).astype(f32)
    allowed = (row >= column) & (label_column == label_row)
    return log_decay, cumulative, total, middle, carried, tail, keep, allowed


def recur_forward_kernel(
    dk, dv, slot_row_ref, slot_column_ref, lengths_ref, up_ref, bias_ref, arrived_ref,
    out_ref, held_ref, states_ref, state, result,
):
    step = pl.program_id(0)
    first = step * SPAN
    end0 = lengths_ref[0, 0]
    end1 = end0 + lengths_ref[0, 1]
    end2 = end1 + lengths_ref[0, 2]
    slots = slot_row_ref.shape[1]

    @pl.when(step == 0)
    def _():
        state[...] = jnp.zeros_like(state)

    position = first + lax.broadcasted_iota(jnp.int32, (SPAN, slots), 0)
    place = (slot_row_ref[...] == position).astype(f32).astype(bf16)
    held = dot(place, arrived_ref[...]).astype(bf16)
    held_ref[...] = held
    queries = held[:, :dk].astype(f32) * (float(dk) ** -0.5)
    keys = held[:, dk : 2 * dk].astype(f32)
    values = held[:, 2 * dk : 2 * dk + dv]
    logits = dot(held[:, 2 * dk + dv :], up_ref[...]) + bias_ref[...]
    _, cumulative, total, middle, carried, tail, keep, allowed = span_terms(
        first, (end0, end1, end2), logits
    )
    query_mid = (queries * jnp.exp(cumulative - middle)).astype(bf16)
    key_mid = (keys * jnp.exp(middle - cumulative)).astype(bf16)
    query_start = (queries * jnp.exp(cumulative) * carried).astype(bf16)
    key_end = (keys * jnp.exp(total - cumulative) * tail).astype(bf16)
    scores = jnp.where(allowed, dot_t(query_mid, key_mid), 0.0).astype(bf16)
    entering = state[...]
    entering_low = entering.astype(bf16)
    states_ref[0] = entering_low
    attended = dot(scores, values) + dot(query_start, entering_low)
    result[pl.ds(pl.multiple_of(first, SPAN), SPAN), :] = attended.astype(bf16)
    decay_column = jnp.transpose(jnp.broadcast_to(keep * jnp.exp(total), (8, dk)))[:, :1]
    state[...] = decay_column * entering + rows_dot(key_end, values)

    @pl.when(step == pl.num_programs(0) - 1)
    def _():
        return_rows(slot_column_ref, result, out_ref)


def return_rows(slot_column_ref, source, out_ref):
    positions = source.shape[0]
    block = 256

    def body(i, carry):
        at = pl.ds(pl.multiple_of(i * block, block), block)
        column = lax.broadcasted_iota(jnp.int32, (block, positions), 1)
        pick = (slot_column_ref[at, :] == column).astype(f32).astype(bf16)
        out_ref[at, :] = dot(pick, source[...]).astype(out_ref.dtype)
        return carry

    lax.fori_loop(0, out_ref.shape[0] // block, body, 0)


def recur_backward_kernel(
    dk, dv, slot_row_ref, slot_column_ref, lengths_ref, up_ref, bias_ref, down_ref, arrived_ref,
    held_ref, states_ref, out_ref, grad_up_ref, grad_bias_ref, d_state, result,
):
    step = pl.num_programs(0) - 1 - pl.program_id(0)
    first = step * SPAN
    end0 = lengths_ref[0, 0]
    end1 = end0 + lengths_ref[0, 1]
    end2 = end1 + lengths_ref[0, 2]
    slots = slot_row_ref.shape[1]

    @pl.when(pl.program_id(0) == 0)
    def _():
        d_state[...] = jnp.zeros_like(d_state)
        grad_up_ref[...] = jnp.zeros_like(grad_up_ref)
        grad_bias_ref[...] = jnp.zeros_like(grad_bias_ref)

    position = first + lax.broadcasted_iota(jnp.int32, (SPAN, slots), 0)
    place = (slot_row_ref[...] == position).astype(f32).astype(bf16)
    d_out = dot(place, arrived_ref[...]).astype(bf16)
    scale = float(dk) ** -0.5
    queries = held_ref[:, :dk].astype(f32) * scale
    keys = held_ref[:, dk : 2 * dk].astype(f32)
    values = held_ref[:, 2 * dk : 2 * dk + dv]
    latent = held_ref[:, 2 * dk + dv :]
    logits = dot(latent, up_ref[...]) + bias_ref[...]
    _, cumulative, total, middle, carried, tail, keep, allowed = span_terms(
        first, (end0, end1, end2), logits
    )
    grow_query = jnp.exp(cumulative - middle)
    grow_key = jnp.exp(middle - cumulative)
    start_decay = jnp.exp(cumulative) * carried
    end_decay = jnp.exp(total - cumulative) * tail
    query_mid = (queries * grow_query).astype(bf16)
    key_mid = (keys * grow_key).astype(bf16)
    query_start = (queries * start_decay).astype(bf16)
    key_end = (keys * end_decay).astype(bf16)
    scores = jnp.where(allowed, dot_t(query_mid, key_mid), 0.0).astype(bf16)
    d_scores = jnp.where(allowed, dot_t(d_out, values), 0.0).astype(bf16)
    leaving = d_state[...]
    leaving_low = leaving.astype(bf16)
    entering = states_ref[0]
    d_values = rows_dot(scores, d_out) + dot(key_end, leaving_low)
    d_queries = dot(d_scores, key_mid) * grow_query + dot_t(d_out, entering) * start_decay
    d_key_end = dot_t(values, leaving_low) * end_decay
    d_keys = rows_dot(d_scores, query_mid) * grow_key + d_key_end
    kept = keep * jnp.exp(total)
    state_pair = jnp.sum(entering.astype(f32) * leaving, axis=1, keepdims=True)
    state_row = jnp.transpose(jnp.broadcast_to(state_pair, (dk, LANES)))[:1, :]
    d_total = jnp.sum(keys * d_key_end, axis=0, keepdims=True) + kept * state_row
    d_cumulative = queries * d_queries - keys * d_keys
    row = lax.broadcasted_iota(jnp.int32, (SPAN, SPAN), 0)
    column = lax.broadcasted_iota(jnp.int32, (SPAN, SPAN), 1)
    upper = (row <= column).astype(f32)
    d_log_decay = (
        jnp.dot(upper, d_cumulative, precision=lax.Precision.HIGHEST, preferred_element_type=f32)
        + d_total
    )
    d_logits = d_log_decay * (1.0 / 16.0) * jax.nn.sigmoid(-logits)
    grad_bias_ref[...] += jnp.broadcast_to(jnp.sum(d_logits, axis=0, keepdims=True), (8, dk))
    d_logits_high = d_logits.astype(bf16)
    d_logits_low = (d_logits - d_logits_high.astype(f32)).astype(bf16)
    grad_up_ref[...] += rows_dot(d_logits_high, latent) + rows_dot(d_logits_low, latent)
    d_latent = dot(d_logits_high, down_ref[...]) + dot(d_logits_low, down_ref[...])
    high = d_latent.astype(bf16).astype(f32)
    lane = lax.broadcasted_iota(jnp.int32, d_latent.shape, 1)
    d_latent_packed = jnp.where(lane < LANES // 4, high, d_latent - high)
    at = pl.ds(pl.multiple_of(first, SPAN), SPAN)
    result[at, :dk] = (d_queries * scale).astype(bf16)
    result[at, dk : 2 * dk] = d_keys.astype(bf16)
    result[at, 2 * dk : 2 * dk + dv] = d_values.astype(bf16)
    result[at, 2 * dk + dv :] = d_latent_packed.astype(bf16)
    kept_column = jnp.transpose(jnp.broadcast_to(kept, (8, dk)))[:, :1]
    d_state[...] = kept_column * leaving + rows_dot(query_start, d_out)

    @pl.when(step == 0)
    def _():
        return_rows(slot_column_ref, result, out_ref)


def whole(shape):
    return pl.BlockSpec(shape, lambda i: (0,) * len(shape))


def recur_forward(slot_map, lengths, up_wide, bias, arrived, dk, dv):
    slots, width = arrived.shape
    steps = OWN_CAP // SPAN
    return pl.pallas_call(
        functools.partial(recur_forward_kernel, dk, dv),
        grid=(steps,),
        in_specs=[
            whole((1, slots)),
            whole((slots, 1)),
            pl.BlockSpec(memory_space=pltpu.SMEM),
            whole((LANES, dk)),
            whole((1, dk)),
            whole((slots, width)),
        ],
        out_specs=[
            whole((slots, dv)),
            pl.BlockSpec((SPAN, width), lambda i: (i, 0)),
            pl.BlockSpec((1, dk, dv), lambda i: (i, 0, 0)),
        ],
        out_shape=[
            jax.ShapeDtypeStruct((slots, dv), bf16),
            jax.ShapeDtypeStruct((OWN_CAP, width), bf16),
            jax.ShapeDtypeStruct((steps, dk, dv), bf16),
        ],
        scratch_shapes=[pltpu.VMEM((dk, dv), f32), pltpu.VMEM((OWN_CAP, dv), bf16)],
        compiler_params=pltpu.CompilerParams(vmem_limit_bytes=40 << 20),
        cost_estimate=pl.CostEstimate(
            flops=6_000_000_000, bytes_accessed=10_000_000, transcendentals=2_000_000
        ),
        name="recur_forward",
    )(slot_map.reshape(1, -1), slot_map.reshape(-1, 1), lengths, up_wide, bias, arrived)


def recur_backward(slot_map, lengths, up_wide, bias, down_wide, arrived, held, states, dk, dv):
    slots = arrived.shape[0]
    width = held.shape[1]
    steps = OWN_CAP // SPAN
    return pl.pallas_call(
        functools.partial(recur_backward_kernel, dk, dv),
        grid=(steps,),
        in_specs=[
            whole((1, slots)),
            whole((slots, 1)),
            pl.BlockSpec(memory_space=pltpu.SMEM),
            whole((LANES, dk)),
            whole((1, dk)),
            whole((dk, LANES)),
            whole((slots, dv)),
            pl.BlockSpec((SPAN, width), lambda i: (steps - 1 - i, 0)),
            pl.BlockSpec((1, dk, dv), lambda i: (steps - 1 - i, 0, 0)),
        ],
        out_specs=[whole((slots, width)), whole((dk, LANES)), whole((8, dk))],
        out_shape=[
            jax.ShapeDtypeStruct((slots, width), bf16),
            jax.ShapeDtypeStruct((dk, LANES), f32),
            jax.ShapeDtypeStruct((8, dk), f32),
        ],
        scratch_shapes=[pltpu.VMEM((dk, dv), f32), pltpu.VMEM((OWN_CAP, width), bf16)],
        compiler_params=pltpu.CompilerParams(vmem_limit_bytes=40 << 20),
        cost_estimate=pl.CostEstimate(
            flops=12_000_000_000, bytes_accessed=12_000_000, transcendentals=4_000_000
        ),
        name="recur_backward",
    )(
        slot_map.reshape(1, -1), slot_map.reshape(-1, 1), lengths, up_wide, bias, down_wide,
        arrived, held, states,
    )


CHUNK = 16


def line_kernel(mode, n, *refs):
    share_ref, x_ref, base_ref, gain_ref = refs[:4]
    if mode == "norm":
        out_ref, kept_ref = refs[4:6]
        scratch = refs[6:]
    elif mode == "back":
        out_ref, kept_ref, gain_grad_ref = refs[4:7]
        scratch = refs[7:]
    else:
        out_ref = refs[4]
        kept_ref = None
        scratch = refs[5:]
    up_in, up_out, down_in, down_out, sems = scratch
    me = lax.axis_index("tensor")
    half = up_in.shape[0]
    count = half // CHUNK

    barrier = pltpu.get_barrier_semaphore()

    @pl.when(me > 0)
    def _():
        pl.semaphore_signal(barrier, inc=1, device_id={"tensor": me - 1}, device_id_type=MESH)

    @pl.when(me < n - 1)
    def _():
        pl.semaphore_signal(barrier, inc=1, device_id={"tensor": me + 1}, device_id_type=MESH)

    inside = (me > 0) & (me < n - 1)

    @pl.when(inside)
    def _():
        pl.semaphore_wait(barrier, 2)

    @pl.when(jnp.logical_not(inside))
    def _():
        pl.semaphore_wait(barrier, 1)

    def at(g):
        return pl.ds(pl.multiple_of(g * CHUNK, CHUNK), CHUNK)

    def low(g):
        return pl.ds(pl.multiple_of(half + g * CHUNK, CHUNK), CHUNK)

    def right(source, target, lane, g):
        return pltpu.make_async_remote_copy(
            source, target, sems.at[2 * lane, g], sems.at[2 * lane + 1, g],
            device_id={"tensor": jnp.minimum(me + 1, n - 1)}, device_id_type=MESH,
        )

    def left(source, target, lane, g):
        return pltpu.make_async_remote_copy(
            source, target, sems.at[2 * lane, g], sems.at[2 * lane + 1, g],
            device_id={"tensor": jnp.maximum(me - 1, 0)}, device_id_type=MESH,
        )

    def up_copy(g):
        return right(up_out.at[at(g), :], up_in.at[at(g), :], 0, g)

    def down_copy(g):
        return left(down_out.at[at(g), :], down_in.at[at(g), :], 1, g)

    def first_up_copy(g):
        return right(share_ref.at[at(g), :], up_in.at[at(g), :], 0, g)

    def first_down_copy(g):
        return left(share_ref.at[low(g), :], down_in.at[at(g), :], 1, g)

    def up_back_copy(g):
        return left(out_ref.at[at(g), :], out_ref.at[at(g), :], 2, g)

    def down_back_copy(g):
        return right(out_ref.at[low(g), :], out_ref.at[low(g), :], 3, g)

    if mode == "back":
        gain_grad_ref[...] = jnp.zeros_like(gain_grad_ref)

    def finish(total, g, place):
        base = base_ref[at(g), :].astype(f32)
        if mode == "sum":
            out_ref[place, :] = (base + total).astype(out_ref.dtype)
            return
        if mode == "norm":
            hidden = base + total
            kept_ref[at(g), :] = hidden
            scaling = lax.rsqrt(jnp.mean(hidden * hidden, axis=1, keepdims=True) + epsilon)
            out_ref[place, :] = (hidden * scaling * gain_ref[...]).astype(out_ref.dtype)
            return
        rows = x_ref[at(g), :].astype(f32)
        scaling = lax.rsqrt(jnp.mean(rows * rows, axis=1, keepdims=True) + epsilon)
        unit = rows * scaling
        gained = gain_ref[...] * total
        grad = base + scaling * (gained - unit * jnp.mean(gained * unit, axis=1, keepdims=True))
        kept_ref[at(g), :] = grad
        out_ref[place, :] = grad.astype(out_ref.dtype)
        term = total * unit
        part = term[0:8, :]
        for i in range(1, CHUNK // 8):
            part = part + term[8 * i : 8 * i + 8, :]
        gain_grad_ref[...] += part

    @pl.when(me == 0)
    def _():
        @pl.loop(0, count)
        def _(g):
            first_up_copy(g).start()

    @pl.when(me == n - 1)
    def _():
        @pl.loop(0, count)
        def _(g):
            first_down_copy(g).start()

    @pl.loop(0, count + n - 2)
    def _(step):
        g_up = step - (me - 1)

        @pl.when((me > 0) & (g_up >= 0) & (g_up < count))
        def _():
            up_copy(g_up).wait_recv()
            total = up_in[at(g_up), :].astype(f32) + share_ref[at(g_up), :].astype(f32)

            @pl.when(me < n - 1)
            def _():
                up_out[at(g_up), :] = total.astype(bf16)
                up_copy(g_up).start()

            @pl.when(me == n - 1)
            def _():
                finish(total, g_up, at(g_up))
                up_back_copy(g_up).start()

        g_down = step - (n - 2 - me)

        @pl.when((me < n - 1) & (g_down >= 0) & (g_down < count))
        def _():
            down_copy(g_down).wait_recv()
            total = down_in[at(g_down), :].astype(f32) + share_ref[low(g_down), :].astype(f32)

            @pl.when(me > 0)
            def _():
                down_out[at(g_down), :] = total.astype(bf16)
                down_copy(g_down).start()

            @pl.when(me == 0)
            def _():
                finish(total, g_down, low(g_down))
                down_back_copy(g_down).start()

    @pl.loop(0, count + n - 2)
    def _(step):
        g_up = step - (n - 2 - me)

        @pl.when((me < n - 1) & (g_up >= 0) & (g_up < count))
        def _():
            up_back_copy(g_up).wait_recv()

            @pl.when(me > 0)
            def _():
                up_back_copy(g_up).start()

        g_down = step - (me - 1)

        @pl.when((me > 0) & (g_down >= 0) & (g_down < count))
        def _():
            down_back_copy(g_down).wait_recv()

            @pl.when(me < n - 1)
            def _():
                down_back_copy(g_down).start()

    @pl.loop(0, count)
    def _(g):
        @pl.when(me < n - 1)
        def _():
            up_copy(g).wait_send()
            down_back_copy(g).wait_send()

        @pl.when(me > 0)
        def _():
            down_copy(g).wait_send()
            up_back_copy(g).wait_send()


def line_sum(mode, call, n, share, x_own, base_own, gain):
    rows, width = share.shape
    half = rows // 2
    vmem = pl.BlockSpec(memory_space=pltpu.VMEM)
    outs = [jax.ShapeDtypeStruct((rows, width), bf16)]
    if mode != "sum":
        outs.append(jax.ShapeDtypeStruct((half, width), f32))
    if mode == "back":
        outs.append(jax.ShapeDtypeStruct((8, width), f32))
    return pl.pallas_call(
        functools.partial(line_kernel, mode, n),
        in_specs=[vmem] * 4,
        out_specs=[vmem] * len(outs),
        out_shape=outs,
        scratch_shapes=[
            pltpu.VMEM((half, width), bf16),
            pltpu.VMEM((half, width), bf16),
            pltpu.VMEM((half, width), bf16),
            pltpu.VMEM((half, width), bf16),
            pltpu.SemaphoreType.DMA((8, half // CHUNK)),
        ],
        compiler_params=pltpu.CompilerParams(
            collective_id=call, has_side_effects=True, vmem_limit_bytes=40 << 20
        ),
        cost_estimate=pl.CostEstimate(
            flops=10_000_000, bytes_accessed=200_000_000, transcendentals=0
        ),
        name="line_" + mode,
    )(share, x_own, base_own, gain)


def small_sum_kernel(groups, n, rows_all, part_ref, out_ref, held, line, line_in, sems, line_sems):
    me = lax.axis_index("dp")
    place = lax.axis_index("tensor")
    barrier = pltpu.get_barrier_semaphore()

    def peer(k):
        return lax.rem(me + k, groups)

    def mate(k):
        return lax.rem(place + k, n)

    @pl.loop(1, groups)
    def _(k):
        pl.semaphore_signal(barrier, inc=1, device_id={"dp": peer(k)}, device_id_type=MESH)

    @pl.loop(1, n)
    def _(k):
        pl.semaphore_signal(barrier, inc=1, device_id={"tensor": mate(k)}, device_id_type=MESH)

    pl.semaphore_wait(barrier, groups + n - 2)

    def copy(k, source):
        return pltpu.make_async_remote_copy(
            part_ref.at[peer(k)], held.at[source], sems.at[0, k], sems.at[1, source],
            device_id={"dp": peer(k)}, device_id_type=MESH,
        )

    def line_copy(k, source):
        return pltpu.make_async_remote_copy(
            line, line_in.at[source], line_sems.at[0, k], line_sems.at[1, source],
            device_id={"tensor": mate(k)}, device_id_type=MESH,
        )

    @pl.loop(1, groups)
    def _(k):
        copy(k, me).start()

    held[pl.ds(me, 1)] = part_ref[pl.ds(me, 1)]

    @pl.loop(1, groups)
    def _(k):
        copy(k, peer(k)).wait_recv()

    total = held[0]
    for i in range(1, groups):
        total = total + held[i]
    line[...] = total[:rows_all]
    out_ref[...] = total

    @pl.loop(1, n)
    def _(k):
        line_copy(k, place).start()

    line_in[pl.ds(place, 1)] = total[None, :rows_all]

    @pl.loop(1, n)
    def _(k):
        line_copy(k, mate(k)).wait_recv()

    total = line_in[0]
    for i in range(1, n):
        total = total + line_in[i]
    out_ref[:rows_all] = total

    @pl.loop(1, groups)
    def _(k):
        copy(k, me).wait_send()

    @pl.loop(1, n)
    def _(k):
        line_copy(k, place).wait_send()


def small_sum(over_all, over_owners, groups, n, call):
    def tiles(blocks):
        short = -blocks.shape[1] % (8 * LANES)
        return jnp.pad(blocks, ((0, 0), (0, short))).reshape(groups, -1, LANES)

    first, second = tiles(over_all), tiles(over_owners)
    rows_all = first.shape[1]
    part = jnp.concatenate([first, second], axis=1)
    vmem = pl.BlockSpec(memory_space=pltpu.VMEM)
    total = pl.pallas_call(
        functools.partial(small_sum_kernel, groups, n, rows_all),
        in_specs=[vmem],
        out_specs=vmem,
        out_shape=jax.ShapeDtypeStruct(part.shape[1:], f32),
        scratch_shapes=[
            pltpu.VMEM(part.shape, f32),
            pltpu.VMEM((rows_all, LANES), f32),
            pltpu.VMEM((n, rows_all, LANES), f32),
            pltpu.SemaphoreType.DMA((2, groups)),
            pltpu.SemaphoreType.DMA((2, n)),
        ],
        compiler_params=pltpu.CompilerParams(collective_id=call, has_side_effects=True),
        name="small_sum",
    )(part)
    return (
        total[:rows_all].reshape(-1)[: over_all.shape[1]],
        total[rows_all:].reshape(-1)[: over_owners.shape[1]],
    )


def per_device(
    tokens,
    cotangent,
    token_slots,
    lengths,
    mixer_gain,
    query_weight,
    key_weight,
    value_weight,
    gate_weight,
    decay_down,
    decay_up,
    decay_bias,
    head_gain,
    out_weight,
    feed_gain,
    feed_gate,
    feed_up,
    feed_down,
):
    groups = lax.axis_size("dp")
    lines = lax.axis_size("tensor")
    member = lax.axis_index("dp")
    place = lax.axis_index("tensor")
    count, width = tokens.shape
    cap = OWN_CAP // groups
    slots = groups * cap
    dk = query_weight.shape[1]
    dv = value_weight.shape[1]
    rank = decay_up.shape[1]
    parity = lax.rem(member, 2)
    pairs = [(i, i ^ 1) for i in range(groups)]
    same_parity = [[i for i in range(groups) if i % 2 == b] for b in range(2)]

    owners = (token_slots // OWN_CAP).reshape(groups, count)
    mine = (owners == member).astype(bf16)
    my_slots = lax.dynamic_slice_in_dim(token_slots, member * count, count)
    my_owner = my_slots // OWN_CAP
    chosen = (my_owner[None, :] == jnp.arange(groups, dtype=jnp.int32)[:, None]).astype(bf16)
    index = jnp.arange(count, dtype=jnp.int32)
    before = (index[:, None] < index[None, :]).astype(bf16)
    ranks = dot(jnp.concatenate([mine, chosen], axis=0), before).astype(jnp.int32)
    recv_rank, send_rank = ranks[:groups], ranks[groups:]
    hit = (recv_rank[:, None, :] == jnp.arange(cap, dtype=jnp.int32)[None, :, None]) & (
        owners == member
    )[:, None, :]
    local = (token_slots % OWN_CAP).reshape(groups, count)
    slot_map = (
        jnp.sum(jnp.where(hit, local[:, None, :] - OWN_CAP, 0), axis=2) + OWN_CAP
    ).reshape(slots)
    send_pos = my_owner * cap + jnp.sum(
        jnp.where(chosen > 0, send_rank, 0), axis=0, dtype=jnp.int32
    )
    slot_ids = jnp.arange(slots, dtype=jnp.int32)
    pack = (slot_ids[:, None] == send_pos[None, :]).astype(bf16)
    unpack = (send_pos[:, None] == slot_ids[None, :]).astype(bf16)

    def exchange(row_block):
        blocks = row_block.reshape(groups, cap, row_block.shape[1])
        moved = lax.all_to_all(blocks, "dp", split_axis=0, concat_axis=0, tiled=True)
        return moved.reshape(slots, row_block.shape[1])

    half = count // 2
    own_at = jnp.where(place == 0, half, 0)
    tokens_own = lax.dynamic_slice_in_dim(tokens, own_at, half)
    cotangent_own = lax.dynamic_slice_in_dim(cotangent, own_at, half)

    tokens_wide = tokens.astype(f32)
    mixer_gain_wide = mixer_gain.astype(f32)
    feed_gain_wide = feed_gain.astype(f32)
    normed = (
        tokens_wide
        * lax.rsqrt(jnp.mean(tokens_wide * tokens_wide, axis=-1, keepdims=True) + epsilon)
        * mixer_gain_wide
    ).astype(bf16)
    queries = dot(normed, query_weight).astype(bf16)
    keys_low = dot(normed, key_weight).astype(bf16)
    value_rows = dot(normed, value_weight).astype(bf16)
    gate_pre = dot(normed, gate_weight)
    third = LANES // 4
    down_pad = jnp.pad(decay_down, ((0, 0), (0, third - rank)))
    latent = dot(
        normed,
        jnp.concatenate([down_pad, down_pad, down_pad, jnp.zeros_like(down_pad)], axis=1),
    )
    latent_high = latent.astype(bf16)
    latent_rest = latent - latent_high.astype(f32)
    latent_mid = latent_rest.astype(bf16)
    latent_low = (latent_rest - latent_mid.astype(f32)).astype(bf16)
    lane = jnp.arange(LANES, dtype=jnp.int32)[None, :]
    latent_packed = jnp.where(
        lane < third, latent_high, jnp.where(lane < 2 * third, latent_mid, latent_low)
    )
    rows_out = jnp.concatenate([queries, keys_low, value_rows, latent_packed], axis=1)
    arrived = exchange(dot(pack, rows_out).astype(bf16))
    up_pad = jnp.pad(decay_up, ((0, 0), (0, third - rank)))
    up_wide = jnp.concatenate([up_pad, up_pad, up_pad, jnp.zeros_like(up_pad)], axis=1).T
    down_wide = jnp.concatenate(
        [up_pad, up_pad, jnp.zeros_like(up_pad), jnp.zeros_like(up_pad)], axis=1
    )
    bias = decay_bias.astype(f32).reshape(1, dk)
    attended_slots, held, states = recur_forward(
        slot_map, lengths, up_wide, bias, arrived, dk, dv
    )
    attended = dot(unpack, exchange(attended_slots))

    head_gain_wide = head_gain.astype(f32)

    def head_output(rows, gate_rows, gain_row):
        scaling = lax.rsqrt(jnp.mean(rows * rows, axis=-1, keepdims=True) + head_floor)
        return rows * scaling * gain_row * jax.nn.silu(gate_rows)

    gated_wide, head_back = jax.vjp(head_output, attended, gate_pre, head_gain_wide)
    gated = gated_wide.astype(bf16)
    mixer_share = dot(gated, out_weight).astype(bf16)
    feed_normed, hidden_own = line_sum(
        "norm", 1, lines, mixer_share, tokens_own, tokens_own, feed_gain_wide.reshape(1, -1)
    )

    gate_hidden = dot(feed_normed, feed_gate)
    up_hidden = dot(feed_normed, feed_up)
    d_active = dot_t(cotangent, feed_down)
    sigmoid_gate = jax.nn.sigmoid(gate_hidden)
    swish_gate = gate_hidden * sigmoid_gate
    active = (swish_gate * up_hidden).astype(bf16)
    d_gate_hidden = (
        d_active * up_hidden * sigmoid_gate * (1.0 + gate_hidden * (1.0 - sigmoid_gate))
    ).astype(bf16)
    d_up_hidden = (d_active * swish_gate).astype(bf16)
    feed_share = (dot_t(d_gate_hidden, feed_gate) + dot_t(d_up_hidden, feed_up)).astype(bf16)
    d_mixed, d_hidden_own, feed_gain_part = line_sum(
        "back", 2, lines, feed_share, hidden_own, cotangent_own, feed_gain_wide.reshape(1, -1)
    )

    d_gated = dot_t(d_mixed, out_weight)
    d_attended, d_gate_pre, head_gain_part = head_back(d_gated)
    d_gate_low = d_gate_pre.astype(bf16)
    d_arrived = exchange(dot(pack, d_attended.astype(bf16)).astype(bf16))
    d_slots, up_part, bias_part = recur_backward(
        slot_map, lengths, up_wide, bias, down_wide, d_arrived, held, states, dk, dv
    )
    d_rows = dot(unpack, exchange(d_slots)).astype(bf16)
    d_query_low = d_rows[:, :dk]
    d_key_low = d_rows[:, dk : 2 * dk]
    d_value_low = d_rows[:, 2 * dk : 2 * dk + dv]
    d_latent_low = d_rows[:, 2 * dk + dv :]
    down_both = jnp.concatenate(
        [down_pad, down_pad, jnp.zeros_like(down_pad), jnp.zeros_like(down_pad)], axis=1
    )
    normed_share = (
        dot_t(d_query_low, query_weight)
        + dot_t(d_key_low, key_weight)
        + dot_t(d_value_low, value_weight)
        + dot_t(d_gate_low, gate_weight)
        + dot_t(d_latent_low, down_both)
    ).astype(bf16)
    token_grad, _, mixer_gain_part = line_sum(
        "back", 3, lines, normed_share, tokens_own, d_hidden_own, mixer_gain_wide.reshape(1, -1)
    )
    hidden_placed = jnp.concatenate(
        [jnp.where(place == lines - 1, hidden_own, 0.0), jnp.where(place == 0, hidden_own, 0.0)],
        axis=0,
    )
    layer_out = lax.psum((dot(active, feed_down) + hidden_placed).astype(bf16), "tensor")

    def halves(row_block, dims):
        split = row_block.reshape(row_block.shape[0], groups // 2, 2, dims // groups)
        keep = lax.dynamic_index_in_dim(split, parity, 2, keepdims=False)
        send = lax.dynamic_index_in_dim(split, 1 - parity, 2, keepdims=False)
        got = lax.ppermute(send, "dp", pairs)
        shape = (row_block.shape[0], dims // 2)
        return keep.reshape(shape), got.reshape(shape)

    def partner(row_block):
        return row_block, lax.ppermute(row_block, "dp", pairs)

    def summed_share(left, right):
        share = (rows_dot(left[0], right[0]) + rows_dot(left[1], right[1])).astype(bf16)
        rows = share.shape[0] // (groups // 2)
        blocks = share.reshape(groups // 2, rows, share.shape[1])
        moved = lax.all_to_all(
            blocks, "dp", split_axis=0, concat_axis=0, tiled=True, axis_index_groups=same_parity
        )
        return jnp.sum(moved.astype(f32), axis=0)

    feed_halves = halves(feed_normed, width)
    normed_halves = halves(normed, width)
    grad_feed_down = summed_share(halves(active, active.shape[1]), partner(cotangent))
    grad_feed_gate = summed_share(feed_halves, partner(d_gate_hidden))
    grad_feed_up = summed_share(feed_halves, partner(d_up_hidden))
    grad_out = summed_share(halves(gated, dv), partner(d_mixed))
    grad_query = summed_share(normed_halves, partner(d_query_low))
    grad_key = summed_share(normed_halves, partner(d_key_low))
    grad_value = summed_share(normed_halves, partner(d_value_low))
    grad_gate = summed_share(normed_halves, partner(d_gate_low))

    down_part = rows_dot(normed, d_latent_low)
    down_part = down_part[:, :rank] + down_part[:, third : third + rank]
    up_part = up_part[:, :rank] + up_part[:, third : third + rank] + (
        up_part[:, 2 * third : 2 * third + rank]
    )

    def by_owner(vector):
        return vector.reshape(groups, -1)

    over_all = jnp.concatenate(
        [
            by_owner(jnp.sum(mixer_gain_part, axis=0)),
            by_owner(jnp.sum(feed_gain_part, axis=0)),
            by_owner(head_gain_part),
            by_owner(down_part),
        ],
        axis=1,
    )
    over_owners = jnp.concatenate([by_owner(up_part), by_owner(bias_part[0])], axis=1)
    summed, small = small_sum(over_all, over_owners, groups, lines, 5)
    per = width // groups
    head_per = dv // groups
    return (
        layer_out,
        token_grad,
        summed[:per],
        grad_query,
        grad_key,
        grad_value,
        grad_gate,
        summed[2 * per + head_per :].reshape(per, rank),
        small[: dk // groups * rank].reshape(1, dk // groups, rank),
        small[dk // groups * rank :].reshape(1, dk // groups),
        summed[2 * per : 2 * per + head_per],
        grad_out[None],
        summed[per : 2 * per],
        grad_feed_gate,
        grad_feed_up,
        grad_feed_down[None],
    )


def solution(mesh):
    placed = (
        P("dp", None),
        P("dp", None),
        P(),
        P("dp", None),
        P(),
        P(None, "tensor"),
        P(None, "tensor"),
        P(None, "tensor"),
        P(None, "tensor"),
        P(),
        P("tensor", None),
        P("tensor"),
        P(),
        P("tensor", None),
        P(),
        P(None, "tensor"),
        P(None, "tensor"),
        P("tensor", None),
    )
    return jax.shard_map(
        per_device,
        mesh=mesh,
        in_specs=placed,
        out_specs=(
            P("dp", None),
            P("dp", None),
            P("dp"),
            P("dp", "tensor"),
            P("dp", "tensor"),
            P("dp", "tensor"),
            P("dp", "tensor"),
            P("dp", None),
            P("tensor", "dp", None),
            P("tensor", "dp"),
            P("dp"),
            P("tensor", "dp", None),
            P("dp"),
            P("dp", "tensor"),
            P("dp", "tensor"),
            P("tensor", "dp", None),
        ),
        check_vma=False,
    )
```

```python
import functools

import jax
import jax.numpy as jnp
from jax import lax
from jax.experimental import pallas as pl
from jax.experimental.pallas import tpu as pltpu
from jax.sharding import PartitionSpec as P

OWN_CAP = 1024
SPAN = 128
LANES = 128
epsilon = 1e-06
head_floor = 1.0

f32 = jnp.float32
bf16 = jnp.bfloat16
MESH = pl.DeviceIdType.MESH


def rows_dot(left, right):
    return lax.dot_general(left, right, (((0,), (0,)), ((), ())), preferred_element_type=f32)


def dot_t(left, right):
    return lax.dot_general(left, right, (((1,), (1,)), ((), ())), preferred_element_type=f32)


def dot(left, right):
    return jnp.dot(left, right, preferred_element_type=f32)


def span_terms(first, ends, logits):
    rows = logits.shape[0]

    def label(position):
        count = jnp.zeros_like(position)
        for end in ends:
            count = count + (position >= end).astype(jnp.int32)
        return count

    log_decay = jax.nn.log_sigmoid(logits) * (1.0 / 16.0)
    row = lax.broadcasted_iota(jnp.int32, (rows, rows), 0)
    column = lax.broadcasted_iota(jnp.int32, (rows, rows), 1)
    lower = (row >= column).astype(f32)
    cumulative = jnp.dot(
        lower, log_decay, precision=lax.Precision.HIGHEST, preferred_element_type=f32
    )
    total = cumulative[rows - 1 :, :]
    middle = cumulative[rows // 2 - 1 : rows // 2, :]
    label_column = label(first + lax.broadcasted_iota(jnp.int32, (rows, 1), 0))
    label_row = label(first + lax.broadcasted_iota(jnp.int32, (1, rows), 1))
    before = jnp.where(first > 0, label(first - 1), -1)
    last = label(first + rows - 1)
    carried = (label_column == before).astype(f32)
    tail = (label_column == last).astype(f32)
    keep = (before == last).astype(f32)
    allowed = (row >= column) & (label_column == label_row)
    return log_decay, cumulative, total, middle, carried, tail, keep, allowed


def recur_forward_kernel(
    dk, dv, slot_row_ref, slot_column_ref, lengths_ref, up_ref, bias_ref, arrived_ref,
    out_ref, held_ref, states_ref, state, result,
):
    step = pl.program_id(0)
    first = step * SPAN
    end0 = lengths_ref[0, 0]
    end1 = end0 + lengths_ref[0, 1]
    end2 = end1 + lengths_ref[0, 2]
    slots = slot_row_ref.shape[1]

    @pl.when(step == 0)
    def _():
        state[...] = jnp.zeros_like(state)

    position = first + lax.broadcasted_iota(jnp.int32, (SPAN, slots), 0)
    place = (slot_row_ref[...] == position).astype(f32).astype(bf16)
    held = dot(place, arrived_ref[...]).astype(bf16)
    held_ref[...] = held
    queries = held[:, :dk].astype(f32) * (float(dk) ** -0.5)
    keys = held[:, dk : 2 * dk].astype(f32)
    values = held[:, 2 * dk : 2 * dk + dv]
    logits = dot(held[:, 2 * dk + dv :], up_ref[...]) + bias_ref[...]
    _, cumulative, total, middle, carried, tail, keep, allowed = span_terms(
        first, (end0, end1, end2), logits
    )
    query_mid = (queries * jnp.exp(cumulative - middle)).astype(bf16)
    key_mid = (keys * jnp.exp(middle - cumulative)).astype(bf16)
    query_start = (queries * jnp.exp(cumulative) * carried).astype(bf16)
    key_end = (keys * jnp.exp(total - cumulative) * tail).astype(bf16)
    scores = jnp.where(allowed, dot_t(query_mid, key_mid), 0.0).astype(bf16)
    entering = state[...]
    entering_low = entering.astype(bf16)
    states_ref[0] = entering_low
    attended = dot(scores, values) + dot(query_start, entering_low)
    result[pl.ds(pl.multiple_of(first, SPAN), SPAN), :] = attended.astype(bf16)
    decay_column = jnp.transpose(jnp.broadcast_to(keep * jnp.exp(total), (8, dk)))[:, :1]
    state[...] = decay_column * entering + rows_dot(key_end, values)

    @pl.when(step == pl.num_programs(0) - 1)
    def _():
        return_rows(slot_column_ref, result, out_ref)


def return_rows(slot_column_ref, source, out_ref):
    positions = source.shape[0]
    block = 256

    def body(i, carry):
        at = pl.ds(pl.multiple_of(i * block, block), block)
        column = lax.broadcasted_iota(jnp.int32, (block, positions), 1)
        pick = (slot_column_ref[at, :] == column).astype(f32).astype(bf16)
        out_ref[at, :] = dot(pick, source[...]).astype(out_ref.dtype)
        return carry

    lax.fori_loop(0, out_ref.shape[0] // block, body, 0)


def recur_backward_kernel(
    dk, dv, slot_row_ref, slot_column_ref, lengths_ref, up_ref, bias_ref, down_ref, arrived_ref,
    held_ref, states_ref, out_ref, grad_up_ref, grad_bias_ref, d_state, result,
):
    step = pl.num_programs(0) - 1 - pl.program_id(0)
    first = step * SPAN
    end0 = lengths_ref[0, 0]
    end1 = end0 + lengths_ref[0, 1]
    end2 = end1 + lengths_ref[0, 2]
    slots = slot_row_ref.shape[1]

    @pl.when(pl.program_id(0) == 0)
    def _():
        d_state[...] = jnp.zeros_like(d_state)
        grad_up_ref[...] = jnp.zeros_like(grad_up_ref)
        grad_bias_ref[...] = jnp.zeros_like(grad_bias_ref)

    position = first + lax.broadcasted_iota(jnp.int32, (SPAN, slots), 0)
    place = (slot_row_ref[...] == position).astype(f32).astype(bf16)
    d_out = dot(place, arrived_ref[...]).astype(bf16)
    scale = float(dk) ** -0.5
    queries = held_ref[:, :dk].astype(f32) * scale
    keys = held_ref[:, dk : 2 * dk].astype(f32)
    values = held_ref[:, 2 * dk : 2 * dk + dv]
    latent = held_ref[:, 2 * dk + dv :]
    logits = dot(latent, up_ref[...]) + bias_ref[...]
    _, cumulative, total, middle, carried, tail, keep, allowed = span_terms(
        first, (end0, end1, end2), logits
    )
    grow_query = jnp.exp(cumulative - middle)
    grow_key = jnp.exp(middle - cumulative)
    start_decay = jnp.exp(cumulative) * carried
    end_decay = jnp.exp(total - cumulative) * tail
    query_mid = (queries * grow_query).astype(bf16)
    key_mid = (keys * grow_key).astype(bf16)
    query_start = (queries * start_decay).astype(bf16)
    key_end = (keys * end_decay).astype(bf16)
    scores = jnp.where(allowed, dot_t(query_mid, key_mid), 0.0).astype(bf16)
    d_scores = jnp.where(allowed, dot_t(d_out, values), 0.0).astype(bf16)
    leaving = d_state[...]
    leaving_low = leaving.astype(bf16)
    entering = states_ref[0]
    d_values = rows_dot(scores, d_out) + dot(key_end, leaving_low)
    d_queries = dot(d_scores, key_mid) * grow_query + dot_t(d_out, entering) * start_decay
    d_key_end = dot_t(values, leaving_low) * end_decay
    d_keys = rows_dot(d_scores, query_mid) * grow_key + d_key_end
    kept = keep * jnp.exp(total)
    state_pair = jnp.sum(entering.astype(f32) * leaving, axis=1, keepdims=True)
    state_row = jnp.transpose(jnp.broadcast_to(state_pair, (dk, LANES)))[:1, :]
    d_total = jnp.sum(keys * d_key_end, axis=0, keepdims=True) + kept * state_row
    d_cumulative = queries * d_queries - keys * d_keys
    row = lax.broadcasted_iota(jnp.int32, (SPAN, SPAN), 0)
    column = lax.broadcasted_iota(jnp.int32, (SPAN, SPAN), 1)
    upper = (row <= column).astype(f32)
    d_log_decay = (
        jnp.dot(upper, d_cumulative, precision=lax.Precision.HIGHEST, preferred_element_type=f32)
        + d_total
    )
    d_logits = d_log_decay * (1.0 / 16.0) * jax.nn.sigmoid(-logits)
    grad_bias_ref[...] += jnp.broadcast_to(jnp.sum(d_logits, axis=0, keepdims=True), (8, dk))
    d_logits_high = d_logits.astype(bf16)
    d_logits_low = (d_logits - d_logits_high.astype(f32)).astype(bf16)
    grad_up_ref[...] += rows_dot(d_logits_high, latent) + rows_dot(d_logits_low, latent)
    d_latent = dot(d_logits_high, down_ref[...]) + dot(d_logits_low, down_ref[...])
    high = d_latent.astype(bf16).astype(f32)
    lane = lax.broadcasted_iota(jnp.int32, d_latent.shape, 1)
    d_latent_packed = jnp.where(lane < LANES // 4, high, d_latent - high)
    at = pl.ds(pl.multiple_of(first, SPAN), SPAN)
    result[at, :dk] = (d_queries * scale).astype(bf16)
    result[at, dk : 2 * dk] = d_keys.astype(bf16)
    result[at, 2 * dk : 2 * dk + dv] = d_values.astype(bf16)
    result[at, 2 * dk + dv :] = d_latent_packed.astype(bf16)
    kept_column = jnp.transpose(jnp.broadcast_to(kept, (8, dk)))[:, :1]
    d_state[...] = kept_column * leaving + rows_dot(query_start, d_out)

    @pl.when(step == 0)
    def _():
        return_rows(slot_column_ref, result, out_ref)


def whole(shape):
    return pl.BlockSpec(shape, lambda i: (0,) * len(shape))


def recur_forward(slot_map, lengths, up_wide, bias, arrived, dk, dv):
    slots, width = arrived.shape
    steps = OWN_CAP // SPAN
    return pl.pallas_call(
        functools.partial(recur_forward_kernel, dk, dv),
        grid=(steps,),
        in_specs=[
            whole((1, slots)),
            whole((slots, 1)),
            pl.BlockSpec(memory_space=pltpu.SMEM),
            whole((LANES, dk)),
            whole((1, dk)),
            whole((slots, width)),
        ],
        out_specs=[
            whole((slots, dv)),
            pl.BlockSpec((SPAN, width), lambda i: (i, 0)),
            pl.BlockSpec((1, dk, dv), lambda i: (i, 0, 0)),
        ],
        out_shape=[
            jax.ShapeDtypeStruct((slots, dv), bf16),
            jax.ShapeDtypeStruct((OWN_CAP, width), bf16),
            jax.ShapeDtypeStruct((steps, dk, dv), bf16),
        ],
        scratch_shapes=[pltpu.VMEM((dk, dv), f32), pltpu.VMEM((OWN_CAP, dv), bf16)],
        compiler_params=pltpu.CompilerParams(vmem_limit_bytes=40 << 20),
        cost_estimate=pl.CostEstimate(
            flops=6_000_000_000, bytes_accessed=10_000_000, transcendentals=2_000_000
        ),
        name="recur_forward",
    )(slot_map.reshape(1, -1), slot_map.reshape(-1, 1), lengths, up_wide, bias, arrived)


def recur_backward(slot_map, lengths, up_wide, bias, down_wide, arrived, held, states, dk, dv):
    slots = arrived.shape[0]
    width = held.shape[1]
    steps = OWN_CAP // SPAN
    return pl.pallas_call(
        functools.partial(recur_backward_kernel, dk, dv),
        grid=(steps,),
        in_specs=[
            whole((1, slots)),
            whole((slots, 1)),
            pl.BlockSpec(memory_space=pltpu.SMEM),
            whole((LANES, dk)),
            whole((1, dk)),
            whole((dk, LANES)),
            whole((slots, dv)),
            pl.BlockSpec((SPAN, width), lambda i: (steps - 1 - i, 0)),
            pl.BlockSpec((1, dk, dv), lambda i: (steps - 1 - i, 0, 0)),
        ],
        out_specs=[whole((slots, width)), whole((dk, LANES)), whole((8, dk))],
        out_shape=[
            jax.ShapeDtypeStruct((slots, width), bf16),
            jax.ShapeDtypeStruct((dk, LANES), f32),
            jax.ShapeDtypeStruct((8, dk), f32),
        ],
        scratch_shapes=[pltpu.VMEM((dk, dv), f32), pltpu.VMEM((OWN_CAP, width), bf16)],
        compiler_params=pltpu.CompilerParams(vmem_limit_bytes=40 << 20),
        cost_estimate=pl.CostEstimate(
            flops=12_000_000_000, bytes_accessed=12_000_000, transcendentals=4_000_000
        ),
        name="recur_backward",
    )(
        slot_map.reshape(1, -1), slot_map.reshape(-1, 1), lengths, up_wide, bias, down_wide,
        arrived, held, states,
    )


CHUNK = 32


def line_kernel(mode, n, *refs):
    share_ref, x_ref, base_ref, gain_ref = refs[:4]
    if mode == "norm":
        out_ref, kept_ref = refs[4:6]
        scratch = refs[6:]
    elif mode == "back":
        out_ref, kept_ref, gain_grad_ref = refs[4:7]
        scratch = refs[7:]
    else:
        out_ref = refs[4]
        kept_ref = None
        scratch = refs[5:]
    up_in, up_out, down_in, down_out, sems = scratch
    me = lax.axis_index("tensor")
    half = up_in.shape[0]
    count = half // CHUNK

    barrier = pltpu.get_barrier_semaphore()

    @pl.when(me > 0)
    def _():
        pl.semaphore_signal(barrier, inc=1, device_id={"tensor": me - 1}, device_id_type=MESH)

    @pl.when(me < n - 1)
    def _():
        pl.semaphore_signal(barrier, inc=1, device_id={"tensor": me + 1}, device_id_type=MESH)

    inside = (me > 0) & (me < n - 1)

    @pl.when(inside)
    def _():
        pl.semaphore_wait(barrier, 2)

    @pl.when(jnp.logical_not(inside))
    def _():
        pl.semaphore_wait(barrier, 1)

    def at(g):
        return pl.ds(pl.multiple_of(g * CHUNK, CHUNK), CHUNK)

    def low(g):
        return pl.ds(pl.multiple_of(half + g * CHUNK, CHUNK), CHUNK)

    def right(source, target, lane, g):
        return pltpu.make_async_remote_copy(
            source, target, sems.at[2 * lane, g], sems.at[2 * lane + 1, g],
            device_id={"tensor": jnp.minimum(me + 1, n - 1)}, device_id_type=MESH,
        )

    def left(source, target, lane, g):
        return pltpu.make_async_remote_copy(
            source, target, sems.at[2 * lane, g], sems.at[2 * lane + 1, g],
            device_id={"tensor": jnp.maximum(me - 1, 0)}, device_id_type=MESH,
        )

    def up_copy(g):
        return right(up_out.at[at(g), :], up_in.at[at(g), :], 0, g)

    def down_copy(g):
        return left(down_out.at[at(g), :], down_in.at[at(g), :], 1, g)

    def first_up_copy(g):
        return right(share_ref.at[at(g), :], up_in.at[at(g), :], 0, g)

    def first_down_copy(g):
        return left(share_ref.at[low(g), :], down_in.at[at(g), :], 1, g)

    def up_back_copy(g):
        return left(out_ref.at[at(g), :], out_ref.at[at(g), :], 2, g)

    def down_back_copy(g):
        return right(out_ref.at[low(g), :], out_ref.at[low(g), :], 3, g)

    if mode == "back":
        gain_grad_ref[...] = jnp.zeros_like(gain_grad_ref)

    def finish(total, g, place):
        base = base_ref[at(g), :].astype(f32)
        if mode == "sum":
            out_ref[place, :] = (base + total).astype(out_ref.dtype)
            return
        if mode == "norm":
            hidden = base + total
            kept_ref[at(g), :] = hidden
            scaling = lax.rsqrt(jnp.mean(hidden * hidden, axis=1, keepdims=True) + epsilon)
            out_ref[place, :] = (hidden * scaling * gain_ref[...]).astype(out_ref.dtype)
            return
        rows = x_ref[at(g), :].astype(f32)
        scaling = lax.rsqrt(jnp.mean(rows * rows, axis=1, keepdims=True) + epsilon)
        unit = rows * scaling
        gained = gain_ref[...] * total
        grad = base + scaling * (gained - unit * jnp.mean(gained * unit, axis=1, keepdims=True))
        kept_ref[at(g), :] = grad
        out_ref[place, :] = grad.astype(out_ref.dtype)
        term = total * unit
        part = term[0:8, :]
        for i in range(1, CHUNK // 8):
            part = part + term[8 * i : 8 * i + 8, :]
        gain_grad_ref[...] += part

    @pl.when(me == 0)
    def _():
        @pl.loop(0, count)
        def _(g):
            first_up_copy(g).start()

    @pl.when(me == n - 1)
    def _():
        @pl.loop(0, count)
        def _(g):
            first_down_copy(g).start()

    @pl.loop(0, count + n - 2)
    def _(step):
        g_up = step - (me - 1)

        @pl.when((me > 0) & (g_up >= 0) & (g_up < count))
        def _():
            up_copy(g_up).wait_recv()
            total = up_in[at(g_up), :].astype(f32) + share_ref[at(g_up), :].astype(f32)

            @pl.when(me < n - 1)
            def _():
                up_out[at(g_up), :] = total.astype(bf16)
                up_copy(g_up).start()

            @pl.when(me == n - 1)
            def _():
                finish(total, g_up, at(g_up))
                up_back_copy(g_up).start()

        g_down = step - (n - 2 - me)

        @pl.when((me < n - 1) & (g_down >= 0) & (g_down < count))
        def _():
            down_copy(g_down).wait_recv()
            total = down_in[at(g_down), :].astype(f32) + share_ref[low(g_down), :].astype(f32)

            @pl.when(me > 0)
            def _():
                down_out[at(g_down), :] = total.astype(bf16)
                down_copy(g_down).start()

            @pl.when(me == 0)
            def _():
                finish(total, g_down, low(g_down))
                down_back_copy(g_down).start()

    @pl.loop(0, count + n - 2)
    def _(step):
        g_up = step - (n - 2 - me)

        @pl.when((me < n - 1) & (g_up >= 0) & (g_up < count))
        def _():
            up_back_copy(g_up).wait_recv()

            @pl.when(me > 0)
            def _():
                up_back_copy(g_up).start()

        g_down = step - (me - 1)

        @pl.when((me > 0) & (g_down >= 0) & (g_down < count))
        def _():
            down_back_copy(g_down).wait_recv()

            @pl.when(me < n - 1)
            def _():
                down_back_copy(g_down).start()

    @pl.loop(0, count)
    def _(g):
        @pl.when(me < n - 1)
        def _():
            up_copy(g).wait_send()
            down_back_copy(g).wait_send()

        @pl.when(me > 0)
        def _():
            down_copy(g).wait_send()
            up_back_copy(g).wait_send()


def line_sum(mode, call, n, share, x_own, base_own, gain):
    rows, width = share.shape
    half = rows // 2
    vmem = pl.BlockSpec(memory_space=pltpu.VMEM)
    outs = [jax.ShapeDtypeStruct((rows, width), bf16)]
    if mode != "sum":
        outs.append(jax.ShapeDtypeStruct((half, width), f32))
    if mode == "back":
        outs.append(jax.ShapeDtypeStruct((8, width), f32))
    return pl.pallas_call(
        functools.partial(line_kernel, mode, n),
        in_specs=[vmem] * 4,
        out_specs=[vmem] * len(outs),
        out_shape=outs,
        scratch_shapes=[
            pltpu.VMEM((half, width), bf16),
            pltpu.VMEM((half, width), bf16),
            pltpu.VMEM((half, width), bf16),
            pltpu.VMEM((half, width), bf16),
            pltpu.SemaphoreType.DMA((8, half // CHUNK)),
        ],
        compiler_params=pltpu.CompilerParams(
            collective_id=call, has_side_effects=True, vmem_limit_bytes=40 << 20
        ),
        cost_estimate=pl.CostEstimate(
            flops=10_000_000, bytes_accessed=200_000_000, transcendentals=0
        ),
        name="line_" + mode,
    )(share, x_own, base_own, gain)


FINE = 16
SKEW = 2


def partner_of(index):
    return index + 1 - 2 * lax.rem(index, 2)


class GradPlan:
    def __init__(self, groups, count, width, row_widths, row_tiles, col_rows):
        self.groups, self.count, self.width = groups, count, width
        self.team = groups // 2
        self.block = width // groups
        self.half = width // 2
        self.row_widths, self.row_tiles, self.col_rows = row_widths, row_tiles, col_rows
        self.offsets = []
        total = 0
        for wide in row_widths:
            self.offsets.append(total)
            total += wide
        self.total = total
        self.col_tile = 256
        self.col_steps = self.half // self.col_tile


def sum_grads_kernel(n, plan, *refs):
    refs = list(refs)

    def take(k):
        out = refs[:k]
        del refs[:k]
        return out

    rows, cols = len(plan.row_widths), len(plan.col_rows)
    share_ref, x_ref, base_ref, gain_ref, left_ref = take(5)
    right_refs = take(rows)
    col_lefts = take(cols)
    col_rights = take(cols)
    out_ref, kept_ref, gain_grad_ref = take(3)
    row_outs = take(rows)
    col_outs = take(cols)
    up_in, down_in, left_in = take(3)
    right_in = take(rows)
    col_left_in = take(cols)
    col_right_in = take(cols)
    row_send, row_recv = take(2)
    col_send = take(cols)
    col_recv = take(cols)
    sems, left_sems, right_sems, row_sems = take(4)
    if cols:
        pair_sems, col_sems = take(2)

    me = lax.axis_index("tensor")
    member = lax.axis_index("dp")
    parity = lax.rem(member, 2)
    mine = member // 2
    partner = partner_of(member)
    groups, team, block = plan.groups, plan.team, plan.block
    half = up_in.shape[0]
    count = half // FINE
    inside = (me > 0) & (me < n - 1)

    barrier = pltpu.get_barrier_semaphore()

    @pl.when(me > 0)
    def _():
        pl.semaphore_signal(barrier, inc=1, device_id={"tensor": me - 1}, device_id_type=MESH)

    @pl.when(me < n - 1)
    def _():
        pl.semaphore_signal(barrier, inc=1, device_id={"tensor": me + 1}, device_id_type=MESH)

    if cols:
        greeted = groups - 1

        @pl.loop(1, groups)
        def _(k):
            pl.semaphore_signal(
                barrier, inc=1, device_id={"dp": lax.rem(member + k, groups)}, device_id_type=MESH
            )
    else:
        greeted = team
        pl.semaphore_signal(barrier, inc=1, device_id={"dp": partner}, device_id_type=MESH)

        @pl.loop(1, team)
        def _(k):
            pl.semaphore_signal(
                barrier, inc=1, device_id={"dp": 2 * lax.rem(mine + k, team) + parity},
                device_id_type=MESH,
            )

    @pl.when(inside)
    def _():
        pl.semaphore_wait(barrier, greeted + 2)

    @pl.when(jnp.logical_not(inside))
    def _():
        pl.semaphore_wait(barrier, greeted + 1)

    def at(g):
        return pl.ds(pl.multiple_of(g * FINE, FINE), FINE)

    def low(g):
        return pl.ds(pl.multiple_of(half + g * FINE, FINE), FINE)

    def right(source, target, lane, g):
        return pltpu.make_async_remote_copy(
            source, target, sems.at[2 * lane, g], sems.at[2 * lane + 1, g],
            device_id={"tensor": jnp.minimum(me + 1, n - 1)}, device_id_type=MESH,
        )

    def left(source, target, lane, g):
        return pltpu.make_async_remote_copy(
            source, target, sems.at[2 * lane, g], sems.at[2 * lane + 1, g],
            device_id={"tensor": jnp.maximum(me - 1, 0)}, device_id_type=MESH,
        )

    def up_copy(g):
        return right(up_in.at[at(g), :], up_in.at[at(g), :], 0, g)

    def down_copy(g):
        return left(down_in.at[at(g), :], down_in.at[at(g), :], 1, g)

    def first_up_copy(g):
        return right(share_ref.at[at(g), :], up_in.at[at(g), :], 0, g)

    def first_down_copy(g):
        return left(share_ref.at[low(g), :], down_in.at[at(g), :], 1, g)

    def up_back_copy(g):
        return left(out_ref.at[at(g), :], out_ref.at[at(g), :], 2, g)

    def down_back_copy(g):
        return right(out_ref.at[low(g), :], out_ref.at[low(g), :], 3, g)

    def to_partner(source, target, send, recv):
        return pltpu.make_async_remote_copy(
            source, target, send, recv, device_id={"dp": partner}, device_id_type=MESH
        )

    def columns(j):
        return pl.ds(pl.multiple_of(j * block, block), block)

    def left_copy(q):
        return to_partner(
            left_ref.at[:, columns(2 * q + 1 - parity)], left_in.at[:, columns(q)],
            left_sems.at[0, q], left_sems.at[1, q],
        )

    def right_copy(i):
        return to_partner(
            right_refs[i].at[:, : plan.row_widths[i]], right_in[i],
            right_sems.at[0, i], right_sems.at[1, i],
        )

    half_of = pl.ds(pl.multiple_of(parity * plan.half, plan.half), plan.half)
    other_half = pl.ds(pl.multiple_of((1 - parity) * plan.half, plan.half), plan.half)

    def pair_copies(i):
        return (
            to_partner(
                col_lefts[i], col_left_in[i], pair_sems.at[0, 2 * i], pair_sems.at[1, 2 * i]
            ),
            to_partner(
                col_rights[i].at[:, other_half], col_right_in[i],
                pair_sems.at[0, 2 * i + 1], pair_sems.at[1, 2 * i + 1],
            ),
        )

    def tile_columns(t):
        i, start, wide = plan.row_tiles[t]
        return pl.ds(plan.offsets[i] + start, wide)

    def row_copy(t, to, source):
        return pltpu.make_async_remote_copy(
            row_send.at[to, :, tile_columns(t)], row_recv.at[source, :, tile_columns(t)],
            row_sems.at[0, t, to], row_sems.at[1, t, source],
            device_id={"dp": 2 * to + parity}, device_id_type=MESH,
        )

    def col_copy(i, to, source):
        size = plan.col_rows[i] // groups
        return pltpu.make_async_remote_copy(
            col_send[i].at[pl.ds(pl.multiple_of(to * size, 16), size), :],
            col_recv[i].at[source],
            col_sems.at[0, i, to], col_sems.at[1, i, source],
            device_id={"dp": to}, device_id_type=MESH,
        )

    gain_grad_ref[...] = jnp.zeros_like(gain_grad_ref)

    def finish(total, g, place):
        rows_x = x_ref[at(g), :].astype(f32)
        scaling = lax.rsqrt(jnp.mean(rows_x * rows_x, axis=1, keepdims=True) + epsilon)
        unit = rows_x * scaling
        gained = gain_ref[...] * total
        grad = base_ref[at(g), :].astype(f32) + scaling * (
            gained - unit * jnp.mean(gained * unit, axis=1, keepdims=True)
        )
        kept_ref[at(g), :] = grad.astype(kept_ref.dtype)
        out_ref[place, :] = grad.astype(out_ref.dtype)
        term = total * unit
        part = term[0:8, :]
        for i in range(1, FINE // 8):
            part = part + term[8 * i : 8 * i + 8, :]
        gain_grad_ref[...] += part

    @pl.when(me == 0)
    def _():
        @pl.loop(0, count)
        def _(g):
            first_up_copy(g).start()

    @pl.when(me == n - 1)
    def _():
        @pl.loop(0, count)
        def _(g):
            first_down_copy(g).start()

    for i in range(cols):
        for c in pair_copies(i):
            c.start()
    for i in range(rows):
        right_copy(i).start()

    @pl.loop(0, team)
    def _(q):
        left_copy(q).start()

    tiles = len(plan.row_tiles)
    col_items = cols * plan.col_steps
    items = col_items + team * tiles

    def work(w):
        for i in range(cols):
            base = i * plan.col_steps

            @pl.when(w == base)
            def _():
                for c in pair_copies(i):
                    c.wait_recv()

            @pl.when((w >= base) & (w < base + plan.col_steps))
            def _():
                offset = pl.multiple_of((w - base) * plan.col_tile, plan.col_tile)
                own = pl.ds(
                    pl.multiple_of(parity * plan.half + offset, plan.col_tile), plan.col_tile
                )
                there = pl.ds(offset, plan.col_tile)
                product = rows_dot(col_lefts[i][...], col_rights[i][:, own]) + rows_dot(
                    col_left_in[i][...], col_right_in[i][:, there]
                )
                col_send[i][:, there] = product.astype(bf16)

            @pl.when(w == base + plan.col_steps - 1)
            def _():
                @pl.loop(1, groups)
                def _(k):
                    col_copy(i, lax.rem(member + k, groups), member).start()

        r = w - col_items

        @pl.when(r == 0)
        def _():
            for i in range(rows):
                right_copy(i).wait_recv()

            @pl.loop(0, team)
            def _(q):
                left_copy(q).wait_recv()

        k = r // tiles
        to = lax.rem(mine + 1 + k, team)
        for t in range(tiles):
            i, start, wide = plan.row_tiles[t]

            @pl.when((r >= 0) & (r < team * tiles) & (lax.rem(r, tiles) == t))
            def _():
                span = pl.ds(start, wide)
                product = rows_dot(
                    left_ref[:, columns(2 * to + parity)], right_refs[i][:, span]
                ) + rows_dot(left_in[:, columns(to)], right_in[i][:, span])
                low_product = product.astype(bf16)

                @pl.when(k < team - 1)
                def _():
                    row_send[to, :, tile_columns(t)] = low_product
                    row_copy(t, to, mine).start()

                @pl.when(k == team - 1)
                def _():
                    row_recv[mine, :, tile_columns(t)] = low_product

    delay = SKEW * (n - 2)
    second = count + 2
    start_work = 8

    @pl.loop(0, second + count + delay)
    def _(step):
        g_up = step - SKEW * (me - 1)

        @pl.when((me > 0) & (g_up >= 0) & (g_up < count))
        def _():
            up_copy(g_up).wait_recv()
            total = up_in[at(g_up), :].astype(f32) + share_ref[at(g_up), :].astype(f32)

            @pl.when(me < n - 1)
            def _():
                up_in[at(g_up), :] = total.astype(bf16)
                up_copy(g_up).start()

            @pl.when(me == n - 1)
            def _():
                finish(total, g_up, at(g_up))
                up_back_copy(g_up).start()

        g_down = step - SKEW * (n - 2 - me)

        @pl.when((me < n - 1) & (g_down >= 0) & (g_down < count))
        def _():
            down_copy(g_down).wait_recv()
            total = down_in[at(g_down), :].astype(f32) + share_ref[low(g_down), :].astype(f32)

            @pl.when(me > 0)
            def _():
                down_in[at(g_down), :] = total.astype(bf16)
                down_copy(g_down).start()

            @pl.when(me == 0)
            def _():
                finish(total, g_down, low(g_down))
                down_back_copy(g_down).start()

        work(step - start_work)

        g_up_back = step - second - SKEW * (n - 2 - me)

        @pl.when((me < n - 1) & (g_up_back >= 0) & (g_up_back < count))
        def _():
            up_back_copy(g_up_back).wait_recv()

            @pl.when(me > 0)
            def _():
                up_back_copy(g_up_back).start()

        g_down_back = step - second - SKEW * (me - 1)

        @pl.when((me > 0) & (g_down_back >= 0) & (g_down_back < count))
        def _():
            down_back_copy(g_down_back).wait_recv()

            @pl.when(me < n - 1)
            def _():
                down_back_copy(g_down_back).start()

    for i in range(cols):
        size = plan.col_rows[i] // groups
        own_rows = pl.ds(pl.multiple_of(member * size, 16), size)
        col_recv[i][pl.ds(member, 1)] = col_send[i][own_rows, :][None]

        @pl.loop(1, groups)
        def _(k):
            col_copy(i, 0, lax.rem(member + k, groups)).wait_recv()

        for b in range(2):
            total = col_recv[i][b].astype(f32)
            for q in range(1, team):
                total = total + col_recv[i][2 * q + b].astype(f32)
            col_outs[i][:, b * plan.half : (b + 1) * plan.half] = total
    for t in range(tiles):
        @pl.loop(1, team)
        def _(k):
            row_copy(t, 0, lax.rem(mine + k, team)).wait_recv()
    for i in range(rows):
        span = pl.ds(plan.offsets[i], plan.row_widths[i])
        total = row_recv[0, :, span].astype(f32)
        for q in range(1, team):
            total = total + row_recv[q, :, span].astype(f32)
        row_outs[i][...] = total

    @pl.loop(0, count)
    def _(g):
        @pl.when(me < n - 1)
        def _():
            up_copy(g).wait_send()
            down_back_copy(g).wait_send()

        @pl.when(me > 0)
        def _():
            down_copy(g).wait_send()
            up_back_copy(g).wait_send()

    for i in range(cols):
        for c in pair_copies(i):
            c.wait_send()

        @pl.loop(1, groups)
        def _(k):
            col_copy(i, lax.rem(member + k, groups), member).wait_send()
    for i in range(rows):
        right_copy(i).wait_send()

    @pl.loop(0, team)
    def _(q):
        left_copy(q).wait_send()

    for t in range(tiles):
        @pl.loop(1, team)
        def _(k):
            row_copy(t, lax.rem(mine + k, team), mine).wait_send()


def tiles_of(widths, most):
    return [
        (i, start, min(most, wide - start))
        for i, wide in enumerate(widths)
        for start in range(0, wide, most)
    ]


def sum_grads(
    name, call, n, groups, share, x_own, base_own, gain, kept_type, row_left, row_rights, row_widths,
    row_tiles, col_pairs,
):
    count, width = share.shape
    half = count // 2
    col_rows = [pair[0].shape[1] for pair in col_pairs]
    plan = GradPlan(groups, count, width, row_widths, row_tiles, col_rows)
    team = plan.team
    vmem = pl.BlockSpec(memory_space=pltpu.VMEM)
    outs = [
        jax.ShapeDtypeStruct((count, width), bf16),
        jax.ShapeDtypeStruct((half, width), kept_type),
        jax.ShapeDtypeStruct((8, width), f32),
    ]
    outs += [jax.ShapeDtypeStruct((plan.block, wide), f32) for wide in row_widths]
    outs += [jax.ShapeDtypeStruct((r // groups, width), f32) for r in col_rows]
    scratch = [
        pltpu.VMEM((half, width), bf16),
        pltpu.VMEM((half, width), bf16),
        pltpu.VMEM((count, plan.half), bf16),
    ]
    scratch += [pltpu.VMEM((count, wide), bf16) for wide in row_widths]
    scratch += [pltpu.VMEM((count, r), bf16) for r in col_rows]
    scratch += [pltpu.VMEM((count, plan.half), bf16) for _ in col_rows]
    scratch += [pltpu.VMEM((team, plan.block, plan.total), bf16)] * 2
    scratch += [pltpu.VMEM((r, plan.half), bf16) for r in col_rows]
    scratch += [pltpu.VMEM((groups, r // groups, plan.half), bf16) for r in col_rows]
    scratch += [
        pltpu.SemaphoreType.DMA((8, half // FINE)),
        pltpu.SemaphoreType.DMA((2, team)),
        pltpu.SemaphoreType.DMA((2, len(row_widths))),
        pltpu.SemaphoreType.DMA((2, len(row_tiles), team)),
    ]
    if col_rows:
        scratch += [
            pltpu.SemaphoreType.DMA((2, 2 * len(col_rows))),
            pltpu.SemaphoreType.DMA((2, len(col_rows), groups)),
        ]
    operands = [share, x_own, base_own, gain, row_left, *row_rights]
    operands += [pair[0] for pair in col_pairs] + [pair[1] for pair in col_pairs]
    return pl.pallas_call(
        functools.partial(sum_grads_kernel, n, plan),
        in_specs=[vmem] * len(operands),
        out_specs=[vmem] * len(outs),
        out_shape=outs,
        scratch_shapes=scratch,
        compiler_params=pltpu.CompilerParams(
            collective_id=call, has_side_effects=True, vmem_limit_bytes=60 << 20
        ),
        cost_estimate=pl.CostEstimate(
            flops=12_000_000_000, bytes_accessed=200_000_000, transcendentals=0
        ),
        name=name,
    )(*operands)


def small_sum_kernel(groups, n, rows_all, part_ref, out_ref, held, line, line_in, sems, line_sems):
    me = lax.axis_index("dp")
    place = lax.axis_index("tensor")
    barrier = pltpu.get_barrier_semaphore()

    def peer(k):
        return lax.rem(me + k, groups)

    def mate(k):
        return lax.rem(place + k, n)

    @pl.loop(1, groups)
    def _(k):
        pl.semaphore_signal(barrier, inc=1, device_id={"dp": peer(k)}, device_id_type=MESH)

    @pl.loop(1, n)
    def _(k):
        pl.semaphore_signal(barrier, inc=1, device_id={"tensor": mate(k)}, device_id_type=MESH)

    pl.semaphore_wait(barrier, groups + n - 2)

    def copy(k, source):
        return pltpu.make_async_remote_copy(
            part_ref.at[peer(k)], held.at[source], sems.at[0, k], sems.at[1, source],
            device_id={"dp": peer(k)}, device_id_type=MESH,
        )

    def line_copy(k, source):
        return pltpu.make_async_remote_copy(
            line, line_in.at[source], line_sems.at[0, k], line_sems.at[1, source],
            device_id={"tensor": mate(k)}, device_id_type=MESH,
        )

    @pl.loop(1, groups)
    def _(k):
        copy(k, me).start()

    held[pl.ds(me, 1)] = part_ref[pl.ds(me, 1)]

    @pl.loop(1, groups)
    def _(k):
        copy(k, peer(k)).wait_recv()

    total = held[0]
    for i in range(1, groups):
        total = total + held[i]
    line[...] = total[:rows_all]
    out_ref[...] = total

    @pl.loop(1, n)
    def _(k):
        line_copy(k, place).start()

    line_in[pl.ds(place, 1)] = total[None, :rows_all]

    @pl.loop(1, n)
    def _(k):
        line_copy(k, mate(k)).wait_recv()

    total = line_in[0]
    for i in range(1, n):
        total = total + line_in[i]
    out_ref[:rows_all] = total

    @pl.loop(1, groups)
    def _(k):
        copy(k, me).wait_send()

    @pl.loop(1, n)
    def _(k):
        line_copy(k, place).wait_send()


def small_sum(over_all, over_owners, groups, n, call):
    def tiles(blocks):
        short = -blocks.shape[1] % (8 * LANES)
        return jnp.pad(blocks, ((0, 0), (0, short))).reshape(groups, -1, LANES)

    first, second = tiles(over_all), tiles(over_owners)
    rows_all = first.shape[1]
    part = jnp.concatenate([first, second], axis=1)
    vmem = pl.BlockSpec(memory_space=pltpu.VMEM)
    total = pl.pallas_call(
        functools.partial(small_sum_kernel, groups, n, rows_all),
        in_specs=[vmem],
        out_specs=vmem,
        out_shape=jax.ShapeDtypeStruct(part.shape[1:], f32),
        scratch_shapes=[
            pltpu.VMEM(part.shape, f32),
            pltpu.VMEM((rows_all, LANES), f32),
            pltpu.VMEM((n, rows_all, LANES), f32),
            pltpu.SemaphoreType.DMA((2, groups)),
            pltpu.SemaphoreType.DMA((2, n)),
        ],
        compiler_params=pltpu.CompilerParams(collective_id=call, has_side_effects=True),
        name="small_sum",
    )(part)
    return (
        total[:rows_all].reshape(-1)[: over_all.shape[1]],
        total[rows_all:].reshape(-1)[: over_owners.shape[1]],
    )


def per_device(
    tokens,
    cotangent,
    token_slots,
    lengths,
    mixer_gain,
    query_weight,
    key_weight,
    value_weight,
    gate_weight,
    decay_down,
    decay_up,
    decay_bias,
    head_gain,
    out_weight,
    feed_gain,
    feed_gate,
    feed_up,
    feed_down,
):
    groups = lax.axis_size("dp")
    lines = lax.axis_size("tensor")
    member = lax.axis_index("dp")
    place = lax.axis_index("tensor")
    count, width = tokens.shape
    cap = OWN_CAP // groups
    slots = groups * cap
    dk = query_weight.shape[1]
    dv = value_weight.shape[1]
    rank = decay_up.shape[1]
    parity = lax.rem(member, 2)
    pairs = [(i, i ^ 1) for i in range(groups)]
    same_parity = [[i for i in range(groups) if i % 2 == b] for b in range(2)]

    owners = (token_slots // OWN_CAP).reshape(groups, count)
    mine = (owners == member).astype(bf16)
    my_slots = lax.dynamic_slice_in_dim(token_slots, member * count, count)
    my_owner = my_slots // OWN_CAP
    chosen = (my_owner[None, :] == jnp.arange(groups, dtype=jnp.int32)[:, None]).astype(bf16)
    index = jnp.arange(count, dtype=jnp.int32)
    before = (index[:, None] < index[None, :]).astype(bf16)
    ranks = dot(jnp.concatenate([mine, chosen], axis=0), before).astype(jnp.int32)
    recv_rank, send_rank = ranks[:groups], ranks[groups:]
    hit = (recv_rank[:, None, :] == jnp.arange(cap, dtype=jnp.int32)[None, :, None]) & (
        owners == member
    )[:, None, :]
    local = (token_slots % OWN_CAP).reshape(groups, count)
    slot_map = (
        jnp.sum(jnp.where(hit, local[:, None, :] - OWN_CAP, 0), axis=2) + OWN_CAP
    ).reshape(slots)
    send_pos = my_owner * cap + jnp.sum(
        jnp.where(chosen > 0, send_rank, 0), axis=0, dtype=jnp.int32
    )
    slot_ids = jnp.arange(slots, dtype=jnp.int32)
    pack = (slot_ids[:, None] == send_pos[None, :]).astype(bf16)
    unpack = (send_pos[:, None] == slot_ids[None, :]).astype(bf16)

    def exchange(row_block):
        blocks = row_block.reshape(groups, cap, row_block.shape[1])
        moved = lax.all_to_all(blocks, "dp", split_axis=0, concat_axis=0, tiled=True)
        return moved.reshape(slots, row_block.shape[1])

    half = count // 2
    own_at = jnp.where(place == 0, half, 0)
    tokens_own = lax.dynamic_slice_in_dim(tokens, own_at, half)
    cotangent_own = lax.dynamic_slice_in_dim(cotangent, own_at, half)

    tokens_wide = tokens.astype(f32)
    mixer_gain_wide = mixer_gain.astype(f32)
    feed_gain_wide = feed_gain.astype(f32)
    normed = (
        tokens_wide
        * lax.rsqrt(jnp.mean(tokens_wide * tokens_wide, axis=-1, keepdims=True) + epsilon)
        * mixer_gain_wide
    ).astype(bf16)
    queries = dot(normed, query_weight).astype(bf16)
    keys_low = dot(normed, key_weight).astype(bf16)
    value_rows = dot(normed, value_weight).astype(bf16)
    gate_pre = dot(normed, gate_weight)
    third = LANES // 4
    down_pad = jnp.pad(decay_down, ((0, 0), (0, third - rank)))
    latent = dot(
        normed,
        jnp.concatenate([down_pad, down_pad, down_pad, jnp.zeros_like(down_pad)], axis=1),
    )
    latent_high = latent.astype(bf16)
    latent_rest = latent - latent_high.astype(f32)
    latent_mid = latent_rest.astype(bf16)
    latent_low = (latent_rest - latent_mid.astype(f32)).astype(bf16)
    lane = jnp.arange(LANES, dtype=jnp.int32)[None, :]
    latent_packed = jnp.where(
        lane < third, latent_high, jnp.where(lane < 2 * third, latent_mid, latent_low)
    )
    rows_out = jnp.concatenate([queries, keys_low, value_rows, latent_packed], axis=1)
    arrived = exchange(dot(pack, rows_out).astype(bf16))
    up_pad = jnp.pad(decay_up, ((0, 0), (0, third - rank)))
    up_wide = jnp.concatenate([up_pad, up_pad, up_pad, jnp.zeros_like(up_pad)], axis=1).T
    down_wide = jnp.concatenate(
        [up_pad, up_pad, jnp.zeros_like(up_pad), jnp.zeros_like(up_pad)], axis=1
    )
    bias = decay_bias.astype(f32).reshape(1, dk)
    attended_slots, held, states = recur_forward(
        slot_map, lengths, up_wide, bias, arrived, dk, dv
    )
    attended = dot(unpack, exchange(attended_slots))

    head_gain_wide = head_gain.astype(f32)

    def head_output(rows, gate_rows, gain_row):
        scaling = lax.rsqrt(jnp.mean(rows * rows, axis=-1, keepdims=True) + head_floor)
        return rows * scaling * gain_row * jax.nn.silu(gate_rows)

    gated_wide, head_back = jax.vjp(head_output, attended, gate_pre, head_gain_wide)
    gated = gated_wide.astype(bf16)
    mixer_share = dot(gated, out_weight).astype(bf16)
    feed_normed, hidden_own = line_sum(
        "norm", 1, lines, mixer_share, tokens_own, tokens_own, feed_gain_wide.reshape(1, -1)
    )

    gate_hidden = dot(feed_normed, feed_gate)
    up_hidden = dot(feed_normed, feed_up)
    d_active = dot_t(cotangent, feed_down)
    sigmoid_gate = jax.nn.sigmoid(gate_hidden)
    swish_gate = gate_hidden * sigmoid_gate
    active = (swish_gate * up_hidden).astype(bf16)
    d_gate_hidden = (
        d_active * up_hidden * sigmoid_gate * (1.0 + gate_hidden * (1.0 - sigmoid_gate))
    ).astype(bf16)
    d_up_hidden = (d_active * swish_gate).astype(bf16)
    feed_share = (dot_t(d_gate_hidden, feed_gate) + dot_t(d_up_hidden, feed_up)).astype(bf16)
    fused = (width // groups) % LANES == 0
    if fused:
        d_mixed, d_hidden_own, feed_gain_part, grad_feed_gate, grad_feed_up = sum_grads(
            "back_feed", 2, lines, groups, feed_share, hidden_own, cotangent_own,
            feed_gain_wide.reshape(1, -1), f32, feed_normed, [d_gate_hidden, d_up_hidden],
            [d_gate_hidden.shape[1]] * 2, tiles_of([d_gate_hidden.shape[1]] * 2, 768), [],
        )
    else:
        d_mixed, d_hidden_own, feed_gain_part = line_sum(
            "back", 2, lines, feed_share, hidden_own, cotangent_own, feed_gain_wide.reshape(1, -1)
        )

    d_gated = dot_t(d_mixed, out_weight)
    d_attended, d_gate_pre, head_gain_part = head_back(d_gated)
    d_gate_low = d_gate_pre.astype(bf16)
    d_arrived = exchange(dot(pack, d_attended.astype(bf16)).astype(bf16))
    d_slots, up_part, bias_part = recur_backward(
        slot_map, lengths, up_wide, bias, down_wide, d_arrived, held, states, dk, dv
    )
    d_rows = dot(unpack, exchange(d_slots)).astype(bf16)
    d_query_low = d_rows[:, :dk]
    d_key_low = d_rows[:, dk : 2 * dk]
    d_value_low = d_rows[:, 2 * dk : 2 * dk + dv]
    d_latent_low = d_rows[:, 2 * dk + dv :]
    down_both = jnp.concatenate(
        [down_pad, down_pad, jnp.zeros_like(down_pad), jnp.zeros_like(down_pad)], axis=1
    )
    normed_share = (
        dot_t(d_query_low, query_weight)
        + dot_t(d_key_low, key_weight)
        + dot_t(d_value_low, value_weight)
        + dot_t(d_gate_low, gate_weight)
        + dot_t(d_latent_low, down_both)
    ).astype(bf16)
    if fused:
        (
            token_grad, _, mixer_gain_part, grad_rows, grad_gate, grad_out, grad_feed_down,
        ) = sum_grads(
            "back_mixer", 3, lines, groups, normed_share, tokens_own, d_hidden_own,
            mixer_gain_wide.reshape(1, -1), bf16, normed, [d_rows, d_gate_low],
            [2 * dk + dv, dv], tiles_of([2 * dk + dv, dv], 512),
            [(gated, d_mixed), (active, cotangent)],
        )
        grad_query = grad_rows[:, :dk]
        grad_key = grad_rows[:, dk : 2 * dk]
        grad_value = grad_rows[:, 2 * dk :]
    else:
        token_grad, _, mixer_gain_part = line_sum(
            "back", 3, lines, normed_share, tokens_own, d_hidden_own,
            mixer_gain_wide.reshape(1, -1),
        )
    hidden_placed = jnp.concatenate(
        [jnp.where(place == lines - 1, hidden_own, 0.0), jnp.where(place == 0, hidden_own, 0.0)],
        axis=0,
    )
    layer_out = lax.psum((dot(active, feed_down) + hidden_placed).astype(bf16), "tensor")

    def halves(row_block, dims):
        split = row_block.reshape(row_block.shape[0], groups // 2, 2, dims // groups)
        keep = lax.dynamic_index_in_dim(split, parity, 2, keepdims=False)
        send = lax.dynamic_index_in_dim(split, 1 - parity, 2, keepdims=False)
        got = lax.ppermute(send, "dp", pairs)
        shape = (row_block.shape[0], dims // 2)
        return keep.reshape(shape), got.reshape(shape)

    def partner(row_block):
        return row_block, lax.ppermute(row_block, "dp", pairs)

    def summed_share(left, right):
        share = (rows_dot(left[0], right[0]) + rows_dot(left[1], right[1])).astype(bf16)
        rows = share.shape[0] // (groups // 2)
        blocks = share.reshape(groups // 2, rows, share.shape[1])
        moved = lax.all_to_all(
            blocks, "dp", split_axis=0, concat_axis=0, tiled=True, axis_index_groups=same_parity
        )
        return jnp.sum(moved.astype(f32), axis=0)

    if not fused:
        feed_halves = halves(feed_normed, width)
        normed_halves = halves(normed, width)
        grad_feed_down = summed_share(halves(active, active.shape[1]), partner(cotangent))
        grad_feed_gate = summed_share(feed_halves, partner(d_gate_hidden))
        grad_feed_up = summed_share(feed_halves, partner(d_up_hidden))
        grad_out = summed_share(halves(gated, dv), partner(d_mixed))
        grad_query = summed_share(normed_halves, partner(d_query_low))
        grad_key = summed_share(normed_halves, partner(d_key_low))
        grad_value = summed_share(normed_halves, partner(d_value_low))
        grad_gate = summed_share(normed_halves, partner(d_gate_low))

    down_part = rows_dot(normed, d_latent_low)
    down_part = down_part[:, :rank] + down_part[:, third : third + rank]
    up_part = up_part[:, :rank] + up_part[:, third : third + rank] + (
        up_part[:, 2 * third : 2 * third + rank]
    )

    def by_owner(vector):
        return vector.reshape(groups, -1)

    over_all = jnp.concatenate(
        [
            by_owner(jnp.sum(mixer_gain_part, axis=0)),
            by_owner(jnp.sum(feed_gain_part, axis=0)),
            by_owner(head_gain_part),
            by_owner(down_part),
        ],
        axis=1,
    )
    over_owners = jnp.concatenate([by_owner(up_part), by_owner(bias_part[0])], axis=1)
    summed, small = small_sum(over_all, over_owners, groups, lines, 5)
    per = width // groups
    head_per = dv // groups
    return (
        layer_out,
        token_grad,
        summed[:per],
        grad_query,
        grad_key,
        grad_value,
        grad_gate,
        summed[2 * per + head_per :].reshape(per, rank),
        small[: dk // groups * rank].reshape(1, dk // groups, rank),
        small[dk // groups * rank :].reshape(1, dk // groups),
        summed[2 * per : 2 * per + head_per],
        grad_out[None],
        summed[per : 2 * per],
        grad_feed_gate,
        grad_feed_up,
        grad_feed_down[None],
    )


def solution(mesh):
    placed = (
        P("dp", None),
        P("dp", None),
        P(),
        P("dp", None),
        P(),
        P(None, "tensor"),
        P(None, "tensor"),
        P(None, "tensor"),
        P(None, "tensor"),
        P(),
        P("tensor", None),
        P("tensor"),
        P(),
        P("tensor", None),
        P(),
        P(None, "tensor"),
        P(None, "tensor"),
        P("tensor", None),
    )
    return jax.shard_map(
        per_device,
        mesh=mesh,
        in_specs=placed,
        out_specs=(
            P("dp", None),
            P("dp", None),
            P("dp"),
            P("dp", "tensor"),
            P("dp", "tensor"),
            P("dp", "tensor"),
            P("dp", "tensor"),
            P("dp", None),
            P("tensor", "dp", None),
            P("tensor", "dp"),
            P("dp"),
            P("tensor", "dp", None),
            P("dp"),
            P("dp", "tensor"),
            P("dp", "tensor"),
            P("tensor", "dp", None),
        ),
        check_vma=False,
    )
```

```python
import functools

import jax
import jax.numpy as jnp
from jax import lax
from jax.experimental import pallas as pl
from jax.experimental.pallas import tpu as pltpu
from jax.sharding import PartitionSpec as P

OWN_CAP = 1024
SPAN = 128
LANES = 128
epsilon = 1e-06
head_floor = 1.0

f32 = jnp.float32
bf16 = jnp.bfloat16
MESH = pl.DeviceIdType.MESH


def rows_dot(left, right):
    return lax.dot_general(left, right, (((0,), (0,)), ((), ())), preferred_element_type=f32)


def dot_t(left, right):
    return lax.dot_general(left, right, (((1,), (1,)), ((), ())), preferred_element_type=f32)


def dot(left, right):
    return jnp.dot(left, right, preferred_element_type=f32)


def span_terms(first, ends, logits):
    rows = logits.shape[0]

    def label(position):
        count = jnp.zeros_like(position)
        for end in ends:
            count = count + (position >= end).astype(jnp.int32)
        return count

    log_decay = jax.nn.log_sigmoid(logits) * (1.0 / 16.0)
    row = lax.broadcasted_iota(jnp.int32, (rows, rows), 0)
    column = lax.broadcasted_iota(jnp.int32, (rows, rows), 1)
    lower = (row >= column).astype(f32)
    cumulative = jnp.dot(
        lower, log_decay, precision=lax.Precision.HIGHEST, preferred_element_type=f32
    )
    total = cumulative[rows - 1 :, :]
    middle = cumulative[rows // 2 - 1 : rows // 2, :]
    label_column = label(first + lax.broadcasted_iota(jnp.int32, (rows, 1), 0))
    label_row = label(first + lax.broadcasted_iota(jnp.int32, (1, rows), 1))
    before = jnp.where(first > 0, label(first - 1), -1)
    last = label(first + rows - 1)
    carried = (label_column == before).astype(f32)
    tail = (label_column == last).astype(f32)
    keep = (before == last).astype(f32)
    allowed = (row >= column) & (label_column == label_row)
    return log_decay, cumulative, total, middle, carried, tail, keep, allowed


def recur_forward_kernel(
    dk, dv, slot_row_ref, slot_column_ref, lengths_ref, up_ref, bias_ref, arrived_ref,
    out_ref, held_ref, states_ref, state, result,
):
    step = pl.program_id(0)
    first = step * SPAN
    end0 = lengths_ref[0, 0]
    end1 = end0 + lengths_ref[0, 1]
    end2 = end1 + lengths_ref[0, 2]
    slots = slot_row_ref.shape[1]

    @pl.when(step == 0)
    def _():
        state[...] = jnp.zeros_like(state)

    position = first + lax.broadcasted_iota(jnp.int32, (SPAN, slots), 0)
    place = (slot_row_ref[...] == position).astype(f32).astype(bf16)
    held = dot(place, arrived_ref[...]).astype(bf16)
    held_ref[...] = held
    queries = held[:, :dk].astype(f32) * (float(dk) ** -0.5)
    keys = held[:, dk : 2 * dk].astype(f32)
    values = held[:, 2 * dk : 2 * dk + dv]
    logits = dot(held[:, 2 * dk + dv :], up_ref[...]) + bias_ref[...]
    _, cumulative, total, middle, carried, tail, keep, allowed = span_terms(
        first, (end0, end1, end2), logits
    )
    query_mid = (queries * jnp.exp(cumulative - middle)).astype(bf16)
    key_mid = (keys * jnp.exp(middle - cumulative)).astype(bf16)
    query_start = (queries * jnp.exp(cumulative) * carried).astype(bf16)
    key_end = (keys * jnp.exp(total - cumulative) * tail).astype(bf16)
    scores = jnp.where(allowed, dot_t(query_mid, key_mid), 0.0).astype(bf16)
    entering = state[...]
    entering_low = entering.astype(bf16)
    states_ref[0] = entering_low
    attended = dot(scores, values) + dot(query_start, entering_low)
    result[pl.ds(pl.multiple_of(first, SPAN), SPAN), :] = attended.astype(bf16)
    decay_column = jnp.transpose(jnp.broadcast_to(keep * jnp.exp(total), (8, dk)))[:, :1]
    state[...] = decay_column * entering + rows_dot(key_end, values)

    @pl.when(step == pl.num_programs(0) - 1)
    def _():
        return_rows(slot_column_ref, result, out_ref)


def return_rows(slot_column_ref, source, out_ref):
    positions = source.shape[0]
    block = 256

    def body(i, carry):
        at = pl.ds(pl.multiple_of(i * block, block), block)
        column = lax.broadcasted_iota(jnp.int32, (block, positions), 1)
        pick = (slot_column_ref[at, :] == column).astype(f32).astype(bf16)
        out_ref[at, :] = dot(pick, source[...]).astype(out_ref.dtype)
        return carry

    lax.fori_loop(0, out_ref.shape[0] // block, body, 0)


def span_backward(
    dk, dv, step, ends, d_out, held_ref, entering, up_ref, bias_ref, down_ref, d_state, result,
    grad_up_ref, grad_bias_ref,
):
    first = step * SPAN
    at = pl.ds(pl.multiple_of(first, SPAN), SPAN)
    scale = float(dk) ** -0.5
    queries = held_ref[at, :dk].astype(f32) * scale
    keys = held_ref[at, dk : 2 * dk].astype(f32)
    values = held_ref[at, 2 * dk : 2 * dk + dv]
    latent = held_ref[at, 2 * dk + dv :]
    logits = dot(latent, up_ref[...]) + bias_ref[...]
    _, cumulative, total, middle, carried, tail, keep, allowed = span_terms(first, ends, logits)
    grow_query = jnp.exp(cumulative - middle)
    grow_key = jnp.exp(middle - cumulative)
    start_decay = jnp.exp(cumulative) * carried
    end_decay = jnp.exp(total - cumulative) * tail
    query_mid = (queries * grow_query).astype(bf16)
    key_mid = (keys * grow_key).astype(bf16)
    query_start = (queries * start_decay).astype(bf16)
    key_end = (keys * end_decay).astype(bf16)
    scores = jnp.where(allowed, dot_t(query_mid, key_mid), 0.0).astype(bf16)
    d_scores = jnp.where(allowed, dot_t(d_out, values), 0.0).astype(bf16)
    leaving = d_state[...]
    leaving_low = leaving.astype(bf16)
    d_values = rows_dot(scores, d_out) + dot(key_end, leaving_low)
    d_queries = dot(d_scores, key_mid) * grow_query + dot_t(d_out, entering) * start_decay
    d_key_end = dot_t(values, leaving_low) * end_decay
    d_keys = rows_dot(d_scores, query_mid) * grow_key + d_key_end
    kept = keep * jnp.exp(total)
    state_pair = jnp.sum(entering.astype(f32) * leaving, axis=1, keepdims=True)
    state_row = jnp.transpose(jnp.broadcast_to(state_pair, (dk, LANES)))[:1, :]
    d_total = jnp.sum(keys * d_key_end, axis=0, keepdims=True) + kept * state_row
    d_cumulative = queries * d_queries - keys * d_keys
    row = lax.broadcasted_iota(jnp.int32, (SPAN, SPAN), 0)
    column = lax.broadcasted_iota(jnp.int32, (SPAN, SPAN), 1)
    upper = (row <= column).astype(f32)
    d_log_decay = (
        jnp.dot(upper, d_cumulative, precision=lax.Precision.HIGHEST, preferred_element_type=f32)
        + d_total
    )
    d_logits = d_log_decay * (1.0 / 16.0) * jax.nn.sigmoid(-logits)
    grad_bias_ref[...] += jnp.broadcast_to(jnp.sum(d_logits, axis=0, keepdims=True), (8, dk))
    d_logits_high = d_logits.astype(bf16)
    d_logits_low = (d_logits - d_logits_high.astype(f32)).astype(bf16)
    grad_up_ref[...] += rows_dot(d_logits_high, latent) + rows_dot(d_logits_low, latent)
    d_latent = dot(d_logits_high, down_ref[...]) + dot(d_logits_low, down_ref[...])
    high = d_latent.astype(bf16).astype(f32)
    lane = lax.broadcasted_iota(jnp.int32, d_latent.shape, 1)
    d_latent_packed = jnp.where(lane < LANES // 4, high, d_latent - high)
    result[at, :dk] = (d_queries * scale).astype(bf16)
    result[at, dk : 2 * dk] = d_keys.astype(bf16)
    result[at, 2 * dk : 2 * dk + dv] = d_values.astype(bf16)
    result[at, 2 * dk + dv :] = d_latent_packed.astype(bf16)
    kept_column = jnp.transpose(jnp.broadcast_to(kept, (8, dk)))[:, :1]
    d_state[...] = kept_column * leaving + rows_dot(query_start, d_out)


def whole(shape):
    return pl.BlockSpec(shape, lambda i: (0,) * len(shape))


def recur_forward(slot_map, lengths, up_wide, bias, arrived, dk, dv):
    slots, width = arrived.shape
    steps = OWN_CAP // SPAN
    return pl.pallas_call(
        functools.partial(recur_forward_kernel, dk, dv),
        grid=(steps,),
        in_specs=[
            whole((1, slots)),
            whole((slots, 1)),
            pl.BlockSpec(memory_space=pltpu.SMEM),
            whole((LANES, dk)),
            whole((1, dk)),
            whole((slots, width)),
        ],
        out_specs=[
            whole((slots, dv)),
            pl.BlockSpec((SPAN, width), lambda i: (i, 0)),
            pl.BlockSpec((1, dk, dv), lambda i: (i, 0, 0)),
        ],
        out_shape=[
            jax.ShapeDtypeStruct((slots, dv), bf16),
            jax.ShapeDtypeStruct((OWN_CAP, width), bf16),
            jax.ShapeDtypeStruct((steps, dk, dv), bf16),
        ],
        scratch_shapes=[pltpu.VMEM((dk, dv), f32), pltpu.VMEM((OWN_CAP, dv), bf16)],
        compiler_params=pltpu.CompilerParams(vmem_limit_bytes=40 << 20),
        cost_estimate=pl.CostEstimate(
            flops=6_000_000_000, bytes_accessed=10_000_000, transcendentals=2_000_000
        ),
        name="recur_forward",
    )(slot_map.reshape(1, -1), slot_map.reshape(-1, 1), lengths, up_wide, bias, arrived)


FINE = 16
SKEW = 2


class Line:
    def __init__(self, n, share_ref, up_in, down_in, out_ref, sems, finish):
        self.n, self.me = n, lax.axis_index("tensor")
        self.share, self.up_in, self.down_in, self.out = share_ref, up_in, down_in, out_ref
        self.sems, self.finish = sems, finish
        self.half = up_in.shape[0]
        self.count = self.half // FINE
        self.second = self.count + 2
        self.steps = self.second + self.count + SKEW * (n - 2)

    @staticmethod
    def scratch(half, width):
        return [pltpu.VMEM((half, width), bf16), pltpu.VMEM((half, width), bf16)]

    @staticmethod
    def semaphores(half):
        return pltpu.SemaphoreType.DMA((8, half // FINE))

    def greet(self, barrier, others):
        n, me = self.n, self.me

        @pl.when(me > 0)
        def _():
            pl.semaphore_signal(barrier, inc=1, device_id={"tensor": me - 1}, device_id_type=MESH)

        @pl.when(me < n - 1)
        def _():
            pl.semaphore_signal(barrier, inc=1, device_id={"tensor": me + 1}, device_id_type=MESH)

        inside = (me > 0) & (me < n - 1)

        @pl.when(inside)
        def _():
            pl.semaphore_wait(barrier, others + 2)

        @pl.when(jnp.logical_not(inside))
        def _():
            pl.semaphore_wait(barrier, others + 1)

    def at(self, g):
        return pl.ds(pl.multiple_of(g * FINE, FINE), FINE)

    def low(self, g):
        return pl.ds(pl.multiple_of(self.half + g * FINE, FINE), FINE)

    def right(self, source, target, lane, g):
        return pltpu.make_async_remote_copy(
            source, target, self.sems.at[2 * lane, g], self.sems.at[2 * lane + 1, g],
            device_id={"tensor": jnp.minimum(self.me + 1, self.n - 1)}, device_id_type=MESH,
        )

    def left(self, source, target, lane, g):
        return pltpu.make_async_remote_copy(
            source, target, self.sems.at[2 * lane, g], self.sems.at[2 * lane + 1, g],
            device_id={"tensor": jnp.maximum(self.me - 1, 0)}, device_id_type=MESH,
        )

    def up_copy(self, g):
        rows = self.up_in.at[self.at(g), :]
        return self.right(rows, rows, 0, g)

    def down_copy(self, g):
        rows = self.down_in.at[self.at(g), :]
        return self.left(rows, rows, 1, g)

    def up_back_copy(self, g):
        rows = self.out.at[self.at(g), :]
        return self.left(rows, rows, 2, g)

    def down_back_copy(self, g):
        rows = self.out.at[self.low(g), :]
        return self.right(rows, rows, 3, g)

    def prime(self):
        @pl.when(self.me == 0)
        def _():
            @pl.loop(0, self.count)
            def _(g):
                self.right(
                    self.share.at[self.at(g), :], self.up_in.at[self.at(g), :], 0, g
                ).start()

        @pl.when(self.me == self.n - 1)
        def _():
            @pl.loop(0, self.count)
            def _(g):
                self.left(
                    self.share.at[self.low(g), :], self.down_in.at[self.at(g), :], 1, g
                ).start()

    def step(self, step):
        n, me, count = self.n, self.me, self.count
        at, low = self.at, self.low
        g_up = step - SKEW * (me - 1)

        @pl.when((me > 0) & (g_up >= 0) & (g_up < count))
        def _():
            self.up_copy(g_up).wait_recv()
            total = self.up_in[at(g_up), :].astype(f32) + self.share[at(g_up), :].astype(f32)

            @pl.when(me < n - 1)
            def _():
                self.up_in[at(g_up), :] = total.astype(bf16)
                self.up_copy(g_up).start()

            @pl.when(me == n - 1)
            def _():
                self.finish(total, at(g_up), at(g_up))
                self.up_back_copy(g_up).start()

        g_down = step - SKEW * (n - 2 - me)

        @pl.when((me < n - 1) & (g_down >= 0) & (g_down < count))
        def _():
            self.down_copy(g_down).wait_recv()
            total = self.down_in[at(g_down), :].astype(f32) + (
                self.share[low(g_down), :].astype(f32)
            )

            @pl.when(me > 0)
            def _():
                self.down_in[at(g_down), :] = total.astype(bf16)
                self.down_copy(g_down).start()

            @pl.when(me == 0)
            def _():
                self.finish(total, at(g_down), low(g_down))
                self.down_back_copy(g_down).start()

        g_up_back = step - self.second - SKEW * (n - 2 - me)

        @pl.when((me < n - 1) & (g_up_back >= 0) & (g_up_back < count))
        def _():
            self.up_back_copy(g_up_back).wait_recv()

            @pl.when(me > 0)
            def _():
                self.up_back_copy(g_up_back).start()

        g_down_back = step - self.second - SKEW * (me - 1)

        @pl.when((me > 0) & (g_down_back >= 0) & (g_down_back < count))
        def _():
            self.down_back_copy(g_down_back).wait_recv()

            @pl.when(me < n - 1)
            def _():
                self.down_back_copy(g_down_back).start()

    def run(self, first, last):
        @pl.loop(first, last)
        def _(step):
            self.step(step)

    def drain(self):
        n, me = self.n, self.me

        @pl.loop(0, self.count)
        def _(g):
            @pl.when(me < n - 1)
            def _():
                self.up_copy(g).wait_send()
                self.down_back_copy(g).wait_send()

            @pl.when(me > 0)
            def _():
                self.down_copy(g).wait_send()
                self.up_back_copy(g).wait_send()


def norm_back(x_ref, base_ref, gain_ref, out_ref, kept_ref, gain_grad_ref):
    gain_grad_ref[...] = jnp.zeros_like(gain_grad_ref)

    def finish(total, own, place):
        rows = x_ref[own, :].astype(f32)
        scaling = lax.rsqrt(jnp.mean(rows * rows, axis=1, keepdims=True) + epsilon)
        unit = rows * scaling
        gained = gain_ref[...] * total
        grad = base_ref[own, :].astype(f32) + scaling * (
            gained - unit * jnp.mean(gained * unit, axis=1, keepdims=True)
        )
        kept_ref[own, :] = grad.astype(kept_ref.dtype)
        out_ref[place, :] = grad.astype(out_ref.dtype)
        term = total * unit
        part = term[0:8, :]
        for i in range(1, FINE // 8):
            part = part + term[8 * i : 8 * i + 8, :]
        gain_grad_ref[...] += part

    return finish


def line_kernel(mode, n, *refs):
    share_ref, x_ref, base_ref, gain_ref, out_ref, kept_ref = refs[:6]
    if mode == "norm":
        up_in, down_in, sems = refs[6:]

        def finish(total, own, place):
            hidden = base_ref[own, :].astype(f32) + total
            kept_ref[own, :] = hidden
            scaling = lax.rsqrt(jnp.mean(hidden * hidden, axis=1, keepdims=True) + epsilon)
            out_ref[place, :] = (hidden * scaling * gain_ref[...]).astype(out_ref.dtype)
    else:
        gain_grad_ref, up_in, down_in, sems = refs[6:]
        finish = norm_back(x_ref, base_ref, gain_ref, out_ref, kept_ref, gain_grad_ref)
    line = Line(n, share_ref, up_in, down_in, out_ref, sems, finish)
    line.greet(pltpu.get_barrier_semaphore(), 0)
    line.prime()
    line.run(0, line.steps)
    line.drain()


def line_sum(mode, call, n, share, x_own, base_own, gain):
    rows, width = share.shape
    half = rows // 2
    vmem = pl.BlockSpec(memory_space=pltpu.VMEM)
    outs = [jax.ShapeDtypeStruct((rows, width), bf16), jax.ShapeDtypeStruct((half, width), f32)]
    if mode == "back":
        outs.append(jax.ShapeDtypeStruct((8, width), f32))
    return pl.pallas_call(
        functools.partial(line_kernel, mode, n),
        in_specs=[vmem] * 4,
        out_specs=[vmem] * len(outs),
        out_shape=outs,
        scratch_shapes=Line.scratch(half, width) + [Line.semaphores(half)],
        compiler_params=pltpu.CompilerParams(
            collective_id=call, has_side_effects=True, vmem_limit_bytes=40 << 20
        ),
        cost_estimate=pl.CostEstimate(
            flops=10_000_000, bytes_accessed=200_000_000, transcendentals=0
        ),
        name="line_" + mode,
    )(share, x_own, base_own, gain)


def partner_of(index):
    return index + 1 - 2 * lax.rem(index, 2)


class GradPlan:
    def __init__(self, groups, count, width, row_widths, row_tiles, col_rows):
        self.groups, self.count, self.width = groups, count, width
        self.team = groups // 2
        self.block = width // groups
        self.half = width // 2
        self.row_widths, self.row_tiles, self.col_rows = row_widths, row_tiles, col_rows
        self.offsets = []
        total = 0
        for wide in row_widths:
            self.offsets.append(total)
            total += wide
        self.total = total
        self.col_tile = 256
        self.col_steps = self.half // self.col_tile


def sum_grads_kernel(n, plan, *refs):
    refs = list(refs)

    def take(k):
        out = refs[:k]
        del refs[:k]
        return out

    rows, cols = len(plan.row_widths), len(plan.col_rows)
    share_ref, x_ref, base_ref, gain_ref, left_ref = take(5)
    right_refs = take(rows)
    col_lefts = take(cols)
    col_rights = take(cols)
    out_ref, kept_ref, gain_grad_ref = take(3)
    row_outs = take(rows)
    col_outs = take(cols)
    up_in, down_in, left_in = take(3)
    right_in = take(rows)
    col_left_in = take(cols)
    col_right_in = take(cols)
    row_send, row_recv = take(2)
    col_send = take(cols)
    col_recv = take(cols)
    sems, left_sems, right_sems, row_sems = take(4)
    if cols:
        pair_sems, col_sems = take(2)

    member = lax.axis_index("dp")
    parity = lax.rem(member, 2)
    mine = member // 2
    partner = partner_of(member)
    groups, team, block = plan.groups, plan.team, plan.block
    finish = norm_back(x_ref, base_ref, gain_ref, out_ref, kept_ref, gain_grad_ref)
    line = Line(n, share_ref, up_in, down_in, out_ref, sems, finish)

    barrier = pltpu.get_barrier_semaphore()
    if cols:
        greeted = groups - 1

        @pl.loop(1, groups)
        def _(k):
            pl.semaphore_signal(
                barrier, inc=1, device_id={"dp": lax.rem(member + k, groups)}, device_id_type=MESH
            )
    else:
        greeted = team
        pl.semaphore_signal(barrier, inc=1, device_id={"dp": partner}, device_id_type=MESH)

        @pl.loop(1, team)
        def _(k):
            pl.semaphore_signal(
                barrier, inc=1, device_id={"dp": 2 * lax.rem(mine + k, team) + parity},
                device_id_type=MESH,
            )
    line.greet(barrier, greeted)

    def to_partner(source, target, send, recv):
        return pltpu.make_async_remote_copy(
            source, target, send, recv, device_id={"dp": partner}, device_id_type=MESH
        )

    def columns(j):
        return pl.ds(pl.multiple_of(j * block, block), block)

    def left_copy(q):
        return to_partner(
            left_ref.at[:, columns(2 * q + 1 - parity)], left_in.at[:, columns(q)],
            left_sems.at[0, q], left_sems.at[1, q],
        )

    def right_copy(i):
        return to_partner(
            right_refs[i].at[:, : plan.row_widths[i]], right_in[i],
            right_sems.at[0, i], right_sems.at[1, i],
        )

    half_of = pl.ds(pl.multiple_of(parity * plan.half, plan.half), plan.half)
    other_half = pl.ds(pl.multiple_of((1 - parity) * plan.half, plan.half), plan.half)

    def pair_copies(i):
        return (
            to_partner(
                col_lefts[i], col_left_in[i], pair_sems.at[0, 2 * i], pair_sems.at[1, 2 * i]
            ),
            to_partner(
                col_rights[i].at[:, other_half], col_right_in[i],
                pair_sems.at[0, 2 * i + 1], pair_sems.at[1, 2 * i + 1],
            ),
        )

    def tile_columns(t):
        i, start, wide = plan.row_tiles[t]
        return pl.ds(plan.offsets[i] + start, wide)

    def row_copy(t, to, source):
        return pltpu.make_async_remote_copy(
            row_send.at[to, :, tile_columns(t)], row_recv.at[source, :, tile_columns(t)],
            row_sems.at[0, t, to], row_sems.at[1, t, source],
            device_id={"dp": 2 * to + parity}, device_id_type=MESH,
        )

    def col_copy(i, to, source):
        size = plan.col_rows[i] // groups
        return pltpu.make_async_remote_copy(
            col_send[i].at[pl.ds(pl.multiple_of(to * size, 16), size), :],
            col_recv[i].at[source],
            col_sems.at[0, i, to], col_sems.at[1, i, source],
            device_id={"dp": to}, device_id_type=MESH,
        )

    line.prime()
    for i in range(cols):
        for c in pair_copies(i):
            c.start()
    for i in range(rows):
        right_copy(i).start()

    @pl.loop(0, team)
    def _(q):
        left_copy(q).start()

    tiles = len(plan.row_tiles)
    col_items = cols * plan.col_steps
    items = col_items + team * tiles

    def work(w):
        for i in range(cols):
            base = i * plan.col_steps

            @pl.when(w == base)
            def _():
                for c in pair_copies(i):
                    c.wait_recv()

            @pl.when((w >= base) & (w < base + plan.col_steps))
            def _():
                offset = pl.multiple_of((w - base) * plan.col_tile, plan.col_tile)
                own = pl.ds(
                    pl.multiple_of(parity * plan.half + offset, plan.col_tile), plan.col_tile
                )
                there = pl.ds(offset, plan.col_tile)
                product = rows_dot(col_lefts[i][...], col_rights[i][:, own]) + rows_dot(
                    col_left_in[i][...], col_right_in[i][:, there]
                )
                col_send[i][:, there] = product.astype(bf16)

            @pl.when(w == base + plan.col_steps - 1)
            def _():
                @pl.loop(1, groups)
                def _(k):
                    col_copy(i, lax.rem(member + k, groups), member).start()

        r = w - col_items

        @pl.when(r == 0)
        def _():
            for i in range(rows):
                right_copy(i).wait_recv()

            @pl.loop(0, team)
            def _(q):
                left_copy(q).wait_recv()

        k = r // tiles
        to = lax.rem(mine + 1 + k, team)
        for t in range(tiles):
            i, start, wide = plan.row_tiles[t]

            @pl.when((r >= 0) & (r < team * tiles) & (lax.rem(r, tiles) == t))
            def _():
                span = pl.ds(start, wide)
                product = rows_dot(
                    left_ref[:, columns(2 * to + parity)], right_refs[i][:, span]
                ) + rows_dot(left_in[:, columns(to)], right_in[i][:, span])
                low_product = product.astype(bf16)

                @pl.when(k < team - 1)
                def _():
                    row_send[to, :, tile_columns(t)] = low_product
                    row_copy(t, to, mine).start()

                @pl.when(k == team - 1)
                def _():
                    row_recv[mine, :, tile_columns(t)] = low_product

    start_work = 8

    @pl.loop(0, line.steps)
    def _(step):
        line.step(step)
        work(step - start_work)

    for i in range(cols):
        size = plan.col_rows[i] // groups
        own_rows = pl.ds(pl.multiple_of(member * size, 16), size)
        col_recv[i][pl.ds(member, 1)] = col_send[i][own_rows, :][None]

        @pl.loop(1, groups)
        def _(k):
            col_copy(i, 0, lax.rem(member + k, groups)).wait_recv()

        for b in range(2):
            total = col_recv[i][b].astype(f32)
            for q in range(1, team):
                total = total + col_recv[i][2 * q + b].astype(f32)
            col_outs[i][:, b * plan.half : (b + 1) * plan.half] = total
    for t in range(tiles):
        @pl.loop(1, team)
        def _(k):
            row_copy(t, 0, lax.rem(mine + k, team)).wait_recv()
    for i in range(rows):
        span = pl.ds(plan.offsets[i], plan.row_widths[i])
        total = row_recv[0, :, span].astype(f32)
        for q in range(1, team):
            total = total + row_recv[q, :, span].astype(f32)
        row_outs[i][...] = total

    line.drain()
    for i in range(cols):
        for c in pair_copies(i):
            c.wait_send()

        @pl.loop(1, groups)
        def _(k):
            col_copy(i, lax.rem(member + k, groups), member).wait_send()
    for i in range(rows):
        right_copy(i).wait_send()

    @pl.loop(0, team)
    def _(q):
        left_copy(q).wait_send()

    for t in range(tiles):
        @pl.loop(1, team)
        def _(k):
            row_copy(t, lax.rem(mine + k, team), mine).wait_send()


def tiles_of(widths, most):
    return [
        (i, start, min(most, wide - start))
        for i, wide in enumerate(widths)
        for start in range(0, wide, most)
    ]


def sum_grads(
    name, call, n, groups, share, x_own, base_own, gain, kept_type, row_left, row_rights, row_widths,
    row_tiles, col_pairs,
):
    count, width = share.shape
    half = count // 2
    col_rows = [pair[0].shape[1] for pair in col_pairs]
    plan = GradPlan(groups, count, width, row_widths, row_tiles, col_rows)
    team = plan.team
    vmem = pl.BlockSpec(memory_space=pltpu.VMEM)
    outs = [
        jax.ShapeDtypeStruct((count, width), bf16),
        jax.ShapeDtypeStruct((half, width), kept_type),
        jax.ShapeDtypeStruct((8, width), f32),
    ]
    outs += [jax.ShapeDtypeStruct((plan.block, wide), f32) for wide in row_widths]
    outs += [jax.ShapeDtypeStruct((r // groups, width), f32) for r in col_rows]
    scratch = Line.scratch(half, width) + [pltpu.VMEM((count, plan.half), bf16)]
    scratch += [pltpu.VMEM((count, wide), bf16) for wide in row_widths]
    scratch += [pltpu.VMEM((count, r), bf16) for r in col_rows]
    scratch += [pltpu.VMEM((count, plan.half), bf16) for _ in col_rows]
    scratch += [pltpu.VMEM((team, plan.block, plan.total), bf16)] * 2
    scratch += [pltpu.VMEM((r, plan.half), bf16) for r in col_rows]
    scratch += [pltpu.VMEM((groups, r // groups, plan.half), bf16) for r in col_rows]
    scratch += [
        Line.semaphores(half),
        pltpu.SemaphoreType.DMA((2, team)),
        pltpu.SemaphoreType.DMA((2, len(row_widths))),
        pltpu.SemaphoreType.DMA((2, len(row_tiles), team)),
    ]
    if col_rows:
        scratch += [
            pltpu.SemaphoreType.DMA((2, 2 * len(col_rows))),
            pltpu.SemaphoreType.DMA((2, len(col_rows), groups)),
        ]
    operands = [share, x_own, base_own, gain, row_left, *row_rights]
    operands += [pair[0] for pair in col_pairs] + [pair[1] for pair in col_pairs]
    return pl.pallas_call(
        functools.partial(sum_grads_kernel, n, plan),
        in_specs=[vmem] * len(operands),
        out_specs=[vmem] * len(outs),
        out_shape=outs,
        scratch_shapes=scratch,
        compiler_params=pltpu.CompilerParams(
            collective_id=call, has_side_effects=True, vmem_limit_bytes=60 << 20
        ),
        cost_estimate=pl.CostEstimate(
            flops=12_000_000_000, bytes_accessed=200_000_000, transcendentals=0
        ),
        name=name,
    )(*operands)


def one_hot(index, base, shape, dim):
    return (index == base + lax.broadcasted_iota(jnp.int32, shape, dim)).astype(f32).astype(bf16)


def recur_back_kernel(n, groups, dk, dv, *refs):
    (
        lengths_ref, send_row_ref, send_column_ref, slot_row_ref, slot_column_ref,
        d_mixed_ref, out_weight_ref, attended_ref, gate_ref, gain_ref, up_ref, bias_ref, down_ref,
        held_ref, states_ref, share_ref, hidden_ref,
        d_rows_ref, d_gate_ref, head_gain_ref, grad_up_ref, grad_bias_ref, layer_ref,
        up_in, down_in, d_attended, sent, came, d_state, result, back_sent, back_came,
        sems, go_sems, back_sems,
    ) = refs
    member = lax.axis_index("dp")
    count = d_mixed_ref.shape[0]
    slots = slot_row_ref.shape[1]
    cap = slots // groups
    end0 = lengths_ref[0, 0]
    end1 = end0 + lengths_ref[0, 1]
    ends = (end0, end1, end1 + lengths_ref[0, 2])

    def finish(total, own, place):
        layer_ref[place, :] = (hidden_ref[own, :] + total).astype(layer_ref.dtype)

    line = Line(n, share_ref, up_in, down_in, layer_ref, sems, finish)
    barrier = pltpu.get_barrier_semaphore()

    @pl.loop(1, groups)
    def _(k):
        pl.semaphore_signal(
            barrier, inc=1, device_id={"dp": lax.rem(member + k, groups)}, device_id_type=MESH
        )

    line.greet(barrier, groups - 1)
    line.prime()

    def part(j):
        return pl.ds(pl.multiple_of(j * cap, cap), cap)

    def go_copy(to, source):
        return pltpu.make_async_remote_copy(
            sent.at[part(to), :], came.at[part(source), :], go_sems.at[0, to],
            go_sems.at[1, source], device_id={"dp": to}, device_id_type=MESH,
        )

    def back_copy(to, source):
        return pltpu.make_async_remote_copy(
            back_sent.at[part(to), :], back_came.at[part(source), :], back_sems.at[0, to],
            back_sems.at[1, source], device_id={"dp": to}, device_id_type=MESH,
        )

    head_gain_ref[...] = jnp.zeros_like(head_gain_ref)
    tile = count // 5

    @pl.loop(0, 5)
    def _(i):
        rows = pl.ds(pl.multiple_of(i * tile, tile), tile)
        d_gated = dot_t(d_mixed_ref[rows, :], out_weight_ref[...])
        attended = attended_ref[rows, :].astype(f32)
        gate = gate_ref[rows, :]
        scaling = lax.rsqrt(jnp.mean(attended * attended, axis=1, keepdims=True) + head_floor)
        unit = attended * scaling
        sigmoid = jax.nn.sigmoid(gate)
        swish = gate * sigmoid
        gained = d_gated * gain_ref[...]
        d_gate_ref[rows, :] = (
            gained * unit * sigmoid * (1.0 + gate * (1.0 - sigmoid))
        ).astype(bf16)
        d_unit = gained * swish
        d_attended[rows, :] = (
            scaling * (d_unit - unit * jnp.mean(d_unit * unit, axis=1, keepdims=True))
        ).astype(bf16)
        term = d_gated * unit * swish
        piece = term[0:8, :]
        for r in range(1, tile // 8):
            piece = piece + term[8 * r : 8 * r + 8, :]
        head_gain_ref[...] += piece
        line.step(i)

    @pl.loop(1, groups + 1)
    def _(k):
        to = lax.rem(member + k, groups)
        pick = one_hot(send_row_ref[...], to * cap, (cap, count), 0)
        block = dot(pick, d_attended[...]).astype(bf16)

        @pl.when(k < groups)
        def _():
            sent[part(to), :] = block
            go_copy(to, member).start()

        @pl.when(k == groups)
        def _():
            came[part(member), :] = block

    d_state[...] = jnp.zeros_like(d_state)
    grad_up_ref[...] = jnp.zeros_like(grad_up_ref)
    grad_bias_ref[...] = jnp.zeros_like(grad_bias_ref)
    line.run(5, 13)

    @pl.loop(1, groups)
    def _(k):
        go_copy(0, lax.rem(member + k, groups)).wait_recv()

    spans = held_ref.shape[0] // SPAN

    @pl.loop(0, spans)
    def _(i):
        step = spans - 1 - i
        place = one_hot(slot_row_ref[...], step * SPAN, (SPAN, slots), 0)
        d_out = dot(place, came[...]).astype(bf16)
        span_backward(
            dk, dv, step, ends, d_out, held_ref, states_ref[step], up_ref, bias_ref, down_ref,
            d_state, result, grad_up_ref, grad_bias_ref,
        )
        line.step(13 + 2 * i)
        line.step(14 + 2 * i)

    positions = result.shape[0]

    @pl.loop(1, groups + 1)
    def _(k):
        to = lax.rem(member + k, groups)
        pick = one_hot(slot_column_ref[part(to), :], 0, (cap, positions), 1)
        block = dot(pick, result[...]).astype(bf16)

        @pl.when(k < groups)
        def _():
            back_sent[part(to), :] = block
            back_copy(to, member).start()

        @pl.when(k == groups)
        def _():
            back_came[part(member), :] = block

    line.run(13 + 2 * spans, line.steps)

    @pl.loop(1, groups)
    def _(k):
        back_copy(0, lax.rem(member + k, groups)).wait_recv()

    @pl.loop(0, 5)
    def _(i):
        rows = pl.ds(pl.multiple_of(i * tile, tile), tile)
        pick = one_hot(send_column_ref[rows, :], 0, (tile, slots), 1)
        d_rows_ref[rows, :] = dot(pick, back_came[...]).astype(bf16)

    line.drain()

    @pl.loop(1, groups)
    def _(k):
        to = lax.rem(member + k, groups)
        go_copy(to, member).wait_send()
        back_copy(to, member).wait_send()


def recur_back(
    call, n, groups, dk, dv, lengths, send_pos, slot_map, d_mixed, out_weight, attended, gate_pre,
    head_gain, up_wide, bias, down_wide, held, states, share, hidden_own,
):
    count, width = d_mixed.shape
    slots, wide = held.shape
    half = count // 2
    vmem = pl.BlockSpec(memory_space=pltpu.VMEM)
    operands = [
        lengths, send_pos.reshape(1, -1), send_pos.reshape(-1, 1), slot_map.reshape(1, -1),
        slot_map.reshape(-1, 1), d_mixed, out_weight, attended, gate_pre, head_gain, up_wide, bias,
        down_wide, held, states, share, hidden_own,
    ]
    return pl.pallas_call(
        functools.partial(recur_back_kernel, n, groups, dk, dv),
        in_specs=[pl.BlockSpec(memory_space=pltpu.SMEM)] + [vmem] * (len(operands) - 1),
        out_specs=[vmem] * 6,
        out_shape=[
            jax.ShapeDtypeStruct((count, wide), bf16),
            jax.ShapeDtypeStruct((count, dv), bf16),
            jax.ShapeDtypeStruct((8, dv), f32),
            jax.ShapeDtypeStruct((dk, LANES), f32),
            jax.ShapeDtypeStruct((8, dk), f32),
            jax.ShapeDtypeStruct((count, width), bf16),
        ],
        scratch_shapes=Line.scratch(half, width)
        + [
            pltpu.VMEM((count, dv), bf16),
            pltpu.VMEM((slots, dv), bf16),
            pltpu.VMEM((slots, dv), bf16),
            pltpu.VMEM((dk, dv), f32),
            pltpu.VMEM((slots, wide), bf16),
            pltpu.VMEM((slots, wide), bf16),
            pltpu.VMEM((slots, wide), bf16),
            Line.semaphores(half),
            pltpu.SemaphoreType.DMA((2, groups)),
            pltpu.SemaphoreType.DMA((2, groups)),
        ],
        compiler_params=pltpu.CompilerParams(
            collective_id=call, has_side_effects=True, vmem_limit_bytes=60 << 20
        ),
        cost_estimate=pl.CostEstimate(
            flops=12_000_000_000, bytes_accessed=200_000_000, transcendentals=4_000_000
        ),
        name="recur_back",
    )(*operands)


def small_sum_kernel(groups, n, rows_all, part_ref, out_ref, held, line, line_in, sems, line_sems):
    me = lax.axis_index("dp")
    place = lax.axis_index("tensor")
    barrier = pltpu.get_barrier_semaphore()

    def peer(k):
        return lax.rem(me + k, groups)

    def mate(k):
        return lax.rem(place + k, n)

    @pl.loop(1, groups)
    def _(k):
        pl.semaphore_signal(barrier, inc=1, device_id={"dp": peer(k)}, device_id_type=MESH)

    @pl.loop(1, n)
    def _(k):
        pl.semaphore_signal(barrier, inc=1, device_id={"tensor": mate(k)}, device_id_type=MESH)

    pl.semaphore_wait(barrier, groups + n - 2)

    def copy(k, source):
        return pltpu.make_async_remote_copy(
            part_ref.at[peer(k)], held.at[source], sems.at[0, k], sems.at[1, source],
            device_id={"dp": peer(k)}, device_id_type=MESH,
        )

    def line_copy(k, source):
        return pltpu.make_async_remote_copy(
            line, line_in.at[source], line_sems.at[0, k], line_sems.at[1, source],
            device_id={"tensor": mate(k)}, device_id_type=MESH,
        )

    @pl.loop(1, groups)
    def _(k):
        copy(k, me).start()

    held[pl.ds(me, 1)] = part_ref[pl.ds(me, 1)]

    @pl.loop(1, groups)
    def _(k):
        copy(k, peer(k)).wait_recv()

    total = held[0]
    for i in range(1, groups):
        total = total + held[i]
    line[...] = total[:rows_all]
    out_ref[...] = total

    @pl.loop(1, n)
    def _(k):
        line_copy(k, place).start()

    line_in[pl.ds(place, 1)] = total[None, :rows_all]

    @pl.loop(1, n)
    def _(k):
        line_copy(k, mate(k)).wait_recv()

    total = line_in[0]
    for i in range(1, n):
        total = total + line_in[i]
    out_ref[:rows_all] = total

    @pl.loop(1, groups)
    def _(k):
        copy(k, me).wait_send()

    @pl.loop(1, n)
    def _(k):
        line_copy(k, place).wait_send()


def small_sum(over_all, over_owners, groups, n, call):
    def tiles(blocks):
        short = -blocks.shape[1] % (8 * LANES)
        return jnp.pad(blocks, ((0, 0), (0, short))).reshape(groups, -1, LANES)

    first, second = tiles(over_all), tiles(over_owners)
    rows_all = first.shape[1]
    part = jnp.concatenate([first, second], axis=1)
    vmem = pl.BlockSpec(memory_space=pltpu.VMEM)
    total = pl.pallas_call(
        functools.partial(small_sum_kernel, groups, n, rows_all),
        in_specs=[vmem],
        out_specs=vmem,
        out_shape=jax.ShapeDtypeStruct(part.shape[1:], f32),
        scratch_shapes=[
            pltpu.VMEM(part.shape, f32),
            pltpu.VMEM((rows_all, LANES), f32),
            pltpu.VMEM((n, rows_all, LANES), f32),
            pltpu.SemaphoreType.DMA((2, groups)),
            pltpu.SemaphoreType.DMA((2, n)),
        ],
        compiler_params=pltpu.CompilerParams(collective_id=call, has_side_effects=True),
        name="small_sum",
    )(part)
    return (
        total[:rows_all].reshape(-1)[: over_all.shape[1]],
        total[rows_all:].reshape(-1)[: over_owners.shape[1]],
    )


def per_device(
    tokens,
    cotangent,
    token_slots,
    lengths,
    mixer_gain,
    query_weight,
    key_weight,
    value_weight,
    gate_weight,
    decay_down,
    decay_up,
    decay_bias,
    head_gain,
    out_weight,
    feed_gain,
    feed_gate,
    feed_up,
    feed_down,
):
    groups = lax.axis_size("dp")
    lines = lax.axis_size("tensor")
    member = lax.axis_index("dp")
    place = lax.axis_index("tensor")
    count, width = tokens.shape
    cap = OWN_CAP // groups
    slots = groups * cap
    dk = query_weight.shape[1]
    dv = value_weight.shape[1]
    rank = decay_up.shape[1]
    parity = lax.rem(member, 2)
    pairs = [(i, i ^ 1) for i in range(groups)]
    same_parity = [[i for i in range(groups) if i % 2 == b] for b in range(2)]

    owners = (token_slots // OWN_CAP).reshape(groups, count)
    mine = (owners == member).astype(bf16)
    my_slots = lax.dynamic_slice_in_dim(token_slots, member * count, count)
    my_owner = my_slots // OWN_CAP
    chosen = (my_owner[None, :] == jnp.arange(groups, dtype=jnp.int32)[:, None]).astype(bf16)
    index = jnp.arange(count, dtype=jnp.int32)
    before = (index[:, None] < index[None, :]).astype(bf16)
    ranks = dot(jnp.concatenate([mine, chosen], axis=0), before).astype(jnp.int32)
    recv_rank, send_rank = ranks[:groups], ranks[groups:]
    hit = (recv_rank[:, None, :] == jnp.arange(cap, dtype=jnp.int32)[None, :, None]) & (
        owners == member
    )[:, None, :]
    local = (token_slots % OWN_CAP).reshape(groups, count)
    slot_map = (
        jnp.sum(jnp.where(hit, local[:, None, :] - OWN_CAP, 0), axis=2) + OWN_CAP
    ).reshape(slots)
    send_pos = my_owner * cap + jnp.sum(
        jnp.where(chosen > 0, send_rank, 0), axis=0, dtype=jnp.int32
    )
    slot_ids = jnp.arange(slots, dtype=jnp.int32)
    pack = (slot_ids[:, None] == send_pos[None, :]).astype(bf16)
    unpack = (send_pos[:, None] == slot_ids[None, :]).astype(bf16)

    def exchange(row_block):
        blocks = row_block.reshape(groups, cap, row_block.shape[1])
        moved = lax.all_to_all(blocks, "dp", split_axis=0, concat_axis=0, tiled=True)
        return moved.reshape(slots, row_block.shape[1])

    half = count // 2
    own_at = jnp.where(place == 0, half, 0)
    tokens_own = lax.dynamic_slice_in_dim(tokens, own_at, half)
    cotangent_own = lax.dynamic_slice_in_dim(cotangent, own_at, half)

    tokens_wide = tokens.astype(f32)
    mixer_gain_wide = mixer_gain.astype(f32)
    feed_gain_wide = feed_gain.astype(f32)
    normed = (
        tokens_wide
        * lax.rsqrt(jnp.mean(tokens_wide * tokens_wide, axis=-1, keepdims=True) + epsilon)
        * mixer_gain_wide
    ).astype(bf16)
    queries = dot(normed, query_weight).astype(bf16)
    keys_low = dot(normed, key_weight).astype(bf16)
    value_rows = dot(normed, value_weight).astype(bf16)
    gate_pre = dot(normed, gate_weight)
    third = LANES // 4
    down_pad = jnp.pad(decay_down, ((0, 0), (0, third - rank)))
    latent = dot(
        normed,
        jnp.concatenate([down_pad, down_pad, down_pad, jnp.zeros_like(down_pad)], axis=1),
    )
    latent_high = latent.astype(bf16)
    latent_rest = latent - latent_high.astype(f32)
    latent_mid = latent_rest.astype(bf16)
    latent_low = (latent_rest - latent_mid.astype(f32)).astype(bf16)
    lane = jnp.arange(LANES, dtype=jnp.int32)[None, :]
    latent_packed = jnp.where(
        lane < third, latent_high, jnp.where(lane < 2 * third, latent_mid, latent_low)
    )
    rows_out = jnp.concatenate([queries, keys_low, value_rows, latent_packed], axis=1)
    arrived = exchange(dot(pack, rows_out).astype(bf16))
    up_pad = jnp.pad(decay_up, ((0, 0), (0, third - rank)))
    up_wide = jnp.concatenate([up_pad, up_pad, up_pad, jnp.zeros_like(up_pad)], axis=1).T
    down_wide = jnp.concatenate(
        [up_pad, up_pad, jnp.zeros_like(up_pad), jnp.zeros_like(up_pad)], axis=1
    )
    bias = decay_bias.astype(f32).reshape(1, dk)
    attended_slots, held, states = recur_forward(
        slot_map, lengths, up_wide, bias, arrived, dk, dv
    )
    attended = dot(unpack, exchange(attended_slots)).astype(bf16)
    head_gain_wide = head_gain.astype(f32)
    attended_wide = attended.astype(f32)
    gated = (
        attended_wide
        * lax.rsqrt(jnp.mean(attended_wide * attended_wide, axis=-1, keepdims=True) + head_floor)
        * head_gain_wide
        * jax.nn.silu(gate_pre)
    ).astype(bf16)
    mixer_share = dot(gated, out_weight).astype(bf16)
    feed_normed, hidden_own = line_sum(
        "norm", 1, lines, mixer_share, tokens_own, tokens_own, feed_gain_wide.reshape(1, -1)
    )

    gate_hidden = dot(feed_normed, feed_gate)
    up_hidden = dot(feed_normed, feed_up)
    d_active = dot_t(cotangent, feed_down)
    sigmoid_gate = jax.nn.sigmoid(gate_hidden)
    swish_gate = gate_hidden * sigmoid_gate
    active = (swish_gate * up_hidden).astype(bf16)
    d_gate_hidden = (
        d_active * up_hidden * sigmoid_gate * (1.0 + gate_hidden * (1.0 - sigmoid_gate))
    ).astype(bf16)
    d_up_hidden = (d_active * swish_gate).astype(bf16)
    feed_share = (dot_t(d_gate_hidden, feed_gate) + dot_t(d_up_hidden, feed_up)).astype(bf16)
    fused = (width // groups) % LANES == 0
    if fused:
        d_mixed, d_hidden_own, feed_gain_part, grad_feed_gate, grad_feed_up = sum_grads(
            "back_feed", 2, lines, groups, feed_share, hidden_own, cotangent_own,
            feed_gain_wide.reshape(1, -1), f32, feed_normed, [d_gate_hidden, d_up_hidden],
            [d_gate_hidden.shape[1]] * 2, tiles_of([d_gate_hidden.shape[1]] * 2, 768), [],
        )
    else:
        d_mixed, d_hidden_own, feed_gain_part = line_sum(
            "back", 2, lines, feed_share, hidden_own, cotangent_own, feed_gain_wide.reshape(1, -1)
        )

    layer_share = dot(active, feed_down).astype(bf16)
    d_rows, d_gate_low, head_gain_part, up_part, bias_part, layer_out = recur_back(
        4, lines, groups, dk, dv, lengths, send_pos, slot_map, d_mixed, out_weight, attended,
        gate_pre, head_gain_wide.reshape(1, -1), up_wide, bias, down_wide, held, states,
        layer_share, hidden_own,
    )
    d_query_low = d_rows[:, :dk]
    d_key_low = d_rows[:, dk : 2 * dk]
    d_value_low = d_rows[:, 2 * dk : 2 * dk + dv]
    d_latent_low = d_rows[:, 2 * dk + dv :]
    down_both = jnp.concatenate(
        [down_pad, down_pad, jnp.zeros_like(down_pad), jnp.zeros_like(down_pad)], axis=1
    )
    normed_share = (
        dot_t(d_query_low, query_weight)
        + dot_t(d_key_low, key_weight)
        + dot_t(d_value_low, value_weight)
        + dot_t(d_gate_low, gate_weight)
        + dot_t(d_latent_low, down_both)
    ).astype(bf16)
    if fused:
        (
            token_grad, _, mixer_gain_part, grad_rows, grad_gate, grad_out, grad_feed_down,
        ) = sum_grads(
            "back_mixer", 3, lines, groups, normed_share, tokens_own, d_hidden_own,
            mixer_gain_wide.reshape(1, -1), bf16, normed, [d_rows, d_gate_low],
            [2 * dk + dv, dv], tiles_of([2 * dk + dv, dv], 512),
            [(gated, d_mixed), (active, cotangent)],
        )
        grad_query = grad_rows[:, :dk]
        grad_key = grad_rows[:, dk : 2 * dk]
        grad_value = grad_rows[:, 2 * dk :]
    else:
        token_grad, _, mixer_gain_part = line_sum(
            "back", 3, lines, normed_share, tokens_own, d_hidden_own,
            mixer_gain_wide.reshape(1, -1),
        )
    def halves(row_block, dims):
        split = row_block.reshape(row_block.shape[0], groups // 2, 2, dims // groups)
        keep = lax.dynamic_index_in_dim(split, parity, 2, keepdims=False)
        send = lax.dynamic_index_in_dim(split, 1 - parity, 2, keepdims=False)
        got = lax.ppermute(send, "dp", pairs)
        shape = (row_block.shape[0], dims // 2)
        return keep.reshape(shape), got.reshape(shape)

    def partner(row_block):
        return row_block, lax.ppermute(row_block, "dp", pairs)

    def summed_share(left, right):
        share = (rows_dot(left[0], right[0]) + rows_dot(left[1], right[1])).astype(bf16)
        rows = share.shape[0] // (groups // 2)
        blocks = share.reshape(groups // 2, rows, share.shape[1])
        moved = lax.all_to_all(
            blocks, "dp", split_axis=0, concat_axis=0, tiled=True, axis_index_groups=same_parity
        )
        return jnp.sum(moved.astype(f32), axis=0)

    if not fused:
        feed_halves = halves(feed_normed, width)
        normed_halves = halves(normed, width)
        grad_feed_down = summed_share(halves(active, active.shape[1]), partner(cotangent))
        grad_feed_gate = summed_share(feed_halves, partner(d_gate_hidden))
        grad_feed_up = summed_share(feed_halves, partner(d_up_hidden))
        grad_out = summed_share(halves(gated, dv), partner(d_mixed))
        grad_query = summed_share(normed_halves, partner(d_query_low))
        grad_key = summed_share(normed_halves, partner(d_key_low))
        grad_value = summed_share(normed_halves, partner(d_value_low))
        grad_gate = summed_share(normed_halves, partner(d_gate_low))

    down_part = rows_dot(normed, d_latent_low)
    down_part = down_part[:, :rank] + down_part[:, third : third + rank]
    up_part = up_part[:, :rank] + up_part[:, third : third + rank] + (
        up_part[:, 2 * third : 2 * third + rank]
    )

    def by_owner(vector):
        return vector.reshape(groups, -1)

    over_all = jnp.concatenate(
        [
            by_owner(jnp.sum(mixer_gain_part, axis=0)),
            by_owner(jnp.sum(feed_gain_part, axis=0)),
            by_owner(jnp.sum(head_gain_part, axis=0)),
            by_owner(down_part),
        ],
        axis=1,
    )
    over_owners = jnp.concatenate([by_owner(up_part), by_owner(bias_part[0])], axis=1)
    summed, small = small_sum(over_all, over_owners, groups, lines, 5)
    per = width // groups
    head_per = dv // groups
    return (
        layer_out,
        token_grad,
        summed[:per],
        grad_query,
        grad_key,
        grad_value,
        grad_gate,
        summed[2 * per + head_per :].reshape(per, rank),
        small[: dk // groups * rank].reshape(1, dk // groups, rank),
        small[dk // groups * rank :].reshape(1, dk // groups),
        summed[2 * per : 2 * per + head_per],
        grad_out[None],
        summed[per : 2 * per],
        grad_feed_gate,
        grad_feed_up,
        grad_feed_down[None],
    )


def solution(mesh):
    placed = (
        P("dp", None),
        P("dp", None),
        P(),
        P("dp", None),
        P(),
        P(None, "tensor"),
        P(None, "tensor"),
        P(None, "tensor"),
        P(None, "tensor"),
        P(),
        P("tensor", None),
        P("tensor"),
        P(),
        P("tensor", None),
        P(),
        P(None, "tensor"),
        P(None, "tensor"),
        P("tensor", None),
    )
    return jax.shard_map(
        per_device,
        mesh=mesh,
        in_specs=placed,
        out_specs=(
            P("dp", None),
            P("dp", None),
            P("dp"),
            P("dp", "tensor"),
            P("dp", "tensor"),
            P("dp", "tensor"),
            P("dp", "tensor"),
            P("dp", None),
            P("tensor", "dp", None),
            P("tensor", "dp"),
            P("dp"),
            P("tensor", "dp", None),
            P("dp"),
            P("dp", "tensor"),
            P("dp", "tensor"),
            P("tensor", "dp", None),
        ),
        check_vma=False,
    )
```

```python
import functools

import jax
import jax.numpy as jnp
from jax import lax
from jax.experimental import pallas as pl
from jax.experimental.pallas import tpu as pltpu
from jax.sharding import PartitionSpec as P

OWN_CAP = 1024
SPAN = 128
LANES = 128
epsilon = 1e-06
head_floor = 1.0

f32 = jnp.float32
bf16 = jnp.bfloat16
MESH = pl.DeviceIdType.MESH


def rows_dot(left, right):
    return lax.dot_general(left, right, (((0,), (0,)), ((), ())), preferred_element_type=f32)


def dot_t(left, right):
    return lax.dot_general(left, right, (((1,), (1,)), ((), ())), preferred_element_type=f32)


def dot(left, right):
    return jnp.dot(left, right, preferred_element_type=f32)


def span_terms(first, ends, logits):
    rows = logits.shape[0]

    def label(position):
        count = jnp.zeros_like(position)
        for end in ends:
            count = count + (position >= end).astype(jnp.int32)
        return count

    log_decay = jax.nn.log_sigmoid(logits) * (1.0 / 16.0)
    row = lax.broadcasted_iota(jnp.int32, (rows, rows), 0)
    column = lax.broadcasted_iota(jnp.int32, (rows, rows), 1)
    lower = (row >= column).astype(f32)
    cumulative = jnp.dot(
        lower, log_decay, precision=lax.Precision.HIGHEST, preferred_element_type=f32
    )
    total = cumulative[rows - 1 :, :]
    middle = cumulative[rows // 2 - 1 : rows // 2, :]
    label_column = label(first + lax.broadcasted_iota(jnp.int32, (rows, 1), 0))
    label_row = label(first + lax.broadcasted_iota(jnp.int32, (1, rows), 1))
    before = jnp.where(first > 0, label(first - 1), -1)
    last = label(first + rows - 1)
    carried = (label_column == before).astype(f32)
    tail = (label_column == last).astype(f32)
    keep = (before == last).astype(f32)
    allowed = (row >= column) & (label_column == label_row)
    return log_decay, cumulative, total, middle, carried, tail, keep, allowed


def recur_forward_kernel(
    dk, dv, slot_row_ref, slot_column_ref, lengths_ref, up_ref, bias_ref, arrived_ref,
    out_ref, held_ref, states_ref, state, result,
):
    step = pl.program_id(0)
    first = step * SPAN
    end0 = lengths_ref[0, 0]
    end1 = end0 + lengths_ref[0, 1]
    end2 = end1 + lengths_ref[0, 2]
    slots = slot_row_ref.shape[1]

    @pl.when(step == 0)
    def _():
        state[...] = jnp.zeros_like(state)

    position = first + lax.broadcasted_iota(jnp.int32, (SPAN, slots), 0)
    place = (slot_row_ref[...] == position).astype(f32).astype(bf16)
    held = dot(place, arrived_ref[...]).astype(bf16)
    held_ref[...] = held
    queries = held[:, :dk].astype(f32) * (float(dk) ** -0.5)
    keys = held[:, dk : 2 * dk].astype(f32)
    values = held[:, 2 * dk : 2 * dk + dv]
    logits = dot(held[:, 2 * dk + dv :], up_ref[...]) + bias_ref[...]
    _, cumulative, total, middle, carried, tail, keep, allowed = span_terms(
        first, (end0, end1, end2), logits
    )
    query_mid = (queries * jnp.exp(cumulative - middle)).astype(bf16)
    key_mid = (keys * jnp.exp(middle - cumulative)).astype(bf16)
    query_start = (queries * jnp.exp(cumulative) * carried).astype(bf16)
    key_end = (keys * jnp.exp(total - cumulative) * tail).astype(bf16)
    scores = jnp.where(allowed, dot_t(query_mid, key_mid), 0.0).astype(bf16)
    entering = state[...]
    entering_low = entering.astype(bf16)
    states_ref[0] = entering_low
    attended = dot(scores, values) + dot(query_start, entering_low)
    result[pl.ds(pl.multiple_of(first, SPAN), SPAN), :] = attended.astype(bf16)
    decay_column = jnp.transpose(jnp.broadcast_to(keep * jnp.exp(total), (8, dk)))[:, :1]
    state[...] = decay_column * entering + rows_dot(key_end, values)

    @pl.when(step == pl.num_programs(0) - 1)
    def _():
        return_rows(slot_column_ref, result, out_ref)


def return_rows(slot_column_ref, source, out_ref):
    positions = source.shape[0]
    block = 256

    def body(i, carry):
        at = pl.ds(pl.multiple_of(i * block, block), block)
        column = lax.broadcasted_iota(jnp.int32, (block, positions), 1)
        pick = (slot_column_ref[at, :] == column).astype(f32).astype(bf16)
        out_ref[at, :] = dot(pick, source[...]).astype(out_ref.dtype)
        return carry

    lax.fori_loop(0, out_ref.shape[0] // block, body, 0)


def span_backward(
    dk, dv, step, ends, d_out, held_ref, entering, up_ref, bias_ref, down_ref, d_state, result,
    grad_up_ref, grad_bias_ref,
):
    first = step * SPAN
    at = pl.ds(pl.multiple_of(first, SPAN), SPAN)
    scale = float(dk) ** -0.5
    queries = held_ref[at, :dk].astype(f32) * scale
    keys = held_ref[at, dk : 2 * dk].astype(f32)
    values = held_ref[at, 2 * dk : 2 * dk + dv]
    latent = held_ref[at, 2 * dk + dv :]
    logits = dot(latent, up_ref[...]) + bias_ref[...]
    _, cumulative, total, middle, carried, tail, keep, allowed = span_terms(first, ends, logits)
    grow_query = jnp.exp(cumulative - middle)
    grow_key = jnp.exp(middle - cumulative)
    start_decay = jnp.exp(cumulative) * carried
    end_decay = jnp.exp(total - cumulative) * tail
    query_mid = (queries * grow_query).astype(bf16)
    key_mid = (keys * grow_key).astype(bf16)
    query_start = (queries * start_decay).astype(bf16)
    key_end = (keys * end_decay).astype(bf16)
    scores = jnp.where(allowed, dot_t(query_mid, key_mid), 0.0).astype(bf16)
    d_scores = jnp.where(allowed, dot_t(d_out, values), 0.0).astype(bf16)
    leaving = d_state[...]
    leaving_low = leaving.astype(bf16)
    d_values = rows_dot(scores, d_out) + dot(key_end, leaving_low)
    d_queries = dot(d_scores, key_mid) * grow_query + dot_t(d_out, entering) * start_decay
    d_key_end = dot_t(values, leaving_low) * end_decay
    d_keys = rows_dot(d_scores, query_mid) * grow_key + d_key_end
    kept = keep * jnp.exp(total)
    state_pair = jnp.sum(entering.astype(f32) * leaving, axis=1, keepdims=True)
    state_row = jnp.transpose(jnp.broadcast_to(state_pair, (dk, LANES)))[:1, :]
    d_total = jnp.sum(keys * d_key_end, axis=0, keepdims=True) + kept * state_row
    d_cumulative = queries * d_queries - keys * d_keys
    row = lax.broadcasted_iota(jnp.int32, (SPAN, SPAN), 0)
    column = lax.broadcasted_iota(jnp.int32, (SPAN, SPAN), 1)
    upper = (row <= column).astype(f32)
    d_log_decay = (
        jnp.dot(upper, d_cumulative, precision=lax.Precision.HIGHEST, preferred_element_type=f32)
        + d_total
    )
    d_logits = d_log_decay * (1.0 / 16.0) * jax.nn.sigmoid(-logits)
    grad_bias_ref[...] += jnp.broadcast_to(jnp.sum(d_logits, axis=0, keepdims=True), (8, dk))
    d_logits_high = d_logits.astype(bf16)
    d_logits_low = (d_logits - d_logits_high.astype(f32)).astype(bf16)
    grad_up_ref[...] += rows_dot(d_logits_high, latent) + rows_dot(d_logits_low, latent)
    d_latent = dot(d_logits_high, down_ref[...]) + dot(d_logits_low, down_ref[...])
    high = d_latent.astype(bf16).astype(f32)
    lane = lax.broadcasted_iota(jnp.int32, d_latent.shape, 1)
    d_latent_packed = jnp.where(lane < LANES // 4, high, d_latent - high)
    result[at, :dk] = (d_queries * scale).astype(bf16)
    result[at, dk : 2 * dk] = d_keys.astype(bf16)
    result[at, 2 * dk : 2 * dk + dv] = d_values.astype(bf16)
    result[at, 2 * dk + dv :] = d_latent_packed.astype(bf16)
    kept_column = jnp.transpose(jnp.broadcast_to(kept, (8, dk)))[:, :1]
    d_state[...] = kept_column * leaving + rows_dot(query_start, d_out)


def whole(shape):
    return pl.BlockSpec(shape, lambda i: (0,) * len(shape))


def recur_forward(slot_map, lengths, up_wide, bias, arrived, dk, dv):
    slots, width = arrived.shape
    steps = OWN_CAP // SPAN
    return pl.pallas_call(
        functools.partial(recur_forward_kernel, dk, dv),
        grid=(steps,),
        in_specs=[
            whole((1, slots)),
            whole((slots, 1)),
            pl.BlockSpec(memory_space=pltpu.SMEM),
            whole((LANES, dk)),
            whole((1, dk)),
            whole((slots, width)),
        ],
        out_specs=[
            whole((slots, dv)),
            pl.BlockSpec((SPAN, width), lambda i: (i, 0)),
            pl.BlockSpec((1, dk, dv), lambda i: (i, 0, 0)),
        ],
        out_shape=[
            jax.ShapeDtypeStruct((slots, dv), bf16),
            jax.ShapeDtypeStruct((OWN_CAP, width), bf16),
            jax.ShapeDtypeStruct((steps, dk, dv), bf16),
        ],
        scratch_shapes=[pltpu.VMEM((dk, dv), f32), pltpu.VMEM((OWN_CAP, dv), bf16)],
        compiler_params=pltpu.CompilerParams(vmem_limit_bytes=40 << 20),
        cost_estimate=pl.CostEstimate(
            flops=6_000_000_000, bytes_accessed=10_000_000, transcendentals=2_000_000
        ),
        name="recur_forward",
    )(slot_map.reshape(1, -1), slot_map.reshape(-1, 1), lengths, up_wide, bias, arrived)


FINE = 16
SKEW = 2


class Line:
    def __init__(self, n, share_ref, up_in, down_in, out_ref, sems, finish):
        self.n, self.me = n, lax.axis_index("tensor")
        self.share, self.up_in, self.down_in, self.out = share_ref, up_in, down_in, out_ref
        self.sems, self.finish = sems, finish
        self.half = up_in.shape[0]
        self.count = self.half // FINE
        self.second = self.count + 2
        self.steps = self.second + self.count + SKEW * (n - 2)

    @staticmethod
    def scratch(half, width):
        return [pltpu.VMEM((half, width), bf16), pltpu.VMEM((half, width), bf16)]

    @staticmethod
    def semaphores(half):
        return pltpu.SemaphoreType.DMA((8, half // FINE))

    def greet(self, barrier, others):
        n, me = self.n, self.me

        @pl.when(me > 0)
        def _():
            pl.semaphore_signal(barrier, inc=1, device_id={"tensor": me - 1}, device_id_type=MESH)

        @pl.when(me < n - 1)
        def _():
            pl.semaphore_signal(barrier, inc=1, device_id={"tensor": me + 1}, device_id_type=MESH)

        inside = (me > 0) & (me < n - 1)

        @pl.when(inside)
        def _():
            pl.semaphore_wait(barrier, others + 2)

        @pl.when(jnp.logical_not(inside))
        def _():
            pl.semaphore_wait(barrier, others + 1)

    def greet_all(self, barrier, others):
        n, me = self.n, self.me

        @pl.when(me > 0)
        def _():
            pl.semaphore_signal(barrier, inc=1, device_id={"tensor": me - 1}, device_id_type=MESH)

        @pl.when(me < n - 1)
        def _():
            pl.semaphore_signal(barrier, inc=1, device_id={"tensor": me + 1}, device_id_type=MESH)

        pl.semaphore_wait(barrier, others + n - 1)

    def at(self, g):
        return pl.ds(pl.multiple_of(g * FINE, FINE), FINE)

    def low(self, g):
        return pl.ds(pl.multiple_of(self.half + g * FINE, FINE), FINE)

    def right(self, source, target, lane, g):
        return pltpu.make_async_remote_copy(
            source, target, self.sems.at[2 * lane, g], self.sems.at[2 * lane + 1, g],
            device_id={"tensor": jnp.minimum(self.me + 1, self.n - 1)}, device_id_type=MESH,
        )

    def left(self, source, target, lane, g):
        return pltpu.make_async_remote_copy(
            source, target, self.sems.at[2 * lane, g], self.sems.at[2 * lane + 1, g],
            device_id={"tensor": jnp.maximum(self.me - 1, 0)}, device_id_type=MESH,
        )

    def up_copy(self, g):
        rows = self.up_in.at[self.at(g), :]
        return self.right(rows, rows, 0, g)

    def down_copy(self, g):
        rows = self.down_in.at[self.at(g), :]
        return self.left(rows, rows, 1, g)

    def up_back_copy(self, g):
        rows = self.out.at[self.at(g), :]
        return self.left(rows, rows, 2, g)

    def down_back_copy(self, g):
        rows = self.out.at[self.low(g), :]
        return self.right(rows, rows, 3, g)

    def prime(self):
        @pl.when(self.me == 0)
        def _():
            @pl.loop(0, self.count)
            def _(g):
                self.right(
                    self.share.at[self.at(g), :], self.up_in.at[self.at(g), :], 0, g
                ).start()

        @pl.when(self.me == self.n - 1)
        def _():
            @pl.loop(0, self.count)
            def _(g):
                self.left(
                    self.share.at[self.low(g), :], self.down_in.at[self.at(g), :], 1, g
                ).start()

    def step(self, step):
        n, me, count = self.n, self.me, self.count
        at, low = self.at, self.low
        g_up = step - SKEW * (me - 1)

        @pl.when((me > 0) & (g_up >= 0) & (g_up < count))
        def _():
            self.up_copy(g_up).wait_recv()
            total = self.up_in[at(g_up), :].astype(f32) + self.share[at(g_up), :].astype(f32)

            @pl.when(me < n - 1)
            def _():
                self.up_in[at(g_up), :] = total.astype(bf16)
                self.up_copy(g_up).start()

            @pl.when(me == n - 1)
            def _():
                self.finish(total, at(g_up), at(g_up))
                self.up_back_copy(g_up).start()

        g_down = step - SKEW * (n - 2 - me)

        @pl.when((me < n - 1) & (g_down >= 0) & (g_down < count))
        def _():
            self.down_copy(g_down).wait_recv()
            total = self.down_in[at(g_down), :].astype(f32) + (
                self.share[low(g_down), :].astype(f32)
            )

            @pl.when(me > 0)
            def _():
                self.down_in[at(g_down), :] = total.astype(bf16)
                self.down_copy(g_down).start()

            @pl.when(me == 0)
            def _():
                self.finish(total, at(g_down), low(g_down))
                self.down_back_copy(g_down).start()

        g_up_back = step - self.second - SKEW * (n - 2 - me)

        @pl.when((me < n - 1) & (g_up_back >= 0) & (g_up_back < count))
        def _():
            self.up_back_copy(g_up_back).wait_recv()

            @pl.when(me > 0)
            def _():
                self.up_back_copy(g_up_back).start()

        g_down_back = step - self.second - SKEW * (me - 1)

        @pl.when((me > 0) & (g_down_back >= 0) & (g_down_back < count))
        def _():
            self.down_back_copy(g_down_back).wait_recv()

            @pl.when(me < n - 1)
            def _():
                self.down_back_copy(g_down_back).start()

    def run(self, first, last):
        @pl.loop(first, last)
        def _(step):
            self.step(step)

    def drain(self):
        n, me = self.n, self.me

        @pl.loop(0, self.count)
        def _(g):
            @pl.when(me < n - 1)
            def _():
                self.up_copy(g).wait_send()
                self.down_back_copy(g).wait_send()

            @pl.when(me > 0)
            def _():
                self.down_copy(g).wait_send()
                self.up_back_copy(g).wait_send()


def norm_back(x_ref, base_ref, gain_ref, out_ref, kept_ref, gain_grad_ref):
    gain_grad_ref[...] = jnp.zeros_like(gain_grad_ref)

    def finish(total, own, place):
        rows = x_ref[own, :].astype(f32)
        scaling = lax.rsqrt(jnp.mean(rows * rows, axis=1, keepdims=True) + epsilon)
        unit = rows * scaling
        gained = gain_ref[...] * total
        grad = base_ref[own, :].astype(f32) + scaling * (
            gained - unit * jnp.mean(gained * unit, axis=1, keepdims=True)
        )
        kept_ref[own, :] = grad.astype(kept_ref.dtype)
        out_ref[place, :] = grad.astype(out_ref.dtype)
        term = total * unit
        part = term[0:8, :]
        for i in range(1, FINE // 8):
            part = part + term[8 * i : 8 * i + 8, :]
        gain_grad_ref[...] += part

    return finish


def line_kernel(mode, n, *refs):
    share_ref, x_ref, base_ref, gain_ref, out_ref, kept_ref = refs[:6]
    if mode == "norm":
        up_in, down_in, sems = refs[6:]

        def finish(total, own, place):
            hidden = base_ref[own, :].astype(f32) + total
            kept_ref[own, :] = hidden
            scaling = lax.rsqrt(jnp.mean(hidden * hidden, axis=1, keepdims=True) + epsilon)
            out_ref[place, :] = (hidden * scaling * gain_ref[...]).astype(out_ref.dtype)
    else:
        gain_grad_ref, up_in, down_in, sems = refs[6:]
        finish = norm_back(x_ref, base_ref, gain_ref, out_ref, kept_ref, gain_grad_ref)
    line = Line(n, share_ref, up_in, down_in, out_ref, sems, finish)
    line.greet(pltpu.get_barrier_semaphore(), 0)
    line.prime()
    line.run(0, line.steps)
    line.drain()


def line_sum(mode, call, n, share, x_own, base_own, gain):
    rows, width = share.shape
    half = rows // 2
    vmem = pl.BlockSpec(memory_space=pltpu.VMEM)
    outs = [jax.ShapeDtypeStruct((rows, width), bf16), jax.ShapeDtypeStruct((half, width), f32)]
    if mode == "back":
        outs.append(jax.ShapeDtypeStruct((8, width), f32))
    return pl.pallas_call(
        functools.partial(line_kernel, mode, n),
        in_specs=[vmem] * 4,
        out_specs=[vmem] * len(outs),
        out_shape=outs,
        scratch_shapes=Line.scratch(half, width) + [Line.semaphores(half)],
        compiler_params=pltpu.CompilerParams(
            collective_id=call, has_side_effects=True, vmem_limit_bytes=40 << 20
        ),
        cost_estimate=pl.CostEstimate(
            flops=10_000_000, bytes_accessed=200_000_000, transcendentals=0
        ),
        name="line_" + mode,
    )(share, x_own, base_own, gain)


def partner_of(index):
    return index + 1 - 2 * lax.rem(index, 2)


def to_dp(source, target, send, recv, device):
    return pltpu.make_async_remote_copy(
        source, target, send, recv, device_id={"dp": device}, device_id_type=MESH
    )


def greet_dp(barrier, groups):
    member = lax.axis_index("dp")

    @pl.loop(1, groups)
    def _(k):
        pl.semaphore_signal(
            barrier, inc=1, device_id={"dp": lax.rem(member + k, groups)}, device_id_type=MESH
        )


class ColGrad:
    TILE = 256

    def __init__(self, groups, left, right, out, refs):
        (
            self.left, self.right, self.left_in, self.right_in, self.send, self.recv,
            self.load_sems, self.pair_sems, self.sems,
        ) = refs
        self.left_far, self.right_far, self.out, self.groups = left, right, out, groups
        self.member = lax.axis_index("dp")
        self.parity = lax.rem(self.member, 2)
        self.half = self.right_in.shape[1]
        self.size = self.send.shape[0] // groups
        self.items = self.half // self.TILE

    @staticmethod
    def scratch(groups, count, rows, width):
        half = width // 2
        return [
            pltpu.VMEM((count, rows), bf16),
            pltpu.VMEM((count, half), bf16),
            pltpu.VMEM((count, rows), bf16),
            pltpu.VMEM((count, half), bf16),
            pltpu.VMEM((rows, half), bf16),
            pltpu.VMEM((groups, rows // groups, half), bf16),
            pltpu.SemaphoreType.DMA((2,)),
            pltpu.SemaphoreType.DMA((2, 2)),
            pltpu.SemaphoreType.DMA((2, groups)),
        ]

    def halves(self, parity):
        return self.right_far.at[:, pl.ds(pl.multiple_of(parity * self.half, self.half), self.half)]

    def loads(self):
        return (
            pltpu.make_async_copy(self.left_far, self.left, self.load_sems.at[0]),
            pltpu.make_async_copy(self.halves(self.parity), self.right, self.load_sems.at[1]),
        )

    def pair_copies(self):
        partner = partner_of(self.member)
        sems = self.pair_sems
        return (
            to_dp(self.left_far, self.left_in, sems.at[0, 0], sems.at[1, 0], partner),
            to_dp(
                self.halves(1 - self.parity), self.right_in, sems.at[0, 1], sems.at[1, 1], partner
            ),
        )

    def start(self):
        for c in self.pair_copies() + self.loads():
            c.start()

    def ready(self):
        for c in self.loads():
            c.wait()
        for c in self.pair_copies():
            c.wait_recv()

    def item(self, t):
        span = pl.ds(pl.multiple_of(t * self.TILE, self.TILE), self.TILE)
        product = rows_dot(self.left[...], self.right[:, span]) + rows_dot(
            self.left_in[...], self.right_in[:, span]
        )
        self.send[:, span] = product.astype(bf16)

    def copy(self, to, source):
        rows = pl.ds(pl.multiple_of(to * self.size, 16), self.size)
        return to_dp(
            self.send.at[rows, :], self.recv.at[source], self.sems.at[0, to],
            self.sems.at[1, source], to,
        )

    def send_all(self):
        @pl.loop(1, self.groups)
        def _(k):
            self.copy(lax.rem(self.member + k, self.groups), self.member).start()

        own = pl.ds(pl.multiple_of(self.member * self.size, 16), self.size)
        self.recv[pl.ds(self.member, 1)] = self.send[own, :][None]

    def receive(self):
        @pl.loop(1, self.groups)
        def _(k):
            self.copy(0, lax.rem(self.member + k, self.groups)).wait_recv()

        for b in range(2):
            total = self.recv[b].astype(f32)
            for q in range(1, self.groups // 2):
                total = total + self.recv[2 * q + b].astype(f32)
            self.out[:, b * self.half : (b + 1) * self.half] = total

    def drain(self):
        for c in self.pair_copies():
            c.wait_send()

        @pl.loop(1, self.groups)
        def _(k):
            self.copy(lax.rem(self.member + k, self.groups), self.member).wait_send()


class RowGrads:
    def __init__(self, groups, left, parts, tiles, outs, outputs, refs):
        (
            self.left, self.all, self.left_in, self.all_in, self.send, self.recv,
            self.load_sems, self.left_sems, self.part_sems, self.sems,
        ) = refs
        self.left_far, self.parts, self.tiles = left, parts, tiles
        self.outs, self.outputs = outs, outputs
        self.member = lax.axis_index("dp")
        self.parity = lax.rem(self.member, 2)
        self.mine = self.member // 2
        self.team = groups // 2
        self.block = left.shape[1] // groups
        self.offsets = [0]
        for part in parts:
            self.offsets.append(self.offsets[-1] + part.shape[1])
        self.items = self.team * len(tiles)

    @staticmethod
    def scratch(groups, count, width, total, parts, tiles):
        team = groups // 2
        return [
            pltpu.VMEM((count, width), bf16),
            pltpu.VMEM((count, total), bf16),
            pltpu.VMEM((count, width // 2), bf16),
            pltpu.VMEM((count, total), bf16),
            pltpu.VMEM((team, width // groups, total), bf16),
            pltpu.VMEM((team, width // groups, total), bf16),
            pltpu.SemaphoreType.DMA((1 + parts,)),
            pltpu.SemaphoreType.DMA((2, team)),
            pltpu.SemaphoreType.DMA((2, parts)),
            pltpu.SemaphoreType.DMA((2, tiles, team)),
        ]

    def columns(self, j):
        return pl.ds(pl.multiple_of(j * self.block, self.block), self.block)

    def left_load(self):
        return pltpu.make_async_copy(self.left_far, self.left, self.load_sems.at[0])

    def part_columns(self, i):
        return pl.ds(self.offsets[i], self.offsets[i + 1] - self.offsets[i])

    def part_load(self, i):
        return pltpu.make_async_copy(
            self.parts[i], self.all.at[:, self.part_columns(i)], self.load_sems.at[1 + i]
        )

    def left_copy(self, q):
        return to_dp(
            self.left_far.at[:, self.columns(2 * q + 1 - self.parity)],
            self.left_in.at[:, self.columns(q)],
            self.left_sems.at[0, q], self.left_sems.at[1, q], partner_of(self.member),
        )

    def part_copy(self, i):
        return to_dp(
            self.parts[i], self.all_in.at[:, self.part_columns(i)],
            self.part_sems.at[0, i], self.part_sems.at[1, i], partner_of(self.member),
        )

    def start_left(self):
        @pl.loop(0, self.team)
        def _(q):
            self.left_copy(q).start()

        self.left_load().start()

    def start_part(self, i):
        self.part_copy(i).start()
        self.part_load(i).start()

    def ready_left(self):
        self.left_load().wait()

        @pl.loop(0, self.team)
        def _(q):
            self.left_copy(q).wait_recv()

    def copy(self, t, to, source):
        start, wide = self.tiles[t]
        span = pl.ds(start, wide)
        return to_dp(
            self.send.at[to, :, span], self.recv.at[source, :, span],
            self.sems.at[0, t, to], self.sems.at[1, t, source], 2 * to + self.parity,
        )

    def item(self, w):
        count = len(self.tiles)
        k = w // count
        to = lax.rem(self.mine + 1 + k, self.team)
        for t in range(count):
            start, wide = self.tiles[t]

            @pl.when((w >= 0) & (w < self.items) & (lax.rem(w, count) == t))
            def _():
                span = pl.ds(start, wide)
                product = rows_dot(
                    self.left[:, self.columns(2 * to + self.parity)], self.all[:, span]
                ) + rows_dot(self.left_in[:, self.columns(to)], self.all_in[:, span])
                low_product = product.astype(bf16)

                @pl.when(k < self.team - 1)
                def _():
                    self.send[to, :, span] = low_product
                    self.copy(t, to, self.mine).start()

                @pl.when(k == self.team - 1)
                def _():
                    self.recv[self.mine, :, span] = low_product

    def receive(self):
        for t in range(len(self.tiles)):
            @pl.loop(1, self.team)
            def _(k):
                self.copy(t, 0, lax.rem(self.mine + k, self.team)).wait_recv()

        for (start, wide), output in zip(self.outs, self.outputs):
            span = pl.ds(start, wide)
            total = self.recv[0, :, span].astype(f32)
            for q in range(1, self.team):
                total = total + self.recv[q, :, span].astype(f32)
            output[...] = total

    def drain(self):
        @pl.loop(0, self.team)
        def _(q):
            self.left_copy(q).wait_send()

        for i in range(len(self.parts)):
            self.part_copy(i).wait_send()
        for t in range(len(self.tiles)):
            @pl.loop(1, self.team)
            def _(k):
                self.copy(t, lax.rem(self.mine + k, self.team), self.mine).wait_send()


def splitter(refs):
    refs = list(refs)

    def take(k):
        out = refs[:k]
        del refs[:k]
        return out

    return take


def back_feed_kernel(n, groups, tiles, outs, *refs):
    take = splitter(refs)
    share_ref, gain_ref, x_far, base_far, left_far = take(5)
    parts = take(2)
    out_ref, kept_ref, gain_grad_ref = take(3)
    outputs = take(2)
    up_in, down_in, x_ref, base_ref, load_sems, sems = take(6)
    rows = RowGrads(groups, left_far, parts, tiles, outs, outputs, take(10))
    finish = norm_back(x_ref, base_ref, gain_ref, out_ref, kept_ref, gain_grad_ref)
    line = Line(n, share_ref, up_in, down_in, out_ref, sems, finish)
    loads = (
        pltpu.make_async_copy(x_far, x_ref, load_sems.at[0]),
        pltpu.make_async_copy(base_far, base_ref, load_sems.at[1]),
    )
    barrier = pltpu.get_barrier_semaphore()
    greet_dp(barrier, groups)
    line.greet(barrier, groups - 1)
    line.prime()
    rows.start_left()
    for i in range(2):
        rows.start_part(i)
    for c in loads:
        c.start()
    for c in loads:
        c.wait()
    first_work = 3

    @pl.loop(0, line.steps)
    def _(step):
        line.step(step)
        w = step - first_work

        @pl.when(w == 0)
        def _():
            rows.ready_left()
            rows.part_load(0).wait()
            rows.part_copy(0).wait_recv()

        @pl.when(w == len(tiles) // 2)
        def _():
            rows.part_load(1).wait()
            rows.part_copy(1).wait_recv()

        rows.item(w)

    rows.receive()
    line.drain()
    rows.drain()


def back_feed(call, n, groups, share, gain, x_own, base_own, left, parts):
    count, width = share.shape
    half = count // 2
    wide = parts[0].shape[1]
    cut = (wide // 2 + LANES - 1) // LANES * LANES
    tiles = [(0, cut), (cut, wide - cut), (wide, cut), (wide + cut, wide - cut)]
    outs = [(0, wide), (wide, wide)]
    vmem = pl.BlockSpec(memory_space=pltpu.VMEM)
    far = pl.BlockSpec(memory_space=pl.ANY)
    return pl.pallas_call(
        functools.partial(back_feed_kernel, n, groups, tiles, outs),
        in_specs=[vmem] * 2 + [far] * 5,
        out_specs=[vmem] * 5,
        out_shape=[
            jax.ShapeDtypeStruct((count, width), bf16),
            jax.ShapeDtypeStruct((half, width), f32),
            jax.ShapeDtypeStruct((8, width), f32),
            jax.ShapeDtypeStruct((width // groups, wide), f32),
            jax.ShapeDtypeStruct((width // groups, wide), f32),
        ],
        scratch_shapes=Line.scratch(half, width)
        + [
            pltpu.VMEM((half, width), x_own.dtype),
            pltpu.VMEM((half, width), base_own.dtype),
            pltpu.SemaphoreType.DMA((2,)),
            Line.semaphores(half),
        ]
        + RowGrads.scratch(groups, count, width, 2 * wide, 2, len(tiles)),
        compiler_params=pltpu.CompilerParams(
            collective_id=call, has_side_effects=True, vmem_limit_bytes=60 << 20
        ),
        cost_estimate=pl.CostEstimate(
            flops=12_000_000_000, bytes_accessed=200_000_000, transcendentals=0
        ),
        name="back_feed",
    )(share, gain, x_own, base_own, left, *parts)


class SmallSum:
    def __init__(self, n, groups, wide, near, near_all, wide_out, near_out, refs):
        (
            self.wide_in, self.near_in, self.wide_line, self.near_line, self.sems, self.line_sems,
        ) = refs
        self.n, self.groups, self.near_all = n, groups, near_all
        self.wide, self.near, self.wide_out, self.near_out = wide, near, wide_out, near_out
        self.member, self.place = lax.axis_index("dp"), lax.axis_index("tensor")
        self.block = wide.shape[1] // groups

    @staticmethod
    def scratch(n, groups, wide, near):
        block = wide[1] // groups
        return [
            pltpu.VMEM((groups, wide[0], block), f32),
            pltpu.VMEM(near, f32),
            pltpu.VMEM((n, wide[0], block), f32),
            pltpu.VMEM((n,) + near[1:], f32),
            pltpu.SemaphoreType.DMA((2, 2, groups)),
            pltpu.SemaphoreType.DMA((2, 2, n)),
        ]

    def greet(self, barrier):
        n, place = self.n, self.place
        for k in range(2, n):
            @pl.when(place + k < n)
            def _():
                pl.semaphore_signal(
                    barrier, inc=1, device_id={"tensor": place + k}, device_id_type=MESH
                )

            @pl.when(place - k >= 0)
            def _():
                pl.semaphore_signal(
                    barrier, inc=1, device_id={"tensor": place - k}, device_id_type=MESH
                )

    def cut(self, j):
        return pl.ds(pl.multiple_of(j * self.block, self.block), self.block)

    def copies(self, to, source):
        return (
            to_dp(
                self.wide.at[:, self.cut(to)], self.wide_in.at[source],
                self.sems.at[0, 0, to], self.sems.at[1, 0, source], to,
            ),
            to_dp(
                self.near.at[to], self.near_in.at[source],
                self.sems.at[0, 1, to], self.sems.at[1, 1, source], to,
            ),
        )

    def line_copies(self, to, source):
        return tuple(
            pltpu.make_async_remote_copy(
                line.at[self.place], line.at[source], self.line_sems.at[0, i, to],
                self.line_sems.at[1, i, source], device_id={"tensor": to}, device_id_type=MESH,
            )
            for i, line in enumerate((self.wide_line, self.near_line))
        )

    def send(self):
        @pl.loop(1, self.groups)
        def _(k):
            for c in self.copies(lax.rem(self.member + k, self.groups), self.member):
                c.start()

        self.wide_in[pl.ds(self.member, 1)] = self.wide[:, self.cut(self.member)][None]
        self.near_in[pl.ds(self.member, 1)] = self.near[pl.ds(self.member, 1)]

    def forward(self):
        @pl.loop(1, self.groups)
        def _(k):
            for c in self.copies(0, lax.rem(self.member + k, self.groups)):
                c.wait_recv()

        for came, line in ((self.wide_in, self.wide_line), (self.near_in, self.near_line)):
            total = came[0]
            for j in range(1, self.groups):
                total = total + came[j]
            line[pl.ds(self.place, 1)] = total[None]

        @pl.loop(1, self.n)
        def _(k):
            for c in self.line_copies(lax.rem(self.place + k, self.n), self.place):
                c.start()

    def receive(self):
        @pl.loop(1, self.n)
        def _(k):
            for c in self.line_copies(0, lax.rem(self.place + k, self.n)):
                c.wait_recv()

        total = self.wide_line[0]
        for j in range(1, self.n):
            total = total + self.wide_line[j]
        self.wide_out[...] = total
        own = self.near_line[pl.ds(self.place, 1)][0]
        total = self.near_line[0]
        for j in range(1, self.n):
            total = total + self.near_line[j]
        row = lax.broadcasted_iota(jnp.int32, own.shape, 0)
        self.near_out[...] = jnp.where(row < self.near_all, total, own)

    def drain(self):
        @pl.loop(1, self.groups)
        def _(k):
            for c in self.copies(lax.rem(self.member + k, self.groups), self.member):
                c.wait_send()

        @pl.loop(1, self.n)
        def _(k):
            for c in self.line_copies(lax.rem(self.place + k, self.n), self.place):
                c.wait_send()


def back_mixer_kernel(n, groups, widths, near_all, tiles, outs, *refs):
    take = splitter(refs)
    gain_ref, near_ref, x_far, base_far, left_far = take(5)
    parts = take(2)
    col_left, col_right = take(2)
    weights = take(len(widths))
    out_ref, wide_out, near_out = take(3)
    outputs = take(len(outs))
    (col_out,) = take(1)
    up_in, down_in, x_ref, base_ref, kept_ref, share_ref, wide_ref, gain_grad_ref = take(8)
    weight_ref, load_sems, sems = take(3)
    rows = RowGrads(groups, left_far, parts, tiles, outs, outputs, take(10))
    cols = ColGrad(groups, col_left, col_right, col_out, take(9))
    small = SmallSum(n, groups, wide_ref, near_ref, near_all, wide_out, near_out, take(6))
    finish = norm_back(x_ref, base_ref, gain_ref, out_ref, kept_ref, gain_grad_ref)
    line = Line(n, share_ref, up_in, down_in, out_ref, sems, finish)
    loads = [
        pltpu.make_async_copy(x_far, x_ref, load_sems.at[0]),
        pltpu.make_async_copy(base_far, base_ref, load_sems.at[1]),
    ]
    weight_loads = []
    offset = 0
    for i, wide in enumerate(widths):
        weight_loads.append(
            pltpu.make_async_copy(
                weights[i], weight_ref.at[:, pl.ds(offset, wide)], load_sems.at[2 + i]
            )
        )
        offset += wide
    for i in range(2):
        rows.part_load(i).start()
    for c in weight_loads:
        c.start()
    barrier = pltpu.get_barrier_semaphore()
    greet_dp(barrier, groups)
    small.greet(barrier)
    line.greet_all(barrier, groups - 1)
    rows.start_left()
    for i in range(2):
        rows.part_copy(i).start()
    cols.start()
    for c in loads:
        c.start()
    for i in range(2):
        rows.part_load(i).wait()
    for c in weight_loads:
        c.wait()

    count, width = share_ref.shape
    tile_rows, tile_columns = count // 2, 512
    across = width // tile_columns

    @pl.loop(0, 2 * across)
    def _(i):
        at = pl.ds(pl.multiple_of((i // across) * tile_rows, tile_rows), tile_rows)
        to = pl.ds(pl.multiple_of(lax.rem(i, across) * tile_columns, tile_columns), tile_columns)
        share_ref[at, to] = dot_t(rows.all[at, :], weight_ref[to, :]).astype(bf16)

    line.prime()
    for c in loads:
        c.wait()
    third = LANES // 4
    latent_at = offset - widths[-1] - LANES
    first_cols = rows.items
    last_item = first_cols + cols.items

    @pl.loop(0, line.steps)
    def _(step):
        line.step(step)

        @pl.when(step == 0)
        def _():
            rows.ready_left()
            for i in range(2):
                rows.part_copy(i).wait_recv()

        rows.item(step)

        @pl.when(step == first_cols)
        def _():
            cols.ready()

        @pl.when((step >= first_cols) & (step < last_item))
        def _():
            cols.item(step - first_cols)

        @pl.when(step == last_item)
        def _():
            cols.send_all()
            product = rows_dot(rows.all[:, pl.ds(latent_at, LANES)], rows.left[...])
            wide_ref[:16, :] = product[:16, :] + product[third : third + 16, :]

        @pl.when(step == line.second + 4)
        def _():
            wide_ref[16:, :] = gain_grad_ref[...]
            small.send()

        @pl.when(step == line.second + 14)
        def _():
            small.forward()

    rows.receive()
    cols.receive()
    small.receive()
    line.drain()
    rows.drain()
    cols.drain()
    small.drain()


def back_mixer(call, n, groups, gain, near, near_all, x_own, base_own, left, parts, outs, pair, weights):
    count, width = left.shape
    half = count // 2
    widths = [w.shape[1] for w in weights]
    total = sum(part.shape[1] for part in parts)
    start = parts[0].shape[1]
    tiles = [(0, 512), (512, 512), (start, parts[1].shape[1])]
    col_rows = pair[0].shape[1]
    vmem = pl.BlockSpec(memory_space=pltpu.VMEM)
    far = pl.BlockSpec(memory_space=pl.ANY)
    wide_shape = (24, width)
    return pl.pallas_call(
        functools.partial(back_mixer_kernel, n, groups, widths, near_all, tiles, outs),
        in_specs=[vmem] * 2 + [far] * (7 + len(weights)),
        out_specs=[vmem] * (4 + len(outs)),
        out_shape=[
            jax.ShapeDtypeStruct((count, width), bf16),
            jax.ShapeDtypeStruct((24, width // groups), f32),
            jax.ShapeDtypeStruct(near.shape[1:], f32),
        ]
        + [jax.ShapeDtypeStruct((width // groups, wide), f32) for _, wide in outs]
        + [jax.ShapeDtypeStruct((col_rows // groups, width), f32)],
        scratch_shapes=Line.scratch(half, width)
        + [
            pltpu.VMEM((half, width), x_own.dtype),
            pltpu.VMEM((half, width), base_own.dtype),
            pltpu.VMEM((half, width), bf16),
            pltpu.VMEM((count, width), bf16),
            pltpu.VMEM(wide_shape, f32),
            pltpu.VMEM((8, width), f32),
            pltpu.VMEM((width, total), bf16),
            pltpu.SemaphoreType.DMA((2 + len(weights),)),
            Line.semaphores(half),
        ]
        + RowGrads.scratch(groups, count, width, total, 2, len(tiles))
        + ColGrad.scratch(groups, count, col_rows, width)
        + SmallSum.scratch(n, groups, wide_shape, near.shape),
        compiler_params=pltpu.CompilerParams(
            collective_id=call, has_side_effects=True, vmem_limit_bytes=61 << 20
        ),
        cost_estimate=pl.CostEstimate(
            flops=12_000_000_000, bytes_accessed=200_000_000, transcendentals=0
        ),
        name="back_mixer",
    )(gain, near, x_own, base_own, left, *parts, *pair, *weights)


def one_hot(index, base, shape, dim):
    return (index == base + lax.broadcasted_iota(jnp.int32, shape, dim)).astype(f32).astype(bf16)


def recur_back_kernel(n, groups, dk, dv, beside, *refs):
    (
        lengths_ref, send_row_ref, send_column_ref, slot_row_ref, slot_column_ref,
        d_mixed_ref, out_weight_ref, attended_ref, gate_ref, gain_ref, up_ref, bias_ref, down_ref,
        share_ref, held_far, states_far, hidden_far, active_far, cotangent_far,
        d_rows_ref, d_gate_ref, head_gain_ref, grad_up_ref, grad_bias_ref, layer_ref, grad_down_ref,
        up_in, down_in, d_attended, sent, came, d_state, result, back_sent, back_came,
        held_ref, states_ref, hidden_ref, load_sems, sems, go_sems, back_sems,
    ) = refs[:42]
    cols = ColGrad(groups, active_far, cotangent_far, grad_down_ref, refs[42:]) if beside else None
    member = lax.axis_index("dp")
    count = d_mixed_ref.shape[0]
    slots = slot_row_ref.shape[1]
    cap = slots // groups
    end0 = lengths_ref[0, 0]
    end1 = end0 + lengths_ref[0, 1]
    ends = (end0, end1, end1 + lengths_ref[0, 2])

    def finish(total, own, place):
        layer_ref[place, :] = (hidden_ref[own, :] + total).astype(layer_ref.dtype)

    line = Line(n, share_ref, up_in, down_in, layer_ref, sems, finish)
    loads = (
        pltpu.make_async_copy(hidden_far, hidden_ref, load_sems.at[0]),
        pltpu.make_async_copy(held_far, held_ref, load_sems.at[1]),
        pltpu.make_async_copy(states_far, states_ref, load_sems.at[2]),
    )
    barrier = pltpu.get_barrier_semaphore()
    greet_dp(barrier, groups)
    line.greet(barrier, groups - 1)
    line.prime()
    for c in loads:
        c.start()
    if beside:
        cols.start()
    loads[0].wait()

    def part(j):
        return pl.ds(pl.multiple_of(j * cap, cap), cap)

    def go_copy(to, source):
        return pltpu.make_async_remote_copy(
            sent.at[part(to), :], came.at[part(source), :], go_sems.at[0, to],
            go_sems.at[1, source], device_id={"dp": to}, device_id_type=MESH,
        )

    def back_copy(to, source):
        return pltpu.make_async_remote_copy(
            back_sent.at[part(to), :], back_came.at[part(source), :], back_sems.at[0, to],
            back_sems.at[1, source], device_id={"dp": to}, device_id_type=MESH,
        )

    head_gain_ref[...] = jnp.zeros_like(head_gain_ref)
    tile = count // 5

    @pl.loop(0, 5)
    def _(i):
        rows = pl.ds(pl.multiple_of(i * tile, tile), tile)
        d_gated = dot_t(d_mixed_ref[rows, :], out_weight_ref[...])
        attended = attended_ref[rows, :].astype(f32)
        gate = gate_ref[rows, :]
        scaling = lax.rsqrt(jnp.mean(attended * attended, axis=1, keepdims=True) + head_floor)
        unit = attended * scaling
        sigmoid = jax.nn.sigmoid(gate)
        swish = gate * sigmoid
        gained = d_gated * gain_ref[...]
        d_gate_ref[rows, :] = (
            gained * unit * sigmoid * (1.0 + gate * (1.0 - sigmoid))
        ).astype(bf16)
        d_unit = gained * swish
        d_attended[rows, :] = (
            scaling * (d_unit - unit * jnp.mean(d_unit * unit, axis=1, keepdims=True))
        ).astype(bf16)
        term = d_gated * unit * swish
        piece = term[0:8, :]
        for r in range(1, tile // 8):
            piece = piece + term[8 * r : 8 * r + 8, :]
        head_gain_ref[...] += piece
        line.step(i)

    @pl.loop(1, groups + 1)
    def _(k):
        to = lax.rem(member + k, groups)
        pick = one_hot(send_row_ref[...], to * cap, (cap, count), 0)
        block = dot(pick, d_attended[...]).astype(bf16)

        @pl.when(k < groups)
        def _():
            sent[part(to), :] = block
            go_copy(to, member).start()

        @pl.when(k == groups)
        def _():
            came[part(member), :] = block

    d_state[...] = jnp.zeros_like(d_state)
    grad_up_ref[...] = jnp.zeros_like(grad_up_ref)
    grad_bias_ref[...] = jnp.zeros_like(grad_bias_ref)
    done = 13
    if beside:
        cols.ready()

        @pl.loop(0, cols.items)
        def _(i):
            cols.item(i)
            line.step(5 + 2 * i)
            line.step(6 + 2 * i)

        done = 5 + 2 * cols.items
        cols.send_all()
    else:
        line.run(5, done)
    for c in loads[1:]:
        c.wait()

    @pl.loop(1, groups)
    def _(k):
        go_copy(0, lax.rem(member + k, groups)).wait_recv()

    spans = held_ref.shape[0] // SPAN

    @pl.loop(0, spans)
    def _(i):
        step = spans - 1 - i
        place = one_hot(slot_row_ref[...], step * SPAN, (SPAN, slots), 0)
        d_out = dot(place, came[...]).astype(bf16)
        span_backward(
            dk, dv, step, ends, d_out, held_ref, states_ref[step], up_ref, bias_ref, down_ref,
            d_state, result, grad_up_ref, grad_bias_ref,
        )
        line.step(done + 2 * i)
        line.step(done + 1 + 2 * i)

    positions = result.shape[0]

    @pl.loop(1, groups + 1)
    def _(k):
        to = lax.rem(member + k, groups)
        pick = one_hot(slot_column_ref[part(to), :], 0, (cap, positions), 1)
        block = dot(pick, result[...]).astype(bf16)

        @pl.when(k < groups)
        def _():
            back_sent[part(to), :] = block
            back_copy(to, member).start()

        @pl.when(k == groups)
        def _():
            back_came[part(member), :] = block

    line.run(done + 2 * spans, line.steps)
    if beside:
        cols.receive()

    @pl.loop(1, groups)
    def _(k):
        back_copy(0, lax.rem(member + k, groups)).wait_recv()

    @pl.loop(0, 5)
    def _(i):
        rows = pl.ds(pl.multiple_of(i * tile, tile), tile)
        pick = one_hot(send_column_ref[rows, :], 0, (tile, slots), 1)
        d_rows_ref[rows, :] = dot(pick, back_came[...]).astype(bf16)

    line.drain()
    if beside:
        cols.drain()

    @pl.loop(1, groups)
    def _(k):
        to = lax.rem(member + k, groups)
        go_copy(to, member).wait_send()
        back_copy(to, member).wait_send()


def recur_back(
    call, n, groups, dk, dv, beside, lengths, send_pos, slot_map, d_mixed, out_weight, attended, gate_pre,
    head_gain, up_wide, bias, down_wide, share, held, states, hidden_own, active, cotangent,
):
    count, width = d_mixed.shape
    slots, wide = held.shape
    half = count // 2
    vmem = pl.BlockSpec(memory_space=pltpu.VMEM)
    operands = [
        lengths, send_pos.reshape(1, -1), send_pos.reshape(-1, 1), slot_map.reshape(1, -1),
        slot_map.reshape(-1, 1), d_mixed, out_weight, attended, gate_pre, head_gain, up_wide, bias,
        down_wide, share, held, states, hidden_own, active, cotangent,
    ]
    far = pl.BlockSpec(memory_space=pl.ANY)
    return pl.pallas_call(
        functools.partial(recur_back_kernel, n, groups, dk, dv, beside),
        in_specs=[pl.BlockSpec(memory_space=pltpu.SMEM)] + [vmem] * (len(operands) - 6) + [far] * 5,
        out_specs=[vmem] * 7,
        out_shape=[
            jax.ShapeDtypeStruct((count, wide), bf16),
            jax.ShapeDtypeStruct((count, dv), bf16),
            jax.ShapeDtypeStruct((8, dv), f32),
            jax.ShapeDtypeStruct((dk, LANES), f32),
            jax.ShapeDtypeStruct((8, dk), f32),
            jax.ShapeDtypeStruct((count, width), bf16),
            jax.ShapeDtypeStruct((active.shape[1] // groups if beside else 8, width), f32),
        ],
        scratch_shapes=Line.scratch(half, width)
        + [
            pltpu.VMEM((count, dv), bf16),
            pltpu.VMEM((slots, dv), bf16),
            pltpu.VMEM((slots, dv), bf16),
            pltpu.VMEM((dk, dv), f32),
            pltpu.VMEM((slots, wide), bf16),
            pltpu.VMEM((slots, wide), bf16),
            pltpu.VMEM((slots, wide), bf16),
            pltpu.VMEM(held.shape, bf16),
            pltpu.VMEM(states.shape, bf16),
            pltpu.VMEM((half, width), f32),
            pltpu.SemaphoreType.DMA((3,)),
            Line.semaphores(half),
            pltpu.SemaphoreType.DMA((2, groups)),
            pltpu.SemaphoreType.DMA((2, groups)),
        ]
        + (ColGrad.scratch(groups, count, active.shape[1], width) if beside else []),
        compiler_params=pltpu.CompilerParams(
            collective_id=call, has_side_effects=True, vmem_limit_bytes=60 << 20
        ),
        cost_estimate=pl.CostEstimate(
            flops=12_000_000_000, bytes_accessed=200_000_000, transcendentals=4_000_000
        ),
        name="recur_back",
    )(*operands)


def small_sum_kernel(groups, n, rows_all, part_ref, out_ref, held, line, line_in, sems, line_sems):
    me = lax.axis_index("dp")
    place = lax.axis_index("tensor")
    barrier = pltpu.get_barrier_semaphore()

    def peer(k):
        return lax.rem(me + k, groups)

    def mate(k):
        return lax.rem(place + k, n)

    @pl.loop(1, groups)
    def _(k):
        pl.semaphore_signal(barrier, inc=1, device_id={"dp": peer(k)}, device_id_type=MESH)

    @pl.loop(1, n)
    def _(k):
        pl.semaphore_signal(barrier, inc=1, device_id={"tensor": mate(k)}, device_id_type=MESH)

    pl.semaphore_wait(barrier, groups + n - 2)

    def copy(k, source):
        return pltpu.make_async_remote_copy(
            part_ref.at[peer(k)], held.at[source], sems.at[0, k], sems.at[1, source],
            device_id={"dp": peer(k)}, device_id_type=MESH,
        )

    def line_copy(k, source):
        return pltpu.make_async_remote_copy(
            line, line_in.at[source], line_sems.at[0, k], line_sems.at[1, source],
            device_id={"tensor": mate(k)}, device_id_type=MESH,
        )

    @pl.loop(1, groups)
    def _(k):
        copy(k, me).start()

    held[pl.ds(me, 1)] = part_ref[pl.ds(me, 1)]

    @pl.loop(1, groups)
    def _(k):
        copy(k, peer(k)).wait_recv()

    total = held[0]
    for i in range(1, groups):
        total = total + held[i]
    line[...] = total[:rows_all]
    out_ref[...] = total

    @pl.loop(1, n)
    def _(k):
        line_copy(k, place).start()

    line_in[pl.ds(place, 1)] = total[None, :rows_all]

    @pl.loop(1, n)
    def _(k):
        line_copy(k, mate(k)).wait_recv()

    total = line_in[0]
    for i in range(1, n):
        total = total + line_in[i]
    out_ref[:rows_all] = total

    @pl.loop(1, groups)
    def _(k):
        copy(k, me).wait_send()

    @pl.loop(1, n)
    def _(k):
        line_copy(k, place).wait_send()


def small_sum(over_all, over_owners, groups, n, call):
    def tiles(blocks):
        short = -blocks.shape[1] % (8 * LANES)
        return jnp.pad(blocks, ((0, 0), (0, short))).reshape(groups, -1, LANES)

    first, second = tiles(over_all), tiles(over_owners)
    rows_all = first.shape[1]
    part = jnp.concatenate([first, second], axis=1)
    vmem = pl.BlockSpec(memory_space=pltpu.VMEM)
    total = pl.pallas_call(
        functools.partial(small_sum_kernel, groups, n, rows_all),
        in_specs=[vmem],
        out_specs=vmem,
        out_shape=jax.ShapeDtypeStruct(part.shape[1:], f32),
        scratch_shapes=[
            pltpu.VMEM(part.shape, f32),
            pltpu.VMEM((rows_all, LANES), f32),
            pltpu.VMEM((n, rows_all, LANES), f32),
            pltpu.SemaphoreType.DMA((2, groups)),
            pltpu.SemaphoreType.DMA((2, n)),
        ],
        compiler_params=pltpu.CompilerParams(collective_id=call, has_side_effects=True),
        name="small_sum",
    )(part)
    return (
        total[:rows_all].reshape(-1)[: over_all.shape[1]],
        total[rows_all:].reshape(-1)[: over_owners.shape[1]],
    )


def per_device(
    tokens,
    cotangent,
    token_slots,
    lengths,
    mixer_gain,
    query_weight,
    key_weight,
    value_weight,
    gate_weight,
    decay_down,
    decay_up,
    decay_bias,
    head_gain,
    out_weight,
    feed_gain,
    feed_gate,
    feed_up,
    feed_down,
):
    groups = lax.axis_size("dp")
    lines = lax.axis_size("tensor")
    member = lax.axis_index("dp")
    place = lax.axis_index("tensor")
    count, width = tokens.shape
    cap = OWN_CAP // groups
    slots = groups * cap
    dk = query_weight.shape[1]
    dv = value_weight.shape[1]
    rank = decay_up.shape[1]
    parity = lax.rem(member, 2)
    pairs = [(i, i ^ 1) for i in range(groups)]
    same_parity = [[i for i in range(groups) if i % 2 == b] for b in range(2)]

    owners = (token_slots // OWN_CAP).reshape(groups, count)
    mine = (owners == member).astype(bf16)
    my_slots = lax.dynamic_slice_in_dim(token_slots, member * count, count)
    my_owner = my_slots // OWN_CAP
    chosen = (my_owner[None, :] == jnp.arange(groups, dtype=jnp.int32)[:, None]).astype(bf16)
    index = jnp.arange(count, dtype=jnp.int32)
    before = (index[:, None] < index[None, :]).astype(bf16)
    ranks = dot(jnp.concatenate([mine, chosen], axis=0), before).astype(jnp.int32)
    recv_rank, send_rank = ranks[:groups], ranks[groups:]
    hit = (recv_rank[:, None, :] == jnp.arange(cap, dtype=jnp.int32)[None, :, None]) & (
        owners == member
    )[:, None, :]
    local = (token_slots % OWN_CAP).reshape(groups, count)
    slot_map = (
        jnp.sum(jnp.where(hit, local[:, None, :] - OWN_CAP, 0), axis=2) + OWN_CAP
    ).reshape(slots)
    send_pos = my_owner * cap + jnp.sum(
        jnp.where(chosen > 0, send_rank, 0), axis=0, dtype=jnp.int32
    )
    slot_ids = jnp.arange(slots, dtype=jnp.int32)
    pack = (slot_ids[:, None] == send_pos[None, :]).astype(bf16)
    unpack = (send_pos[:, None] == slot_ids[None, :]).astype(bf16)

    def exchange(row_block):
        blocks = row_block.reshape(groups, cap, row_block.shape[1])
        moved = lax.all_to_all(blocks, "dp", split_axis=0, concat_axis=0, tiled=True)
        return moved.reshape(slots, row_block.shape[1])

    half = count // 2
    own_at = jnp.where(place == 0, half, 0)
    tokens_own = lax.dynamic_slice_in_dim(tokens, own_at, half)
    cotangent_own = lax.dynamic_slice_in_dim(cotangent, own_at, half)

    tokens_wide = tokens.astype(f32)
    mixer_gain_wide = mixer_gain.astype(f32)
    feed_gain_wide = feed_gain.astype(f32)
    normed = (
        tokens_wide
        * lax.rsqrt(jnp.mean(tokens_wide * tokens_wide, axis=-1, keepdims=True) + epsilon)
        * mixer_gain_wide
    ).astype(bf16)
    queries = dot(normed, query_weight).astype(bf16)
    keys_low = dot(normed, key_weight).astype(bf16)
    value_rows = dot(normed, value_weight).astype(bf16)
    gate_pre = dot(normed, gate_weight)
    third = LANES // 4
    down_pad = jnp.pad(decay_down, ((0, 0), (0, third - rank)))
    latent = dot(
        normed,
        jnp.concatenate([down_pad, down_pad, down_pad, jnp.zeros_like(down_pad)], axis=1),
    )
    latent_high = latent.astype(bf16)
    latent_rest = latent - latent_high.astype(f32)
    latent_mid = latent_rest.astype(bf16)
    latent_low = (latent_rest - latent_mid.astype(f32)).astype(bf16)
    lane = jnp.arange(LANES, dtype=jnp.int32)[None, :]
    latent_packed = jnp.where(
        lane < third, latent_high, jnp.where(lane < 2 * third, latent_mid, latent_low)
    )
    rows_out = jnp.concatenate([queries, keys_low, value_rows, latent_packed], axis=1)
    arrived = exchange(dot(pack, rows_out).astype(bf16))
    up_pad = jnp.pad(decay_up, ((0, 0), (0, third - rank)))
    up_wide = jnp.concatenate([up_pad, up_pad, up_pad, jnp.zeros_like(up_pad)], axis=1).T
    down_wide = jnp.concatenate(
        [up_pad, up_pad, jnp.zeros_like(up_pad), jnp.zeros_like(up_pad)], axis=1
    )
    bias = decay_bias.astype(f32).reshape(1, dk)
    attended_slots, held, states = recur_forward(
        slot_map, lengths, up_wide, bias, arrived, dk, dv
    )
    attended = dot(unpack, exchange(attended_slots)).astype(bf16)
    head_gain_wide = head_gain.astype(f32)
    attended_wide = attended.astype(f32)
    gated = (
        attended_wide
        * lax.rsqrt(jnp.mean(attended_wide * attended_wide, axis=-1, keepdims=True) + head_floor)
        * head_gain_wide
        * jax.nn.silu(gate_pre)
    ).astype(bf16)
    mixer_share = dot(gated, out_weight).astype(bf16)
    feed_normed, hidden_own = line_sum(
        "norm", 1, lines, mixer_share, tokens_own, tokens_own, feed_gain_wide.reshape(1, -1)
    )

    gate_hidden = dot(feed_normed, feed_gate)
    up_hidden = dot(feed_normed, feed_up)
    d_active = dot_t(cotangent, feed_down)
    sigmoid_gate = jax.nn.sigmoid(gate_hidden)
    swish_gate = gate_hidden * sigmoid_gate
    active = (swish_gate * up_hidden).astype(bf16)
    d_gate_hidden = (
        d_active * up_hidden * sigmoid_gate * (1.0 + gate_hidden * (1.0 - sigmoid_gate))
    ).astype(bf16)
    d_up_hidden = (d_active * swish_gate).astype(bf16)
    feed_share = (dot_t(d_gate_hidden, feed_gate) + dot_t(d_up_hidden, feed_up)).astype(bf16)
    fused = (width // groups) % LANES == 0
    if fused:
        d_mixed, d_hidden_own, feed_gain_part, grad_feed_gate, grad_feed_up = back_feed(
            2, lines, groups, feed_share, feed_gain_wide.reshape(1, -1), hidden_own, cotangent_own,
            feed_normed, [d_gate_hidden, d_up_hidden],
        )
    else:
        d_mixed, d_hidden_own, feed_gain_part = line_sum(
            "back", 2, lines, feed_share, hidden_own, cotangent_own, feed_gain_wide.reshape(1, -1)
        )

    layer_share = dot(active, feed_down).astype(bf16)
    d_rows, d_gate_low, head_gain_part, up_part, bias_part, layer_out, grad_feed_down = recur_back(
        4, lines, groups, dk, dv, fused, lengths, send_pos, slot_map, d_mixed, out_weight, attended,
        gate_pre, head_gain_wide.reshape(1, -1), up_wide, bias, down_wide, layer_share, held, states,
        hidden_own, active, cotangent,
    )
    down_both = jnp.concatenate(
        [down_pad, down_pad, jnp.zeros_like(down_pad), jnp.zeros_like(down_pad)], axis=1
    )
    up_part = up_part[:, :rank] + up_part[:, third : third + rank] + (
        up_part[:, 2 * third : 2 * third + rank]
    )

    def by_owner(vector):
        return vector.reshape(groups, -1)

    per = width // groups
    head_per = dv // groups
    up_per = dk // groups * rank
    if fused:
        near = [
            by_owner(jnp.sum(feed_gain_part, axis=0)),
            jnp.pad(by_owner(jnp.sum(head_gain_part, axis=0)), ((0, 0), (0, -head_per % LANES))),
            by_owner(up_part),
            jnp.pad(by_owner(bias_part[0]), ((0, 0), (0, -(dk // groups) % LANES))),
        ]
        near_all = (per + head_per + LANES - 1) // LANES
        near = jnp.concatenate(near, axis=1)
        near = jnp.pad(near, ((0, 0), (0, -near.shape[1] % (8 * LANES))))
        (
            token_grad, wide_sum, near_sum, grad_query, grad_key, grad_value, grad_gate, grad_out,
        ) = back_mixer(
            3, lines, groups, mixer_gain_wide.reshape(1, -1), near.reshape(groups, -1, LANES),
            near_all, tokens_own, d_hidden_own, normed, [d_rows, d_gate_low],
            [(0, dk), (dk, dk), (2 * dk, dv), (2 * dk + dv + LANES, dv)], (gated, d_mixed),
            [query_weight, key_weight, value_weight, down_both, gate_weight],
        )
        near_sum = near_sum.reshape(-1)
        mixer_sum = jnp.sum(wide_sum[16:], axis=0)
        feed_sum = near_sum[:per]
        head_sum = near_sum[per : per + head_per]
        down_sum = wide_sum[:16].T
        up_sum = near_sum[near_all * LANES : near_all * LANES + up_per]
        bias_sum = near_sum[near_all * LANES + up_per :][: dk // groups]
    else:
        d_query_low = d_rows[:, :dk]
        d_key_low = d_rows[:, dk : 2 * dk]
        d_value_low = d_rows[:, 2 * dk : 2 * dk + dv]
        d_latent_low = d_rows[:, 2 * dk + dv :]
        normed_share = (
            dot_t(d_query_low, query_weight)
            + dot_t(d_key_low, key_weight)
            + dot_t(d_value_low, value_weight)
            + dot_t(d_gate_low, gate_weight)
            + dot_t(d_latent_low, down_both)
        ).astype(bf16)
        token_grad, _, mixer_gain_part = line_sum(
            "back", 3, lines, normed_share, tokens_own, d_hidden_own,
            mixer_gain_wide.reshape(1, -1),
        )
        down_part = rows_dot(normed, d_latent_low)
        down_part = down_part[:, :rank] + down_part[:, third : third + rank]
        over_all = jnp.concatenate(
            [
                by_owner(jnp.sum(mixer_gain_part, axis=0)),
                by_owner(jnp.sum(feed_gain_part, axis=0)),
                by_owner(jnp.sum(head_gain_part, axis=0)),
                by_owner(down_part),
            ],
            axis=1,
        )
        over_owners = jnp.concatenate([by_owner(up_part), by_owner(bias_part[0])], axis=1)
        summed, small = small_sum(over_all, over_owners, groups, lines, 5)
        mixer_sum = summed[:per]
        feed_sum = summed[per : 2 * per]
        head_sum = summed[2 * per : 2 * per + head_per]
        down_sum = summed[2 * per + head_per :].reshape(per, rank)
        up_sum = small[:up_per]
        bias_sum = small[up_per:]

    def halves(row_block, dims):
        split = row_block.reshape(row_block.shape[0], groups // 2, 2, dims // groups)
        keep = lax.dynamic_index_in_dim(split, parity, 2, keepdims=False)
        send = lax.dynamic_index_in_dim(split, 1 - parity, 2, keepdims=False)
        got = lax.ppermute(send, "dp", pairs)
        shape = (row_block.shape[0], dims // 2)
        return keep.reshape(shape), got.reshape(shape)

    def partner(row_block):
        return row_block, lax.ppermute(row_block, "dp", pairs)

    def summed_share(left, right):
        share = (rows_dot(left[0], right[0]) + rows_dot(left[1], right[1])).astype(bf16)
        rows = share.shape[0] // (groups // 2)
        blocks = share.reshape(groups // 2, rows, share.shape[1])
        moved = lax.all_to_all(
            blocks, "dp", split_axis=0, concat_axis=0, tiled=True, axis_index_groups=same_parity
        )
        return jnp.sum(moved.astype(f32), axis=0)

    if not fused:
        grad_feed_down = summed_share(halves(active, active.shape[1]), partner(cotangent))
        feed_halves = halves(feed_normed, width)
        normed_halves = halves(normed, width)
        grad_feed_gate = summed_share(feed_halves, partner(d_gate_hidden))
        grad_feed_up = summed_share(feed_halves, partner(d_up_hidden))
        grad_out = summed_share(halves(gated, dv), partner(d_mixed))
        grad_query = summed_share(normed_halves, partner(d_query_low))
        grad_key = summed_share(normed_halves, partner(d_key_low))
        grad_value = summed_share(normed_halves, partner(d_value_low))
        grad_gate = summed_share(normed_halves, partner(d_gate_low))

    return (
        layer_out,
        token_grad,
        mixer_sum,
        grad_query,
        grad_key,
        grad_value,
        grad_gate,
        down_sum,
        up_sum.reshape(1, dk // groups, rank),
        bias_sum.reshape(1, dk // groups),
        head_sum,
        grad_out[None],
        feed_sum,
        grad_feed_gate,
        grad_feed_up,
        grad_feed_down[None],
    )


def solution(mesh):
    placed = (
        P("dp", None),
        P("dp", None),
        P(),
        P("dp", None),
        P(),
        P(None, "tensor"),
        P(None, "tensor"),
        P(None, "tensor"),
        P(None, "tensor"),
        P(),
        P("tensor", None),
        P("tensor"),
        P(),
        P("tensor", None),
        P(),
        P(None, "tensor"),
        P(None, "tensor"),
        P("tensor", None),
    )
    return jax.shard_map(
        per_device,
        mesh=mesh,
        in_specs=placed,
        out_specs=(
            P("dp", None),
            P("dp", None),
            P("dp"),
            P("dp", "tensor"),
            P("dp", "tensor"),
            P("dp", "tensor"),
            P("dp", "tensor"),
            P("dp", None),
            P("tensor", "dp", None),
            P("tensor", "dp"),
            P("dp"),
            P("tensor", "dp", None),
            P("dp"),
            P("dp", "tensor"),
            P("dp", "tensor"),
            P("tensor", "dp", None),
        ),
        check_vma=False,
    )
```

```python
import functools

import jax
import jax.numpy as jnp
from jax import lax
from jax.experimental import pallas as pl
from jax.experimental.pallas import tpu as pltpu
from jax.sharding import PartitionSpec as P

OWN_CAP = 1024
SPAN = 128
LANES = 128
epsilon = 1e-06
head_floor = 1.0

f32 = jnp.float32
bf16 = jnp.bfloat16
MESH = pl.DeviceIdType.MESH


def rows_dot(left, right):
    return lax.dot_general(left, right, (((0,), (0,)), ((), ())), preferred_element_type=f32)


def dot_t(left, right):
    return lax.dot_general(left, right, (((1,), (1,)), ((), ())), preferred_element_type=f32)


def dot(left, right):
    return jnp.dot(left, right, preferred_element_type=f32)


def span_terms(first, ends, logits):
    rows = logits.shape[0]

    def label(position):
        count = jnp.zeros_like(position)
        for end in ends:
            count = count + (position >= end).astype(jnp.int32)
        return count

    log_decay = jax.nn.log_sigmoid(logits) * (1.0 / 16.0)
    row = lax.broadcasted_iota(jnp.int32, (rows, rows), 0)
    column = lax.broadcasted_iota(jnp.int32, (rows, rows), 1)
    lower = (row >= column).astype(f32)
    cumulative = jnp.dot(
        lower, log_decay, precision=lax.Precision.HIGHEST, preferred_element_type=f32
    )
    total = cumulative[rows - 1 :, :]
    middle = cumulative[rows // 2 - 1 : rows // 2, :]
    label_column = label(first + lax.broadcasted_iota(jnp.int32, (rows, 1), 0))
    label_row = label(first + lax.broadcasted_iota(jnp.int32, (1, rows), 1))
    before = jnp.where(first > 0, label(first - 1), -1)
    last = label(first + rows - 1)
    carried = (label_column == before).astype(f32)
    tail = (label_column == last).astype(f32)
    keep = (before == last).astype(f32)
    allowed = (row >= column) & (label_column == label_row)
    return log_decay, cumulative, total, middle, carried, tail, keep, allowed


def span_forward(dk, dv, step, ends, held_ref, up_ref, bias_ref, state, states_ref, result):
    first = step * SPAN
    at = pl.ds(pl.multiple_of(first, SPAN), SPAN)
    queries = held_ref[at, :dk].astype(f32) * (float(dk) ** -0.5)
    keys = held_ref[at, dk : 2 * dk].astype(f32)
    values = held_ref[at, 2 * dk : 2 * dk + dv]
    logits = dot(held_ref[at, 2 * dk + dv :], up_ref[...]) + bias_ref[...]
    _, cumulative, total, middle, carried, tail, keep, allowed = span_terms(first, ends, logits)
    query_mid = (queries * jnp.exp(cumulative - middle)).astype(bf16)
    key_mid = (keys * jnp.exp(middle - cumulative)).astype(bf16)
    query_start = (queries * jnp.exp(cumulative) * carried).astype(bf16)
    key_end = (keys * jnp.exp(total - cumulative) * tail).astype(bf16)
    scores = jnp.where(allowed, dot_t(query_mid, key_mid), 0.0).astype(bf16)
    entering = state[...]
    entering_low = entering.astype(bf16)
    states_ref[step] = entering_low
    attended = dot(scores, values) + dot(query_start, entering_low)
    result[at, :] = attended.astype(bf16)
    decay_column = jnp.transpose(jnp.broadcast_to(keep * jnp.exp(total), (8, dk)))[:, :1]
    state[...] = decay_column * entering + rows_dot(key_end, values)


def span_backward(
    dk, dv, step, ends, d_out, held_ref, entering, up_ref, bias_ref, down_ref, d_state, result,
    grad_up_ref, grad_bias_ref,
):
    first = step * SPAN
    at = pl.ds(pl.multiple_of(first, SPAN), SPAN)
    scale = float(dk) ** -0.5
    queries = held_ref[at, :dk].astype(f32) * scale
    keys = held_ref[at, dk : 2 * dk].astype(f32)
    values = held_ref[at, 2 * dk : 2 * dk + dv]
    latent = held_ref[at, 2 * dk + dv :]
    logits = dot(latent, up_ref[...]) + bias_ref[...]
    _, cumulative, total, middle, carried, tail, keep, allowed = span_terms(first, ends, logits)
    grow_query = jnp.exp(cumulative - middle)
    grow_key = jnp.exp(middle - cumulative)
    start_decay = jnp.exp(cumulative) * carried
    end_decay = jnp.exp(total - cumulative) * tail
    query_mid = (queries * grow_query).astype(bf16)
    key_mid = (keys * grow_key).astype(bf16)
    query_start = (queries * start_decay).astype(bf16)
    key_end = (keys * end_decay).astype(bf16)
    scores = jnp.where(allowed, dot_t(query_mid, key_mid), 0.0).astype(bf16)
    d_scores = jnp.where(allowed, dot_t(d_out, values), 0.0).astype(bf16)
    leaving = d_state[...]
    leaving_low = leaving.astype(bf16)
    d_values = rows_dot(scores, d_out) + dot(key_end, leaving_low)
    d_queries = dot(d_scores, key_mid) * grow_query + dot_t(d_out, entering) * start_decay
    d_key_end = dot_t(values, leaving_low) * end_decay
    d_keys = rows_dot(d_scores, query_mid) * grow_key + d_key_end
    kept = keep * jnp.exp(total)
    state_pair = jnp.sum(entering.astype(f32) * leaving, axis=1, keepdims=True)
    state_row = jnp.transpose(jnp.broadcast_to(state_pair, (dk, LANES)))[:1, :]
    d_total = jnp.sum(keys * d_key_end, axis=0, keepdims=True) + kept * state_row
    d_cumulative = queries * d_queries - keys * d_keys
    row = lax.broadcasted_iota(jnp.int32, (SPAN, SPAN), 0)
    column = lax.broadcasted_iota(jnp.int32, (SPAN, SPAN), 1)
    upper = (row <= column).astype(f32)
    d_log_decay = (
        jnp.dot(upper, d_cumulative, precision=lax.Precision.HIGHEST, preferred_element_type=f32)
        + d_total
    )
    d_logits = d_log_decay * (1.0 / 16.0) * jax.nn.sigmoid(-logits)
    grad_bias_ref[...] += jnp.broadcast_to(jnp.sum(d_logits, axis=0, keepdims=True), (8, dk))
    d_logits_high = d_logits.astype(bf16)
    d_logits_low = (d_logits - d_logits_high.astype(f32)).astype(bf16)
    grad_up_ref[...] += rows_dot(d_logits_high, latent) + rows_dot(d_logits_low, latent)
    d_latent = dot(d_logits_high, down_ref[...]) + dot(d_logits_low, down_ref[...])
    high = d_latent.astype(bf16).astype(f32)
    lane = lax.broadcasted_iota(jnp.int32, d_latent.shape, 1)
    d_latent_packed = jnp.where(lane < LANES // 4, high, d_latent - high)
    result[at, :dk] = (d_queries * scale).astype(bf16)
    result[at, dk : 2 * dk] = d_keys.astype(bf16)
    result[at, 2 * dk : 2 * dk + dv] = d_values.astype(bf16)
    result[at, 2 * dk + dv :] = d_latent_packed.astype(bf16)
    kept_column = jnp.transpose(jnp.broadcast_to(kept, (8, dk)))[:, :1]
    d_state[...] = kept_column * leaving + rows_dot(query_start, d_out)


FINE = 16
SKEW = 2


class Line:
    def __init__(self, n, share_ref, up_in, down_in, out_ref, sems, finish):
        self.n, self.me = n, lax.axis_index("tensor")
        self.share, self.up_in, self.down_in, self.out = share_ref, up_in, down_in, out_ref
        self.sems, self.finish = sems, finish
        self.half = up_in.shape[0]
        self.count = self.half // FINE
        self.second = self.count + 2
        self.steps = self.second + self.count + SKEW * (n - 2)

    @staticmethod
    def scratch(half, width):
        return [pltpu.VMEM((half, width), bf16), pltpu.VMEM((half, width), bf16)]

    @staticmethod
    def semaphores(half):
        return pltpu.SemaphoreType.DMA((8, half // FINE))

    def greet(self, barrier, others):
        n, me = self.n, self.me

        @pl.when(me > 0)
        def _():
            pl.semaphore_signal(barrier, inc=1, device_id={"tensor": me - 1}, device_id_type=MESH)

        @pl.when(me < n - 1)
        def _():
            pl.semaphore_signal(barrier, inc=1, device_id={"tensor": me + 1}, device_id_type=MESH)

        inside = (me > 0) & (me < n - 1)

        @pl.when(inside)
        def _():
            pl.semaphore_wait(barrier, others + 2)

        @pl.when(jnp.logical_not(inside))
        def _():
            pl.semaphore_wait(barrier, others + 1)

    def greet_all(self, barrier, others):
        n, me = self.n, self.me

        @pl.when(me > 0)
        def _():
            pl.semaphore_signal(barrier, inc=1, device_id={"tensor": me - 1}, device_id_type=MESH)

        @pl.when(me < n - 1)
        def _():
            pl.semaphore_signal(barrier, inc=1, device_id={"tensor": me + 1}, device_id_type=MESH)

        pl.semaphore_wait(barrier, others + n - 1)

    def at(self, g):
        return pl.ds(pl.multiple_of(g * FINE, FINE), FINE)

    def low(self, g):
        return pl.ds(pl.multiple_of(self.half + g * FINE, FINE), FINE)

    def right(self, source, target, lane, g):
        return pltpu.make_async_remote_copy(
            source, target, self.sems.at[2 * lane, g], self.sems.at[2 * lane + 1, g],
            device_id={"tensor": jnp.minimum(self.me + 1, self.n - 1)}, device_id_type=MESH,
        )

    def left(self, source, target, lane, g):
        return pltpu.make_async_remote_copy(
            source, target, self.sems.at[2 * lane, g], self.sems.at[2 * lane + 1, g],
            device_id={"tensor": jnp.maximum(self.me - 1, 0)}, device_id_type=MESH,
        )

    def up_copy(self, g):
        rows = self.up_in.at[self.at(g), :]
        return self.right(rows, rows, 0, g)

    def down_copy(self, g):
        rows = self.down_in.at[self.at(g), :]
        return self.left(rows, rows, 1, g)

    def up_back_copy(self, g):
        rows = self.out.at[self.at(g), :]
        return self.left(rows, rows, 2, g)

    def down_back_copy(self, g):
        rows = self.out.at[self.low(g), :]
        return self.right(rows, rows, 3, g)

    def prime(self, top=True, bottom=True):
        @pl.when((self.me == 0) & top)
        def _():
            @pl.loop(0, self.count)
            def _(g):
                self.right(
                    self.share.at[self.at(g), :], self.up_in.at[self.at(g), :], 0, g
                ).start()

        @pl.when((self.me == self.n - 1) & bottom)
        def _():
            @pl.loop(0, self.count)
            def _(g):
                self.left(
                    self.share.at[self.low(g), :], self.down_in.at[self.at(g), :], 1, g
                ).start()

    def step(self, step):
        n, me, count = self.n, self.me, self.count
        at, low = self.at, self.low
        g_up = step - SKEW * (me - 1)

        @pl.when((me > 0) & (g_up >= 0) & (g_up < count))
        def _():
            self.up_copy(g_up).wait_recv()
            total = self.up_in[at(g_up), :].astype(f32) + self.share[at(g_up), :].astype(f32)

            @pl.when(me < n - 1)
            def _():
                self.up_in[at(g_up), :] = total.astype(bf16)
                self.up_copy(g_up).start()

            @pl.when(me == n - 1)
            def _():
                self.finish(total, at(g_up), at(g_up))
                self.up_back_copy(g_up).start()

        g_down = step - SKEW * (n - 2 - me)

        @pl.when((me < n - 1) & (g_down >= 0) & (g_down < count))
        def _():
            self.down_copy(g_down).wait_recv()
            total = self.down_in[at(g_down), :].astype(f32) + (
                self.share[low(g_down), :].astype(f32)
            )

            @pl.when(me > 0)
            def _():
                self.down_in[at(g_down), :] = total.astype(bf16)
                self.down_copy(g_down).start()

            @pl.when(me == 0)
            def _():
                self.finish(total, at(g_down), low(g_down))
                self.down_back_copy(g_down).start()

        g_up_back = step - self.second - SKEW * (n - 2 - me)

        @pl.when((me < n - 1) & (g_up_back >= 0) & (g_up_back < count))
        def _():
            self.up_back_copy(g_up_back).wait_recv()

            @pl.when(me > 0)
            def _():
                self.up_back_copy(g_up_back).start()

        g_down_back = step - self.second - SKEW * (me - 1)

        @pl.when((me > 0) & (g_down_back >= 0) & (g_down_back < count))
        def _():
            self.down_back_copy(g_down_back).wait_recv()

            @pl.when(me < n - 1)
            def _():
                self.down_back_copy(g_down_back).start()

    def run(self, first, last):
        @pl.loop(first, last)
        def _(step):
            self.step(step)

    def drain(self):
        n, me = self.n, self.me

        @pl.loop(0, self.count)
        def _(g):
            @pl.when(me < n - 1)
            def _():
                self.up_copy(g).wait_send()
                self.down_back_copy(g).wait_send()

            @pl.when(me > 0)
            def _():
                self.down_copy(g).wait_send()
                self.up_back_copy(g).wait_send()


def norm_back(x_ref, base_ref, gain_ref, out_ref, kept_ref, gain_grad_ref):
    gain_grad_ref[...] = jnp.zeros_like(gain_grad_ref)

    def finish(total, own, place):
        rows = x_ref[own, :].astype(f32)
        scaling = lax.rsqrt(jnp.mean(rows * rows, axis=1, keepdims=True) + epsilon)
        unit = rows * scaling
        gained = gain_ref[...] * total
        grad = base_ref[own, :].astype(f32) + scaling * (
            gained - unit * jnp.mean(gained * unit, axis=1, keepdims=True)
        )
        kept_ref[own, :] = grad.astype(kept_ref.dtype)
        out_ref[place, :] = grad.astype(out_ref.dtype)
        term = total * unit
        part = term[0:8, :]
        for i in range(1, FINE // 8):
            part = part + term[8 * i : 8 * i + 8, :]
        gain_grad_ref[...] += part

    return finish


def line_kernel(n, *refs):
    share_ref, x_ref, base_ref, gain_ref, out_ref, kept_ref, gain_grad_ref = refs[:7]
    up_in, down_in, sems = refs[7:]
    finish = norm_back(x_ref, base_ref, gain_ref, out_ref, kept_ref, gain_grad_ref)
    line = Line(n, share_ref, up_in, down_in, out_ref, sems, finish)
    line.greet(pltpu.get_barrier_semaphore(), 0)
    line.prime()
    line.run(0, line.steps)
    line.drain()


def line_sum(call, n, share, x_own, base_own, gain):
    rows, width = share.shape
    half = rows // 2
    vmem = pl.BlockSpec(memory_space=pltpu.VMEM)
    return pl.pallas_call(
        functools.partial(line_kernel, n),
        in_specs=[vmem] * 4,
        out_specs=[vmem] * 3,
        out_shape=[
            jax.ShapeDtypeStruct((rows, width), bf16),
            jax.ShapeDtypeStruct((half, width), f32),
            jax.ShapeDtypeStruct((8, width), f32),
        ],
        scratch_shapes=Line.scratch(half, width) + [Line.semaphores(half)],
        compiler_params=pltpu.CompilerParams(
            collective_id=call, has_side_effects=True, vmem_limit_bytes=40 << 20
        ),
        name="line_back",
    )(share, x_own, base_own, gain)


def partner_of(index):
    return index + 1 - 2 * lax.rem(index, 2)


def to_dp(source, target, send, recv, device):
    return pltpu.make_async_remote_copy(
        source, target, send, recv, device_id={"dp": device}, device_id_type=MESH
    )


def greet_dp(barrier, groups):
    member = lax.axis_index("dp")

    @pl.loop(1, groups)
    def _(k):
        pl.semaphore_signal(
            barrier, inc=1, device_id={"dp": lax.rem(member + k, groups)}, device_id_type=MESH
        )


class ColGrad:
    TILE = 256

    def __init__(self, groups, left, right, out, refs):
        (
            self.left, self.right, self.left_in, self.right_in, self.send, self.recv,
            self.load_sems, self.pair_sems, self.sems,
        ) = refs
        self.left_far, self.right_far, self.out, self.groups = left, right, out, groups
        self.member = lax.axis_index("dp")
        self.parity = lax.rem(self.member, 2)
        self.half = self.right_in.shape[1]
        self.size = self.send.shape[0] // groups
        self.items = self.half // self.TILE

    @staticmethod
    def scratch(groups, count, rows, width):
        half = width // 2
        return [
            pltpu.VMEM((count, rows), bf16),
            pltpu.VMEM((count, half), bf16),
            pltpu.VMEM((count, rows), bf16),
            pltpu.VMEM((count, half), bf16),
            pltpu.VMEM((rows, half), bf16),
            pltpu.VMEM((groups, rows // groups, half), bf16),
            pltpu.SemaphoreType.DMA((2,)),
            pltpu.SemaphoreType.DMA((2, 2)),
            pltpu.SemaphoreType.DMA((2, groups)),
        ]

    def halves(self, parity):
        return self.right_far.at[:, pl.ds(pl.multiple_of(parity * self.half, self.half), self.half)]

    def loads(self):
        return (
            pltpu.make_async_copy(self.left_far, self.left, self.load_sems.at[0]),
            pltpu.make_async_copy(self.halves(self.parity), self.right, self.load_sems.at[1]),
        )

    def pair_copies(self):
        partner = partner_of(self.member)
        sems = self.pair_sems
        return (
            to_dp(self.left_far, self.left_in, sems.at[0, 0], sems.at[1, 0], partner),
            to_dp(
                self.halves(1 - self.parity), self.right_in, sems.at[0, 1], sems.at[1, 1], partner
            ),
        )

    def start(self):
        for c in self.pair_copies() + self.loads():
            c.start()

    def ready(self):
        for c in self.loads():
            c.wait()
        for c in self.pair_copies():
            c.wait_recv()

    def item(self, t):
        span = pl.ds(pl.multiple_of(t * self.TILE, self.TILE), self.TILE)
        product = rows_dot(self.left[...], self.right[:, span]) + rows_dot(
            self.left_in[...], self.right_in[:, span]
        )
        self.send[:, span] = product.astype(bf16)

    def copy(self, to, source):
        rows = pl.ds(pl.multiple_of(to * self.size, 16), self.size)
        return to_dp(
            self.send.at[rows, :], self.recv.at[source], self.sems.at[0, to],
            self.sems.at[1, source], to,
        )

    def send_all(self):
        @pl.loop(1, self.groups)
        def _(k):
            self.copy(lax.rem(self.member + k, self.groups), self.member).start()

        own = pl.ds(pl.multiple_of(self.member * self.size, 16), self.size)
        self.recv[pl.ds(self.member, 1)] = self.send[own, :][None]

    def receive(self):
        @pl.loop(1, self.groups)
        def _(k):
            self.copy(0, lax.rem(self.member + k, self.groups)).wait_recv()

        for b in range(2):
            total = self.recv[b].astype(f32)
            for q in range(1, self.groups // 2):
                total = total + self.recv[2 * q + b].astype(f32)
            self.out[:, b * self.half : (b + 1) * self.half] = total

    def drain(self):
        for c in self.pair_copies():
            c.wait_send()

        @pl.loop(1, self.groups)
        def _(k):
            self.copy(lax.rem(self.member + k, self.groups), self.member).wait_send()


class RowGrads:
    def __init__(self, groups, left, tiles, outs, outputs, refs):
        (
            self.left, self.all, self.left_in, self.all_in, self.send, self.recv,
            self.load_sems, self.left_sems, self.piece_sems, self.sems,
        ) = refs
        self.left_far, self.tiles = left, tiles
        self.outs, self.outputs = outs, outputs
        self.member = lax.axis_index("dp")
        self.parity = lax.rem(self.member, 2)
        self.mine = self.member // 2
        self.team = groups // 2
        self.block = left.shape[1] // groups
        self.items = self.team * len(tiles)

    @staticmethod
    def scratch(groups, count, width, total, pieces, tiles):
        team = groups // 2
        return [
            pltpu.VMEM((count, width), bf16),
            pltpu.VMEM((count, total), bf16),
            pltpu.VMEM((count, width // 2), bf16),
            pltpu.VMEM((count, total), bf16),
            pltpu.VMEM((team, width // groups, total), bf16),
            pltpu.VMEM((team, width // groups, total), bf16),
            pltpu.SemaphoreType.DMA((1 + pieces,)),
            pltpu.SemaphoreType.DMA((2, team)),
            pltpu.SemaphoreType.DMA((2, pieces)),
            pltpu.SemaphoreType.DMA((2, tiles, team)),
        ]

    def columns(self, j):
        return pl.ds(pl.multiple_of(j * self.block, self.block), self.block)

    def left_load(self):
        return pltpu.make_async_copy(self.left_far, self.left, self.load_sems.at[0])

    def piece_load(self, p, source, span):
        return pltpu.make_async_copy(source, self.all.at[:, span], self.load_sems.at[1 + p])

    def left_copy(self, q):
        return to_dp(
            self.left_far.at[:, self.columns(2 * q + 1 - self.parity)],
            self.left_in.at[:, self.columns(q)],
            self.left_sems.at[0, q], self.left_sems.at[1, q], partner_of(self.member),
        )

    def piece_copy(self, p, source, span):
        return to_dp(
            source, self.all_in.at[:, span], self.piece_sems.at[0, p], self.piece_sems.at[1, p],
            partner_of(self.member),
        )

    def start_left(self):
        @pl.loop(0, self.team)
        def _(q):
            self.left_copy(q).start()

        self.left_load().start()

    def ready_left(self):
        self.left_load().wait()

        @pl.loop(0, self.team)
        def _(q):
            self.left_copy(q).wait_recv()

    def copy(self, t, to, source):
        start, wide = self.tiles[t]
        span = pl.ds(start, wide)
        return to_dp(
            self.send.at[to, :, span], self.recv.at[source, :, span],
            self.sems.at[0, t, to], self.sems.at[1, t, source], 2 * to + self.parity,
        )

    def item(self, w):
        count = len(self.tiles)
        k = w // count
        to = lax.rem(self.mine + 1 + k, self.team)
        for t in range(count):
            start, wide = self.tiles[t]

            @pl.when((w >= 0) & (w < self.items) & (lax.rem(w, count) == t))
            def _():
                span = pl.ds(start, wide)
                product = rows_dot(
                    self.left[:, self.columns(2 * to + self.parity)], self.all[:, span]
                ) + rows_dot(self.left_in[:, self.columns(to)], self.all_in[:, span])
                low_product = product.astype(bf16)

                @pl.when(k < self.team - 1)
                def _():
                    self.send[to, :, span] = low_product
                    self.copy(t, to, self.mine).start()

                @pl.when(k == self.team - 1)
                def _():
                    self.recv[self.mine, :, span] = low_product

    def receive(self):
        for t in range(len(self.tiles)):
            @pl.loop(1, self.team)
            def _(k):
                self.copy(t, 0, lax.rem(self.mine + k, self.team)).wait_recv()

        for (start, wide), output in zip(self.outs, self.outputs):
            span = pl.ds(start, wide)
            total = self.recv[0, :, span].astype(f32)
            for q in range(1, self.team):
                total = total + self.recv[q, :, span].astype(f32)
            output[...] = total

    def drain(self):
        @pl.loop(0, self.team)
        def _(q):
            self.left_copy(q).wait_send()

        for t in range(len(self.tiles)):
            @pl.loop(1, self.team)
            def _(k):
                self.copy(t, lax.rem(self.mine + k, self.team), self.mine).wait_send()


def splitter(refs):
    refs = list(refs)

    def take(k):
        out = refs[:k]
        del refs[:k]
        return out

    return take


def one_hot(index, base, shape, dim):
    return (index == base + lax.broadcasted_iota(jnp.int32, shape, dim)).astype(f32).astype(bf16)


class Exchange:
    def __init__(self, groups, sent, came, sems):
        self.groups, self.sent, self.came, self.sems = groups, sent, came, sems
        self.member = lax.axis_index("dp")
        self.cap = sent.shape[0] // groups

    @staticmethod
    def scratch(groups, slots, width):
        return [
            pltpu.VMEM((slots, width), bf16),
            pltpu.VMEM((slots, width), bf16),
            pltpu.SemaphoreType.DMA((2, groups)),
        ]

    def part(self, j):
        return pl.ds(pl.multiple_of(j * self.cap, self.cap), self.cap)

    def copy(self, to, source):
        return to_dp(
            self.sent.at[self.part(to), :], self.came.at[self.part(source), :],
            self.sems.at[0, to], self.sems.at[1, source], to,
        )

    def send(self, index_ref, dim, source):
        groups, count = self.groups, source.shape[0]
        rows = self.sent.shape[0] // 2

        @pl.loop(0, 2)
        def _(h):
            at = pl.ds(pl.multiple_of(h * rows, rows), rows)
            if dim == 0:
                pick = one_hot(index_ref[...], h * rows, (rows, count), 0)
            else:
                pick = one_hot(index_ref[at, :], 0, (rows, count), 1)
            self.sent[at, :] = dot(pick, source[...]).astype(bf16)

            @pl.loop(0, groups // 2)
            def _(k):
                to = h * (groups // 2) + lax.rem(self.member + k, groups // 2)

                @pl.when(to != self.member)
                def _():
                    self.copy(to, self.member).start()

        self.came[self.part(self.member), :] = self.sent[self.part(self.member), :]

    def receive(self):
        @pl.loop(1, self.groups)
        def _(k):
            self.copy(0, lax.rem(self.member + k, self.groups)).wait_recv()

    def drain(self):
        @pl.loop(1, self.groups)
        def _(k):
            self.copy(lax.rem(self.member + k, self.groups), self.member).wait_send()


def place_rows(slot_row_ref, came, held):
    positions, slots = held.shape[0], came.shape[0]
    rows = positions // 2

    @pl.loop(0, 2)
    def _(h):
        at = pl.ds(pl.multiple_of(h * rows, rows), rows)
        pick = one_hot(slot_row_ref[...], h * rows, (rows, slots), 0)
        held[at, :] = dot(pick, came[...]).astype(bf16)


def front_kernel(n, groups, dk, dv, *refs):
    take = splitter(refs)
    lengths_ref, slots_ref, tokens_ref, mixer_gain_ref, feed_gain_ref, head_gain_ref = take(6)
    up_ref, bias_ref = take(2)
    weights_far = take(4)
    gate_far, out_far, cotangent_far, down_far = take(4)
    normed_ref, gate_ref, attended_ref, gated_ref, feed_ref, hidden_ref, d_active_ref = take(7)
    held_ref, states_ref, send_row_ref, send_column_ref, slot_row_ref, slot_column_ref = take(6)
    up_in, down_in, weight_ref, gate_weight_ref, out_weight_ref, cotangent_ref, down_ref = take(7)
    rows_out, share_ref, state, result, rank_ref, load_sems, sems = take(7)
    go = Exchange(groups, *take(3))
    back = Exchange(groups, *take(3))
    member = lax.axis_index("dp")
    count, width = tokens_ref.shape
    cap = OWN_CAP // groups
    half = count // 2
    end0 = lengths_ref[0, 0]
    end1 = end0 + lengths_ref[0, 1]
    ends = (end0, end1, end1 + lengths_ref[0, 2])
    third = LANES // 4

    def finish(total, own, place):
        hidden = tokens_ref[place, :].astype(f32) + total
        hidden_ref[own, :] = hidden
        scaling = lax.rsqrt(jnp.mean(hidden * hidden, axis=1, keepdims=True) + epsilon)
        feed_ref[place, :] = (hidden * scaling * feed_gain_ref[...]).astype(bf16)

    line = Line(n, share_ref, up_in, down_in, feed_ref, sems, finish)
    loads = []
    offset = 0
    for i, far in enumerate(weights_far):
        wide = far.shape[1]
        loads.append(
            pltpu.make_async_copy(far, weight_ref.at[:, pl.ds(offset, wide)], load_sems.at[i])
        )
        offset += wide
    later = [
        pltpu.make_async_copy(gate_far, gate_weight_ref, load_sems.at[4]),
        pltpu.make_async_copy(out_far, out_weight_ref, load_sems.at[5]),
    ]
    latest = [
        pltpu.make_async_copy(cotangent_far, cotangent_ref, load_sems.at[6]),
        pltpu.make_async_copy(down_far, down_ref, load_sems.at[7]),
    ]
    for c in loads + later + latest:
        c.start()
    barrier = pltpu.get_barrier_semaphore()
    greet_dp(barrier, groups)
    line.greet(barrier, groups - 1)

    owners = slots_ref[...] // OWN_CAP
    mine = owners == member
    my_slots = slots_ref[pl.ds(member, 1), :]
    my_owner = my_slots // OWN_CAP
    device = lax.broadcasted_iota(jnp.int32, (groups, count), 0)
    chosen = (my_owner == device).astype(f32)
    before = (
        lax.broadcasted_iota(jnp.int32, (count, count), 0)
        < lax.broadcasted_iota(jnp.int32, (count, count), 1)
    ).astype(f32).astype(bf16)
    send_rank = jnp.sum(chosen * dot(chosen.astype(bf16), before), axis=0, keepdims=True)
    send_row = my_owner * cap + send_rank.astype(jnp.int32)
    send_row_ref[...] = send_row
    send_column_ref[...] = jnp.transpose(
        jnp.broadcast_to(send_row.astype(f32), (8, count))
    )[:, :1].astype(jnp.int32)
    rank_ref[...] = jnp.where(mine, dot(mine.astype(f32).astype(bf16), before), -1.0)

    tile = count // 5

    @pl.loop(0, 5)
    def _(i):
        at = pl.ds(pl.multiple_of(i * tile, tile), tile)
        rows = tokens_ref[at, :].astype(f32)
        scaling = lax.rsqrt(jnp.mean(rows * rows, axis=1, keepdims=True) + epsilon)
        normed_ref[at, :] = (rows * scaling * mixer_gain_ref[...]).astype(bf16)

    for c in loads:
        c.wait()
    body = 2 * dk + dv

    @pl.loop(0, body // 256)
    def _(i):
        to = pl.ds(pl.multiple_of(i * 256, 256), 256)
        rows_out[:, to] = dot(normed_ref[...], weight_ref[:, to]).astype(bf16)

    latent = dot(normed_ref[...], weight_ref[:, body:])
    high = latent.astype(bf16).astype(f32)
    middle = (latent - high).astype(bf16).astype(f32)
    lane = lax.broadcasted_iota(jnp.int32, latent.shape, 1)
    rows_out[:, body:] = jnp.where(
        lane < third, high, jnp.where(lane < 2 * third, middle, latent - high - middle)
    ).astype(bf16)
    go.send(send_row_ref, 0, rows_out)

    for c in later:
        c.wait()

    @pl.loop(0, dv // 256)
    def _(i):
        to = pl.ds(pl.multiple_of(i * 256, 256), 256)
        gate_ref[:, to] = dot(normed_ref[...], gate_weight_ref[:, to])

    @pl.loop(0, groups)
    def _(j):
        rank = rank_ref[pl.ds(j, 1), :]
        local = (lax.rem(slots_ref[pl.ds(j, 1), :], OWN_CAP) - OWN_CAP).astype(f32)
        wanted = lax.broadcasted_iota(jnp.int32, (cap, count), 0).astype(f32)
        at = jnp.sum(jnp.where(rank == wanted, local, 0.0), axis=1, keepdims=True)
        slot_column_ref[go.part(j), :] = at.astype(jnp.int32) + OWN_CAP

    slots = slot_row_ref.shape[1]
    slot_row_ref[...] = jnp.transpose(
        jnp.broadcast_to(slot_column_ref[...].astype(f32), (slots, LANES))
    )[:1, :].astype(jnp.int32)
    state[...] = jnp.zeros_like(state)
    go.receive()
    place_rows(slot_row_ref, go.came, held_ref)

    @pl.loop(0, held_ref.shape[0] // SPAN)
    def _(step):
        span_forward(dk, dv, step, ends, held_ref, up_ref, bias_ref, state, states_ref, result)

    back.send(slot_column_ref, 1, result)
    back.receive()

    def head_rows(at):
        pick = one_hot(send_column_ref[at, :], 0, (half, slots), 1)
        attended = dot(pick, back.came[...])
        attended_ref[at, :] = attended.astype(bf16)
        gate = gate_ref[at, :]
        scaling = lax.rsqrt(jnp.mean(attended * attended, axis=1, keepdims=True) + head_floor)
        gated = attended * scaling * head_gain_ref[...] * (gate * jax.nn.sigmoid(gate))
        gated_ref[at, :] = gated.astype(bf16)

        @pl.loop(0, width // 512)
        def _(i):
            to = pl.ds(pl.multiple_of(i * 512, 512), 512)
            share_ref[at, to] = dot(gated_ref[at, :], out_weight_ref[:, to]).astype(bf16)

    last = line.me == n - 1

    @pl.loop(0, 2)
    def _(i):
        bottom = jnp.where(last, 1 - i, i)
        head_rows(pl.ds(pl.multiple_of(bottom * half, half), half))
        line.prime(i == 0, i == 0)

    wide = d_active_ref.shape[1]
    full, rest = wide // 256, wide % 256

    def hidden_units(i, size):
        at = pl.ds(pl.multiple_of(i * 256, 256), size)
        d_active_ref[:, at] = dot_t(cotangent_ref[...], down_ref[at, :]).astype(bf16)

    for c in latest:
        c.wait()

    @pl.loop(0, line.steps)
    def _(step):
        line.step(step)
        i = step // 2 - 2

        @pl.when((lax.rem(step, 2) == 0) & (i >= 0) & (i < full))
        def _():
            hidden_units(i, 256)

        if rest:
            @pl.when(step == 2 * full + 4)
            def _():
                hidden_units(full, rest)

    line.drain()
    go.drain()
    back.drain()


def front(
    call, n, groups, lengths, slots, tokens, mixer_gain, feed_gain, head_gain, up_wide, bias, weights,
    gate_weight, out_weight, cotangent, feed_down,
):
    count, width = tokens.shape
    dk, dv = weights[0].shape[1], weights[2].shape[1]
    wide = sum(w.shape[1] for w in weights)
    half = count // 2
    spans = OWN_CAP // SPAN
    vmem = pl.BlockSpec(memory_space=pltpu.VMEM)
    far = pl.BlockSpec(memory_space=pl.ANY)
    smem = pl.BlockSpec(memory_space=pltpu.SMEM)
    shape = jax.ShapeDtypeStruct
    return pl.pallas_call(
        functools.partial(front_kernel, n, groups, dk, dv),
        in_specs=[smem] + [vmem] * 7 + [far] * 8,
        out_specs=[vmem] * 13,
        out_shape=[
            shape((count, width), bf16),
            shape((count, dv), f32),
            shape((count, dv), bf16),
            shape((count, dv), bf16),
            shape((count, width), bf16),
            shape((half, width), f32),
            shape((count, feed_down.shape[0]), bf16),
            shape((OWN_CAP, wide), bf16),
            shape((spans, dk, dv), bf16),
            shape((1, count), jnp.int32),
            shape((count, 1), jnp.int32),
            shape((1, OWN_CAP), jnp.int32),
            shape((OWN_CAP, 1), jnp.int32),
        ],
        scratch_shapes=Line.scratch(half, width)
        + [
            pltpu.VMEM((width, wide), bf16),
            pltpu.VMEM((width, dv), bf16),
            pltpu.VMEM((dv, width), bf16),
            pltpu.VMEM((count, width), bf16),
            pltpu.VMEM(feed_down.shape, bf16),
            pltpu.VMEM((count, wide), bf16),
            pltpu.VMEM((count, width), bf16),
            pltpu.VMEM((dk, dv), f32),
            pltpu.VMEM((OWN_CAP, dv), bf16),
            pltpu.VMEM((groups, count), f32),
            pltpu.SemaphoreType.DMA((8,)),
            Line.semaphores(half),
        ]
        + Exchange.scratch(groups, OWN_CAP, wide)
        + Exchange.scratch(groups, OWN_CAP, dv),
        compiler_params=pltpu.CompilerParams(
            collective_id=call, has_side_effects=True, vmem_limit_bytes=60 << 20
        ),
        cost_estimate=pl.CostEstimate(
            flops=12_000_000_000, bytes_accessed=200_000_000, transcendentals=4_000_000
        ),
        name="front",
    )(
        lengths, slots, tokens, mixer_gain, feed_gain, head_gain, up_wide, bias, *weights,
        gate_weight, out_weight, cotangent, feed_down,
    )


def back_feed_kernel(n, groups, tiles, outs, *refs):
    take = splitter(refs)
    gain_ref, x_far, base_far, left_far, d_active_far, gate_far, up_far, down_far = take(8)
    out_ref, kept_ref, gain_grad_ref = take(3)
    outputs = take(2)
    active_ref, layer_ref = take(2)
    up_in, down_in, x_ref, base_ref, share_ref, weight_ref, d_active_ref = take(7)
    load_sems, weight_sems, sems = take(3)
    rows = RowGrads(groups, left_far, tiles, outs, outputs, take(10))
    finish = norm_back(x_ref, base_ref, gain_ref, out_ref, kept_ref, gain_grad_ref)
    line = Line(n, share_ref, up_in, down_in, out_ref, sems, finish)
    count, width = share_ref.shape
    wide = active_ref.shape[1]
    full, rest = wide // 256, wide % 256
    pieces = full + (rest > 0)
    loads = (
        pltpu.make_async_copy(d_active_far, d_active_ref, load_sems.at[2]),
        pltpu.make_async_copy(x_far, x_ref, load_sems.at[0]),
        pltpu.make_async_copy(base_far, base_ref, load_sems.at[1]),
    )
    down_load = pltpu.make_async_copy(
        down_far, weight_ref.at[pl.ds(0, wide), pl.ds(0, width)], load_sems.at[3]
    )

    def spans(i, size):
        start = pl.multiple_of(i * 256, 256)
        return pl.ds(start, size), pl.ds(pl.multiple_of(wide + start, LANES), size)

    def weight_loads(i, size):
        gate_span, up_span = spans(i, size)
        return (
            pltpu.make_async_copy(
                gate_far.at[:, gate_span], weight_ref.at[:, gate_span], weight_sems.at[0, i]
            ),
            pltpu.make_async_copy(
                up_far.at[:, gate_span], weight_ref.at[:, up_span], weight_sems.at[1, i]
            ),
        )

    def piece_copies(i, size):
        gate_span, up_span = spans(i, size)
        return (
            rows.piece_copy(2 * i, rows.all.at[:, gate_span], gate_span),
            rows.piece_copy(2 * i + 1, rows.all.at[:, up_span], up_span),
        )

    def each(action):
        @pl.loop(0, full)
        def _(i):
            action(i, 256)

        if rest:
            action(full, rest)

    def start_weights(i, size):
        for c in weight_loads(i, size):
            c.start()

    rows.left_load().start()
    each(start_weights)
    for c in loads:
        c.start()
    barrier = pltpu.get_barrier_semaphore()
    greet_dp(barrier, groups)
    line.greet(barrier, groups - 1)

    @pl.loop(0, rows.team)
    def _(q):
        rows.left_copy(q).start()

    rows.left_load().wait()
    for c in loads:
        c.wait()

    def hidden_units(i, size):
        for c in weight_loads(i, size):
            c.wait()
        gate_span, up_span = spans(i, size)
        gate = dot(rows.left[...], weight_ref[:, gate_span])
        up = dot(rows.left[...], weight_ref[:, up_span])
        d_active = d_active_ref[:, gate_span].astype(f32)
        sigmoid = jax.nn.sigmoid(gate)
        swish = gate * sigmoid
        active_ref[:, gate_span] = (swish * up).astype(bf16)
        rows.all[:, gate_span] = (
            d_active * up * sigmoid * (1.0 + gate * (1.0 - sigmoid))
        ).astype(bf16)
        rows.all[:, up_span] = (d_active * swish).astype(bf16)
        for c in piece_copies(i, size):
            c.start()

    each(hidden_units)

    half = count // 2
    last = line.me == n - 1

    @pl.loop(0, 2)
    def _(i):
        bottom = jnp.where(last, 1 - i, i)
        at = pl.ds(pl.multiple_of(bottom * half, half), half)

        @pl.loop(0, width // 256)
        def _(j):
            to = pl.ds(pl.multiple_of(j * 256, 256), 256)
            share_ref[at, to] = dot_t(rows.all[at, :], weight_ref[to, :]).astype(bf16)

        line.prime(i == 0, i == 0)

    down_load.start()

    def piece_arrived(i, size):
        for c in piece_copies(i, size):
            c.wait_recv()

    layer_items = width // 512

    @pl.loop(0, line.steps)
    def _(step):
        line.step(step)

        @pl.when(step == 0)
        def _():
            @pl.loop(0, rows.team)
            def _(q):
                rows.left_copy(q).wait_recv()

            each(piece_arrived)

        rows.item(step)
        layer_item = step - rows.items

        @pl.when(layer_item == 0)
        def _():
            down_load.wait()

        @pl.when((layer_item >= 0) & (layer_item < layer_items))
        def _():
            to = pl.ds(pl.multiple_of(layer_item * 512, 512), 512)
            layer_ref[:, to] = dot(active_ref[...], weight_ref[pl.ds(0, wide), to]).astype(bf16)

    rows.receive()
    line.drain()
    rows.drain()

    def piece_sent(i, size):
        for c in piece_copies(i, size):
            c.wait_send()

    each(piece_sent)


def back_feed(call, n, groups, gain, x_own, base_own, left, d_active, feed_gate, feed_up, feed_down):
    count, width = left.shape
    half = count // 2
    wide = feed_gate.shape[1]
    pieces = (wide + 255) // 256
    cut = (wide // 2 + LANES - 1) // LANES * LANES
    tiles = [(0, cut), (cut, wide - cut), (wide, cut), (wide + cut, wide - cut)]
    outs = [(0, wide), (wide, wide)]
    vmem = pl.BlockSpec(memory_space=pltpu.VMEM)
    far = pl.BlockSpec(memory_space=pl.ANY)
    return pl.pallas_call(
        functools.partial(back_feed_kernel, n, groups, tiles, outs),
        in_specs=[vmem] + [far] * 7,
        out_specs=[vmem] * 7,
        out_shape=[
            jax.ShapeDtypeStruct((count, width), bf16),
            jax.ShapeDtypeStruct((half, width), f32),
            jax.ShapeDtypeStruct((8, width), f32),
            jax.ShapeDtypeStruct((width // groups, wide), f32),
            jax.ShapeDtypeStruct((width // groups, wide), f32),
            jax.ShapeDtypeStruct((count, wide), bf16),
            jax.ShapeDtypeStruct((count, width), bf16),
        ],
        scratch_shapes=Line.scratch(half, width)
        + [
            pltpu.VMEM((half, width), x_own.dtype),
            pltpu.VMEM((half, width), base_own.dtype),
            pltpu.VMEM((count, width), bf16),
            pltpu.VMEM((width, 2 * wide), bf16),
            pltpu.VMEM((count, wide), bf16),
            pltpu.SemaphoreType.DMA((4,)),
            pltpu.SemaphoreType.DMA((2, pieces)),
            Line.semaphores(half),
        ]
        + RowGrads.scratch(groups, count, width, 2 * wide, 2 * pieces, len(tiles)),
        compiler_params=pltpu.CompilerParams(
            collective_id=call, has_side_effects=True, vmem_limit_bytes=61 << 20
        ),
        cost_estimate=pl.CostEstimate(
            flops=30_000_000_000, bytes_accessed=200_000_000, transcendentals=0
        ),
        name="back_feed",
    )(gain, x_own, base_own, left, d_active, feed_gate, feed_up, feed_down)


class SmallSum:
    def __init__(self, n, groups, wide, near, near_all, wide_out, near_out, refs):
        (
            self.wide_in, self.near_in, self.wide_line, self.near_line, self.sems, self.line_sems,
        ) = refs
        self.n, self.groups, self.near_all = n, groups, near_all
        self.wide, self.near, self.wide_out, self.near_out = wide, near, wide_out, near_out
        self.member, self.place = lax.axis_index("dp"), lax.axis_index("tensor")
        self.block = wide.shape[1] // groups

    @staticmethod
    def scratch(n, groups, wide, near):
        block = wide[1] // groups
        return [
            pltpu.VMEM((groups, wide[0], block), f32),
            pltpu.VMEM(near, f32),
            pltpu.VMEM((n, wide[0], block), f32),
            pltpu.VMEM((n,) + near[1:], f32),
            pltpu.SemaphoreType.DMA((2, 2, groups)),
            pltpu.SemaphoreType.DMA((2, 2, n)),
        ]

    def greet(self, barrier):
        n, place = self.n, self.place
        for k in range(2, n):
            @pl.when(place + k < n)
            def _():
                pl.semaphore_signal(
                    barrier, inc=1, device_id={"tensor": place + k}, device_id_type=MESH
                )

            @pl.when(place - k >= 0)
            def _():
                pl.semaphore_signal(
                    barrier, inc=1, device_id={"tensor": place - k}, device_id_type=MESH
                )

    def cut(self, j):
        return pl.ds(pl.multiple_of(j * self.block, self.block), self.block)

    def copies(self, to, source):
        return (
            to_dp(
                self.wide.at[:, self.cut(to)], self.wide_in.at[source],
                self.sems.at[0, 0, to], self.sems.at[1, 0, source], to,
            ),
            to_dp(
                self.near.at[to], self.near_in.at[source],
                self.sems.at[0, 1, to], self.sems.at[1, 1, source], to,
            ),
        )

    def line_copies(self, to, source):
        return tuple(
            pltpu.make_async_remote_copy(
                line.at[self.place], line.at[source], self.line_sems.at[0, i, to],
                self.line_sems.at[1, i, source], device_id={"tensor": to}, device_id_type=MESH,
            )
            for i, line in enumerate((self.wide_line, self.near_line))
        )

    def send(self):
        @pl.loop(1, self.groups)
        def _(k):
            for c in self.copies(lax.rem(self.member + k, self.groups), self.member):
                c.start()

        self.wide_in[pl.ds(self.member, 1)] = self.wide[:, self.cut(self.member)][None]
        self.near_in[pl.ds(self.member, 1)] = self.near[pl.ds(self.member, 1)]

    def forward(self):
        @pl.loop(1, self.groups)
        def _(k):
            for c in self.copies(0, lax.rem(self.member + k, self.groups)):
                c.wait_recv()

        for came, line in ((self.wide_in, self.wide_line), (self.near_in, self.near_line)):
            total = came[0]
            for j in range(1, self.groups):
                total = total + came[j]
            line[pl.ds(self.place, 1)] = total[None]

        @pl.loop(1, self.n)
        def _(k):
            for c in self.line_copies(lax.rem(self.place + k, self.n), self.place):
                c.start()

    def receive(self):
        @pl.loop(1, self.n)
        def _(k):
            for c in self.line_copies(0, lax.rem(self.place + k, self.n)):
                c.wait_recv()

        total = self.wide_line[0]
        for j in range(1, self.n):
            total = total + self.wide_line[j]
        self.wide_out[...] = total
        own = self.near_line[pl.ds(self.place, 1)][0]
        total = self.near_line[0]
        for j in range(1, self.n):
            total = total + self.near_line[j]
        row = lax.broadcasted_iota(jnp.int32, own.shape, 0)
        self.near_out[...] = jnp.where(row < self.near_all, total, own)

    def drain(self):
        @pl.loop(1, self.groups)
        def _(k):
            for c in self.copies(lax.rem(self.member + k, self.groups), self.member):
                c.wait_send()

        @pl.loop(1, self.n)
        def _(k):
            for c in self.line_copies(lax.rem(self.place + k, self.n), self.place):
                c.wait_send()


def back_mixer_kernel(n, groups, widths, near_all, tiles, outs, *refs):
    take = splitter(refs)
    gain_ref, near_ref, x_far, base_far, left_far = take(5)
    parts = take(2)
    col_left, col_right = take(2)
    weights = take(len(widths))
    out_ref, wide_out, near_out = take(3)
    outputs = take(len(outs))
    (col_out,) = take(1)
    up_in, down_in, x_ref, base_ref, kept_ref, share_ref, wide_ref, gain_grad_ref = take(8)
    weight_ref, load_sems, sems = take(3)
    rows = RowGrads(groups, left_far, tiles, outs, outputs, take(10))
    part_spans = [
        pl.ds(0, parts[0].shape[1]), pl.ds(parts[0].shape[1], parts[1].shape[1])
    ]
    part_loads = [rows.piece_load(i, parts[i], part_spans[i]) for i in range(2)]
    part_copies = [rows.piece_copy(i, parts[i], part_spans[i]) for i in range(2)]
    cols = ColGrad(groups, col_left, col_right, col_out, take(9))
    small = SmallSum(n, groups, wide_ref, near_ref, near_all, wide_out, near_out, take(6))
    finish = norm_back(x_ref, base_ref, gain_ref, out_ref, kept_ref, gain_grad_ref)
    line = Line(n, share_ref, up_in, down_in, out_ref, sems, finish)
    loads = [
        pltpu.make_async_copy(x_far, x_ref, load_sems.at[0]),
        pltpu.make_async_copy(base_far, base_ref, load_sems.at[1]),
    ]
    weight_loads = []
    offset = 0
    for i, wide in enumerate(widths):
        weight_loads.append(
            pltpu.make_async_copy(
                weights[i], weight_ref.at[:, pl.ds(offset, wide)], load_sems.at[2 + i]
            )
        )
        offset += wide
    for c in part_loads + weight_loads:
        c.start()
    barrier = pltpu.get_barrier_semaphore()
    greet_dp(barrier, groups)
    small.greet(barrier)
    line.greet_all(barrier, groups - 1)
    rows.start_left()
    for c in part_copies:
        c.start()
    cols.start()
    for c in loads:
        c.start()
    for c in part_loads + weight_loads:
        c.wait()

    count, width = share_ref.shape
    tile_rows, tile_columns = count // 2, 512
    across = width // tile_columns

    @pl.loop(0, 2 * across)
    def _(i):
        at = pl.ds(pl.multiple_of((i // across) * tile_rows, tile_rows), tile_rows)
        to = pl.ds(pl.multiple_of(lax.rem(i, across) * tile_columns, tile_columns), tile_columns)
        share_ref[at, to] = dot_t(rows.all[at, :], weight_ref[to, :]).astype(bf16)

    line.prime()
    for c in loads:
        c.wait()
    third = LANES // 4
    latent_at = offset - widths[-1] - LANES
    first_cols = rows.items
    last_item = first_cols + cols.items

    @pl.loop(0, line.steps)
    def _(step):
        line.step(step)

        @pl.when(step == 0)
        def _():
            rows.ready_left()
            for c in part_copies:
                c.wait_recv()

        rows.item(step)

        @pl.when(step == first_cols)
        def _():
            cols.ready()

        @pl.when((step >= first_cols) & (step < last_item))
        def _():
            cols.item(step - first_cols)

        @pl.when(step == last_item)
        def _():
            cols.send_all()
            product = rows_dot(rows.all[:, pl.ds(latent_at, LANES)], rows.left[...])
            wide_ref[:16, :] = product[:16, :] + product[third : third + 16, :]

        @pl.when(step == line.second + 4)
        def _():
            wide_ref[16:, :] = gain_grad_ref[...]
            small.send()

        @pl.when(step == line.second + 14)
        def _():
            small.forward()

    rows.receive()
    cols.receive()
    small.receive()
    line.drain()
    rows.drain()
    for c in part_copies:
        c.wait_send()
    cols.drain()
    small.drain()


def back_mixer(call, n, groups, gain, near, near_all, x_own, base_own, left, parts, outs, pair, weights):
    count, width = left.shape
    half = count // 2
    widths = [w.shape[1] for w in weights]
    total = sum(part.shape[1] for part in parts)
    start = parts[0].shape[1]
    tiles = [(0, 512), (512, 512), (start, parts[1].shape[1])]
    col_rows = pair[0].shape[1]
    vmem = pl.BlockSpec(memory_space=pltpu.VMEM)
    far = pl.BlockSpec(memory_space=pl.ANY)
    wide_shape = (24, width)
    return pl.pallas_call(
        functools.partial(back_mixer_kernel, n, groups, widths, near_all, tiles, outs),
        in_specs=[vmem] * 2 + [far] * (7 + len(weights)),
        out_specs=[vmem] * (4 + len(outs)),
        out_shape=[
            jax.ShapeDtypeStruct((count, width), bf16),
            jax.ShapeDtypeStruct((24, width // groups), f32),
            jax.ShapeDtypeStruct(near.shape[1:], f32),
        ]
        + [jax.ShapeDtypeStruct((width // groups, wide), f32) for _, wide in outs]
        + [jax.ShapeDtypeStruct((col_rows // groups, width), f32)],
        scratch_shapes=Line.scratch(half, width)
        + [
            pltpu.VMEM((half, width), x_own.dtype),
            pltpu.VMEM((half, width), base_own.dtype),
            pltpu.VMEM((half, width), bf16),
            pltpu.VMEM((count, width), bf16),
            pltpu.VMEM(wide_shape, f32),
            pltpu.VMEM((8, width), f32),
            pltpu.VMEM((width, total), bf16),
            pltpu.SemaphoreType.DMA((2 + len(weights),)),
            Line.semaphores(half),
        ]
        + RowGrads.scratch(groups, count, width, total, 2, len(tiles))
        + ColGrad.scratch(groups, count, col_rows, width)
        + SmallSum.scratch(n, groups, wide_shape, near.shape),
        compiler_params=pltpu.CompilerParams(
            collective_id=call, has_side_effects=True, vmem_limit_bytes=61 << 20
        ),
        cost_estimate=pl.CostEstimate(
            flops=12_000_000_000, bytes_accessed=200_000_000, transcendentals=0
        ),
        name="back_mixer",
    )(gain, near, x_own, base_own, left, *parts, *pair, *weights)


def recur_back_kernel(n, groups, dk, dv, beside, *refs):
    (
        lengths_ref, send_row_ref, send_column_ref, slot_row_ref, slot_column_ref,
        d_mixed_ref, out_weight_ref, attended_ref, gate_ref, gain_ref, up_ref, bias_ref, down_ref,
        share_ref, held_far, states_far, hidden_far, active_far, cotangent_far,
        d_rows_ref, d_gate_ref, head_gain_ref, grad_up_ref, grad_bias_ref, layer_ref, grad_down_ref,
        up_in, down_in, d_attended, d_placed, d_state, result,
        held_ref, states_ref, hidden_ref, load_sems, sems,
    ) = refs[:37]
    go = Exchange(groups, *refs[37:40])
    back = Exchange(groups, *refs[40:43])
    cols = ColGrad(groups, active_far, cotangent_far, grad_down_ref, refs[43:]) if beside else None
    count = d_mixed_ref.shape[0]
    slots = slot_row_ref.shape[1]
    end0 = lengths_ref[0, 0]
    end1 = end0 + lengths_ref[0, 1]
    ends = (end0, end1, end1 + lengths_ref[0, 2])

    def finish(total, own, place):
        layer_ref[place, :] = (hidden_ref[own, :] + total).astype(layer_ref.dtype)

    line = Line(n, share_ref, up_in, down_in, layer_ref, sems, finish)
    loads = (
        pltpu.make_async_copy(hidden_far, hidden_ref, load_sems.at[0]),
        pltpu.make_async_copy(held_far, held_ref, load_sems.at[1]),
        pltpu.make_async_copy(states_far, states_ref, load_sems.at[2]),
    )
    barrier = pltpu.get_barrier_semaphore()
    greet_dp(barrier, groups)
    line.greet(barrier, groups - 1)
    line.prime()
    for c in loads:
        c.start()
    if beside:
        cols.start()
    loads[0].wait()

    head_gain_ref[...] = jnp.zeros_like(head_gain_ref)
    tile = count // 2

    @pl.loop(0, 2)
    def _(i):
        rows = pl.ds(pl.multiple_of(i * tile, tile), tile)
        d_gated = dot_t(d_mixed_ref[rows, :], out_weight_ref[...])
        attended = attended_ref[rows, :].astype(f32)
        gate = gate_ref[rows, :]
        scaling = lax.rsqrt(jnp.mean(attended * attended, axis=1, keepdims=True) + head_floor)
        unit = attended * scaling
        sigmoid = jax.nn.sigmoid(gate)
        swish = gate * sigmoid
        gained = d_gated * gain_ref[...]
        d_gate_ref[rows, :] = (
            gained * unit * sigmoid * (1.0 + gate * (1.0 - sigmoid))
        ).astype(bf16)
        d_unit = gained * swish
        d_attended[rows, :] = (
            scaling * (d_unit - unit * jnp.mean(d_unit * unit, axis=1, keepdims=True))
        ).astype(bf16)
        term = d_gated * unit * swish
        piece = term[0:8, :]
        for r in range(1, tile // 8):
            piece = piece + term[8 * r : 8 * r + 8, :]
        head_gain_ref[...] += piece
        line.step(2 * i)
        line.step(2 * i + 1)

    go.send(send_row_ref, 0, d_attended)
    d_state[...] = jnp.zeros_like(d_state)
    grad_up_ref[...] = jnp.zeros_like(grad_up_ref)
    grad_bias_ref[...] = jnp.zeros_like(grad_bias_ref)
    done = 12
    if beside:
        cols.ready()

        @pl.loop(0, cols.items)
        def _(i):
            cols.item(i)
            line.step(4 + 2 * i)
            line.step(5 + 2 * i)

        done = 4 + 2 * cols.items
        cols.send_all()
    else:
        line.run(4, done)
    for c in loads[1:]:
        c.wait()

    go.receive()
    place_rows(slot_row_ref, go.came, d_placed)
    spans = held_ref.shape[0] // SPAN

    @pl.loop(0, spans)
    def _(i):
        step = spans - 1 - i
        d_out = d_placed[pl.ds(pl.multiple_of(step * SPAN, SPAN), SPAN), :]
        span_backward(
            dk, dv, step, ends, d_out, held_ref, states_ref[step], up_ref, bias_ref, down_ref,
            d_state, result, grad_up_ref, grad_bias_ref,
        )
        line.step(done + 2 * i)
        line.step(done + 1 + 2 * i)

    back.send(slot_column_ref, 1, result)
    line.run(done + 2 * spans, line.steps)
    if beside:
        cols.receive()

    back.receive()

    @pl.loop(0, 2)
    def _(i):
        rows = pl.ds(pl.multiple_of(i * tile, tile), tile)
        pick = one_hot(send_column_ref[rows, :], 0, (tile, slots), 1)
        d_rows_ref[rows, :] = dot(pick, back.came[...]).astype(bf16)

    line.drain()
    if beside:
        cols.drain()
    go.drain()
    back.drain()


def recur_back(
    call, n, groups, dk, dv, beside, lengths, send_row, send_column, slot_row, slot_column, d_mixed, out_weight, attended, gate_pre,
    head_gain, up_wide, bias, down_wide, share, held, states, hidden_own, active, cotangent,
):
    count, width = d_mixed.shape
    slots, wide = held.shape
    half = count // 2
    vmem = pl.BlockSpec(memory_space=pltpu.VMEM)
    operands = [
        lengths, send_row, send_column, slot_row, slot_column, d_mixed, out_weight, attended, gate_pre, head_gain, up_wide, bias,
        down_wide, share, held, states, hidden_own, active, cotangent,
    ]
    far = pl.BlockSpec(memory_space=pl.ANY)
    return pl.pallas_call(
        functools.partial(recur_back_kernel, n, groups, dk, dv, beside),
        in_specs=[pl.BlockSpec(memory_space=pltpu.SMEM)] + [vmem] * (len(operands) - 6) + [far] * 5,
        out_specs=[vmem] * 7,
        out_shape=[
            jax.ShapeDtypeStruct((count, wide), bf16),
            jax.ShapeDtypeStruct((count, dv), bf16),
            jax.ShapeDtypeStruct((8, dv), f32),
            jax.ShapeDtypeStruct((dk, LANES), f32),
            jax.ShapeDtypeStruct((8, dk), f32),
            jax.ShapeDtypeStruct((count, width), bf16),
            jax.ShapeDtypeStruct((active.shape[1] // groups if beside else 8, width), f32),
        ],
        scratch_shapes=Line.scratch(half, width)
        + [
            pltpu.VMEM((count, dv), bf16),
            pltpu.VMEM((slots, dv), bf16),
            pltpu.VMEM((dk, dv), f32),
            pltpu.VMEM((slots, wide), bf16),
            pltpu.VMEM(held.shape, bf16),
            pltpu.VMEM(states.shape, bf16),
            pltpu.VMEM((half, width), f32),
            pltpu.SemaphoreType.DMA((3,)),
            Line.semaphores(half),
        ]
        + Exchange.scratch(groups, slots, dv)
        + Exchange.scratch(groups, slots, wide)
        + (ColGrad.scratch(groups, count, active.shape[1], width) if beside else []),
        compiler_params=pltpu.CompilerParams(
            collective_id=call, has_side_effects=True, vmem_limit_bytes=60 << 20
        ),
        cost_estimate=pl.CostEstimate(
            flops=12_000_000_000, bytes_accessed=200_000_000, transcendentals=4_000_000
        ),
        name="recur_back",
    )(*operands)


def small_sum_kernel(groups, n, rows_all, part_ref, out_ref, held, line, line_in, sems, line_sems):
    me = lax.axis_index("dp")
    place = lax.axis_index("tensor")
    barrier = pltpu.get_barrier_semaphore()

    def peer(k):
        return lax.rem(me + k, groups)

    def mate(k):
        return lax.rem(place + k, n)

    @pl.loop(1, groups)
    def _(k):
        pl.semaphore_signal(barrier, inc=1, device_id={"dp": peer(k)}, device_id_type=MESH)

    @pl.loop(1, n)
    def _(k):
        pl.semaphore_signal(barrier, inc=1, device_id={"tensor": mate(k)}, device_id_type=MESH)

    pl.semaphore_wait(barrier, groups + n - 2)

    def copy(k, source):
        return pltpu.make_async_remote_copy(
            part_ref.at[peer(k)], held.at[source], sems.at[0, k], sems.at[1, source],
            device_id={"dp": peer(k)}, device_id_type=MESH,
        )

    def line_copy(k, source):
        return pltpu.make_async_remote_copy(
            line, line_in.at[source], line_sems.at[0, k], line_sems.at[1, source],
            device_id={"tensor": mate(k)}, device_id_type=MESH,
        )

    @pl.loop(1, groups)
    def _(k):
        copy(k, me).start()

    held[pl.ds(me, 1)] = part_ref[pl.ds(me, 1)]

    @pl.loop(1, groups)
    def _(k):
        copy(k, peer(k)).wait_recv()

    total = held[0]
    for i in range(1, groups):
        total = total + held[i]
    line[...] = total[:rows_all]
    out_ref[...] = total

    @pl.loop(1, n)
    def _(k):
        line_copy(k, place).start()

    line_in[pl.ds(place, 1)] = total[None, :rows_all]

    @pl.loop(1, n)
    def _(k):
        line_copy(k, mate(k)).wait_recv()

    total = line_in[0]
    for i in range(1, n):
        total = total + line_in[i]
    out_ref[:rows_all] = total

    @pl.loop(1, groups)
    def _(k):
        copy(k, me).wait_send()

    @pl.loop(1, n)
    def _(k):
        line_copy(k, place).wait_send()


def small_sum(over_all, over_owners, groups, n, call):
    def tiles(blocks):
        short = -blocks.shape[1] % (8 * LANES)
        return jnp.pad(blocks, ((0, 0), (0, short))).reshape(groups, -1, LANES)

    first, second = tiles(over_all), tiles(over_owners)
    rows_all = first.shape[1]
    part = jnp.concatenate([first, second], axis=1)
    vmem = pl.BlockSpec(memory_space=pltpu.VMEM)
    total = pl.pallas_call(
        functools.partial(small_sum_kernel, groups, n, rows_all),
        in_specs=[vmem],
        out_specs=vmem,
        out_shape=jax.ShapeDtypeStruct(part.shape[1:], f32),
        scratch_shapes=[
            pltpu.VMEM(part.shape, f32),
            pltpu.VMEM((rows_all, LANES), f32),
            pltpu.VMEM((n, rows_all, LANES), f32),
            pltpu.SemaphoreType.DMA((2, groups)),
            pltpu.SemaphoreType.DMA((2, n)),
        ],
        compiler_params=pltpu.CompilerParams(collective_id=call, has_side_effects=True),
        name="small_sum",
    )(part)
    return (
        total[:rows_all].reshape(-1)[: over_all.shape[1]],
        total[rows_all:].reshape(-1)[: over_owners.shape[1]],
    )


def per_device(
    tokens,
    cotangent,
    token_slots,
    lengths,
    mixer_gain,
    query_weight,
    key_weight,
    value_weight,
    gate_weight,
    decay_down,
    decay_up,
    decay_bias,
    head_gain,
    out_weight,
    feed_gain,
    feed_gate,
    feed_up,
    feed_down,
):
    groups = lax.axis_size("dp")
    lines = lax.axis_size("tensor")
    member = lax.axis_index("dp")
    place = lax.axis_index("tensor")
    count, width = tokens.shape
    dk = query_weight.shape[1]
    dv = value_weight.shape[1]
    rank = decay_up.shape[1]
    parity = lax.rem(member, 2)
    pairs = [(i, i ^ 1) for i in range(groups)]
    same_parity = [[i for i in range(groups) if i % 2 == b] for b in range(2)]

    half = count // 2
    own_at = jnp.where(place == 0, half, 0)
    tokens_own = lax.dynamic_slice_in_dim(tokens, own_at, half)
    cotangent_own = lax.dynamic_slice_in_dim(cotangent, own_at, half)

    mixer_gain_wide = mixer_gain.astype(f32)
    feed_gain_wide = feed_gain.astype(f32)
    head_gain_wide = head_gain.astype(f32)
    third = LANES // 4
    down_pad = jnp.pad(decay_down, ((0, 0), (0, third - rank)))
    down_none = jnp.zeros_like(down_pad)
    down_all = jnp.concatenate([down_pad, down_pad, down_pad, down_none], axis=1)
    up_pad = jnp.pad(decay_up, ((0, 0), (0, third - rank)))
    up_none = jnp.zeros_like(up_pad)
    up_wide = jnp.concatenate([up_pad, up_pad, up_pad, up_none], axis=1).T
    down_wide = jnp.concatenate([up_pad, up_pad, up_none, up_none], axis=1)
    bias = decay_bias.astype(f32).reshape(1, dk)
    (
        normed, gate_pre, attended, gated, feed_normed, hidden_own, d_active, held, states,
        send_row, send_column, slot_row, slot_column,
    ) = front(
        1, lines, groups, lengths, token_slots.reshape(groups, count), tokens,
        mixer_gain_wide.reshape(1, -1), feed_gain_wide.reshape(1, -1),
        head_gain_wide.reshape(1, -1), up_wide, bias,
        [query_weight, key_weight, value_weight, down_all], gate_weight, out_weight, cotangent,
        feed_down,
    )

    fused = (width // groups) % LANES == 0
    if fused:
        (
            d_mixed, d_hidden_own, feed_gain_part, grad_feed_gate, grad_feed_up, active, layer_share,
        ) = back_feed(
            2, lines, groups, feed_gain_wide.reshape(1, -1), hidden_own, cotangent_own, feed_normed,
            d_active, feed_gate, feed_up, feed_down,
        )
    else:
        gate_hidden = dot(feed_normed, feed_gate)
        up_hidden = dot(feed_normed, feed_up)
        d_active = d_active.astype(f32)
        sigmoid_gate = jax.nn.sigmoid(gate_hidden)
        swish_gate = gate_hidden * sigmoid_gate
        active = (swish_gate * up_hidden).astype(bf16)
        d_gate_hidden = (
            d_active * up_hidden * sigmoid_gate * (1.0 + gate_hidden * (1.0 - sigmoid_gate))
        ).astype(bf16)
        d_up_hidden = (d_active * swish_gate).astype(bf16)
        feed_share = (dot_t(d_gate_hidden, feed_gate) + dot_t(d_up_hidden, feed_up)).astype(bf16)
        d_mixed, d_hidden_own, feed_gain_part = line_sum(
            2, lines, feed_share, hidden_own, cotangent_own, feed_gain_wide.reshape(1, -1)
        )
        layer_share = dot(active, feed_down).astype(bf16)

    d_rows, d_gate_low, head_gain_part, up_part, bias_part, layer_out, grad_feed_down = recur_back(
        4, lines, groups, dk, dv, fused, lengths, send_row, send_column, slot_row, slot_column, d_mixed,
        out_weight, attended, gate_pre, head_gain_wide.reshape(1, -1), up_wide, bias, down_wide, layer_share, held, states,
        hidden_own, active, cotangent,
    )
    down_both = jnp.concatenate([down_pad, down_pad, down_none, down_none], axis=1)
    up_part = up_part[:, :rank] + up_part[:, third : third + rank] + (
        up_part[:, 2 * third : 2 * third + rank]
    )

    def by_owner(vector):
        return vector.reshape(groups, -1)

    per = width // groups
    head_per = dv // groups
    up_per = dk // groups * rank
    if fused:
        near = [
            by_owner(jnp.sum(feed_gain_part, axis=0)),
            jnp.pad(by_owner(jnp.sum(head_gain_part, axis=0)), ((0, 0), (0, -head_per % LANES))),
            by_owner(up_part),
            jnp.pad(by_owner(bias_part[0]), ((0, 0), (0, -(dk // groups) % LANES))),
        ]
        near_all = (per + head_per + LANES - 1) // LANES
        near = jnp.concatenate(near, axis=1)
        near = jnp.pad(near, ((0, 0), (0, -near.shape[1] % (8 * LANES))))
        (
            token_grad, wide_sum, near_sum, grad_query, grad_key, grad_value, grad_gate, grad_out,
        ) = back_mixer(
            3, lines, groups, mixer_gain_wide.reshape(1, -1), near.reshape(groups, -1, LANES),
            near_all, tokens_own, d_hidden_own, normed, [d_rows, d_gate_low],
            [(0, dk), (dk, dk), (2 * dk, dv), (2 * dk + dv + LANES, dv)], (gated, d_mixed),
            [query_weight, key_weight, value_weight, down_both, gate_weight],
        )
        near_sum = near_sum.reshape(-1)
        mixer_sum = jnp.sum(wide_sum[16:], axis=0)
        feed_sum = near_sum[:per]
        head_sum = near_sum[per : per + head_per]
        down_sum = wide_sum[:16].T
        up_sum = near_sum[near_all * LANES : near_all * LANES + up_per]
        bias_sum = near_sum[near_all * LANES + up_per :][: dk // groups]
    else:
        d_query_low = d_rows[:, :dk]
        d_key_low = d_rows[:, dk : 2 * dk]
        d_value_low = d_rows[:, 2 * dk : 2 * dk + dv]
        d_latent_low = d_rows[:, 2 * dk + dv :]
        normed_share = (
            dot_t(d_query_low, query_weight)
            + dot_t(d_key_low, key_weight)
            + dot_t(d_value_low, value_weight)
            + dot_t(d_gate_low, gate_weight)
            + dot_t(d_latent_low, down_both)
        ).astype(bf16)
        token_grad, _, mixer_gain_part = line_sum(
            3, lines, normed_share, tokens_own, d_hidden_own,
            mixer_gain_wide.reshape(1, -1),
        )
        down_part = rows_dot(normed, d_latent_low)
        down_part = down_part[:, :rank] + down_part[:, third : third + rank]
        over_all = jnp.concatenate(
            [
                by_owner(jnp.sum(mixer_gain_part, axis=0)),
                by_owner(jnp.sum(feed_gain_part, axis=0)),
                by_owner(jnp.sum(head_gain_part, axis=0)),
                by_owner(down_part),
            ],
            axis=1,
        )
        over_owners = jnp.concatenate([by_owner(up_part), by_owner(bias_part[0])], axis=1)
        summed, small = small_sum(over_all, over_owners, groups, lines, 5)
        mixer_sum = summed[:per]
        feed_sum = summed[per : 2 * per]
        head_sum = summed[2 * per : 2 * per + head_per]
        down_sum = summed[2 * per + head_per :].reshape(per, rank)
        up_sum = small[:up_per]
        bias_sum = small[up_per:]

    def halves(row_block, dims):
        split = row_block.reshape(row_block.shape[0], groups // 2, 2, dims // groups)
        keep = lax.dynamic_index_in_dim(split, parity, 2, keepdims=False)
        send = lax.dynamic_index_in_dim(split, 1 - parity, 2, keepdims=False)
        got = lax.ppermute(send, "dp", pairs)
        shape = (row_block.shape[0], dims // 2)
        return keep.reshape(shape), got.reshape(shape)

    def partner(row_block):
        return row_block, lax.ppermute(row_block, "dp", pairs)

    def summed_share(left, right):
        share = (rows_dot(left[0], right[0]) + rows_dot(left[1], right[1])).astype(bf16)
        rows = share.shape[0] // (groups // 2)
        blocks = share.reshape(groups // 2, rows, share.shape[1])
        moved = lax.all_to_all(
            blocks, "dp", split_axis=0, concat_axis=0, tiled=True, axis_index_groups=same_parity
        )
        return jnp.sum(moved.astype(f32), axis=0)

    if not fused:
        grad_feed_down = summed_share(halves(active, active.shape[1]), partner(cotangent))
        feed_halves = halves(feed_normed, width)
        normed_halves = halves(normed, width)
        grad_feed_gate = summed_share(feed_halves, partner(d_gate_hidden))
        grad_feed_up = summed_share(feed_halves, partner(d_up_hidden))
        grad_out = summed_share(halves(gated, dv), partner(d_mixed))
        grad_query = summed_share(normed_halves, partner(d_query_low))
        grad_key = summed_share(normed_halves, partner(d_key_low))
        grad_value = summed_share(normed_halves, partner(d_value_low))
        grad_gate = summed_share(normed_halves, partner(d_gate_low))

    return (
        layer_out,
        token_grad,
        mixer_sum,
        grad_query,
        grad_key,
        grad_value,
        grad_gate,
        down_sum,
        up_sum.reshape(1, dk // groups, rank),
        bias_sum.reshape(1, dk // groups),
        head_sum,
        grad_out[None],
        feed_sum,
        grad_feed_gate,
        grad_feed_up,
        grad_feed_down[None],
    )


def solution(mesh):
    placed = (
        P("dp", None),
        P("dp", None),
        P(),
        P("dp", None),
        P(),
        P(None, "tensor"),
        P(None, "tensor"),
        P(None, "tensor"),
        P(None, "tensor"),
        P(),
        P("tensor", None),
        P("tensor"),
        P(),
        P("tensor", None),
        P(),
        P(None, "tensor"),
        P(None, "tensor"),
        P("tensor", None),
    )
    return jax.shard_map(
        per_device,
        mesh=mesh,
        in_specs=placed,
        out_specs=(
            P("dp", None),
            P("dp", None),
            P("dp"),
            P("dp", "tensor"),
            P("dp", "tensor"),
            P("dp", "tensor"),
            P("dp", "tensor"),
            P("dp", None),
            P("tensor", "dp", None),
            P("tensor", "dp"),
            P("dp"),
            P("tensor", "dp", None),
            P("dp"),
            P("dp", "tensor"),
            P("dp", "tensor"),
            P("tensor", "dp", None),
        ),
        check_vma=False,
    )
```

```python
import functools

import jax
import jax.numpy as jnp
from jax import lax
from jax.experimental import pallas as pl
from jax.experimental.pallas import tpu as pltpu
from jax.sharding import PartitionSpec as P

OWN_CAP = 1024
SPAN = 128
LANES = 128
epsilon = 1e-06
head_floor = 1.0

f32 = jnp.float32
bf16 = jnp.bfloat16
MESH = pl.DeviceIdType.MESH


def rows_dot(left, right):
    return lax.dot_general(left, right, (((0,), (0,)), ((), ())), preferred_element_type=f32)


def dot_t(left, right):
    return lax.dot_general(left, right, (((1,), (1,)), ((), ())), preferred_element_type=f32)


def dot(left, right):
    return jnp.dot(left, right, preferred_element_type=f32)


def span_terms(first, ends, logits):
    rows = logits.shape[0]

    def label(position):
        count = jnp.zeros_like(position)
        for end in ends:
            count = count + (position >= end).astype(jnp.int32)
        return count

    log_decay = jax.nn.log_sigmoid(logits) * (1.0 / 16.0)
    row = lax.broadcasted_iota(jnp.int32, (rows, rows), 0)
    column = lax.broadcasted_iota(jnp.int32, (rows, rows), 1)
    lower = (row >= column).astype(f32)
    cumulative = jnp.dot(
        lower, log_decay, precision=lax.Precision.HIGHEST, preferred_element_type=f32
    )
    total = cumulative[rows - 1 :, :]
    middle = cumulative[rows // 2 - 1 : rows // 2, :]
    label_column = label(first + lax.broadcasted_iota(jnp.int32, (rows, 1), 0))
    label_row = label(first + lax.broadcasted_iota(jnp.int32, (1, rows), 1))
    before = jnp.where(first > 0, label(first - 1), -1)
    last = label(first + rows - 1)
    carried = (label_column == before).astype(f32)
    tail = (label_column == last).astype(f32)
    keep = (before == last).astype(f32)
    allowed = (row >= column) & (label_column == label_row)
    return log_decay, cumulative, total, middle, carried, tail, keep, allowed


def span_forward(dk, dv, step, ends, held_ref, up_ref, bias_ref, state, states_ref, result):
    first = step * SPAN
    at = pl.ds(pl.multiple_of(first, SPAN), SPAN)
    queries = held_ref[at, :dk].astype(f32) * (float(dk) ** -0.5)
    keys = held_ref[at, dk : 2 * dk].astype(f32)
    values = held_ref[at, 2 * dk : 2 * dk + dv]
    logits = dot(held_ref[at, 2 * dk + dv :], up_ref[...]) + bias_ref[...]
    _, cumulative, total, middle, carried, tail, keep, allowed = span_terms(first, ends, logits)
    query_mid = (queries * jnp.exp(cumulative - middle)).astype(bf16)
    key_mid = (keys * jnp.exp(middle - cumulative)).astype(bf16)
    query_start = (queries * jnp.exp(cumulative) * carried).astype(bf16)
    key_end = (keys * jnp.exp(total - cumulative) * tail).astype(bf16)
    scores = jnp.where(allowed, dot_t(query_mid, key_mid), 0.0).astype(bf16)
    entering = state[...]
    entering_low = entering.astype(bf16)
    states_ref[step] = entering_low
    attended = dot(scores, values) + dot(query_start, entering_low)
    result[at, :] = attended.astype(bf16)
    decay_column = jnp.transpose(jnp.broadcast_to(keep * jnp.exp(total), (8, dk)))[:, :1]
    state[...] = decay_column * entering + rows_dot(key_end, values)


def span_backward(
    dk, dv, step, ends, d_out, held_ref, entering, up_ref, bias_ref, down_ref, d_state, result,
    grad_up_ref, grad_bias_ref,
):
    first = step * SPAN
    at = pl.ds(pl.multiple_of(first, SPAN), SPAN)
    scale = float(dk) ** -0.5
    queries = held_ref[at, :dk].astype(f32) * scale
    keys = held_ref[at, dk : 2 * dk].astype(f32)
    values = held_ref[at, 2 * dk : 2 * dk + dv]
    latent = held_ref[at, 2 * dk + dv :]
    logits = dot(latent, up_ref[...]) + bias_ref[...]
    _, cumulative, total, middle, carried, tail, keep, allowed = span_terms(first, ends, logits)
    grow_query = jnp.exp(cumulative - middle)
    grow_key = jnp.exp(middle - cumulative)
    start_decay = jnp.exp(cumulative) * carried
    end_decay = jnp.exp(total - cumulative) * tail
    query_mid = (queries * grow_query).astype(bf16)
    key_mid = (keys * grow_key).astype(bf16)
    query_start = (queries * start_decay).astype(bf16)
    key_end = (keys * end_decay).astype(bf16)
    scores = jnp.where(allowed, dot_t(query_mid, key_mid), 0.0).astype(bf16)
    d_scores = jnp.where(allowed, dot_t(d_out, values), 0.0).astype(bf16)
    leaving = d_state[...]
    leaving_low = leaving.astype(bf16)
    d_values = rows_dot(scores, d_out) + dot(key_end, leaving_low)
    d_queries = dot(d_scores, key_mid) * grow_query + dot_t(d_out, entering) * start_decay
    d_key_end = dot_t(values, leaving_low) * end_decay
    d_keys = rows_dot(d_scores, query_mid) * grow_key + d_key_end
    kept = keep * jnp.exp(total)
    state_pair = jnp.sum(entering.astype(f32) * leaving, axis=1, keepdims=True)
    state_row = jnp.transpose(jnp.broadcast_to(state_pair, (dk, LANES)))[:1, :]
    d_total = jnp.sum(keys * d_key_end, axis=0, keepdims=True) + kept * state_row
    d_cumulative = queries * d_queries - keys * d_keys
    row = lax.broadcasted_iota(jnp.int32, (SPAN, SPAN), 0)
    column = lax.broadcasted_iota(jnp.int32, (SPAN, SPAN), 1)
    upper = (row <= column).astype(f32)
    d_log_decay = (
        jnp.dot(upper, d_cumulative, precision=lax.Precision.HIGHEST, preferred_element_type=f32)
        + d_total
    )
    d_logits = d_log_decay * (1.0 / 16.0) * jax.nn.sigmoid(-logits)
    grad_bias_ref[...] += jnp.broadcast_to(jnp.sum(d_logits, axis=0, keepdims=True), (8, dk))
    d_logits_high = d_logits.astype(bf16)
    d_logits_low = (d_logits - d_logits_high.astype(f32)).astype(bf16)
    grad_up_ref[...] += rows_dot(d_logits_high, latent) + rows_dot(d_logits_low, latent)
    d_latent = dot_t(d_logits_high, down_ref[...]) + dot_t(d_logits_low, down_ref[...])
    high = d_latent.astype(bf16).astype(f32)
    lane = lax.broadcasted_iota(jnp.int32, d_latent.shape, 1)
    d_latent_packed = jnp.where(lane < LANES // 4, high, d_latent - high)
    result[at, :dk] = (d_queries * scale).astype(bf16)
    result[at, dk : 2 * dk] = d_keys.astype(bf16)
    result[at, 2 * dk : 2 * dk + dv] = d_values.astype(bf16)
    result[at, 2 * dk + dv :] = d_latent_packed.astype(bf16)
    kept_column = jnp.transpose(jnp.broadcast_to(kept, (8, dk)))[:, :1]
    d_state[...] = kept_column * leaving + rows_dot(query_start, d_out)


FINE = 16
SKEW = 2


class Line:
    def __init__(self, n, share_ref, up_in, down_in, out_ref, sems, finish):
        self.n, self.me = n, lax.axis_index("tensor")
        self.share, self.up_in, self.down_in, self.out = share_ref, up_in, down_in, out_ref
        self.sems, self.finish = sems, finish
        self.half = up_in.shape[0]
        self.count = self.half // FINE
        self.second = self.count + 2
        self.steps = self.second + self.count + SKEW * (n - 2)

    @staticmethod
    def scratch(half, width):
        return [pltpu.VMEM((half, width), bf16), pltpu.VMEM((half, width), bf16)]

    @staticmethod
    def semaphores(half):
        return pltpu.SemaphoreType.DMA((8, half // FINE))

    def own_half(self):
        return pl.ds(pl.multiple_of(jnp.where(self.me == 0, self.half, 0), self.half), self.half)

    def greet(self, barrier, others):
        n, me = self.n, self.me

        @pl.when(me > 0)
        def _():
            pl.semaphore_signal(barrier, inc=1, device_id={"tensor": me - 1}, device_id_type=MESH)

        @pl.when(me < n - 1)
        def _():
            pl.semaphore_signal(barrier, inc=1, device_id={"tensor": me + 1}, device_id_type=MESH)

        inside = (me > 0) & (me < n - 1)

        @pl.when(inside)
        def _():
            pl.semaphore_wait(barrier, others + 2)

        @pl.when(jnp.logical_not(inside))
        def _():
            pl.semaphore_wait(barrier, others + 1)

    def greet_all(self, barrier, others):
        n, me = self.n, self.me

        @pl.when(me > 0)
        def _():
            pl.semaphore_signal(barrier, inc=1, device_id={"tensor": me - 1}, device_id_type=MESH)

        @pl.when(me < n - 1)
        def _():
            pl.semaphore_signal(barrier, inc=1, device_id={"tensor": me + 1}, device_id_type=MESH)

        pl.semaphore_wait(barrier, others + n - 1)

    def at(self, g):
        return pl.ds(pl.multiple_of(g * FINE, FINE), FINE)

    def low(self, g):
        return pl.ds(pl.multiple_of(self.half + g * FINE, FINE), FINE)

    def right(self, source, target, lane, g):
        return pltpu.make_async_remote_copy(
            source, target, self.sems.at[2 * lane, g], self.sems.at[2 * lane + 1, g],
            device_id={"tensor": jnp.minimum(self.me + 1, self.n - 1)}, device_id_type=MESH,
        )

    def left(self, source, target, lane, g):
        return pltpu.make_async_remote_copy(
            source, target, self.sems.at[2 * lane, g], self.sems.at[2 * lane + 1, g],
            device_id={"tensor": jnp.maximum(self.me - 1, 0)}, device_id_type=MESH,
        )

    def up_copy(self, g):
        rows = self.up_in.at[self.at(g), :]
        return self.right(rows, rows, 0, g)

    def down_copy(self, g):
        rows = self.down_in.at[self.at(g), :]
        return self.left(rows, rows, 1, g)

    def up_back_copy(self, g):
        rows = self.out.at[self.at(g), :]
        return self.left(rows, rows, 2, g)

    def down_back_copy(self, g):
        rows = self.out.at[self.low(g), :]
        return self.right(rows, rows, 3, g)

    def prime(self, top=True, bottom=True):
        @pl.when((self.me == 0) & top)
        def _():
            @pl.loop(0, self.count)
            def _(g):
                self.right(
                    self.share.at[self.at(g), :], self.up_in.at[self.at(g), :], 0, g
                ).start()

        @pl.when((self.me == self.n - 1) & bottom)
        def _():
            @pl.loop(0, self.count)
            def _(g):
                self.left(
                    self.share.at[self.low(g), :], self.down_in.at[self.at(g), :], 1, g
                ).start()

    def step(self, step):
        n, me, count = self.n, self.me, self.count
        at, low = self.at, self.low
        g_up = step - SKEW * (me - 1)

        @pl.when((me > 0) & (g_up >= 0) & (g_up < count))
        def _():
            self.up_copy(g_up).wait_recv()
            total = self.up_in[at(g_up), :].astype(f32) + self.share[at(g_up), :].astype(f32)

            @pl.when(me < n - 1)
            def _():
                self.up_in[at(g_up), :] = total.astype(bf16)
                self.up_copy(g_up).start()

            @pl.when(me == n - 1)
            def _():
                self.finish(total, at(g_up), at(g_up))
                self.up_back_copy(g_up).start()

        g_down = step - SKEW * (n - 2 - me)

        @pl.when((me < n - 1) & (g_down >= 0) & (g_down < count))
        def _():
            self.down_copy(g_down).wait_recv()
            total = self.down_in[at(g_down), :].astype(f32) + (
                self.share[low(g_down), :].astype(f32)
            )

            @pl.when(me > 0)
            def _():
                self.down_in[at(g_down), :] = total.astype(bf16)
                self.down_copy(g_down).start()

            @pl.when(me == 0)
            def _():
                self.finish(total, at(g_down), low(g_down))
                self.down_back_copy(g_down).start()

        g_up_back = step - self.second - SKEW * (n - 2 - me)

        @pl.when((me < n - 1) & (g_up_back >= 0) & (g_up_back < count))
        def _():
            self.up_back_copy(g_up_back).wait_recv()

            @pl.when(me > 0)
            def _():
                self.up_back_copy(g_up_back).start()

        g_down_back = step - self.second - SKEW * (me - 1)

        @pl.when((me > 0) & (g_down_back >= 0) & (g_down_back < count))
        def _():
            self.down_back_copy(g_down_back).wait_recv()

            @pl.when(me < n - 1)
            def _():
                self.down_back_copy(g_down_back).start()

    def run(self, first, last):
        @pl.loop(first, last)
        def _(step):
            self.step(step)

    def drain(self):
        n, me = self.n, self.me

        @pl.loop(0, self.count)
        def _(g):
            @pl.when(me < n - 1)
            def _():
                self.up_copy(g).wait_send()
                self.down_back_copy(g).wait_send()

            @pl.when(me > 0)
            def _():
                self.down_copy(g).wait_send()
                self.up_back_copy(g).wait_send()


def norm_back(x_ref, base_ref, gain, out_ref, kept_ref, gain_grad_ref):
    gain_grad_ref[...] = jnp.zeros_like(gain_grad_ref)

    def finish(total, own, place):
        rows = x_ref[own, :].astype(f32)
        scaling = lax.rsqrt(jnp.mean(rows * rows, axis=1, keepdims=True) + epsilon)
        unit = rows * scaling
        gained = gain() * total
        grad = base_ref[own, :].astype(f32) + scaling * (
            gained - unit * jnp.mean(gained * unit, axis=1, keepdims=True)
        )
        if kept_ref is not None:
            kept_ref[own, :] = grad
        out_ref[place, :] = grad.astype(out_ref.dtype)
        term = total * unit
        part = term[0:8, :]
        for i in range(1, FINE // 8):
            part = part + term[8 * i : 8 * i + 8, :]
        gain_grad_ref[...] += part

    return finish


def line_kernel(n, *refs):
    share_ref, x_ref, base_ref, gain_ref, out_ref, kept_ref, gain_grad_ref = refs[:7]
    up_in, down_in, sems = refs[7:]
    finish = norm_back(x_ref, base_ref, lambda: gain_ref[...], out_ref, kept_ref, gain_grad_ref)
    line = Line(n, share_ref, up_in, down_in, out_ref, sems, finish)
    line.greet(pltpu.get_barrier_semaphore(), 0)
    line.prime()
    line.run(0, line.steps)
    line.drain()


def line_sum(call, n, share, x_own, base_own, gain):
    rows, width = share.shape
    half = rows // 2
    vmem = pl.BlockSpec(memory_space=pltpu.VMEM)
    return pl.pallas_call(
        functools.partial(line_kernel, n),
        in_specs=[vmem] * 4,
        out_specs=[vmem] * 3,
        out_shape=[
            jax.ShapeDtypeStruct((rows, width), bf16),
            jax.ShapeDtypeStruct((half, width), f32),
            jax.ShapeDtypeStruct((8, width), f32),
        ],
        scratch_shapes=Line.scratch(half, width) + [Line.semaphores(half)],
        compiler_params=pltpu.CompilerParams(
            collective_id=call, has_side_effects=True, vmem_limit_bytes=40 << 20
        ),
        name="line_back",
    )(share, x_own, base_own, gain)


def partner_of(index):
    return index + 1 - 2 * lax.rem(index, 2)


def to_dp(source, target, send, recv, device):
    return pltpu.make_async_remote_copy(
        source, target, send, recv, device_id={"dp": device}, device_id_type=MESH
    )


def greet_dp(barrier, groups):
    member = lax.axis_index("dp")

    @pl.loop(1, groups)
    def _(k):
        pl.semaphore_signal(
            barrier, inc=1, device_id={"dp": lax.rem(member + k, groups)}, device_id_type=MESH
        )


class ColGrad:
    TILE = 256

    def __init__(self, groups, left, right, first, recv, refs):
        (
            self.left, self.right, self.left_in, self.right_in, self.send,
            self.load_sems, self.pair_sems, self.sems,
        ) = refs
        self.left_far, self.right_far, self.recv, self.groups = left, right, recv, groups
        self.member = lax.axis_index("dp")
        self.parity = lax.rem(self.member, 2)
        self.half = right.shape[1] // 2
        self.first, self.wide = first, self.right_in.shape[1]
        self.size = self.send.shape[0] // groups
        self.items = self.wide // self.TILE

    @staticmethod
    def scratch(groups, count, rows, wide):
        return [
            pltpu.VMEM((count, rows), bf16),
            pltpu.VMEM((count, wide), bf16),
            pltpu.VMEM((count, rows), bf16),
            pltpu.VMEM((count, wide), bf16),
            pltpu.VMEM((rows, wide), bf16),
            pltpu.SemaphoreType.DMA((3,)),
            pltpu.SemaphoreType.DMA((2, 2)),
            pltpu.SemaphoreType.DMA((2, groups)),
        ]

    def halves(self, parity):
        start = pl.multiple_of(parity * self.half + self.first, self.TILE)
        return self.right_far.at[:, pl.ds(start, self.wide)]

    def loads(self):
        return (
            pltpu.make_async_copy(self.left_far, self.left, self.load_sems.at[0]),
            pltpu.make_async_copy(self.halves(self.parity), self.right, self.load_sems.at[1]),
        )

    def pair_copies(self):
        partner = partner_of(self.member)
        sems = self.pair_sems
        return (
            to_dp(self.left_far, self.left_in, sems.at[0, 0], sems.at[1, 0], partner),
            to_dp(
                self.halves(1 - self.parity), self.right_in, sems.at[0, 1], sems.at[1, 1], partner
            ),
        )

    def start(self):
        for c in self.pair_copies() + self.loads():
            c.start()

    def ready(self):
        for c in self.loads():
            c.wait()
        for c in self.pair_copies():
            c.wait_recv()

    def item(self, t):
        span = pl.ds(pl.multiple_of(t * self.TILE, self.TILE), self.TILE)
        product = rows_dot(self.left[...], self.right[:, span]) + rows_dot(
            self.left_in[...], self.right_in[:, span]
        )
        self.send[:, span] = product.astype(bf16)

    def copy(self, to, source):
        rows = pl.ds(pl.multiple_of(to * self.size, 16), self.size)
        return to_dp(
            self.send.at[rows, :], self.recv.at[source], self.sems.at[0, to],
            self.sems.at[1, source], to,
        )

    def send_all(self):
        @pl.loop(1, self.groups)
        def _(k):
            self.copy(lax.rem(self.member + k, self.groups), self.member).start()

        self.keep().start()

    def keep(self):
        own = pl.ds(pl.multiple_of(self.member * self.size, 16), self.size)
        return pltpu.make_async_copy(
            self.send.at[own, :], self.recv.at[self.member], self.load_sems.at[2]
        )

    def receive(self):
        self.keep().wait()

        @pl.loop(1, self.groups)
        def _(k):
            self.copy(0, lax.rem(self.member + k, self.groups)).wait_recv()

    def drain(self):
        for c in self.pair_copies():
            c.wait_send()

        @pl.loop(1, self.groups)
        def _(k):
            self.copy(lax.rem(self.member + k, self.groups), self.member).wait_send()


class RowGrads:
    def __init__(self, groups, left, tiles, recv, refs):
        (
            self.left, self.all, self.left_in, self.all_in, self.send,
            self.load_sems, self.left_sems, self.piece_sems, self.sems, self.keep_sems,
        ) = refs
        self.left_far, self.tiles, self.recv = left, tiles, recv
        self.member = lax.axis_index("dp")
        self.parity = lax.rem(self.member, 2)
        self.mine = self.member // 2
        self.team = groups // 2
        self.block = left.shape[1] // groups
        self.items = self.team * len(tiles)

    @staticmethod
    def scratch(groups, count, width, total, pieces, tiles):
        team = groups // 2
        return [
            pltpu.VMEM((count, width), bf16),
            pltpu.VMEM((count, total), bf16),
            pltpu.VMEM((count, width // 2), bf16),
            pltpu.VMEM((count, total), bf16),
            pltpu.VMEM((team, width // groups, total), bf16),
            pltpu.SemaphoreType.DMA((1 + pieces,)),
            pltpu.SemaphoreType.DMA((2, team)),
            pltpu.SemaphoreType.DMA((2, pieces)),
            pltpu.SemaphoreType.DMA((2, tiles, team)),
            pltpu.SemaphoreType.DMA((tiles,)),
        ]

    def columns(self, j):
        return pl.ds(pl.multiple_of(j * self.block, self.block), self.block)

    def left_load(self):
        return pltpu.make_async_copy(self.left_far, self.left, self.load_sems.at[0])

    def piece_load(self, p, source, span):
        return pltpu.make_async_copy(source, self.all.at[:, span], self.load_sems.at[1 + p])

    def left_copy(self, q):
        return to_dp(
            self.left_far.at[:, self.columns(2 * q + 1 - self.parity)],
            self.left_in.at[:, self.columns(q)],
            self.left_sems.at[0, q], self.left_sems.at[1, q], partner_of(self.member),
        )

    def piece_copy(self, p, source, span):
        return to_dp(
            source, self.all_in.at[:, span], self.piece_sems.at[0, p], self.piece_sems.at[1, p],
            partner_of(self.member),
        )

    def start_left(self):
        @pl.loop(0, self.team)
        def _(q):
            self.left_copy(q).start()

        self.left_load().start()

    def ready_left(self):
        self.left_load().wait()

        @pl.loop(0, self.team)
        def _(q):
            self.left_copy(q).wait_recv()

    def copy(self, t, to, source):
        start, wide = self.tiles[t]
        span = pl.ds(start, wide)
        return to_dp(
            self.send.at[to, :, span], self.recv.at[source, :, span],
            self.sems.at[0, t, to], self.sems.at[1, t, source], 2 * to + self.parity,
        )

    def item(self, w):
        count = len(self.tiles)
        k = w // count
        to = lax.rem(self.mine + 1 + k, self.team)
        for t in range(count):
            start, wide = self.tiles[t]

            @pl.when((w >= 0) & (w < self.items) & (lax.rem(w, count) == t))
            def _():
                span = pl.ds(start, wide)
                product = rows_dot(
                    self.left[:, self.columns(2 * to + self.parity)], self.all[:, span]
                ) + rows_dot(self.left_in[:, self.columns(to)], self.all_in[:, span])
                self.send[to, :, span] = product.astype(bf16)

                @pl.when(k < self.team - 1)
                def _():
                    self.copy(t, to, self.mine).start()

                @pl.when(k == self.team - 1)
                def _():
                    self.keep(t).start()

    def keep(self, t):
        start, wide = self.tiles[t]
        span = pl.ds(start, wide)
        return pltpu.make_async_copy(
            self.send.at[self.mine, :, span], self.recv.at[self.mine, :, span], self.keep_sems.at[t]
        )

    def receive(self):
        for t in range(len(self.tiles)):
            self.keep(t).wait()

            @pl.loop(1, self.team)
            def _(k):
                self.copy(t, 0, lax.rem(self.mine + k, self.team)).wait_recv()

    def drain(self):
        @pl.loop(0, self.team)
        def _(q):
            self.left_copy(q).wait_send()

        for t in range(len(self.tiles)):
            @pl.loop(1, self.team)
            def _(k):
                self.copy(t, lax.rem(self.mine + k, self.team), self.mine).wait_send()


def splitter(refs):
    refs = list(refs)

    def take(k):
        out = refs[:k]
        del refs[:k]
        return out

    return take


def one_hot(index, base, shape, dim):
    return (index == base + lax.broadcasted_iota(jnp.int32, shape, dim)).astype(f32).astype(bf16)


def thirds(source, terms, target):
    third = LANES // 4
    size = source.shape[0]
    target[...] = jnp.zeros_like(target)
    for i in range(terms):
        target[i * third : i * third + size, :] = source[...]


class Exchange:
    def __init__(self, groups, cuts, sent, came, sems):
        self.groups, self.sent, self.came, self.sems = groups, sent, came, sems
        self.spans = [pl.ds(a, b - a) for a, b in zip((0,) + cuts, cuts + (sent.shape[1],))]
        self.member = lax.axis_index("dp")
        self.cap = sent.shape[0] // groups

    @staticmethod
    def scratch(groups, slots, width, pieces):
        return [
            pltpu.VMEM((slots, width), bf16),
            pltpu.VMEM((slots, width), bf16),
            pltpu.SemaphoreType.DMA((2, pieces, groups)),
        ]

    def part(self, j):
        return pl.ds(pl.multiple_of(j * self.cap, self.cap), self.cap)

    def copy(self, p, to, source):
        span = self.spans[p]
        return to_dp(
            self.sent.at[self.part(to), span], self.came.at[self.part(source), span],
            self.sems.at[0, p, to], self.sems.at[1, p, source], to,
        )

    def send(self, p, index_ref, dim, source):
        span = self.spans[p]
        groups, count = self.groups, source.shape[0]
        rows = self.sent.shape[0] // 2

        @pl.loop(0, 2)
        def _(h):
            at = pl.ds(pl.multiple_of(h * rows, rows), rows)
            if dim == 0:
                pick = one_hot(index_ref[...], h * rows, (rows, count), 0)
            else:
                pick = one_hot(index_ref[at, :], 0, (rows, count), 1)
            self.sent[at, span] = dot(pick, source[:, span]).astype(bf16)

            @pl.loop(0, groups // 2)
            def _(k):
                to = h * (groups // 2) + lax.rem(self.member + k, groups // 2)

                @pl.when(to != self.member)
                def _():
                    self.copy(p, to, self.member).start()

        own = self.part(self.member)
        self.came[own, span] = self.sent[own, span]

    def receive(self, p):
        @pl.loop(1, self.groups)
        def _(k):
            self.copy(p, 0, lax.rem(self.member + k, self.groups)).wait_recv()

    def drain(self):
        for p in range(len(self.spans)):
            @pl.loop(1, self.groups)
            def _(k):
                self.copy(p, lax.rem(self.member + k, self.groups), self.member).wait_send()


def place_rows(slot_row_ref, came, held, span):
    positions, slots = held.shape[0], came.shape[0]
    rows = positions // 2

    @pl.loop(0, 2)
    def _(h):
        at = pl.ds(pl.multiple_of(h * rows, rows), rows)
        pick = one_hot(slot_row_ref[...], h * rows, (rows, slots), 0)
        held[at, span] = dot(pick, came[:, span]).astype(bf16)


def front_kernel(n, groups, dk, dv, *refs):
    take = splitter(refs)
    lengths_ref, slots_ref, tokens_ref, gains_ref, up_rows_ref, down_rows_ref = take(6)
    weights_far = take(3)
    gate_far, out_far, cotangent_far, down_far = take(4)
    spilled = take(6)
    feed_ref, hidden_ref, d_active_ref = take(3)
    send_row_ref, send_column_ref, slot_row_ref, slot_column_ref = take(4)
    normed_ref, gate_ref, attended_ref, gated_ref, held_ref, states_ref = kept = take(6)
    up_in, down_in, weight_ref, gate_weight_ref, out_weight_ref, cotangent_ref, down_ref = take(7)
    rows_out, share_ref, state, result, rank_ref, up_ref, bias_ref, latent_ref = take(8)
    load_sems, sems = take(2)
    go = Exchange(groups, (2 * dk,), *take(3))
    back = Exchange(groups, (), *take(3))
    (spill_sems,) = take(1)
    member = lax.axis_index("dp")
    count, width = tokens_ref.shape
    cap = OWN_CAP // groups
    half = count // 2
    spills = [
        pltpu.make_async_copy(kept[i], spilled[i], spill_sems.at[i]) for i in range(6)
    ]

    def spill(*which):
        for i in which:
            spills[i].start()

    end0 = lengths_ref[0, 0]
    end1 = end0 + lengths_ref[0, 1]
    ends = (end0, end1, end1 + lengths_ref[0, 2])
    third = LANES // 4

    def finish(total, own, place):
        hidden = tokens_ref[place, :].astype(f32) + total
        hidden_ref[own, :] = hidden
        scaling = lax.rsqrt(jnp.mean(hidden * hidden, axis=1, keepdims=True) + epsilon)
        feed_ref[place, :] = (hidden * scaling * gains_ref[1:2, :]).astype(bf16)

    line = Line(n, share_ref, up_in, down_in, feed_ref, sems, finish)
    loads = []
    offset = 0
    for i, far in enumerate(weights_far):
        wide = far.shape[1]
        loads.append(
            pltpu.make_async_copy(far, weight_ref.at[:, pl.ds(offset, wide)], load_sems.at[i])
        )
        offset += wide
    later = [
        pltpu.make_async_copy(gate_far, gate_weight_ref, load_sems.at[4]),
        pltpu.make_async_copy(out_far, out_weight_ref, load_sems.at[5]),
    ]
    latest = [
        pltpu.make_async_copy(cotangent_far, cotangent_ref, load_sems.at[6]),
        pltpu.make_async_copy(down_far, down_ref, load_sems.at[7]),
    ]
    for c in loads + later + latest:
        c.start()
    barrier = pltpu.get_barrier_semaphore()
    greet_dp(barrier, groups)
    line.greet(barrier, groups - 1)

    owners = slots_ref[...] // OWN_CAP
    mine = owners == member
    my_slots = slots_ref[pl.ds(member, 1), :]
    my_owner = my_slots // OWN_CAP
    device = lax.broadcasted_iota(jnp.int32, (groups, count), 0)
    chosen = (my_owner == device).astype(f32)
    before = (
        lax.broadcasted_iota(jnp.int32, (count, count), 0)
        < lax.broadcasted_iota(jnp.int32, (count, count), 1)
    ).astype(f32).astype(bf16)
    send_rank = jnp.sum(chosen * dot(chosen.astype(bf16), before), axis=0, keepdims=True)
    send_row = my_owner * cap + send_rank.astype(jnp.int32)
    send_row_ref[...] = send_row
    send_column_ref[...] = jnp.transpose(
        jnp.broadcast_to(send_row.astype(f32), (8, count))
    )[:, :1].astype(jnp.int32)
    rank_ref[...] = jnp.where(mine, dot(mine.astype(f32).astype(bf16), before), -1.0)

    bias_ref[...] = gains_ref[2:3, dv : dv + dk]
    thirds(up_rows_ref, 3, up_ref)
    thirds(down_rows_ref, 3, latent_ref)

    tile = count // 5

    @pl.loop(0, 5)
    def _(i):
        at = pl.ds(pl.multiple_of(i * tile, tile), tile)
        rows = tokens_ref[at, :].astype(f32)
        scaling = lax.rsqrt(jnp.mean(rows * rows, axis=1, keepdims=True) + epsilon)
        normed_ref[at, :] = (rows * scaling * gains_ref[0:1, :]).astype(bf16)

    for c in loads[:2]:
        c.wait()
    body = 2 * dk + dv

    spill(0)

    def project(first, last):
        @pl.loop(first // 256, last // 256)
        def _(i):
            to = pl.ds(pl.multiple_of(i * 256, 256), 256)
            rows_out[:, to] = dot(normed_ref[...], weight_ref[:, to]).astype(bf16)

    project(0, 2 * dk)
    go.send(0, send_row_ref, 0, rows_out)
    for c in loads[2:]:
        c.wait()
    project(2 * dk, body)
    latent = dot_t(normed_ref[...], latent_ref[...])
    high = latent.astype(bf16).astype(f32)
    middle = (latent - high).astype(bf16).astype(f32)
    lane = lax.broadcasted_iota(jnp.int32, latent.shape, 1)
    rows_out[:, body:] = jnp.where(
        lane < third, high, jnp.where(lane < 2 * third, middle, latent - high - middle)
    ).astype(bf16)
    go.send(1, send_row_ref, 0, rows_out)

    for c in later:
        c.wait()

    @pl.loop(0, dv // 256)
    def _(i):
        to = pl.ds(pl.multiple_of(i * 256, 256), 256)
        gate_ref[:, to] = dot(normed_ref[...], gate_weight_ref[:, to])

    spill(1)

    @pl.loop(0, groups)
    def _(j):
        rank = rank_ref[pl.ds(j, 1), :]
        local = (lax.rem(slots_ref[pl.ds(j, 1), :], OWN_CAP) - OWN_CAP).astype(f32)
        wanted = lax.broadcasted_iota(jnp.int32, (cap, count), 0).astype(f32)
        at = jnp.sum(jnp.where(rank == wanted, local, 0.0), axis=1, keepdims=True)
        slot_column_ref[go.part(j), :] = at.astype(jnp.int32) + OWN_CAP

    slots = slot_row_ref.shape[1]
    slot_row_ref[...] = jnp.transpose(
        jnp.broadcast_to(slot_column_ref[...].astype(f32), (slots, LANES))
    )[:1, :].astype(jnp.int32)
    state[...] = jnp.zeros_like(state)
    for p in range(2):
        go.receive(p)
        place_rows(slot_row_ref, go.came, held_ref, go.spans[p])

    @pl.loop(0, held_ref.shape[0] // SPAN)
    def _(step):
        span_forward(dk, dv, step, ends, held_ref, up_ref, bias_ref, state, states_ref, result)

    back.send(0, slot_column_ref, 1, result)
    spill(4, 5)
    back.receive(0)

    def head_rows(at):
        pick = one_hot(send_column_ref[at, :], 0, (half, slots), 1)
        attended = dot(pick, back.came[...])
        attended_ref[at, :] = attended.astype(bf16)
        gate = gate_ref[at, :]
        scaling = lax.rsqrt(jnp.mean(attended * attended, axis=1, keepdims=True) + head_floor)
        gated = attended * scaling * gains_ref[2:3, :dv] * (gate * jax.nn.sigmoid(gate))
        gated_ref[at, :] = gated.astype(bf16)

        @pl.loop(0, width // 512)
        def _(i):
            to = pl.ds(pl.multiple_of(i * 512, 512), 512)
            share_ref[at, to] = dot(gated_ref[at, :], out_weight_ref[:, to]).astype(bf16)

    last = line.me == n - 1

    @pl.loop(0, 2)
    def _(i):
        bottom = jnp.where(last, 1 - i, i)
        head_rows(pl.ds(pl.multiple_of(bottom * half, half), half))
        line.prime(i == 0, i == 0)

    spill(2, 3)
    wide = d_active_ref.shape[1]
    full, rest = wide // 256, wide % 256

    def hidden_units(i, size):
        at = pl.ds(pl.multiple_of(i * 256, 256), size)
        d_active_ref[:, at] = dot_t(cotangent_ref[...], down_ref[at, :]).astype(bf16)

    for c in latest:
        c.wait()

    @pl.loop(0, line.steps)
    def _(step):
        line.step(step)
        i = step // 2 - 2

        @pl.when((lax.rem(step, 2) == 0) & (i >= 0) & (i < full))
        def _():
            hidden_units(i, 256)

        if rest:
            @pl.when(step == 2 * full + 4)
            def _():
                hidden_units(full, rest)

    line.drain()
    go.drain()
    back.drain()
    for c in spills:
        c.wait()


def front(
    call, n, groups, lengths, slots, tokens, gains, up_rows, down_rows, weights, gate_weight,
    out_weight, cotangent, feed_down,
):
    count, width = tokens.shape
    dk, dv = weights[0].shape[1], weights[2].shape[1]
    body = 2 * dk + dv
    wide = body + LANES
    half = count // 2
    spans = OWN_CAP // SPAN
    vmem = pl.BlockSpec(memory_space=pltpu.VMEM)
    far = pl.BlockSpec(memory_space=pl.ANY)
    smem = pl.BlockSpec(memory_space=pltpu.SMEM)
    shape = jax.ShapeDtypeStruct
    saved = [
        shape((count, width), bf16),
        shape((count, dv), f32),
        shape((count, dv), bf16),
        shape((count, dv), bf16),
        shape((OWN_CAP, wide), bf16),
        shape((spans, dk, dv), bf16),
    ]
    return pl.pallas_call(
        functools.partial(front_kernel, n, groups, dk, dv),
        in_specs=[smem] + [vmem] * 5 + [far] * 7,
        out_specs=[far] * 6 + [vmem] * 7,
        out_shape=[
            *saved,
            shape((count, width), bf16),
            shape((half, width), f32),
            shape((count, feed_down.shape[0]), bf16),
            shape((1, count), jnp.int32),
            shape((count, 1), jnp.int32),
            shape((1, OWN_CAP), jnp.int32),
            shape((OWN_CAP, 1), jnp.int32),
        ],
        scratch_shapes=[pltpu.VMEM(a.shape, a.dtype) for a in saved]
        + Line.scratch(half, width)
        + [
            pltpu.VMEM((width, body), bf16),
            pltpu.VMEM((width, dv), bf16),
            pltpu.VMEM((dv, width), bf16),
            pltpu.VMEM((count, width), bf16),
            pltpu.VMEM(feed_down.shape, bf16),
            pltpu.VMEM((count, wide), bf16),
            pltpu.VMEM((count, width), bf16),
            pltpu.VMEM((dk, dv), f32),
            pltpu.VMEM((OWN_CAP, dv), bf16),
            pltpu.VMEM((groups, count), f32),
            pltpu.VMEM((LANES, dk), bf16),
            pltpu.VMEM((1, dk), f32),
            pltpu.VMEM((LANES, width), bf16),
            pltpu.SemaphoreType.DMA((8,)),
            Line.semaphores(half),
        ]
        + Exchange.scratch(groups, OWN_CAP, wide, 2)
        + Exchange.scratch(groups, OWN_CAP, dv, 1)
        + [pltpu.SemaphoreType.DMA((6,))],
        compiler_params=pltpu.CompilerParams(
            collective_id=call, has_side_effects=True, vmem_limit_bytes=60 << 20
        ),
        cost_estimate=pl.CostEstimate(
            flops=12_000_000_000, bytes_accessed=200_000_000, transcendentals=4_000_000
        ),
        name="front",
    )(
        lengths, slots, tokens, gains, up_rows, down_rows, *weights, gate_weight, out_weight,
        cotangent, feed_down,
    )


def back_feed_kernel(n, groups, tiles, *refs):
    take = splitter(refs)
    gains_ref, x_far, base_far, left_far, d_active_far, gate_far, up_far, down_far = take(8)
    out_ref, kept_ref, gain_grad_ref, recv, active_far, layer_far = take(6)
    active_ref, layer_ref = take(2)
    up_in, down_in, x_ref, base_ref, share_ref, weight_ref, d_active_ref = take(7)
    load_sems, weight_sems, sems = take(3)
    active_spill = pltpu.make_async_copy(active_ref, active_far, load_sems.at[4])
    layer_spill = pltpu.make_async_copy(layer_ref, layer_far, load_sems.at[5])
    rows = RowGrads(groups, left_far, tiles, recv, take(10))
    finish = norm_back(
        x_ref, base_ref, lambda: gains_ref[1:2, :], out_ref, kept_ref, gain_grad_ref
    )
    line = Line(n, share_ref, up_in, down_in, out_ref, sems, finish)
    count, width = share_ref.shape
    wide = active_ref.shape[1]
    full, rest = wide // 256, wide % 256
    pieces = full + (rest > 0)
    loads = (
        pltpu.make_async_copy(d_active_far, d_active_ref, load_sems.at[2]),
        pltpu.make_async_copy(x_far, x_ref, load_sems.at[0]),
        pltpu.make_async_copy(base_far.at[line.own_half(), :], base_ref, load_sems.at[1]),
    )
    down_load = pltpu.make_async_copy(
        down_far, weight_ref.at[pl.ds(0, wide), pl.ds(0, width)], load_sems.at[3]
    )

    def spans(i, size):
        start = pl.multiple_of(i * 256, 256)
        return pl.ds(start, size), pl.ds(pl.multiple_of(wide + start, LANES), size)

    def weight_loads(i, size):
        gate_span, up_span = spans(i, size)
        return (
            pltpu.make_async_copy(
                gate_far.at[:, gate_span], weight_ref.at[:, gate_span], weight_sems.at[0, i]
            ),
            pltpu.make_async_copy(
                up_far.at[:, gate_span], weight_ref.at[:, up_span], weight_sems.at[1, i]
            ),
        )

    def piece_copies(i, size):
        gate_span, up_span = spans(i, size)
        return (
            rows.piece_copy(2 * i, rows.all.at[:, gate_span], gate_span),
            rows.piece_copy(2 * i + 1, rows.all.at[:, up_span], up_span),
        )

    def each(action):
        @pl.loop(0, full)
        def _(i):
            action(i, 256)

        if rest:
            action(full, rest)

    def start_weights(i, size):
        for c in weight_loads(i, size):
            c.start()

    rows.left_load().start()
    each(start_weights)
    for c in loads:
        c.start()
    barrier = pltpu.get_barrier_semaphore()
    greet_dp(barrier, groups)
    line.greet(barrier, groups - 1)

    @pl.loop(0, rows.team)
    def _(q):
        rows.left_copy(q).start()

    rows.left_load().wait()
    for c in loads:
        c.wait()

    def hidden_units(i, size):
        for c in weight_loads(i, size):
            c.wait()
        gate_span, up_span = spans(i, size)
        gate = dot(rows.left[...], weight_ref[:, gate_span])
        up = dot(rows.left[...], weight_ref[:, up_span])
        d_active = d_active_ref[:, gate_span].astype(f32)
        sigmoid = jax.nn.sigmoid(gate)
        swish = gate * sigmoid
        active_ref[:, gate_span] = (swish * up).astype(bf16)
        rows.all[:, gate_span] = (
            d_active * up * sigmoid * (1.0 + gate * (1.0 - sigmoid))
        ).astype(bf16)
        rows.all[:, up_span] = (d_active * swish).astype(bf16)
        for c in piece_copies(i, size):
            c.start()

    each(hidden_units)
    active_spill.start()

    half = count // 2
    last = line.me == n - 1

    @pl.loop(0, 2)
    def _(i):
        bottom = jnp.where(last, 1 - i, i)
        at = pl.ds(pl.multiple_of(bottom * half, half), half)

        @pl.loop(0, width // 256)
        def _(j):
            to = pl.ds(pl.multiple_of(j * 256, 256), 256)
            share_ref[at, to] = dot_t(rows.all[at, :], weight_ref[to, :]).astype(bf16)

        line.prime(i == 0, i == 0)

    down_load.start()

    def piece_arrived(i, size):
        for c in piece_copies(i, size):
            c.wait_recv()

    layer_items = width // 512

    @pl.loop(0, line.steps)
    def _(step):
        line.step(step)

        @pl.when(step == 0)
        def _():
            @pl.loop(0, rows.team)
            def _(q):
                rows.left_copy(q).wait_recv()

            each(piece_arrived)

        rows.item(step)
        layer_item = step - rows.items

        @pl.when(layer_item == 0)
        def _():
            down_load.wait()

        @pl.when((layer_item >= 0) & (layer_item < layer_items))
        def _():
            to = pl.ds(pl.multiple_of(layer_item * 512, 512), 512)
            layer_ref[:, to] = dot(active_ref[...], weight_ref[pl.ds(0, wide), to]).astype(bf16)

        @pl.when(layer_item == layer_items)
        def _():
            layer_spill.start()

    rows.receive()
    line.drain()
    rows.drain()
    active_spill.wait()
    layer_spill.wait()

    def piece_sent(i, size):
        for c in piece_copies(i, size):
            c.wait_send()

    each(piece_sent)


def back_feed(call, n, groups, gains, x_own, base, left, d_active, feed_gate, feed_up, feed_down):
    count, width = left.shape
    half = count // 2
    wide = feed_gate.shape[1]
    pieces = (wide + 255) // 256
    cut = (wide // 2 + LANES - 1) // LANES * LANES
    tiles = [(0, cut), (cut, wide - cut), (wide, cut), (wide + cut, wide - cut)]
    vmem = pl.BlockSpec(memory_space=pltpu.VMEM)
    far = pl.BlockSpec(memory_space=pl.ANY)
    return pl.pallas_call(
        functools.partial(back_feed_kernel, n, groups, tiles),
        in_specs=[vmem] + [far] * 7,
        out_specs=[vmem] * 3 + [far] * 3,
        out_shape=[
            jax.ShapeDtypeStruct((count, width), bf16),
            jax.ShapeDtypeStruct((half, width), f32),
            jax.ShapeDtypeStruct((8, width), f32),
            jax.ShapeDtypeStruct((groups // 2, width // groups, 2 * wide), bf16),
            jax.ShapeDtypeStruct((count, wide), bf16),
            jax.ShapeDtypeStruct((count, width), bf16),
        ],
        scratch_shapes=[pltpu.VMEM((count, wide), bf16), pltpu.VMEM((count, width), bf16)]
        + Line.scratch(half, width)
        + [
            pltpu.VMEM((half, width), x_own.dtype),
            pltpu.VMEM((half, width), base.dtype),
            pltpu.VMEM((count, width), bf16),
            pltpu.VMEM((width, 2 * wide), bf16),
            pltpu.VMEM((count, wide), bf16),
            pltpu.SemaphoreType.DMA((6,)),
            pltpu.SemaphoreType.DMA((2, pieces)),
            Line.semaphores(half),
        ]
        + RowGrads.scratch(groups, count, width, 2 * wide, 2 * pieces, len(tiles)),
        compiler_params=pltpu.CompilerParams(
            collective_id=call, has_side_effects=True, vmem_limit_bytes=61 << 20
        ),
        cost_estimate=pl.CostEstimate(
            flops=30_000_000_000, bytes_accessed=200_000_000, transcendentals=0
        ),
        name="back_feed",
    )(gains, x_own, base, left, d_active, feed_gate, feed_up, feed_down)


class SmallSum:
    def __init__(self, n, groups, wide, near, near_all, wide_out, near_out, refs):
        (
            self.wide_in, self.near_in, self.wide_line, self.near_line, self.sems, self.line_sems,
        ) = refs
        self.n, self.groups, self.near_all = n, groups, near_all
        self.wide, self.near, self.wide_out, self.near_out = wide, near, wide_out, near_out
        self.member, self.place = lax.axis_index("dp"), lax.axis_index("tensor")
        self.block = wide.shape[1] // groups

    @staticmethod
    def scratch(n, groups, wide, near):
        block = wide[1] // groups
        return [
            pltpu.VMEM((groups, wide[0], block), f32),
            pltpu.VMEM(near, f32),
            pltpu.VMEM((n, wide[0], block), f32),
            pltpu.VMEM((n,) + near[1:], f32),
            pltpu.SemaphoreType.DMA((2, 2, groups)),
            pltpu.SemaphoreType.DMA((2, 2, n)),
        ]

    def greet(self, barrier):
        n, place = self.n, self.place
        for k in range(2, n):
            @pl.when(place + k < n)
            def _():
                pl.semaphore_signal(
                    barrier, inc=1, device_id={"tensor": place + k}, device_id_type=MESH
                )

            @pl.when(place - k >= 0)
            def _():
                pl.semaphore_signal(
                    barrier, inc=1, device_id={"tensor": place - k}, device_id_type=MESH
                )

    def cut(self, j):
        return pl.ds(pl.multiple_of(j * self.block, self.block), self.block)

    def copies(self, to, source):
        return (
            to_dp(
                self.wide.at[:, self.cut(to)], self.wide_in.at[source],
                self.sems.at[0, 0, to], self.sems.at[1, 0, source], to,
            ),
            to_dp(
                self.near.at[to], self.near_in.at[source],
                self.sems.at[0, 1, to], self.sems.at[1, 1, source], to,
            ),
        )

    def line_copies(self, to, source):
        return tuple(
            pltpu.make_async_remote_copy(
                line.at[self.place], line.at[source], self.line_sems.at[0, i, to],
                self.line_sems.at[1, i, source], device_id={"tensor": to}, device_id_type=MESH,
            )
            for i, line in enumerate((self.wide_line, self.near_line))
        )

    def send(self):
        @pl.loop(1, self.groups)
        def _(k):
            for c in self.copies(lax.rem(self.member + k, self.groups), self.member):
                c.start()

        self.wide_in[pl.ds(self.member, 1)] = self.wide[:, self.cut(self.member)][None]
        self.near_in[pl.ds(self.member, 1)] = self.near[pl.ds(self.member, 1)]

    def forward(self):
        @pl.loop(1, self.groups)
        def _(k):
            for c in self.copies(0, lax.rem(self.member + k, self.groups)):
                c.wait_recv()

        for came, line in ((self.wide_in, self.wide_line), (self.near_in, self.near_line)):
            total = came[0]
            for j in range(1, self.groups):
                total = total + came[j]
            line[pl.ds(self.place, 1)] = total[None]

        @pl.loop(1, self.n)
        def _(k):
            for c in self.line_copies(lax.rem(self.place + k, self.n), self.place):
                c.start()

    def receive(self):
        @pl.loop(1, self.n)
        def _(k):
            for c in self.line_copies(0, lax.rem(self.place + k, self.n)):
                c.wait_recv()

        total = self.wide_line[0]
        for j in range(1, self.n):
            total = total + self.wide_line[j]
        self.wide_out[...] = total
        own = self.near_line[pl.ds(self.place, 1)][0]
        total = self.near_line[0]
        for j in range(1, self.n):
            total = total + self.near_line[j]
        row = lax.broadcasted_iota(jnp.int32, own.shape, 0)
        self.near_out[...] = jnp.where(row < self.near_all, total, own)

    def drain(self):
        @pl.loop(1, self.groups)
        def _(k):
            for c in self.copies(lax.rem(self.member + k, self.groups), self.member):
                c.wait_send()

        @pl.loop(1, self.n)
        def _(k):
            for c in self.line_copies(lax.rem(self.place + k, self.n), self.place):
                c.wait_send()


def back_mixer_kernel(n, groups, widths, near_all, tiles, *refs):
    take = splitter(refs)
    gains_ref, near_ref, down_rows_ref, x_far, base_far, left_far = take(6)
    parts = take(2)
    col_left, col_right = take(2)
    weights = take(len(widths))
    out_ref, wide_out, near_out, recv, col_recv = take(5)
    up_in, down_in, x_ref, base_ref, share_ref, wide_ref, gain_grad_ref = take(7)
    weight_ref, latent_ref, load_sems, sems = take(4)
    rows = RowGrads(groups, left_far, tiles, recv, take(10))
    part_spans = [
        pl.ds(0, parts[0].shape[1]), pl.ds(parts[0].shape[1], parts[1].shape[1])
    ]
    part_loads = [rows.piece_load(i, parts[i], part_spans[i]) for i in range(2)]
    part_copies = [rows.piece_copy(i, parts[i], part_spans[i]) for i in range(2)]
    cols = ColGrad(groups, col_left, col_right, 0, col_recv, take(8))
    small = SmallSum(n, groups, wide_ref, near_ref, near_all, wide_out, near_out, take(6))
    finish = norm_back(x_ref, base_ref, lambda: gains_ref[0:1, :], out_ref, None, gain_grad_ref)
    line = Line(n, share_ref, up_in, down_in, out_ref, sems, finish)
    loads = [
        pltpu.make_async_copy(x_far.at[line.own_half(), :], x_ref, load_sems.at[0]),
        pltpu.make_async_copy(base_far, base_ref, load_sems.at[1]),
    ]
    weight_loads = []
    offset = 0
    for i, wide in enumerate(widths):
        if i == len(widths) - 1:
            latent_at = offset
            offset += LANES
        weight_loads.append(
            pltpu.make_async_copy(
                weights[i], weight_ref.at[:, pl.ds(offset, wide)], load_sems.at[2 + i]
            )
        )
        offset += wide
    for c in part_loads + weight_loads:
        c.start()
    thirds(down_rows_ref, 2, latent_ref)
    weight_ref[:, pl.ds(latent_at, LANES)] = jnp.transpose(latent_ref[...].astype(f32)).astype(bf16)
    barrier = pltpu.get_barrier_semaphore()
    greet_dp(barrier, groups)
    small.greet(barrier)
    line.greet_all(barrier, groups - 1)
    rows.start_left()
    for c in part_copies:
        c.start()
    cols.start()
    for c in loads:
        c.start()
    for c in part_loads + weight_loads:
        c.wait()

    count, width = share_ref.shape
    tile_rows, tile_columns = count // 2, 512
    across = width // tile_columns

    @pl.loop(0, 2 * across)
    def _(i):
        at = pl.ds(pl.multiple_of((i // across) * tile_rows, tile_rows), tile_rows)
        to = pl.ds(pl.multiple_of(lax.rem(i, across) * tile_columns, tile_columns), tile_columns)
        share_ref[at, to] = dot_t(rows.all[at, :], weight_ref[to, :]).astype(bf16)

    line.prime()
    for c in loads:
        c.wait()
    third = LANES // 4
    first_cols = rows.items
    last_item = first_cols + cols.items

    @pl.loop(0, line.steps)
    def _(step):
        line.step(step)

        @pl.when(step == 0)
        def _():
            rows.ready_left()
            for c in part_copies:
                c.wait_recv()

        rows.item(step)

        @pl.when(step == first_cols)
        def _():
            cols.ready()

        @pl.when((step >= first_cols) & (step < last_item))
        def _():
            cols.item(step - first_cols)

        @pl.when(step == last_item)
        def _():
            cols.send_all()
            product = rows_dot(rows.all[:, pl.ds(latent_at, LANES)], rows.left[...])
            wide_ref[:16, :] = product[:16, :] + product[third : third + 16, :]

        @pl.when(step == line.second + 4)
        def _():
            wide_ref[16:, :] = gain_grad_ref[...]
            small.send()

        @pl.when(step == line.second + 14)
        def _():
            small.forward()

    rows.receive()
    cols.receive()
    small.receive()
    line.drain()
    rows.drain()
    for c in part_copies:
        c.wait_send()
    cols.drain()
    small.drain()


def back_mixer(
    call, n, groups, gains, near, near_all, down_rows, x, base_own, left, parts, pair, weights
):
    count, width = left.shape
    half = count // 2
    widths = [w.shape[1] for w in weights]
    total = sum(part.shape[1] for part in parts)
    start = parts[0].shape[1]
    tiles = [(0, 512), (512, 512), (start, parts[1].shape[1])]
    col_rows = pair[0].shape[1]
    vmem = pl.BlockSpec(memory_space=pltpu.VMEM)
    far = pl.BlockSpec(memory_space=pl.ANY)
    wide_shape = (24, width)
    return pl.pallas_call(
        functools.partial(back_mixer_kernel, n, groups, widths, near_all, tiles),
        in_specs=[vmem] * 3 + [far] * (7 + len(weights)),
        out_specs=[vmem] * 3 + [far] * 2,
        out_shape=[
            jax.ShapeDtypeStruct((count, width), bf16),
            jax.ShapeDtypeStruct((24, width // groups), f32),
            jax.ShapeDtypeStruct(near.shape[1:], f32),
            jax.ShapeDtypeStruct((groups // 2, width // groups, total), bf16),
            jax.ShapeDtypeStruct((groups, col_rows // groups, width // 2), bf16),
        ],
        scratch_shapes=Line.scratch(half, width)
        + [
            pltpu.VMEM((half, width), x.dtype),
            pltpu.VMEM((half, width), base_own.dtype),
            pltpu.VMEM((count, width), bf16),
            pltpu.VMEM(wide_shape, f32),
            pltpu.VMEM((8, width), f32),
            pltpu.VMEM((width, total), bf16),
            pltpu.VMEM((LANES, width), bf16),
            pltpu.SemaphoreType.DMA((2 + len(weights),)),
            Line.semaphores(half),
        ]
        + RowGrads.scratch(groups, count, width, total, 2, len(tiles))
        + ColGrad.scratch(groups, count, col_rows, width // 2)
        + SmallSum.scratch(n, groups, wide_shape, near.shape),
        compiler_params=pltpu.CompilerParams(
            collective_id=call, has_side_effects=True, vmem_limit_bytes=61 << 20
        ),
        cost_estimate=pl.CostEstimate(
            flops=12_000_000_000, bytes_accessed=200_000_000, transcendentals=0
        ),
        name="back_mixer",
    )(gains, near, down_rows, x, base_own, left, *parts, *pair, *weights)


def outputs_kernel(dk, dv, rank, near_all, *refs):
    take = splitter(refs)
    feed_ref, rows_ref, down_ref, out_ref = take(4)
    wide_ref, near_ref, token_ref, layer_ref = take(4)
    token_out, layer_out, query_out, key_out, value_out, gate_out = take(6)
    feed_gate_out, feed_up_out, feed_down_out, out_out, decay_out, vector_out = take(6)
    step = pl.program_id(0)

    def total(ref, start, wide):
        span = pl.ds(start, wide)
        result = ref[0, :, span].astype(f32)
        for q in range(1, ref.shape[0]):
            result = result + ref[q, :, span].astype(f32)
        return result

    wide = feed_gate_out.shape[1]
    feed_gate_out[...] = total(feed_ref, 0, wide)
    feed_up_out[...] = total(feed_ref, wide, wide)
    query_out[...] = total(rows_ref, 0, dk)
    key_out[...] = total(rows_ref, dk, dk)
    value_out[...] = total(rows_ref, 2 * dk, dv)
    gate_out[...] = total(rows_ref, 2 * dk + dv + LANES, dv)
    token_out[...] = token_ref[...]
    layer_out[...] = layer_ref[...]

    @pl.when(lax.rem(step, 4) == 0)
    def _():
        half = out_out.shape[2] // 2
        for ref, out in ((down_ref, feed_down_out), (out_ref, out_out)):
            for b in range(2):
                result = ref[b].astype(f32)
                for q in range(1, ref.shape[0] // 2):
                    result = result + ref[2 * q + b].astype(f32)
                out[0, :, b * half : (b + 1) * half] = result

    @pl.when(step == 0)
    def _():
        decay_out[...] = wide_ref[:rank, :]
        vector_out[...] = jnp.sum(wide_ref[rank:, :], axis=0, keepdims=True)


def outputs(
    groups, dk, dv, rank, near_all, feed, rows, down, out, wide_sum, near_sum, token, layer
):
    steps = 8
    count, width = token.shape
    wide = feed.shape[2] // 2
    per = width // groups
    block = per // steps
    shape = jax.ShapeDtypeStruct

    def rows_of(columns):
        return pl.BlockSpec((block, columns), lambda i: (i, 0))

    def fixed(array):
        return pl.BlockSpec(array.shape, lambda i: (0,) * array.ndim)

    def recv(array):
        return pl.BlockSpec((array.shape[0], block, array.shape[2]), lambda i: (0, i, 0))

    def recv_half(array):
        return pl.BlockSpec(
            (array.shape[0], array.shape[1] // 2, array.shape[2]), lambda i: (0, i // 4, 0)
        )

    def out_half(array):
        return pl.BlockSpec((1, array.shape[1] // 2, width), lambda i: (0, i // 4, 0))

    tokens_block = pl.BlockSpec((count // steps, width), lambda i: (i, 0))
    return pl.pallas_call(
        functools.partial(outputs_kernel, dk, dv, rank, near_all),
        grid=(steps,),
        in_specs=[
            recv(feed), recv(rows), recv_half(down), recv_half(out), fixed(wide_sum),
            fixed(near_sum), tokens_block, tokens_block,
        ],
        out_specs=[
            tokens_block, tokens_block, rows_of(dk), rows_of(dk), rows_of(dv), rows_of(dv),
            rows_of(wide), rows_of(wide), out_half(down), out_half(out),
            pl.BlockSpec((rank, per), lambda i: (0, 0)),
            pl.BlockSpec((1, per), lambda i: (0, 0)),
        ],
        out_shape=[
            shape((count, width), bf16),
            shape((count, width), bf16),
            shape((per, dk), f32),
            shape((per, dk), f32),
            shape((per, dv), f32),
            shape((per, dv), f32),
            shape((per, wide), f32),
            shape((per, wide), f32),
            shape((1, down.shape[1], width), f32),
            shape((1, out.shape[1], width), f32),
            shape((rank, per), f32),
            shape((1, per), f32),
        ],
        compiler_params=pltpu.CompilerParams(vmem_limit_bytes=60 << 20),
        name="outputs",
    )(feed, rows, down, out, wide_sum, near_sum, token, layer)


def recur_back_kernel(n, groups, dk, dv, beside, *refs):
    (
        lengths_ref, send_row_ref, send_column_ref, slot_row_ref, slot_column_ref,
        d_mixed_ref, out_weight_ref, attended_ref, gate_ref, gains_ref, up_rows_ref,
        share_ref, held_far, states_far, hidden_far, active_far, cotangent_far,
        d_rows_ref, d_gate_ref, head_gain_ref, grad_up_ref, grad_bias_ref, layer_ref, grad_down_ref,
        up_in, down_in, d_attended, d_placed, d_state, result,
        held_ref, states_ref, hidden_ref, up_ref, down_ref, bias_ref, load_sems, sems,
    ) = refs[:38]
    go = Exchange(groups, (), *refs[38:41])
    back = Exchange(groups, (2 * dk,), *refs[41:44])
    cols = None
    if beside:
        cols = ColGrad(groups, active_far, cotangent_far, 0, grad_down_ref, refs[44:])
    count = d_mixed_ref.shape[0]
    slots = slot_row_ref.shape[1]
    end0 = lengths_ref[0, 0]
    end1 = end0 + lengths_ref[0, 1]
    ends = (end0, end1, end1 + lengths_ref[0, 2])

    def finish(total, own, place):
        layer_ref[place, :] = (hidden_ref[own, :] + total).astype(layer_ref.dtype)

    line = Line(n, share_ref, up_in, down_in, layer_ref, sems, finish)
    loads = (
        pltpu.make_async_copy(hidden_far, hidden_ref, load_sems.at[0]),
        pltpu.make_async_copy(held_far, held_ref, load_sems.at[1]),
        pltpu.make_async_copy(states_far, states_ref, load_sems.at[2]),
    )
    barrier = pltpu.get_barrier_semaphore()
    greet_dp(barrier, groups)
    line.greet(barrier, groups - 1)
    line.prime()
    for c in loads:
        c.start()
    if beside:
        cols.start()
    loads[0].wait()

    bias_ref[...] = gains_ref[2:3, dv : dv + dk]
    thirds(up_rows_ref, 3, up_ref)
    thirds(up_rows_ref, 2, down_ref)

    head_gain_ref[...] = jnp.zeros_like(head_gain_ref)
    tile = count // 2

    @pl.loop(0, 2)
    def _(i):
        rows = pl.ds(pl.multiple_of(i * tile, tile), tile)
        d_gated = dot_t(d_mixed_ref[rows, :], out_weight_ref[...])
        attended = attended_ref[rows, :].astype(f32)
        gate = gate_ref[rows, :]
        scaling = lax.rsqrt(jnp.mean(attended * attended, axis=1, keepdims=True) + head_floor)
        unit = attended * scaling
        sigmoid = jax.nn.sigmoid(gate)
        swish = gate * sigmoid
        gained = d_gated * gains_ref[2:3, :dv]
        d_gate_ref[rows, :] = (
            gained * unit * sigmoid * (1.0 + gate * (1.0 - sigmoid))
        ).astype(bf16)
        d_unit = gained * swish
        d_attended[rows, :] = (
            scaling * (d_unit - unit * jnp.mean(d_unit * unit, axis=1, keepdims=True))
        ).astype(bf16)
        term = d_gated * unit * swish
        piece = term[0:8, :]
        for r in range(1, tile // 8):
            piece = piece + term[8 * r : 8 * r + 8, :]
        head_gain_ref[...] += piece
        line.step(2 * i)
        line.step(2 * i + 1)

    go.send(0, send_row_ref, 0, d_attended)
    d_state[...] = jnp.zeros_like(d_state)
    grad_up_ref[...] = jnp.zeros_like(grad_up_ref)
    grad_bias_ref[...] = jnp.zeros_like(grad_bias_ref)
    done = 12
    if beside:
        cols.ready()

        @pl.loop(0, cols.items)
        def _(i):
            cols.item(i)
            line.step(4 + 2 * i)
            line.step(5 + 2 * i)

        done = 4 + 2 * cols.items
        cols.send_all()
    else:
        line.run(4, done)
    for c in loads[1:]:
        c.wait()

    go.receive(0)
    place_rows(slot_row_ref, go.came, d_placed, go.spans[0])
    spans = held_ref.shape[0] // SPAN

    @pl.loop(0, spans)
    def _(i):
        step = spans - 1 - i
        d_out = d_placed[pl.ds(pl.multiple_of(step * SPAN, SPAN), SPAN), :]
        span_backward(
            dk, dv, step, ends, d_out, held_ref, states_ref[step], up_ref, bias_ref, down_ref,
            d_state, result, grad_up_ref, grad_bias_ref,
        )
        line.step(done + 2 * i)
        line.step(done + 1 + 2 * i)

    for p in range(2):
        back.send(p, slot_column_ref, 1, result)
    line.run(done + 2 * spans, line.steps)
    if beside:
        cols.receive()

    for p in range(2):
        back.receive(p)
        span = back.spans[p]

        @pl.loop(0, 2)
        def _(i):
            rows = pl.ds(pl.multiple_of(i * tile, tile), tile)
            pick = one_hot(send_column_ref[rows, :], 0, (tile, slots), 1)
            d_rows_ref[rows, span] = dot(pick, back.came[:, span]).astype(bf16)

    line.drain()
    if beside:
        cols.drain()
    go.drain()
    back.drain()


def recur_back(
    call, n, groups, dk, dv, beside, lengths, send_row, send_column, slot_row, slot_column, d_mixed, out_weight, attended, gate_pre,
    gains, up_rows, share, held, states, hidden_own, active, cotangent,
):
    count, width = d_mixed.shape
    slots, wide = held.shape
    half = count // 2
    vmem = pl.BlockSpec(memory_space=pltpu.VMEM)
    operands = [
        lengths, send_row, send_column, slot_row, slot_column, d_mixed, out_weight, attended, gate_pre, gains, up_rows, share, held, states, hidden_own, active, cotangent,
    ]
    far = pl.BlockSpec(memory_space=pl.ANY)
    return pl.pallas_call(
        functools.partial(recur_back_kernel, n, groups, dk, dv, beside),
        in_specs=[pl.BlockSpec(memory_space=pltpu.SMEM)] + [vmem] * (len(operands) - 6) + [far] * 5,
        out_specs=[vmem] * 6 + [far],
        out_shape=[
            jax.ShapeDtypeStruct((count, wide), bf16),
            jax.ShapeDtypeStruct((count, dv), bf16),
            jax.ShapeDtypeStruct((8, dv), f32),
            jax.ShapeDtypeStruct((dk, LANES), f32),
            jax.ShapeDtypeStruct((8, dk), f32),
            jax.ShapeDtypeStruct((count, width), bf16),
            jax.ShapeDtypeStruct(
                (groups, active.shape[1] // groups if beside else 8, width // 2), bf16
            ),
        ],
        scratch_shapes=Line.scratch(half, width)
        + [
            pltpu.VMEM((count, dv), bf16),
            pltpu.VMEM((slots, dv), bf16),
            pltpu.VMEM((dk, dv), f32),
            pltpu.VMEM((slots, wide), bf16),
            pltpu.VMEM(held.shape, bf16),
            pltpu.VMEM(states.shape, bf16),
            pltpu.VMEM((half, width), f32),
            pltpu.VMEM((LANES, dk), bf16),
            pltpu.VMEM((LANES, dk), bf16),
            pltpu.VMEM((1, dk), f32),
            pltpu.SemaphoreType.DMA((3,)),
            Line.semaphores(half),
        ]
        + Exchange.scratch(groups, slots, dv, 1)
        + Exchange.scratch(groups, slots, wide, 2)
        + (ColGrad.scratch(groups, count, active.shape[1], width // 2) if beside else []),
        compiler_params=pltpu.CompilerParams(
            collective_id=call, has_side_effects=True, vmem_limit_bytes=60 << 20
        ),
        cost_estimate=pl.CostEstimate(
            flops=12_000_000_000, bytes_accessed=200_000_000, transcendentals=4_000_000
        ),
        name="recur_back",
    )(*operands)


def small_sum_kernel(groups, n, rows_all, part_ref, out_ref, held, line, line_in, sems, line_sems):
    me = lax.axis_index("dp")
    place = lax.axis_index("tensor")
    barrier = pltpu.get_barrier_semaphore()

    def peer(k):
        return lax.rem(me + k, groups)

    def mate(k):
        return lax.rem(place + k, n)

    @pl.loop(1, groups)
    def _(k):
        pl.semaphore_signal(barrier, inc=1, device_id={"dp": peer(k)}, device_id_type=MESH)

    @pl.loop(1, n)
    def _(k):
        pl.semaphore_signal(barrier, inc=1, device_id={"tensor": mate(k)}, device_id_type=MESH)

    pl.semaphore_wait(barrier, groups + n - 2)

    def copy(k, source):
        return pltpu.make_async_remote_copy(
            part_ref.at[peer(k)], held.at[source], sems.at[0, k], sems.at[1, source],
            device_id={"dp": peer(k)}, device_id_type=MESH,
        )

    def line_copy(k, source):
        return pltpu.make_async_remote_copy(
            line, line_in.at[source], line_sems.at[0, k], line_sems.at[1, source],
            device_id={"tensor": mate(k)}, device_id_type=MESH,
        )

    @pl.loop(1, groups)
    def _(k):
        copy(k, me).start()

    held[pl.ds(me, 1)] = part_ref[pl.ds(me, 1)]

    @pl.loop(1, groups)
    def _(k):
        copy(k, peer(k)).wait_recv()

    total = held[0]
    for i in range(1, groups):
        total = total + held[i]
    line[...] = total[:rows_all]
    out_ref[...] = total

    @pl.loop(1, n)
    def _(k):
        line_copy(k, place).start()

    line_in[pl.ds(place, 1)] = total[None, :rows_all]

    @pl.loop(1, n)
    def _(k):
        line_copy(k, mate(k)).wait_recv()

    total = line_in[0]
    for i in range(1, n):
        total = total + line_in[i]
    out_ref[:rows_all] = total

    @pl.loop(1, groups)
    def _(k):
        copy(k, me).wait_send()

    @pl.loop(1, n)
    def _(k):
        line_copy(k, place).wait_send()


def small_sum(over_all, over_owners, groups, n, call):
    def tiles(blocks):
        short = -blocks.shape[1] % (8 * LANES)
        return jnp.pad(blocks, ((0, 0), (0, short))).reshape(groups, -1, LANES)

    first, second = tiles(over_all), tiles(over_owners)
    rows_all = first.shape[1]
    part = jnp.concatenate([first, second], axis=1)
    vmem = pl.BlockSpec(memory_space=pltpu.VMEM)
    total = pl.pallas_call(
        functools.partial(small_sum_kernel, groups, n, rows_all),
        in_specs=[vmem],
        out_specs=vmem,
        out_shape=jax.ShapeDtypeStruct(part.shape[1:], f32),
        scratch_shapes=[
            pltpu.VMEM(part.shape, f32),
            pltpu.VMEM((rows_all, LANES), f32),
            pltpu.VMEM((n, rows_all, LANES), f32),
            pltpu.SemaphoreType.DMA((2, groups)),
            pltpu.SemaphoreType.DMA((2, n)),
        ],
        compiler_params=pltpu.CompilerParams(collective_id=call, has_side_effects=True),
        name="small_sum",
    )(part)
    return (
        total[:rows_all].reshape(-1)[: over_all.shape[1]],
        total[rows_all:].reshape(-1)[: over_owners.shape[1]],
    )


def per_device(
    tokens,
    cotangent,
    token_slots,
    lengths,
    mixer_gain,
    query_weight,
    key_weight,
    value_weight,
    gate_weight,
    decay_down,
    decay_up,
    decay_bias,
    head_gain,
    out_weight,
    feed_gain,
    feed_gate,
    feed_up,
    feed_down,
):
    groups = lax.axis_size("dp")
    lines = lax.axis_size("tensor")
    member = lax.axis_index("dp")
    place = lax.axis_index("tensor")
    count, width = tokens.shape
    dk = query_weight.shape[1]
    dv = value_weight.shape[1]
    rank = decay_up.shape[1]
    parity = lax.rem(member, 2)
    pairs = [(i, i ^ 1) for i in range(groups)]
    same_parity = [[i for i in range(groups) if i % 2 == b] for b in range(2)]

    fused = (width // groups) % LANES == 0
    third = LANES // 4
    down_rows = decay_down.T
    up_rows = decay_up.T
    last = jnp.pad(jnp.concatenate([head_gain, decay_bias]), (0, width - dv - dk))
    gains = jnp.stack([mixer_gain, feed_gain, last]).astype(f32)
    (
        normed, gate_pre, attended, gated, held, states, feed_normed, hidden_own, d_active, send_row,
        send_column, slot_row, slot_column,
    ) = front(
        1, lines, groups, lengths, token_slots.reshape(groups, count), tokens, gains, up_rows,
        down_rows, [query_weight, key_weight, value_weight], gate_weight, out_weight, cotangent,
        feed_down,
    )

    if fused:
        d_mixed, d_hidden_own, feed_gain_part, feed_recv, active, layer_share = back_feed(
            2, lines, groups, gains, hidden_own, cotangent, feed_normed,
            d_active, feed_gate, feed_up, feed_down,
        )
    else:
        half = count // 2
        own_at = jnp.where(place == 0, half, 0)
        tokens_own = lax.dynamic_slice_in_dim(tokens, own_at, half)
        cotangent_own = lax.dynamic_slice_in_dim(cotangent, own_at, half)
        gate_hidden = dot(feed_normed, feed_gate)
        up_hidden = dot(feed_normed, feed_up)
        d_active = d_active.astype(f32)
        sigmoid_gate = jax.nn.sigmoid(gate_hidden)
        swish_gate = gate_hidden * sigmoid_gate
        active = (swish_gate * up_hidden).astype(bf16)
        d_gate_hidden = (
            d_active * up_hidden * sigmoid_gate * (1.0 + gate_hidden * (1.0 - sigmoid_gate))
        ).astype(bf16)
        d_up_hidden = (d_active * swish_gate).astype(bf16)
        feed_share = (dot_t(d_gate_hidden, feed_gate) + dot_t(d_up_hidden, feed_up)).astype(bf16)
        d_mixed, d_hidden_own, feed_gain_part = line_sum(
            2, lines, feed_share, hidden_own, cotangent_own, gains[1:2]
        )
        layer_share = dot(active, feed_down).astype(bf16)

    d_rows, d_gate_low, head_gain_part, up_part, bias_part, layer_out, down_recv = recur_back(
        4, lines, groups, dk, dv, fused, lengths, send_row, send_column, slot_row, slot_column, d_mixed,
        out_weight, attended, gate_pre, gains, up_rows, layer_share, held, states, hidden_own, active,
        cotangent,
    )
    up_part = up_part[:, :rank] + up_part[:, third : third + rank] + (
        up_part[:, 2 * third : 2 * third + rank]
    )

    def by_owner(vector):
        return vector.reshape(groups, -1)

    per = width // groups
    head_per = dv // groups
    up_per = dk // groups * rank
    if fused:
        near = [
            by_owner(jnp.sum(feed_gain_part, axis=0)),
            jnp.pad(by_owner(jnp.sum(head_gain_part, axis=0)), ((0, 0), (0, -head_per % LANES))),
            by_owner(up_part),
            jnp.pad(by_owner(bias_part[0]), ((0, 0), (0, -(dk // groups) % LANES))),
        ]
        near_all = (per + head_per + LANES - 1) // LANES
        near = jnp.concatenate(near, axis=1)
        near = jnp.pad(near, ((0, 0), (0, -near.shape[1] % (8 * LANES))))
        token_grad, wide_sum, near_sum, rows_recv, out_recv = back_mixer(
            3, lines, groups, gains, near.reshape(groups, -1, LANES), near_all, down_rows, tokens,
            d_hidden_own, normed, [d_rows, d_gate_low], (gated, d_mixed),
            [query_weight, key_weight, value_weight, gate_weight],
        )
        (
            token_grad, layer_out, grad_query, grad_key, grad_value, grad_gate, grad_feed_gate,
            grad_feed_up, grad_feed_down, grad_out, down_sum, mixer_sum,
        ) = outputs(
            groups, dk, dv, rank, near_all, feed_recv, rows_recv, down_recv, out_recv,
            wide_sum, near_sum, token_grad, layer_out,
        )
        near_sum = near_sum.reshape(-1)
        mixer_sum = mixer_sum.reshape(-1)
        down_sum = down_sum.T
        feed_sum = near_sum[:per]
        head_sum = near_sum[per : per + head_per]
        up_sum = near_sum[near_all * LANES : near_all * LANES + up_per]
        bias_sum = near_sum[near_all * LANES + up_per :][: dk // groups]
    else:
        down_pad = jnp.pad(decay_down, ((0, 0), (0, third - rank)))
        down_none = jnp.zeros_like(down_pad)
        down_both = jnp.concatenate([down_pad, down_pad, down_none, down_none], axis=1)
        d_query_low = d_rows[:, :dk]
        d_key_low = d_rows[:, dk : 2 * dk]
        d_value_low = d_rows[:, 2 * dk : 2 * dk + dv]
        d_latent_low = d_rows[:, 2 * dk + dv :]
        normed_share = (
            dot_t(d_query_low, query_weight)
            + dot_t(d_key_low, key_weight)
            + dot_t(d_value_low, value_weight)
            + dot_t(d_gate_low, gate_weight)
            + dot_t(d_latent_low, down_both)
        ).astype(bf16)
        token_grad, _, mixer_gain_part = line_sum(
            3, lines, normed_share, tokens_own, d_hidden_own, gains[0:1],
        )
        down_part = rows_dot(normed, d_latent_low)
        down_part = down_part[:, :rank] + down_part[:, third : third + rank]
        over_all = jnp.concatenate(
            [
                by_owner(jnp.sum(mixer_gain_part, axis=0)),
                by_owner(jnp.sum(feed_gain_part, axis=0)),
                by_owner(jnp.sum(head_gain_part, axis=0)),
                by_owner(down_part),
            ],
            axis=1,
        )
        over_owners = jnp.concatenate([by_owner(up_part), by_owner(bias_part[0])], axis=1)
        summed, small = small_sum(over_all, over_owners, groups, lines, 5)
        mixer_sum = summed[:per]
        feed_sum = summed[per : 2 * per]
        head_sum = summed[2 * per : 2 * per + head_per]
        down_sum = summed[2 * per + head_per :].reshape(per, rank)
        up_sum = small[:up_per]
        bias_sum = small[up_per:]

    def halves(row_block, dims):
        split = row_block.reshape(row_block.shape[0], groups // 2, 2, dims // groups)
        keep = lax.dynamic_index_in_dim(split, parity, 2, keepdims=False)
        send = lax.dynamic_index_in_dim(split, 1 - parity, 2, keepdims=False)
        got = lax.ppermute(send, "dp", pairs)
        shape = (row_block.shape[0], dims // 2)
        return keep.reshape(shape), got.reshape(shape)

    def partner(row_block):
        return row_block, lax.ppermute(row_block, "dp", pairs)

    def summed_share(left, right):
        share = (rows_dot(left[0], right[0]) + rows_dot(left[1], right[1])).astype(bf16)
        rows = share.shape[0] // (groups // 2)
        blocks = share.reshape(groups // 2, rows, share.shape[1])
        moved = lax.all_to_all(
            blocks, "dp", split_axis=0, concat_axis=0, tiled=True, axis_index_groups=same_parity
        )
        return jnp.sum(moved.astype(f32), axis=0)

    if not fused:
        grad_feed_down = summed_share(halves(active, active.shape[1]), partner(cotangent))[None]
        feed_halves = halves(feed_normed, width)
        normed_halves = halves(normed, width)
        grad_feed_gate = summed_share(feed_halves, partner(d_gate_hidden))
        grad_feed_up = summed_share(feed_halves, partner(d_up_hidden))
        grad_out = summed_share(halves(gated, dv), partner(d_mixed))[None]
        grad_query = summed_share(normed_halves, partner(d_query_low))
        grad_key = summed_share(normed_halves, partner(d_key_low))
        grad_value = summed_share(normed_halves, partner(d_value_low))
        grad_gate = summed_share(normed_halves, partner(d_gate_low))

    return (
        layer_out,
        token_grad,
        mixer_sum,
        grad_query,
        grad_key,
        grad_value,
        grad_gate,
        down_sum,
        up_sum.reshape(1, dk // groups, rank),
        bias_sum.reshape(1, dk // groups),
        head_sum,
        grad_out,
        feed_sum,
        grad_feed_gate,
        grad_feed_up,
        grad_feed_down,
    )


def solution(mesh):
    placed = (
        P("dp", None),
        P("dp", None),
        P(),
        P("dp", None),
        P(),
        P(None, "tensor"),
        P(None, "tensor"),
        P(None, "tensor"),
        P(None, "tensor"),
        P(),
        P("tensor", None),
        P("tensor"),
        P(),
        P("tensor", None),
        P(),
        P(None, "tensor"),
        P(None, "tensor"),
        P("tensor", None),
    )
    return jax.shard_map(
        per_device,
        mesh=mesh,
        in_specs=placed,
        out_specs=(
            P("dp", None),
            P("dp", None),
            P("dp"),
            P("dp", "tensor"),
            P("dp", "tensor"),
            P("dp", "tensor"),
            P("dp", "tensor"),
            P("dp", None),
            P("tensor", "dp", None),
            P("tensor", "dp"),
            P("dp"),
            P("tensor", "dp", None),
            P("dp"),
            P("dp", "tensor"),
            P("dp", "tensor"),
            P("tensor", "dp", None),
        ),
        check_vma=False,
    )
```

```python
import functools

import jax
import jax.numpy as jnp
from jax import lax
from jax.experimental import pallas as pl
from jax.experimental.pallas import tpu as pltpu
from jax.sharding import PartitionSpec as P

OWN_CAP = 1024
SPAN = 128
LANES = 128
epsilon = 1e-06
head_floor = 1.0

f32 = jnp.float32
bf16 = jnp.bfloat16
MESH = pl.DeviceIdType.MESH


def rows_dot(left, right):
    return lax.dot_general(left, right, (((0,), (0,)), ((), ())), preferred_element_type=f32)


def dot_t(left, right):
    return lax.dot_general(left, right, (((1,), (1,)), ((), ())), preferred_element_type=f32)


def dot(left, right):
    return jnp.dot(left, right, preferred_element_type=f32)


def span_terms(first, ends, logits):
    rows = logits.shape[0]

    def label(position):
        count = jnp.zeros_like(position)
        for end in ends:
            count = count + (position >= end).astype(jnp.int32)
        return count

    log_decay = jax.nn.log_sigmoid(logits) * (1.0 / 16.0)
    row = lax.broadcasted_iota(jnp.int32, (rows, rows), 0)
    column = lax.broadcasted_iota(jnp.int32, (rows, rows), 1)
    lower = (row >= column).astype(f32)
    cumulative = jnp.dot(
        lower, log_decay, precision=lax.Precision.HIGHEST, preferred_element_type=f32
    )
    total = cumulative[rows - 1 :, :]
    middle = cumulative[rows // 2 - 1 : rows // 2, :]
    label_column = label(first + lax.broadcasted_iota(jnp.int32, (rows, 1), 0))
    label_row = label(first + lax.broadcasted_iota(jnp.int32, (1, rows), 1))
    before = jnp.where(first > 0, label(first - 1), -1)
    last = label(first + rows - 1)
    carried = (label_column == before).astype(f32)
    tail = (label_column == last).astype(f32)
    keep = (before == last).astype(f32)
    allowed = (row >= column) & (label_column == label_row)
    return log_decay, cumulative, total, middle, carried, tail, keep, allowed


def span_forward(dk, dv, step, ends, held_ref, up_ref, bias_ref, state, states_ref, result):
    first = step * SPAN
    at = pl.ds(pl.multiple_of(first, SPAN), SPAN)
    queries = held_ref[at, :dk].astype(f32) * (float(dk) ** -0.5)
    keys = held_ref[at, dk : 2 * dk].astype(f32)
    values = held_ref[at, 2 * dk : 2 * dk + dv]
    logits = dot(held_ref[at, 2 * dk + dv :], up_ref[...]) + bias_ref[...]
    _, cumulative, total, middle, carried, tail, keep, allowed = span_terms(first, ends, logits)
    query_mid = (queries * jnp.exp(cumulative - middle)).astype(bf16)
    key_mid = (keys * jnp.exp(middle - cumulative)).astype(bf16)
    query_start = (queries * jnp.exp(cumulative) * carried).astype(bf16)
    key_end = (keys * jnp.exp(total - cumulative) * tail).astype(bf16)
    scores = jnp.where(allowed, dot_t(query_mid, key_mid), 0.0).astype(bf16)
    entering = state[...]
    entering_low = entering.astype(bf16)
    states_ref[step] = entering_low
    attended = dot(scores, values) + dot(query_start, entering_low)
    result[at, :] = attended.astype(bf16)
    decay_column = jnp.transpose(jnp.broadcast_to(keep * jnp.exp(total), (8, dk)))[:, :1]
    state[...] = decay_column * entering + rows_dot(key_end, values)


def span_backward(
    dk, dv, step, ends, d_out, held_ref, entering, up_ref, bias_ref, down_ref, d_state, result,
    grad_up_ref, grad_bias_ref,
):
    first = step * SPAN
    at = pl.ds(pl.multiple_of(first, SPAN), SPAN)
    scale = float(dk) ** -0.5
    queries = held_ref[at, :dk].astype(f32) * scale
    keys = held_ref[at, dk : 2 * dk].astype(f32)
    values = held_ref[at, 2 * dk : 2 * dk + dv]
    latent = held_ref[at, 2 * dk + dv :]
    logits = dot(latent, up_ref[...]) + bias_ref[...]
    _, cumulative, total, middle, carried, tail, keep, allowed = span_terms(first, ends, logits)
    grow_query = jnp.exp(cumulative - middle)
    grow_key = jnp.exp(middle - cumulative)
    start_decay = jnp.exp(cumulative) * carried
    end_decay = jnp.exp(total - cumulative) * tail
    query_mid = (queries * grow_query).astype(bf16)
    key_mid = (keys * grow_key).astype(bf16)
    query_start = (queries * start_decay).astype(bf16)
    key_end = (keys * end_decay).astype(bf16)
    scores = jnp.where(allowed, dot_t(query_mid, key_mid), 0.0).astype(bf16)
    d_scores = jnp.where(allowed, dot_t(d_out, values), 0.0).astype(bf16)
    leaving = d_state[...]
    leaving_low = leaving.astype(bf16)
    d_values = rows_dot(scores, d_out) + dot(key_end, leaving_low)
    d_queries = dot(d_scores, key_mid) * grow_query + dot_t(d_out, entering) * start_decay
    d_key_end = dot_t(values, leaving_low) * end_decay
    d_keys = rows_dot(d_scores, query_mid) * grow_key + d_key_end
    kept = keep * jnp.exp(total)
    state_pair = jnp.sum(entering.astype(f32) * leaving, axis=1, keepdims=True)
    state_row = jnp.transpose(jnp.broadcast_to(state_pair, (dk, LANES)))[:1, :]
    d_total = jnp.sum(keys * d_key_end, axis=0, keepdims=True) + kept * state_row
    d_cumulative = queries * d_queries - keys * d_keys
    row = lax.broadcasted_iota(jnp.int32, (SPAN, SPAN), 0)
    column = lax.broadcasted_iota(jnp.int32, (SPAN, SPAN), 1)
    upper = (row <= column).astype(f32)
    d_log_decay = (
        jnp.dot(upper, d_cumulative, precision=lax.Precision.HIGHEST, preferred_element_type=f32)
        + d_total
    )
    d_logits = d_log_decay * (1.0 / 16.0) * jax.nn.sigmoid(-logits)
    grad_bias_ref[...] += jnp.broadcast_to(jnp.sum(d_logits, axis=0, keepdims=True), (8, dk))
    d_logits_high = d_logits.astype(bf16)
    d_logits_low = (d_logits - d_logits_high.astype(f32)).astype(bf16)
    grad_up_ref[...] += rows_dot(d_logits_high, latent) + rows_dot(d_logits_low, latent)
    d_latent = dot_t(d_logits_high, down_ref[...]) + dot_t(d_logits_low, down_ref[...])
    high = d_latent.astype(bf16).astype(f32)
    lane = lax.broadcasted_iota(jnp.int32, d_latent.shape, 1)
    d_latent_packed = jnp.where(lane < LANES // 4, high, d_latent - high)
    result[at, :dk] = (d_queries * scale).astype(bf16)
    result[at, dk : 2 * dk] = d_keys.astype(bf16)
    result[at, 2 * dk : 2 * dk + dv] = d_values.astype(bf16)
    result[at, 2 * dk + dv :] = d_latent_packed.astype(bf16)
    kept_column = jnp.transpose(jnp.broadcast_to(kept, (8, dk)))[:, :1]
    d_state[...] = kept_column * leaving + rows_dot(query_start, d_out)


FINE = 16
SKEW = 3


class Line:
    def __init__(self, n, share_ref, up_in, down_in, out_ref, sems, finish):
        self.n, self.me = n, lax.axis_index("tensor")
        self.share, self.up_in, self.down_in, self.out = share_ref, up_in, down_in, out_ref
        self.sems, self.finish = sems, finish
        self.half = up_in.shape[0]
        self.block = self.half // 2
        self.count = self.half // FINE
        self.second = self.count + 2
        self.steps = self.second + self.count + SKEW * (n - 2)

    @staticmethod
    def scratch(half, width):
        return [pltpu.VMEM((half, width), bf16), pltpu.VMEM((half, width), bf16)]

    @staticmethod
    def semaphores(half):
        return pltpu.SemaphoreType.DMA((8, half // FINE))

    def own_copies(self, source, target, sems):
        block = self.block
        return [
            pltpu.make_async_copy(
                source.at[
                    pl.ds(
                        pl.multiple_of(2 * i * block + jnp.where(self.me == 0, block, 0), block),
                        block,
                    ),
                    :,
                ],
                target.at[pl.ds(i * block, block), :],
                sems[i],
            )
            for i in range(2)
        ]

    def greet(self, barrier, others):
        n, me = self.n, self.me

        @pl.when(me > 0)
        def _():
            pl.semaphore_signal(barrier, inc=1, device_id={"tensor": me - 1}, device_id_type=MESH)

        @pl.when(me < n - 1)
        def _():
            pl.semaphore_signal(barrier, inc=1, device_id={"tensor": me + 1}, device_id_type=MESH)

        inside = (me > 0) & (me < n - 1)

        @pl.when(inside)
        def _():
            pl.semaphore_wait(barrier, others + 2)

        @pl.when(jnp.logical_not(inside))
        def _():
            pl.semaphore_wait(barrier, others + 1)

    def greet_all(self, barrier, others):
        n, me = self.n, self.me

        @pl.when(me > 0)
        def _():
            pl.semaphore_signal(barrier, inc=1, device_id={"tensor": me - 1}, device_id_type=MESH)

        @pl.when(me < n - 1)
        def _():
            pl.semaphore_signal(barrier, inc=1, device_id={"tensor": me + 1}, device_id_type=MESH)

        pl.semaphore_wait(barrier, others + n - 1)

    def own(self, g):
        return pl.ds(pl.multiple_of(g * FINE, FINE), FINE)

    def at(self, g):
        per = self.block // FINE
        return pl.ds(
            pl.multiple_of((g // per) * 2 * self.block + lax.rem(g, per) * FINE, FINE), FINE
        )

    def low(self, g):
        per = self.block // FINE
        start = (g // per) * 2 * self.block + self.block + lax.rem(g, per) * FINE
        return pl.ds(pl.multiple_of(start, FINE), FINE)

    def right(self, source, target, lane, g):
        return pltpu.make_async_remote_copy(
            source, target, self.sems.at[2 * lane, g], self.sems.at[2 * lane + 1, g],
            device_id={"tensor": jnp.minimum(self.me + 1, self.n - 1)}, device_id_type=MESH,
        )

    def left(self, source, target, lane, g):
        return pltpu.make_async_remote_copy(
            source, target, self.sems.at[2 * lane, g], self.sems.at[2 * lane + 1, g],
            device_id={"tensor": jnp.maximum(self.me - 1, 0)}, device_id_type=MESH,
        )

    def up_copy(self, g):
        rows = self.up_in.at[self.own(g), :]
        return self.right(rows, rows, 0, g)

    def down_copy(self, g):
        rows = self.down_in.at[self.own(g), :]
        return self.left(rows, rows, 1, g)

    def up_back_copy(self, g):
        rows = self.out.at[self.at(g), :]
        return self.left(rows, rows, 2, g)

    def down_back_copy(self, g):
        rows = self.out.at[self.low(g), :]
        return self.right(rows, rows, 3, g)

    def prime(self, block=None):
        first, last = (0, self.count)
        if block is not None:
            per = self.block // FINE
            first, last = block * per, block * per + per

        @pl.when(self.me == 0)
        def _():
            @pl.loop(first, last)
            def _(g):
                self.right(
                    self.share.at[self.at(g), :], self.up_in.at[self.own(g), :], 0, g
                ).start()

        @pl.when(self.me == self.n - 1)
        def _():
            @pl.loop(first, last)
            def _(g):
                self.left(
                    self.share.at[self.low(g), :], self.down_in.at[self.own(g), :], 1, g
                ).start()

    def step(self, step):
        n, me, count = self.n, self.me, self.count
        at, low, own = self.at, self.low, self.own
        g_up = step - SKEW * (me - 1)

        @pl.when((me > 0) & (g_up >= 0) & (g_up < count))
        def _():
            self.up_copy(g_up).wait_recv()
            total = self.up_in[own(g_up), :].astype(f32) + self.share[at(g_up), :].astype(f32)

            @pl.when(me < n - 1)
            def _():
                self.up_in[own(g_up), :] = total.astype(bf16)
                self.up_copy(g_up).start()

            @pl.when(me == n - 1)
            def _():
                self.finish(total, own(g_up), at(g_up))
                self.up_back_copy(g_up).start()

        g_down = step - SKEW * (n - 2 - me)

        @pl.when((me < n - 1) & (g_down >= 0) & (g_down < count))
        def _():
            self.down_copy(g_down).wait_recv()
            total = self.down_in[own(g_down), :].astype(f32) + (
                self.share[low(g_down), :].astype(f32)
            )

            @pl.when(me > 0)
            def _():
                self.down_in[own(g_down), :] = total.astype(bf16)
                self.down_copy(g_down).start()

            @pl.when(me == 0)
            def _():
                self.finish(total, own(g_down), low(g_down))
                self.down_back_copy(g_down).start()

        g_up_back = step - self.second - SKEW * (n - 2 - me)

        @pl.when((me < n - 1) & (g_up_back >= 0) & (g_up_back < count))
        def _():
            self.up_back_copy(g_up_back).wait_recv()

            @pl.when(me > 0)
            def _():
                self.up_back_copy(g_up_back).start()

        g_down_back = step - self.second - SKEW * (me - 1)

        @pl.when((me > 0) & (g_down_back >= 0) & (g_down_back < count))
        def _():
            self.down_back_copy(g_down_back).wait_recv()

            @pl.when(me < n - 1)
            def _():
                self.down_back_copy(g_down_back).start()

    def run(self, first, last):
        @pl.loop(first, last)
        def _(step):
            self.step(step)

    def drain(self):
        n, me = self.n, self.me

        @pl.loop(0, self.count)
        def _(g):
            @pl.when(me < n - 1)
            def _():
                self.up_copy(g).wait_send()
                self.down_back_copy(g).wait_send()

            @pl.when(me > 0)
            def _():
                self.down_copy(g).wait_send()
                self.up_back_copy(g).wait_send()


def norm_back(x_ref, base, gain, out_ref, kept_ref, gain_grad_ref):
    gain_grad_ref[...] = jnp.zeros_like(gain_grad_ref)

    def finish(total, own, place):
        rows = x_ref[own, :].astype(f32)
        scaling = lax.rsqrt(jnp.mean(rows * rows, axis=1, keepdims=True) + epsilon)
        unit = rows * scaling
        gained = gain() * total
        grad = base(own, place).astype(f32) + scaling * (
            gained - unit * jnp.mean(gained * unit, axis=1, keepdims=True)
        )
        if kept_ref is not None:
            kept_ref[own, :] = grad
        out_ref[place, :] = grad.astype(out_ref.dtype)
        term = total * unit
        part = term[0:8, :]
        for i in range(1, FINE // 8):
            part = part + term[8 * i : 8 * i + 8, :]
        gain_grad_ref[...] += part

    return finish


def norm_forward(base, gain, out_ref, kept_ref):
    def finish(total, own, place):
        hidden = base(own, place).astype(f32) + total
        kept_ref[own, :] = hidden
        scaling = lax.rsqrt(jnp.mean(hidden * hidden, axis=1, keepdims=True) + epsilon)
        out_ref[place, :] = (hidden * scaling * gain()).astype(bf16)

    return finish


def line_kernel(mode, n, *refs):
    share_ref, x_ref, base_ref, gain_ref, out_ref, kept_ref, gain_grad_ref = refs[:7]
    up_in, down_in, sems = refs[7:]

    def base(own, place):
        return base_ref[own, :]

    def gain():
        return gain_ref[...]

    gain_grad_ref[...] = jnp.zeros_like(gain_grad_ref)
    if mode == "norm":
        finish = norm_forward(base, gain, out_ref, kept_ref)
    else:
        finish = norm_back(x_ref, base, gain, out_ref, kept_ref, gain_grad_ref)
    line = Line(n, share_ref, up_in, down_in, out_ref, sems, finish)
    line.greet(pltpu.get_barrier_semaphore(), 0)
    line.prime()
    line.run(0, line.steps)
    line.drain()


def line_sum(mode, call, n, share, x_own, base_own, gain):
    rows, width = share.shape
    half = rows // 2
    vmem = pl.BlockSpec(memory_space=pltpu.VMEM)
    return pl.pallas_call(
        functools.partial(line_kernel, mode, n),
        in_specs=[vmem] * 4,
        out_specs=[vmem] * 3,
        out_shape=[
            jax.ShapeDtypeStruct((rows, width), bf16),
            jax.ShapeDtypeStruct((half, width), f32),
            jax.ShapeDtypeStruct((8, width), f32),
        ],
        scratch_shapes=Line.scratch(half, width) + [Line.semaphores(half)],
        compiler_params=pltpu.CompilerParams(
            collective_id=call, has_side_effects=True, vmem_limit_bytes=40 << 20
        ),
        name="line_" + mode,
    )(share, x_own, base_own, gain)


def partner_of(index):
    return index + 1 - 2 * lax.rem(index, 2)


def to_dp(source, target, send, recv, device):
    return pltpu.make_async_remote_copy(
        source, target, send, recv, device_id={"dp": device}, device_id_type=MESH
    )


def greet_dp(barrier, groups):
    member = lax.axis_index("dp")

    @pl.loop(1, groups)
    def _(k):
        pl.semaphore_signal(
            barrier, inc=1, device_id={"dp": lax.rem(member + k, groups)}, device_id_type=MESH
        )


class ColGrad:
    TILE = 256

    def __init__(self, groups, left, right, first, recv, refs):
        (
            self.left, self.right, self.left_in, self.right_in, self.send,
            self.load_sems, self.pair_sems, self.sems,
        ) = refs
        self.left_far, self.right_far, self.recv, self.groups = left, right, recv, groups
        self.member = lax.axis_index("dp")
        self.parity = lax.rem(self.member, 2)
        self.half = right.shape[1] // 2
        self.first, self.wide = first, self.right_in.shape[1]
        self.size = self.send.shape[0] // groups
        self.items = self.wide // self.TILE

    @staticmethod
    def scratch(groups, count, rows, wide):
        return [
            pltpu.VMEM((count, rows), bf16),
            pltpu.VMEM((count, wide), bf16),
            pltpu.VMEM((count, rows), bf16),
            pltpu.VMEM((count, wide), bf16),
            pltpu.VMEM((rows, wide), bf16),
            pltpu.SemaphoreType.DMA((3,)),
            pltpu.SemaphoreType.DMA((2, 2)),
            pltpu.SemaphoreType.DMA((2, groups)),
        ]

    def halves(self, parity):
        start = pl.multiple_of(parity * self.half + self.first, self.TILE)
        return self.right_far.at[:, pl.ds(start, self.wide)]

    def loads(self):
        return (
            pltpu.make_async_copy(self.left_far, self.left, self.load_sems.at[0]),
            pltpu.make_async_copy(self.halves(self.parity), self.right, self.load_sems.at[1]),
        )

    def pair_copies(self):
        partner = partner_of(self.member)
        sems = self.pair_sems
        return (
            to_dp(self.left_far, self.left_in, sems.at[0, 0], sems.at[1, 0], partner),
            to_dp(
                self.halves(1 - self.parity), self.right_in, sems.at[0, 1], sems.at[1, 1], partner
            ),
        )

    def start(self):
        for c in self.pair_copies() + self.loads():
            c.start()

    def ready(self):
        for c in self.loads():
            c.wait()
        for c in self.pair_copies():
            c.wait_recv()

    def item(self, t):
        span = pl.ds(pl.multiple_of(t * self.TILE, self.TILE), self.TILE)
        product = rows_dot(self.left[...], self.right[:, span]) + rows_dot(
            self.left_in[...], self.right_in[:, span]
        )
        self.send[:, span] = product.astype(bf16)

    def copy(self, to, source):
        rows = pl.ds(pl.multiple_of(to * self.size, 16), self.size)
        return to_dp(
            self.send.at[rows, :], self.recv.at[source], self.sems.at[0, to],
            self.sems.at[1, source], to,
        )

    def send_all(self):
        @pl.loop(1, self.groups)
        def _(k):
            self.copy(lax.rem(self.member + k, self.groups), self.member).start()

        self.keep().start()

    def keep(self):
        own = pl.ds(pl.multiple_of(self.member * self.size, 16), self.size)
        return pltpu.make_async_copy(
            self.send.at[own, :], self.recv.at[self.member], self.load_sems.at[2]
        )

    def receive(self):
        self.keep().wait()

        @pl.loop(1, self.groups)
        def _(k):
            self.copy(0, lax.rem(self.member + k, self.groups)).wait_recv()

    def drain(self):
        for c in self.pair_copies():
            c.wait_send()

        @pl.loop(1, self.groups)
        def _(k):
            self.copy(lax.rem(self.member + k, self.groups), self.member).wait_send()


class RowGrads:
    def __init__(self, groups, left, tiles, recv, refs, deferred=0):
        (
            self.left, self.all, self.left_in, self.all_in, self.send,
            self.load_sems, self.left_sems, self.piece_sems, self.sems, self.keep_sems,
        ) = refs
        self.left_far, self.tiles, self.recv = left, tiles, recv
        self.live = len(tiles) - deferred
        if left is None:
            self.left_far = self.left
        self.member = lax.axis_index("dp")
        self.parity = lax.rem(self.member, 2)
        self.mine = self.member // 2
        self.team = groups // 2
        self.block = self.left.shape[1] // groups
        self.items = self.team * len(tiles)

    @staticmethod
    def scratch(groups, count, width, total, pieces, tiles):
        team = groups // 2
        return [
            pltpu.VMEM((count, width), bf16),
            pltpu.VMEM((count, total), bf16),
            pltpu.VMEM((count, width // 2), bf16),
            pltpu.VMEM((count, total), bf16),
            pltpu.VMEM((team, width // groups, total), bf16),
            pltpu.SemaphoreType.DMA((1 + pieces,)),
            pltpu.SemaphoreType.DMA((2, team)),
            pltpu.SemaphoreType.DMA((2, pieces)),
            pltpu.SemaphoreType.DMA((2, tiles, team)),
            pltpu.SemaphoreType.DMA((tiles,)),
        ]

    def columns(self, j):
        return pl.ds(pl.multiple_of(j * self.block, self.block), self.block)

    def left_load(self):
        return pltpu.make_async_copy(self.left_far, self.left, self.load_sems.at[0])

    def piece_load(self, p, source, span):
        return pltpu.make_async_copy(source, self.all.at[:, span], self.load_sems.at[1 + p])

    def left_copy(self, q):
        return to_dp(
            self.left_far.at[:, self.columns(2 * q + 1 - self.parity)],
            self.left_in.at[:, self.columns(q)],
            self.left_sems.at[0, q], self.left_sems.at[1, q], partner_of(self.member),
        )

    def piece_copy(self, p, source, span, rows=slice(None)):
        return to_dp(
            source, self.all_in.at[rows, span], self.piece_sems.at[0, p], self.piece_sems.at[1, p],
            partner_of(self.member),
        )

    def start_left(self):
        @pl.loop(0, self.team)
        def _(q):
            self.left_copy(q).start()

        self.left_load().start()

    def ready_left(self):
        self.left_load().wait()

        @pl.loop(0, self.team)
        def _(q):
            self.left_copy(q).wait_recv()

    def copy(self, t, to, source):
        start, wide = self.tiles[t]
        span = pl.ds(start, wide)
        return to_dp(
            self.send.at[to, :, span], self.recv.at[source, :, span],
            self.sems.at[0, t, to], self.sems.at[1, t, source], 2 * to + self.parity,
        )

    def item(self, w):
        count = len(self.tiles)
        k = w // count
        to = lax.rem(self.mine + 1 + k, self.team)
        for t in range(count):
            start, wide = self.tiles[t]

            @pl.when((w >= 0) & (w < self.items) & (lax.rem(w, count) == t))
            def _():
                span = pl.ds(start, wide)
                product = rows_dot(
                    self.left[:, self.columns(2 * to + self.parity)], self.all[:, span]
                ) + rows_dot(self.left_in[:, self.columns(to)], self.all_in[:, span])
                self.send[to, :, span] = product.astype(bf16)

                if t < self.live:
                    @pl.when(k < self.team - 1)
                    def _():
                        self.copy(t, to, self.mine).start()

                    @pl.when(k == self.team - 1)
                    def _():
                        self.keep(t).start()

    def keep(self, t):
        start, wide = self.tiles[t]
        span = pl.ds(start, wide)
        return pltpu.make_async_copy(
            self.send.at[self.mine, :, span], self.recv.at[self.mine, :, span], self.keep_sems.at[t]
        )

    def receive(self):
        for t in range(self.live):
            self.keep(t).wait()

            @pl.loop(1, self.team)
            def _(k):
                self.copy(t, 0, lax.rem(self.mine + k, self.team)).wait_recv()

    def drain(self):
        @pl.loop(0, self.team)
        def _(q):
            self.left_copy(q).wait_send()

        for t in range(self.live):
            @pl.loop(1, self.team)
            def _(k):
                self.copy(t, lax.rem(self.mine + k, self.team), self.mine).wait_send()


def splitter(refs):
    refs = list(refs)

    def take(k):
        out = refs[:k]
        del refs[:k]
        return out

    return take


def one_hot(index, base, shape, dim):
    return (index == base + lax.broadcasted_iota(jnp.int32, shape, dim)).astype(f32).astype(bf16)


def thirds(source, terms, target):
    third = LANES // 4
    size = source.shape[0]
    target[...] = jnp.zeros_like(target)
    for i in range(terms):
        target[i * third : i * third + size, :] = source[...]


class Exchange:
    def __init__(self, groups, cuts, sent, came, sems):
        self.groups, self.sent, self.came, self.sems = groups, sent, came, sems
        self.spans = [pl.ds(a, b - a) for a, b in zip((0,) + cuts, cuts + (sent.shape[1],))]
        self.member = lax.axis_index("dp")
        self.cap = sent.shape[0] // groups

    @staticmethod
    def scratch(groups, slots, width, pieces):
        return [
            pltpu.VMEM((slots, width), bf16),
            pltpu.VMEM((slots, width), bf16),
            pltpu.SemaphoreType.DMA((2, pieces, groups)),
        ]

    def part(self, j):
        return pl.ds(pl.multiple_of(j * self.cap, self.cap), self.cap)

    def copy(self, p, to, source):
        span = self.spans[p]
        return to_dp(
            self.sent.at[self.part(to), span], self.came.at[self.part(source), span],
            self.sems.at[0, p, to], self.sems.at[1, p, source], to,
        )

    def send(self, p, index_ref, dim, source, between=None):
        span = self.spans[p]
        groups, count = self.groups, source.shape[0]
        rows = self.sent.shape[0] // 2

        @pl.loop(0, 2)
        def _(h):
            at = pl.ds(pl.multiple_of(h * rows, rows), rows)
            if dim == 0:
                pick = one_hot(index_ref[...], h * rows, (rows, count), 0)
            else:
                pick = one_hot(index_ref[at, :], 0, (rows, count), 1)
            self.sent[at, span] = dot(pick, source[:, span]).astype(bf16)

            @pl.loop(0, groups // 2)
            def _(k):
                to = h * (groups // 2) + lax.rem(self.member + k, groups // 2)

                @pl.when(to != self.member)
                def _():
                    self.copy(p, to, self.member).start()

            if between is not None:
                between(h)

        own = self.part(self.member)
        self.came[own, span] = self.sent[own, span]

    def receive(self, p):
        @pl.loop(1, self.groups)
        def _(k):
            self.copy(p, 0, lax.rem(self.member + k, self.groups)).wait_recv()

    def drain(self):
        for p in range(len(self.spans)):
            @pl.loop(1, self.groups)
            def _(k):
                self.copy(p, lax.rem(self.member + k, self.groups), self.member).wait_send()


def place_rows(slot_row_ref, came, held, span, between=None):
    positions, slots = held.shape[0], came.shape[0]
    rows = positions // 2

    @pl.loop(0, 2)
    def _(h):
        at = pl.ds(pl.multiple_of(h * rows, rows), rows)
        pick = one_hot(slot_row_ref[...], h * rows, (rows, slots), 0)
        held[at, span] = dot(pick, came[:, span]).astype(bf16)
        if between is not None:
            between(h)


def front_kernel(groups, dk, dv, *refs):
    take = splitter(refs)
    lengths_ref, slot_rows_ref, tokens_ref, gains_ref, up_rows_ref, down_rows_ref = take(6)
    weights_far = take(3)
    gate_far, out_far = take(2)
    spilled = take(6)
    (share_ref,) = take(1)
    send_row_ref, send_column_ref, slot_row_ref, slot_column_ref = take(4)
    normed_ref, gate_ref, attended_ref, gated_ref, held_ref, states_ref = kept = take(6)
    weight_ref, gate_weight_ref, out_weight_ref = take(3)
    rows_out, state, result, rank_ref, up_ref, bias_ref, latent_ref = take(7)
    slots_ref, load_sems = take(2)
    go = Exchange(groups, (2 * dk,), *take(3))
    back = Exchange(groups, (), *take(3))
    (spill_sems,) = take(1)
    member = lax.axis_index("dp")
    count, width = tokens_ref.shape
    cap = OWN_CAP // groups
    half = count // 2
    spills = [
        pltpu.make_async_copy(kept[i], spilled[i], spill_sems.at[i]) for i in range(6)
    ]

    def spill(*which):
        for i in which:
            spills[i].start()

    end0 = lengths_ref[0, 0]
    end1 = end0 + lengths_ref[0, 1]
    ends = (end0, end1, end1 + lengths_ref[0, 2])
    third = LANES // 4

    loads = []
    offset = 0
    for i, far in enumerate(weights_far):
        wide = far.shape[1]
        loads.append(
            pltpu.make_async_copy(far, weight_ref.at[:, pl.ds(offset, wide)], load_sems.at[i])
        )
        offset += wide
    later = [
        pltpu.make_async_copy(gate_far, gate_weight_ref, load_sems.at[4]),
        pltpu.make_async_copy(out_far, out_weight_ref, load_sems.at[5]),
    ]
    for c in loads + later:
        c.start()
    barrier = pltpu.get_barrier_semaphore()
    greet_dp(barrier, groups)
    pl.semaphore_wait(barrier, groups - 1)

    pieces = count // LANES
    for i in range(pieces):
        slots_ref[:, i * LANES : (i + 1) * LANES] = slot_rows_ref[pl.ds(i, groups, stride=pieces), :]
    owners = slots_ref[...] // OWN_CAP
    mine = owners == member
    my_slots = slots_ref[pl.ds(member, 1), :]
    my_owner = my_slots // OWN_CAP
    device = lax.broadcasted_iota(jnp.int32, (groups, count), 0)
    chosen = (my_owner == device).astype(f32)
    before = (
        lax.broadcasted_iota(jnp.int32, (count, count), 0)
        < lax.broadcasted_iota(jnp.int32, (count, count), 1)
    ).astype(f32).astype(bf16)
    send_rank = jnp.sum(chosen * dot(chosen.astype(bf16), before), axis=0, keepdims=True)
    send_row = my_owner * cap + send_rank.astype(jnp.int32)
    send_row_ref[...] = send_row
    send_column_ref[...] = jnp.transpose(
        jnp.broadcast_to(send_row.astype(f32), (8, count))
    )[:, :1].astype(jnp.int32)
    rank_ref[...] = jnp.where(mine, dot(mine.astype(f32).astype(bf16), before), -1.0)

    bias_ref[...] = gains_ref[2:3, dv : dv + dk]
    thirds(up_rows_ref, 3, up_ref)
    thirds(down_rows_ref, 3, latent_ref)

    tile = count // 5

    @pl.loop(0, 5)
    def _(i):
        at = pl.ds(pl.multiple_of(i * tile, tile), tile)
        rows = tokens_ref[at, :].astype(f32)
        scaling = lax.rsqrt(jnp.mean(rows * rows, axis=1, keepdims=True) + epsilon)
        normed_ref[at, :] = (rows * scaling * gains_ref[0:1, :]).astype(bf16)

    for c in loads[:2]:
        c.wait()
    body = 2 * dk + dv

    spill(0)

    def project(first, last):
        @pl.loop(first // 256, last // 256)
        def _(i):
            to = pl.ds(pl.multiple_of(i * 256, 256), 256)
            rows_out[:, to] = dot(normed_ref[...], weight_ref[:, to]).astype(bf16)

    project(0, 2 * dk)
    go.send(0, send_row_ref, 0, rows_out)
    for c in loads[2:]:
        c.wait()
    project(2 * dk, body)
    latent = dot_t(normed_ref[...], latent_ref[...])
    high = latent.astype(bf16).astype(f32)
    middle = (latent - high).astype(bf16).astype(f32)
    lane = lax.broadcasted_iota(jnp.int32, latent.shape, 1)
    rows_out[:, body:] = jnp.where(
        lane < third, high, jnp.where(lane < 2 * third, middle, latent - high - middle)
    ).astype(bf16)
    go.send(1, send_row_ref, 0, rows_out)

    for c in later:
        c.wait()

    @pl.loop(0, dv // 256)
    def _(i):
        to = pl.ds(pl.multiple_of(i * 256, 256), 256)
        gate_ref[:, to] = dot(normed_ref[...], gate_weight_ref[:, to])

    spill(1)

    @pl.loop(0, groups)
    def _(j):
        rank = rank_ref[pl.ds(j, 1), :]
        local = (lax.rem(slots_ref[pl.ds(j, 1), :], OWN_CAP) - OWN_CAP).astype(f32)
        wanted = lax.broadcasted_iota(jnp.int32, (cap, count), 0).astype(f32)
        at = jnp.sum(jnp.where(rank == wanted, local, 0.0), axis=1, keepdims=True)
        slot_column_ref[go.part(j), :] = at.astype(jnp.int32) + OWN_CAP

    slots = slot_row_ref.shape[1]
    slot_row_ref[...] = jnp.transpose(
        jnp.broadcast_to(slot_column_ref[...].astype(f32), (slots, LANES))
    )[:1, :].astype(jnp.int32)
    state[...] = jnp.zeros_like(state)
    for p in range(2):
        go.receive(p)
        place_rows(slot_row_ref, go.came, held_ref, go.spans[p])

    @pl.loop(0, held_ref.shape[0] // SPAN)
    def _(step):
        span_forward(dk, dv, step, ends, held_ref, up_ref, bias_ref, state, states_ref, result)

    back.send(0, slot_column_ref, 1, result)
    spill(4, 5)
    back.receive(0)

    def head_rows(at):
        pick = one_hot(send_column_ref[at, :], 0, (half, slots), 1)
        attended = dot(pick, back.came[...])
        attended_ref[at, :] = attended.astype(bf16)
        gate = gate_ref[at, :]
        scaling = lax.rsqrt(jnp.mean(attended * attended, axis=1, keepdims=True) + head_floor)
        gated = attended * scaling * gains_ref[2:3, :dv] * (gate * jax.nn.sigmoid(gate))
        gated_ref[at, :] = gated.astype(bf16)

        @pl.loop(0, width // 512)
        def _(i):
            to = pl.ds(pl.multiple_of(i * 512, 512), 512)
            share_ref[at, to] = dot(gated_ref[at, :], out_weight_ref[:, to]).astype(bf16)

    @pl.loop(0, 2)
    def _(i):
        head_rows(pl.ds(pl.multiple_of(i * half, half), half))

    spill(2, 3)
    go.drain()
    back.drain()
    for c in spills:
        c.wait()


def front(
    call, groups, lengths, slots, tokens, gains, up_rows, down_rows, weights, gate_weight,
    out_weight,
):
    count, width = tokens.shape
    dk, dv = weights[0].shape[1], weights[2].shape[1]
    body = 2 * dk + dv
    wide = body + LANES
    spans = OWN_CAP // SPAN
    vmem = pl.BlockSpec(memory_space=pltpu.VMEM)
    far = pl.BlockSpec(memory_space=pl.ANY)
    smem = pl.BlockSpec(memory_space=pltpu.SMEM)
    shape = jax.ShapeDtypeStruct
    saved = [
        shape((count, width), bf16),
        shape((count, dv), f32),
        shape((count, dv), bf16),
        shape((count, dv), bf16),
        shape((OWN_CAP, wide), bf16),
        shape((spans, dk, dv), bf16),
    ]
    return pl.pallas_call(
        functools.partial(front_kernel, groups, dk, dv),
        in_specs=[smem] + [vmem] * 5 + [far] * 5,
        out_specs=[far] * 6 + [vmem] * 5,
        out_shape=[
            *saved,
            shape((count, width), bf16),
            shape((1, count), jnp.int32),
            shape((count, 1), jnp.int32),
            shape((1, OWN_CAP), jnp.int32),
            shape((OWN_CAP, 1), jnp.int32),
        ],
        scratch_shapes=[pltpu.VMEM(a.shape, a.dtype) for a in saved]
        + [
            pltpu.VMEM((width, body), bf16),
            pltpu.VMEM((width, dv), bf16),
            pltpu.VMEM((dv, width), bf16),
            pltpu.VMEM((count, wide), bf16),
            pltpu.VMEM((dk, dv), f32),
            pltpu.VMEM((OWN_CAP, dv), bf16),
            pltpu.VMEM((groups, count), f32),
            pltpu.VMEM((LANES, dk), bf16),
            pltpu.VMEM((1, dk), f32),
            pltpu.VMEM((LANES, width), bf16),
            pltpu.VMEM((groups, count), jnp.int32),
            pltpu.SemaphoreType.DMA((8,)),
        ]
        + Exchange.scratch(groups, OWN_CAP, wide, 2)
        + Exchange.scratch(groups, OWN_CAP, dv, 1)
        + [pltpu.SemaphoreType.DMA((6,))],
        compiler_params=pltpu.CompilerParams(
            collective_id=call, has_side_effects=True, vmem_limit_bytes=60 << 20
        ),
        cost_estimate=pl.CostEstimate(
            flops=12_000_000_000, bytes_accessed=200_000_000, transcendentals=4_000_000
        ),
        name="front",
    )(
        lengths, slots, tokens, gains, up_rows, down_rows, *weights, gate_weight, out_weight,
    )


def back_feed_kernel(n, groups, tiles, *refs):
    take = splitter(refs)
    gains_ref, first_share_ref, tokens_far, cotangent_far, gate_far, up_far, down_far = take(7)
    out_ref, kept_ref, gain_grad_ref = take(3)
    recv, more_far, active_far, layer_far, hidden_far = take(5)
    active_ref, layer_ref, first_up, first_down, up_in, down_in = take(6)
    hidden_ref, tokens_ref, cotangent_ref, share_ref, weight_ref, d_active_ref = take(6)
    load_sems, weight_sems, first_sems, sems = take(4)
    rows = RowGrads(groups, None, tiles, recv, take(10), deferred=1)
    feed_ref = rows.left
    count, width = share_ref.shape
    wide = active_ref.shape[1]
    full, rest = wide // 256, wide % 256
    pieces = full + (rest > 0)
    half = count // 2
    first_line = Line(
        n, first_share_ref, first_up, first_down, feed_ref, first_sems,
        norm_forward(
            lambda own, place: tokens_ref[own, :], lambda: gains_ref[1:2, :], feed_ref, hidden_ref
        ),
    )
    line = Line(
        n, share_ref, up_in, down_in, out_ref, sems,
        norm_back(
            hidden_ref, lambda own, place: cotangent_ref[place, :], lambda: gains_ref[1:2, :],
            out_ref, kept_ref, gain_grad_ref,
        ),
    )
    token_loads = first_line.own_copies(tokens_far, tokens_ref, [load_sems.at[0], load_sems.at[1]])
    cotangent_load = pltpu.make_async_copy(cotangent_far, cotangent_ref, load_sems.at[2])
    down_load = pltpu.make_async_copy(
        down_far, weight_ref.at[pl.ds(0, wide), pl.ds(0, width)], load_sems.at[3]
    )
    active_spill = pltpu.make_async_copy(active_ref, active_far, load_sems.at[4])
    layer_spill = pltpu.make_async_copy(layer_ref, layer_far, load_sems.at[5])
    hidden_spill = pltpu.make_async_copy(hidden_ref, hidden_far, load_sems.at[6])
    more_start, more_wide = tiles[-1]
    more_spill = pltpu.make_async_copy(
        rows.send.at[:, :, pl.ds(more_start, more_wide)], more_far, load_sems.at[7]
    )

    def spans(i, size):
        start = pl.multiple_of(i * 256, 256)
        return pl.ds(start, size), pl.ds(pl.multiple_of(wide + start, LANES), size)

    def weight_loads(i, size):
        gate_span, up_span = spans(i, size)
        return (
            pltpu.make_async_copy(
                gate_far.at[:, gate_span], weight_ref.at[:, gate_span], weight_sems.at[0, i]
            ),
            pltpu.make_async_copy(
                up_far.at[:, gate_span], weight_ref.at[:, up_span], weight_sems.at[1, i]
            ),
        )

    def block_rows(b):
        return pl.ds(b * half, half)

    def piece_copies(b, i, size):
        gate_span, up_span = spans(i, size)
        at = block_rows(b)
        return tuple(
            rows.piece_copy(2 * (b * pieces + i) + j, rows.all.at[at, span], span, at)
            for j, span in enumerate((gate_span, up_span))
        )

    def each(action):
        @pl.loop(0, full)
        def _(i):
            action(i, 256)

        if rest:
            action(full, rest)

    def at_item(w, action):
        @pl.when((w >= 0) & (w < full))
        def _():
            action(w, 256)

        if rest:
            @pl.when(w == full)
            def _():
                action(full, rest)

    down_load.start()
    cotangent_load.start()
    for c in token_loads:
        c.start()
    barrier = pltpu.get_barrier_semaphore()
    greet_dp(barrier, groups)
    line.greet(barrier, groups - 1)
    first_line.prime()
    for c in token_loads:
        c.wait()

    def make_d_active(i, size):
        span, _ = spans(i, size)
        d_active_ref[:, span] = dot_t(
            cotangent_ref[...], weight_ref[span, pl.ds(0, width)]
        ).astype(bf16)

    def start_weights(i, size):
        for c in weight_loads(i, size):
            c.start()

    def hidden_units(b, i, size):
        if b == 0:
            for c in weight_loads(i, size):
                c.wait()
        gate_span, up_span = spans(i, size)
        at = block_rows(b)
        gate = dot(feed_ref[at, :], weight_ref[:, gate_span])
        up = dot(feed_ref[at, :], weight_ref[:, up_span])
        d_active = d_active_ref[at, gate_span].astype(f32)
        sigmoid = jax.nn.sigmoid(gate)
        swish = gate * sigmoid
        active_ref[at, gate_span] = (swish * up).astype(bf16)
        rows.all[at, gate_span] = (
            d_active * up * sigmoid * (1.0 + gate * (1.0 - sigmoid))
        ).astype(bf16)
        rows.all[at, up_span] = (d_active * swish).astype(bf16)
        for c in piece_copies(b, i, size):
            c.start()

    share_items = width // 256

    def make_share(b, w):
        @pl.when((w >= 0) & (w < share_items))
        def _():
            to = pl.ds(pl.multiple_of(w * 256, 256), 256)
            at = block_rows(b)
            share_ref[at, to] = dot_t(rows.all[at, :], weight_ref[to, :]).astype(bf16)

    per = first_line.block // FINE
    arrived = first_line.second + SKEW * (n - 2) + per
    d_first = 3

    @pl.loop(0, first_line.steps)
    def _(step):
        first_line.step(step)

        @pl.when(step == d_first)
        def _():
            down_load.wait()
            cotangent_load.wait()

        at_item(step - d_first, make_d_active)

        @pl.when(step == d_first + pieces)
        def _():
            each(start_weights)

        at_item(step - arrived, lambda i, size: hidden_units(0, i, size))
        w = 2 * (step - arrived - pieces)
        make_share(0, w)
        make_share(0, w + 1)

    done_share = 2 * (first_line.steps - arrived - pieces)

    @pl.loop(done_share, max(share_items, done_share))
    def _(w):
        make_share(0, w)

    line.prime(0)
    hidden_spill.start()

    @pl.loop(0, rows.team)
    def _(q):
        rows.left_copy(q).start()

    layer_items = width // 512
    first_work = 8

    def row_work(w):
        @pl.when(w == 0)
        def _():
            @pl.loop(0, rows.team)
            def _(q):
                rows.left_copy(q).wait_recv()

            for b in range(2):
                def arrive(i, size, b=b):
                    for c in piece_copies(b, i, size):
                        c.wait_recv()

                each(arrive)

        rows.item(w)

    @pl.loop(0, per)
    def _(step):
        line.step(step)
        at_item(step, lambda i, size: hidden_units(1, i, size))
        w = 2 * (step - pieces)
        make_share(1, w)
        make_share(1, w + 1)
        row_work(step - first_work)

    done_more = 2 * (per - pieces)

    @pl.loop(done_more, max(share_items, done_more))
    def _(w):
        make_share(1, w)

    line.prime(1)
    active_spill.start()
    down_load.start()

    @pl.loop(per, line.steps)
    def _(step):
        line.step(step)
        w = step - first_work
        row_work(w)

        @pl.when(w == rows.items)
        def _():
            more_spill.start()
            down_load.wait()

        layer_item = w - rows.items

        @pl.when((layer_item >= 0) & (layer_item < layer_items))
        def _():
            to = pl.ds(pl.multiple_of(layer_item * 512, 512), 512)
            layer_ref[:, to] = dot(active_ref[...], weight_ref[pl.ds(0, wide), to]).astype(bf16)

        @pl.when(layer_item == layer_items)
        def _():
            layer_spill.start()

    rows.receive()
    first_line.drain()
    line.drain()
    rows.drain()
    for c in (active_spill, layer_spill, hidden_spill, more_spill):
        c.wait()
    for b in range(2):
        def sent(i, size, b=b):
            for c in piece_copies(b, i, size):
                c.wait_send()

        each(sent)


def back_feed(call, n, groups, gains, share, tokens, cotangent, feed_gate, feed_up, feed_down):
    count, width = share.shape
    half = count // 2
    wide = feed_gate.shape[1]
    pieces = (wide + 255) // 256
    cut = (wide // 2 + LANES - 1) // LANES * LANES
    tiles = [(0, cut), (cut, wide - cut), (wide, cut), (wide + cut, wide - cut)]
    team, per = groups // 2, width // groups
    vmem = pl.BlockSpec(memory_space=pltpu.VMEM)
    far = pl.BlockSpec(memory_space=pl.ANY)
    shape = jax.ShapeDtypeStruct
    return pl.pallas_call(
        functools.partial(back_feed_kernel, n, groups, tiles),
        in_specs=[vmem] * 2 + [far] * 5,
        out_specs=[vmem] * 3 + [far] * 5,
        out_shape=[
            shape((count, width), bf16),
            shape((half, width), f32),
            shape((8, width), f32),
            shape((team, per, wide + cut), bf16),
            shape((team, per, wide - cut), bf16),
            shape((count, wide), bf16),
            shape((count, width), bf16),
            shape((half, width), f32),
        ],
        scratch_shapes=[pltpu.VMEM((count, wide), bf16), pltpu.VMEM((count, width), bf16)]
        + Line.scratch(half, width)
        + Line.scratch(half, width)
        + [
            pltpu.VMEM((half, width), f32),
            pltpu.VMEM((half, width), bf16),
            pltpu.VMEM((count, width), bf16),
            pltpu.VMEM((count, width), bf16),
            pltpu.VMEM((width, 2 * wide), bf16),
            pltpu.VMEM((count, wide), bf16),
            pltpu.SemaphoreType.DMA((8,)),
            pltpu.SemaphoreType.DMA((2, pieces)),
            Line.semaphores(half),
            Line.semaphores(half),
        ]
        + RowGrads.scratch(groups, count, width, 2 * wide, 4 * pieces, len(tiles)),
        compiler_params=pltpu.CompilerParams(
            collective_id=call, has_side_effects=True, vmem_limit_bytes=61 << 20
        ),
        cost_estimate=pl.CostEstimate(
            flops=30_000_000_000, bytes_accessed=200_000_000, transcendentals=0
        ),
        name="back_feed",
    )(gains, share, tokens, cotangent, feed_gate, feed_up, feed_down)


class SmallSum:
    def __init__(self, n, groups, wide, near, near_all, wide_out, near_out, refs):
        (
            self.wide_in, self.near_in, self.wide_line, self.near_line, self.sems, self.line_sems,
        ) = refs
        self.n, self.groups, self.near_all = n, groups, near_all
        self.wide, self.near, self.wide_out, self.near_out = wide, near, wide_out, near_out
        self.member, self.place = lax.axis_index("dp"), lax.axis_index("tensor")
        self.block = wide.shape[1] // groups

    @staticmethod
    def scratch(n, groups, wide, near):
        block = wide[1] // groups
        return [
            pltpu.VMEM((groups, wide[0], block), f32),
            pltpu.VMEM(near, f32),
            pltpu.VMEM((n, wide[0], block), f32),
            pltpu.VMEM((n,) + near[1:], f32),
            pltpu.SemaphoreType.DMA((2, 2, groups)),
            pltpu.SemaphoreType.DMA((2, 2, n)),
        ]

    def greet(self, barrier):
        n, place = self.n, self.place
        for k in range(2, n):
            @pl.when(place + k < n)
            def _():
                pl.semaphore_signal(
                    barrier, inc=1, device_id={"tensor": place + k}, device_id_type=MESH
                )

            @pl.when(place - k >= 0)
            def _():
                pl.semaphore_signal(
                    barrier, inc=1, device_id={"tensor": place - k}, device_id_type=MESH
                )

    def cut(self, j):
        return pl.ds(pl.multiple_of(j * self.block, self.block), self.block)

    def copies(self, to, source):
        return (
            to_dp(
                self.wide.at[:, self.cut(to)], self.wide_in.at[source],
                self.sems.at[0, 0, to], self.sems.at[1, 0, source], to,
            ),
            to_dp(
                self.near.at[to], self.near_in.at[source],
                self.sems.at[0, 1, to], self.sems.at[1, 1, source], to,
            ),
        )

    def line_copies(self, to, source):
        return tuple(
            pltpu.make_async_remote_copy(
                line.at[self.place], line.at[source], self.line_sems.at[0, i, to],
                self.line_sems.at[1, i, source], device_id={"tensor": to}, device_id_type=MESH,
            )
            for i, line in enumerate((self.wide_line, self.near_line))
        )

    def send(self):
        @pl.loop(1, self.groups)
        def _(k):
            for c in self.copies(lax.rem(self.member + k, self.groups), self.member):
                c.start()

        self.wide_in[pl.ds(self.member, 1)] = self.wide[:, self.cut(self.member)][None]
        self.near_in[pl.ds(self.member, 1)] = self.near[pl.ds(self.member, 1)]

    def forward(self):
        @pl.loop(1, self.groups)
        def _(k):
            for c in self.copies(0, lax.rem(self.member + k, self.groups)):
                c.wait_recv()

        for came, line in ((self.wide_in, self.wide_line), (self.near_in, self.near_line)):
            total = came[0]
            for j in range(1, self.groups):
                total = total + came[j]
            line[pl.ds(self.place, 1)] = total[None]

        @pl.loop(1, self.n)
        def _(k):
            for c in self.line_copies(lax.rem(self.place + k, self.n), self.place):
                c.start()

    def receive(self):
        @pl.loop(1, self.n)
        def _(k):
            for c in self.line_copies(0, lax.rem(self.place + k, self.n)):
                c.wait_recv()

        total = self.wide_line[0]
        for j in range(1, self.n):
            total = total + self.wide_line[j]
        self.wide_out[...] = total
        own = self.near_line[pl.ds(self.place, 1)][0]
        total = self.near_line[0]
        for j in range(1, self.n):
            total = total + self.near_line[j]
        row = lax.broadcasted_iota(jnp.int32, own.shape, 0)
        self.near_out[...] = jnp.where(row < self.near_all, total, own)

    def drain(self):
        @pl.loop(1, self.groups)
        def _(k):
            for c in self.copies(lax.rem(self.member + k, self.groups), self.member):
                c.wait_send()

        @pl.loop(1, self.n)
        def _(k):
            for c in self.line_copies(lax.rem(self.place + k, self.n), self.place):
                c.wait_send()


def back_mixer_kernel(n, groups, widths, near_all, tiles, *refs):
    take = splitter(refs)
    gains_ref, near_ref, down_rows_ref, x_far, base_far, left_far = take(6)
    parts = take(2)
    col_left, col_right, more_far = take(3)
    weights = take(len(widths))
    out_ref, wide_out, near_out, recv, col_recv, more_recv = take(6)
    more_ref, more_sems, more_load_sems = take(3)
    up_in, down_in, x_ref, base_ref, share_ref, wide_ref, gain_grad_ref = take(7)
    weight_ref, latent_ref, load_sems, sems = take(4)
    rows = RowGrads(groups, left_far, tiles, recv, take(10))
    part_spans = [
        pl.ds(0, parts[0].shape[1]), pl.ds(parts[0].shape[1], parts[1].shape[1])
    ]
    part_loads = [rows.piece_load(i, parts[i], part_spans[i]) for i in range(2)]
    part_copies = [rows.piece_copy(i, parts[i], part_spans[i]) for i in range(2)]
    cols = ColGrad(groups, col_left, col_right, 0, col_recv, take(8))
    small = SmallSum(n, groups, wide_ref, near_ref, near_all, wide_out, near_out, take(6))
    finish = norm_back(
        x_ref, lambda own, place: base_ref[own, :], lambda: gains_ref[0:1, :], out_ref, None,
        gain_grad_ref,
    )
    line = Line(n, share_ref, up_in, down_in, out_ref, sems, finish)
    loads = line.own_copies(x_far, x_ref, [load_sems.at[0], more_load_sems.at[0]])
    loads.append(pltpu.make_async_copy(base_far, base_ref, load_sems.at[1]))
    more_load = pltpu.make_async_copy(more_far, more_ref, more_load_sems.at[1])

    def more_copy(to, source):
        return to_dp(
            more_ref.at[to], more_recv.at[source], more_sems.at[0, to], more_sems.at[1, source],
            2 * to + rows.parity,
        )

    more_keep = pltpu.make_async_copy(
        more_ref.at[rows.mine], more_recv.at[rows.mine], more_load_sems.at[2]
    )
    more_load.start()
    weight_loads = []
    offset = 0
    for i, wide in enumerate(widths):
        if i == len(widths) - 1:
            latent_at = offset
            offset += LANES
        weight_loads.append(
            pltpu.make_async_copy(
                weights[i], weight_ref.at[:, pl.ds(offset, wide)], load_sems.at[2 + i]
            )
        )
        offset += wide
    for c in part_loads + weight_loads:
        c.start()
    thirds(down_rows_ref, 2, latent_ref)
    weight_ref[:, pl.ds(latent_at, LANES)] = jnp.transpose(latent_ref[...].astype(f32)).astype(bf16)
    barrier = pltpu.get_barrier_semaphore()
    greet_dp(barrier, groups)
    small.greet(barrier)
    line.greet_all(barrier, groups - 1)
    rows.start_left()
    for c in part_copies:
        c.start()
    cols.start()
    for c in loads:
        c.start()
    more_load.wait()
    more_keep.start()

    @pl.loop(1, rows.team)
    def _(k):
        more_copy(lax.rem(rows.mine + k, rows.team), rows.mine).start()

    for c in part_loads + weight_loads:
        c.wait()

    count, width = share_ref.shape
    tile_rows, tile_columns = count // 2, 512
    across = width // tile_columns

    for c in loads:
        c.wait()
    for b in range(2):
        at = pl.ds(b * tile_rows, tile_rows)

        @pl.loop(0, across)
        def _(i):
            to = pl.ds(pl.multiple_of(i * tile_columns, tile_columns), tile_columns)
            share_ref[at, to] = dot_t(rows.all[at, :], weight_ref[to, :]).astype(bf16)

        line.prime(b)

    third = LANES // 4
    first_cols = rows.items
    last_item = first_cols + cols.items

    @pl.loop(0, line.steps)
    def _(step):
        line.step(step)

        @pl.when(step == 0)
        def _():
            rows.ready_left()
            for c in part_copies:
                c.wait_recv()

        rows.item(step)

        @pl.when(step == first_cols)
        def _():
            cols.ready()

        @pl.when((step >= first_cols) & (step < last_item))
        def _():
            cols.item(step - first_cols)

        @pl.when(step == last_item)
        def _():
            cols.send_all()
            product = rows_dot(rows.all[:, pl.ds(latent_at, LANES)], rows.left[...])
            wide_ref[:16, :] = product[:16, :] + product[third : third + 16, :]

        @pl.when(step == line.count + SKEW * (n - 2) + 2)
        def _():
            wide_ref[16:, :] = gain_grad_ref[...]
            small.send()

        @pl.when(step == line.second + 14)
        def _():
            small.forward()

    more_keep.wait()

    @pl.loop(1, rows.team)
    def _(k):
        more_copy(0, lax.rem(rows.mine + k, rows.team)).wait_recv()
        more_copy(lax.rem(rows.mine + k, rows.team), rows.mine).wait_send()

    rows.receive()
    cols.receive()
    small.receive()
    line.drain()
    rows.drain()
    for c in part_copies:
        c.wait_send()
    cols.drain()
    small.drain()


def back_mixer(
    call, n, groups, gains, near, near_all, down_rows, x, base_own, left, parts, pair, weights
):
    count, width = left.shape
    half = count // 2
    widths = [w.shape[1] for w in weights]
    total = sum(part.shape[1] for part in parts)
    start = parts[0].shape[1]
    tiles = [(0, 512), (512, 512), (start, parts[1].shape[1])]
    col_rows = pair[0].shape[1]
    vmem = pl.BlockSpec(memory_space=pltpu.VMEM)
    far = pl.BlockSpec(memory_space=pl.ANY)
    wide_shape = (24, width)
    return pl.pallas_call(
        functools.partial(back_mixer_kernel, n, groups, widths, near_all, tiles),
        in_specs=[vmem] * 3 + [far] * (8 + len(weights)),
        out_specs=[vmem] * 3 + [far] * 3,
        out_shape=[
            jax.ShapeDtypeStruct((count, width), bf16),
            jax.ShapeDtypeStruct((24, width // groups), f32),
            jax.ShapeDtypeStruct(near.shape[1:], f32),
            jax.ShapeDtypeStruct((groups // 2, width // groups, total), bf16),
            jax.ShapeDtypeStruct((groups, col_rows // groups, width // 2), bf16),
            jax.ShapeDtypeStruct(pair[2].shape, bf16),
        ],
        scratch_shapes=[
            pltpu.VMEM(pair[2].shape, bf16),
            pltpu.SemaphoreType.DMA((2, groups // 2)),
            pltpu.SemaphoreType.DMA((3,)),
        ]
        + Line.scratch(half, width)
        + [
            pltpu.VMEM((half, width), x.dtype),
            pltpu.VMEM((half, width), base_own.dtype),
            pltpu.VMEM((count, width), bf16),
            pltpu.VMEM(wide_shape, f32),
            pltpu.VMEM((8, width), f32),
            pltpu.VMEM((width, total), bf16),
            pltpu.VMEM((LANES, width), bf16),
            pltpu.SemaphoreType.DMA((2 + len(weights),)),
            Line.semaphores(half),
        ]
        + RowGrads.scratch(groups, count, width, total, 2, len(tiles))
        + ColGrad.scratch(groups, count, col_rows, width // 2)
        + SmallSum.scratch(n, groups, wide_shape, near.shape),
        compiler_params=pltpu.CompilerParams(
            collective_id=call, has_side_effects=True, vmem_limit_bytes=61 << 20
        ),
        cost_estimate=pl.CostEstimate(
            flops=12_000_000_000, bytes_accessed=200_000_000, transcendentals=0
        ),
        name="back_mixer",
    )(gains, near, down_rows, x, base_own, left, *parts, *pair, *weights)


def outputs_kernel(dk, dv, rank, near_all, *refs):
    take = splitter(refs)
    feed_ref, feed_more_ref, rows_ref, down_ref, out_ref = take(5)
    wide_ref, near_ref, token_ref, layer_ref = take(4)
    token_out, layer_out, query_out, key_out, value_out, gate_out = take(6)
    feed_gate_out, feed_up_out, feed_down_out, out_out, decay_out, vector_out = take(6)
    step = pl.program_id(0)

    def total(ref, start, wide):
        span = pl.ds(start, wide)
        result = ref[0, :, span].astype(f32)
        for q in range(1, ref.shape[0]):
            result = result + ref[q, :, span].astype(f32)
        return result

    wide = feed_gate_out.shape[1]
    feed_gate_out[...] = total(feed_ref, 0, wide)
    there = feed_ref.shape[2] - wide
    feed_up_out[:, :there] = total(feed_ref, wide, there)
    feed_up_out[:, there:] = total(feed_more_ref, 0, wide - there)
    query_out[...] = total(rows_ref, 0, dk)
    key_out[...] = total(rows_ref, dk, dk)
    value_out[...] = total(rows_ref, 2 * dk, dv)
    gate_out[...] = total(rows_ref, 2 * dk + dv + LANES, dv)
    token_out[...] = token_ref[...]
    layer_out[...] = layer_ref[...]

    @pl.when(lax.rem(step, pl.num_programs(0) // 2) == 0)
    def _():
        half = out_out.shape[2] // 2
        for ref, out in ((down_ref, feed_down_out), (out_ref, out_out)):
            for b in range(2):
                result = ref[b].astype(f32)
                for q in range(1, ref.shape[0] // 2):
                    result = result + ref[2 * q + b].astype(f32)
                out[0, :, b * half : (b + 1) * half] = result

    @pl.when(step == 0)
    def _():
        decay_out[...] = wide_ref[:rank, :]
        vector_out[...] = jnp.sum(wide_ref[rank:, :], axis=0, keepdims=True)


def outputs(
    groups, dk, dv, rank, near_all, feed, feed_more, rows, down, out, wide_sum, near_sum, token,
    layer,
):
    steps = 4
    count, width = token.shape
    wide = (feed.shape[2] + feed_more.shape[2]) // 2
    per = width // groups
    block = per // steps
    shape = jax.ShapeDtypeStruct

    def rows_of(columns):
        return pl.BlockSpec((block, columns), lambda i: (i, 0))

    def fixed(array):
        return pl.BlockSpec(array.shape, lambda i: (0,) * array.ndim)

    def recv(array):
        return pl.BlockSpec((array.shape[0], block, array.shape[2]), lambda i: (0, i, 0))

    def recv_half(array):
        return pl.BlockSpec(
            (array.shape[0], array.shape[1] // 2, array.shape[2]), lambda i: (0, i // (steps // 2), 0)
        )

    def out_half(array):
        return pl.BlockSpec((1, array.shape[1] // 2, width), lambda i: (0, i // (steps // 2), 0))

    tokens_block = pl.BlockSpec((count // steps, width), lambda i: (i, 0))
    return pl.pallas_call(
        functools.partial(outputs_kernel, dk, dv, rank, near_all),
        grid=(steps,),
        in_specs=[
            recv(feed), recv(feed_more), recv(rows), recv_half(down), recv_half(out), fixed(wide_sum),
            fixed(near_sum), tokens_block, tokens_block,
        ],
        out_specs=[
            tokens_block, tokens_block, rows_of(dk), rows_of(dk), rows_of(dv), rows_of(dv),
            rows_of(wide), rows_of(wide), out_half(down), out_half(out),
            pl.BlockSpec((rank, per), lambda i: (0, 0)),
            pl.BlockSpec((1, per), lambda i: (0, 0)),
        ],
        out_shape=[
            shape((count, width), bf16),
            shape((count, width), bf16),
            shape((per, dk), f32),
            shape((per, dk), f32),
            shape((per, dv), f32),
            shape((per, dv), f32),
            shape((per, wide), f32),
            shape((per, wide), f32),
            shape((1, down.shape[1], width), f32),
            shape((1, out.shape[1], width), f32),
            shape((rank, per), f32),
            shape((1, per), f32),
        ],
        compiler_params=pltpu.CompilerParams(vmem_limit_bytes=60 << 20),
        name="outputs",
    )(feed, feed_more, rows, down, out, wide_sum, near_sum, token, layer)


def recur_back_kernel(n, groups, dk, dv, beside, *refs):
    (
        lengths_ref, send_row_ref, send_column_ref, slot_row_ref, slot_column_ref,
        d_mixed_ref, out_weight_ref, attended_ref, gate_ref, gains_ref, up_rows_ref,
        share_ref, held_far, states_far, hidden_far, active_far, cotangent_far,
        d_rows_ref, d_gate_ref, head_gain_ref, grad_up_ref, grad_bias_ref, layer_ref, grad_down_ref,
        up_in, down_in, d_attended, d_placed, d_state, result,
        held_ref, states_ref, hidden_ref, up_ref, down_ref, bias_ref, load_sems, sems,
    ) = refs[:38]
    go = Exchange(groups, (), *refs[38:41])
    back = Exchange(groups, (2 * dk,), *refs[41:44])
    cols = None
    if beside:
        cols = ColGrad(groups, active_far, cotangent_far, 0, grad_down_ref, refs[44:])
    count = d_mixed_ref.shape[0]
    slots = slot_row_ref.shape[1]
    end0 = lengths_ref[0, 0]
    end1 = end0 + lengths_ref[0, 1]
    ends = (end0, end1, end1 + lengths_ref[0, 2])

    def finish(total, own, place):
        layer_ref[place, :] = (hidden_ref[own, :] + total).astype(layer_ref.dtype)

    line = Line(n, share_ref, up_in, down_in, layer_ref, sems, finish)
    loads = (
        pltpu.make_async_copy(hidden_far, hidden_ref, load_sems.at[0]),
        pltpu.make_async_copy(held_far, held_ref, load_sems.at[1]),
        pltpu.make_async_copy(states_far, states_ref, load_sems.at[2]),
    )
    barrier = pltpu.get_barrier_semaphore()
    greet_dp(barrier, groups)
    line.greet(barrier, groups - 1)
    line.prime()
    for c in loads:
        c.start()
    if beside:
        cols.start()
    loads[0].wait()

    bias_ref[...] = gains_ref[2:3, dv : dv + dk]
    thirds(up_rows_ref, 3, up_ref)
    thirds(up_rows_ref, 2, down_ref)

    head_gain_ref[...] = jnp.zeros_like(head_gain_ref)
    tile = count // 2

    @pl.loop(0, 2)
    def _(i):
        rows = pl.ds(pl.multiple_of(i * tile, tile), tile)
        d_gated = dot_t(d_mixed_ref[rows, :], out_weight_ref[...])
        attended = attended_ref[rows, :].astype(f32)
        gate = gate_ref[rows, :]
        scaling = lax.rsqrt(jnp.mean(attended * attended, axis=1, keepdims=True) + head_floor)
        unit = attended * scaling
        sigmoid = jax.nn.sigmoid(gate)
        swish = gate * sigmoid
        gained = d_gated * gains_ref[2:3, :dv]
        d_gate_ref[rows, :] = (
            gained * unit * sigmoid * (1.0 + gate * (1.0 - sigmoid))
        ).astype(bf16)
        d_unit = gained * swish
        d_attended[rows, :] = (
            scaling * (d_unit - unit * jnp.mean(d_unit * unit, axis=1, keepdims=True))
        ).astype(bf16)
        term = d_gated * unit * swish
        piece = term[0:8, :]
        for r in range(1, tile // 8):
            piece = piece + term[8 * r : 8 * r + 8, :]
        head_gain_ref[...] += piece
        line.step(2 * i)
        line.step(2 * i + 1)

    go.send(0, send_row_ref, 0, d_attended, lambda h: line.step(4 + h))
    d_state[...] = jnp.zeros_like(d_state)
    grad_up_ref[...] = jnp.zeros_like(grad_up_ref)
    grad_bias_ref[...] = jnp.zeros_like(grad_bias_ref)
    done = 14
    if beside:
        cols.ready()

        @pl.loop(0, cols.items)
        def _(i):
            cols.item(i)
            line.step(6 + 2 * i)
            line.step(7 + 2 * i)

        done = 6 + 2 * cols.items
        cols.send_all()
    else:
        line.run(6, done)
    for c in loads[1:]:
        c.wait()

    go.receive(0)
    place_rows(slot_row_ref, go.came, d_placed, go.spans[0], lambda h: line.step(done + h))
    spanned = done + 2
    spans = held_ref.shape[0] // SPAN

    @pl.loop(0, spans)
    def _(i):
        step = spans - 1 - i
        d_out = d_placed[pl.ds(pl.multiple_of(step * SPAN, SPAN), SPAN), :]
        span_backward(
            dk, dv, step, ends, d_out, held_ref, states_ref[step], up_ref, bias_ref, down_ref,
            d_state, result, grad_up_ref, grad_bias_ref,
        )
        line.step(spanned + 2 * i)
        line.step(spanned + 1 + 2 * i)

    sent = spanned + 2 * spans
    for p in range(2):
        back.send(
            p, slot_column_ref, 1, result, lambda h, p=p: line.step(sent + 2 * p + h)
        )
    last_steps = (sent + 4, sent + 4 + (line.steps - sent - 4) * 2 // 3, line.steps)
    for p in range(2):
        line.run(last_steps[p], last_steps[p + 1])
        if beside and p:
            cols.receive()
        back.receive(p)
        span = back.spans[p]

        @pl.loop(0, 2)
        def _(i):
            rows = pl.ds(pl.multiple_of(i * tile, tile), tile)
            pick = one_hot(send_column_ref[rows, :], 0, (tile, slots), 1)
            d_rows_ref[rows, span] = dot(pick, back.came[:, span]).astype(bf16)

    line.drain()
    if beside:
        cols.drain()
    go.drain()
    back.drain()


def recur_back(
    call, n, groups, dk, dv, beside, lengths, send_row, send_column, slot_row, slot_column, d_mixed, out_weight, attended, gate_pre,
    gains, up_rows, share, held, states, hidden_own, active, cotangent,
):
    count, width = d_mixed.shape
    slots, wide = held.shape
    half = count // 2
    vmem = pl.BlockSpec(memory_space=pltpu.VMEM)
    operands = [
        lengths, send_row, send_column, slot_row, slot_column, d_mixed, out_weight, attended, gate_pre, gains, up_rows, share, held, states, hidden_own, active, cotangent,
    ]
    far = pl.BlockSpec(memory_space=pl.ANY)
    return pl.pallas_call(
        functools.partial(recur_back_kernel, n, groups, dk, dv, beside),
        in_specs=[pl.BlockSpec(memory_space=pltpu.SMEM)] + [vmem] * (len(operands) - 6) + [far] * 5,
        out_specs=[vmem] * 6 + [far],
        out_shape=[
            jax.ShapeDtypeStruct((count, wide), bf16),
            jax.ShapeDtypeStruct((count, dv), bf16),
            jax.ShapeDtypeStruct((8, dv), f32),
            jax.ShapeDtypeStruct((dk, LANES), f32),
            jax.ShapeDtypeStruct((8, dk), f32),
            jax.ShapeDtypeStruct((count, width), bf16),
            jax.ShapeDtypeStruct(
                (groups, active.shape[1] // groups if beside else 8, width // 2), bf16
            ),
        ],
        scratch_shapes=Line.scratch(half, width)
        + [
            pltpu.VMEM((count, dv), bf16),
            pltpu.VMEM((slots, dv), bf16),
            pltpu.VMEM((dk, dv), f32),
            pltpu.VMEM((slots, wide), bf16),
            pltpu.VMEM(held.shape, bf16),
            pltpu.VMEM(states.shape, bf16),
            pltpu.VMEM((half, width), f32),
            pltpu.VMEM((LANES, dk), bf16),
            pltpu.VMEM((LANES, dk), bf16),
            pltpu.VMEM((1, dk), f32),
            pltpu.SemaphoreType.DMA((3,)),
            Line.semaphores(half),
        ]
        + Exchange.scratch(groups, slots, dv, 1)
        + Exchange.scratch(groups, slots, wide, 2)
        + (ColGrad.scratch(groups, count, active.shape[1], width // 2) if beside else []),
        compiler_params=pltpu.CompilerParams(
            collective_id=call, has_side_effects=True, vmem_limit_bytes=60 << 20
        ),
        cost_estimate=pl.CostEstimate(
            flops=12_000_000_000, bytes_accessed=200_000_000, transcendentals=4_000_000
        ),
        name="recur_back",
    )(*operands)


def small_sum_kernel(groups, n, rows_all, part_ref, out_ref, held, line, line_in, sems, line_sems):
    me = lax.axis_index("dp")
    place = lax.axis_index("tensor")
    barrier = pltpu.get_barrier_semaphore()

    def peer(k):
        return lax.rem(me + k, groups)

    def mate(k):
        return lax.rem(place + k, n)

    @pl.loop(1, groups)
    def _(k):
        pl.semaphore_signal(barrier, inc=1, device_id={"dp": peer(k)}, device_id_type=MESH)

    @pl.loop(1, n)
    def _(k):
        pl.semaphore_signal(barrier, inc=1, device_id={"tensor": mate(k)}, device_id_type=MESH)

    pl.semaphore_wait(barrier, groups + n - 2)

    def copy(k, source):
        return pltpu.make_async_remote_copy(
            part_ref.at[peer(k)], held.at[source], sems.at[0, k], sems.at[1, source],
            device_id={"dp": peer(k)}, device_id_type=MESH,
        )

    def line_copy(k, source):
        return pltpu.make_async_remote_copy(
            line, line_in.at[source], line_sems.at[0, k], line_sems.at[1, source],
            device_id={"tensor": mate(k)}, device_id_type=MESH,
        )

    @pl.loop(1, groups)
    def _(k):
        copy(k, me).start()

    held[pl.ds(me, 1)] = part_ref[pl.ds(me, 1)]

    @pl.loop(1, groups)
    def _(k):
        copy(k, peer(k)).wait_recv()

    total = held[0]
    for i in range(1, groups):
        total = total + held[i]
    line[...] = total[:rows_all]
    out_ref[...] = total

    @pl.loop(1, n)
    def _(k):
        line_copy(k, place).start()

    line_in[pl.ds(place, 1)] = total[None, :rows_all]

    @pl.loop(1, n)
    def _(k):
        line_copy(k, mate(k)).wait_recv()

    total = line_in[0]
    for i in range(1, n):
        total = total + line_in[i]
    out_ref[:rows_all] = total

    @pl.loop(1, groups)
    def _(k):
        copy(k, me).wait_send()

    @pl.loop(1, n)
    def _(k):
        line_copy(k, place).wait_send()


def small_sum(over_all, over_owners, groups, n, call):
    def tiles(blocks):
        short = -blocks.shape[1] % (8 * LANES)
        return jnp.pad(blocks, ((0, 0), (0, short))).reshape(groups, -1, LANES)

    first, second = tiles(over_all), tiles(over_owners)
    rows_all = first.shape[1]
    part = jnp.concatenate([first, second], axis=1)
    vmem = pl.BlockSpec(memory_space=pltpu.VMEM)
    total = pl.pallas_call(
        functools.partial(small_sum_kernel, groups, n, rows_all),
        in_specs=[vmem],
        out_specs=vmem,
        out_shape=jax.ShapeDtypeStruct(part.shape[1:], f32),
        scratch_shapes=[
            pltpu.VMEM(part.shape, f32),
            pltpu.VMEM((rows_all, LANES), f32),
            pltpu.VMEM((n, rows_all, LANES), f32),
            pltpu.SemaphoreType.DMA((2, groups)),
            pltpu.SemaphoreType.DMA((2, n)),
        ],
        compiler_params=pltpu.CompilerParams(collective_id=call, has_side_effects=True),
        name="small_sum",
    )(part)
    return (
        total[:rows_all].reshape(-1)[: over_all.shape[1]],
        total[rows_all:].reshape(-1)[: over_owners.shape[1]],
    )


def per_device(
    tokens,
    cotangent,
    token_slots,
    lengths,
    mixer_gain,
    query_weight,
    key_weight,
    value_weight,
    gate_weight,
    decay_down,
    decay_up,
    decay_bias,
    head_gain,
    out_weight,
    feed_gain,
    feed_gate,
    feed_up,
    feed_down,
):
    groups = lax.axis_size("dp")
    lines = lax.axis_size("tensor")
    member = lax.axis_index("dp")
    place = lax.axis_index("tensor")
    count, width = tokens.shape
    dk = query_weight.shape[1]
    dv = value_weight.shape[1]
    rank = decay_up.shape[1]
    parity = lax.rem(member, 2)
    pairs = [(i, i ^ 1) for i in range(groups)]
    same_parity = [[i for i in range(groups) if i % 2 == b] for b in range(2)]

    fused = (width // groups) % LANES == 0
    third = LANES // 4
    down_rows = decay_down.T
    up_rows = decay_up.T
    last = jnp.pad(jnp.concatenate([head_gain, decay_bias]), (0, width - dv - dk))
    gains = jnp.stack([mixer_gain, feed_gain, last]).astype(f32)
    (
        normed, gate_pre, attended, gated, held, states, mixer_share, send_row, send_column, slot_row,
        slot_column,
    ) = front(
        1, groups, lengths, token_slots.reshape(-1, LANES), tokens, gains, up_rows,
        down_rows, [query_weight, key_weight, value_weight], gate_weight, out_weight,
    )

    if fused:
        (
            d_mixed, d_hidden_own, feed_gain_part, feed_recv, feed_more, active, layer_share,
            hidden_own,
        ) = back_feed(
            2, lines, groups, gains, mixer_share, tokens, cotangent, feed_gate, feed_up, feed_down
        )
    else:
        quarter = count // 4

        def own_rows(rows):
            blocks = rows.reshape(2, 2, quarter, width)
            return jnp.where(place == 0, blocks[:, 1], blocks[:, 0]).reshape(2 * quarter, width)

        tokens_own, cotangent_own = own_rows(tokens), own_rows(cotangent)
        feed_normed, hidden_own, _ = line_sum(
            "norm", 5, lines, mixer_share, tokens_own, tokens_own, gains[1:2]
        )
        d_active = dot_t(cotangent, feed_down).astype(bf16)
        gate_hidden = dot(feed_normed, feed_gate)
        up_hidden = dot(feed_normed, feed_up)
        d_active = d_active.astype(f32)
        sigmoid_gate = jax.nn.sigmoid(gate_hidden)
        swish_gate = gate_hidden * sigmoid_gate
        active = (swish_gate * up_hidden).astype(bf16)
        d_gate_hidden = (
            d_active * up_hidden * sigmoid_gate * (1.0 + gate_hidden * (1.0 - sigmoid_gate))
        ).astype(bf16)
        d_up_hidden = (d_active * swish_gate).astype(bf16)
        feed_share = (dot_t(d_gate_hidden, feed_gate) + dot_t(d_up_hidden, feed_up)).astype(bf16)
        d_mixed, d_hidden_own, feed_gain_part = line_sum(
            "back", 2, lines, feed_share, hidden_own, cotangent_own, gains[1:2]
        )
        layer_share = dot(active, feed_down).astype(bf16)

    d_rows, d_gate_low, head_gain_part, up_part, bias_part, layer_out, down_recv = recur_back(
        4, lines, groups, dk, dv, fused, lengths, send_row, send_column, slot_row, slot_column, d_mixed,
        out_weight, attended, gate_pre, gains, up_rows, layer_share, held, states, hidden_own, active,
        cotangent,
    )
    up_part = up_part[:, :rank] + up_part[:, third : third + rank] + (
        up_part[:, 2 * third : 2 * third + rank]
    )

    def by_owner(vector):
        return vector.reshape(groups, -1)

    per = width // groups
    head_per = dv // groups
    up_per = dk // groups * rank
    if fused:
        near = [
            by_owner(jnp.sum(feed_gain_part, axis=0)),
            jnp.pad(by_owner(jnp.sum(head_gain_part, axis=0)), ((0, 0), (0, -head_per % LANES))),
            by_owner(up_part),
            jnp.pad(by_owner(bias_part[0]), ((0, 0), (0, -(dk // groups) % LANES))),
        ]
        near_all = (per + head_per + LANES - 1) // LANES
        near = jnp.concatenate(near, axis=1)
        near = jnp.pad(near, ((0, 0), (0, -near.shape[1] % (8 * LANES))))
        token_grad, wide_sum, near_sum, rows_recv, out_recv, feed_more = back_mixer(
            3, lines, groups, gains, near.reshape(groups, -1, LANES), near_all, down_rows, tokens,
            d_hidden_own, normed, [d_rows, d_gate_low], (gated, d_mixed, feed_more),
            [query_weight, key_weight, value_weight, gate_weight],
        )
        (
            token_grad, layer_out, grad_query, grad_key, grad_value, grad_gate, grad_feed_gate,
            grad_feed_up, grad_feed_down, grad_out, down_sum, mixer_sum,
        ) = outputs(
            groups, dk, dv, rank, near_all, feed_recv, feed_more, rows_recv, down_recv, out_recv,
            wide_sum, near_sum, token_grad, layer_out,
        )
        near_sum = near_sum.reshape(-1)
        mixer_sum = mixer_sum.reshape(-1)
        down_sum = down_sum.T
        feed_sum = near_sum[:per]
        head_sum = near_sum[per : per + head_per]
        up_sum = near_sum[near_all * LANES : near_all * LANES + up_per]
        bias_sum = near_sum[near_all * LANES + up_per :][: dk // groups]
    else:
        down_pad = jnp.pad(decay_down, ((0, 0), (0, third - rank)))
        down_none = jnp.zeros_like(down_pad)
        down_both = jnp.concatenate([down_pad, down_pad, down_none, down_none], axis=1)
        d_query_low = d_rows[:, :dk]
        d_key_low = d_rows[:, dk : 2 * dk]
        d_value_low = d_rows[:, 2 * dk : 2 * dk + dv]
        d_latent_low = d_rows[:, 2 * dk + dv :]
        normed_share = (
            dot_t(d_query_low, query_weight)
            + dot_t(d_key_low, key_weight)
            + dot_t(d_value_low, value_weight)
            + dot_t(d_gate_low, gate_weight)
            + dot_t(d_latent_low, down_both)
        ).astype(bf16)
        token_grad, _, mixer_gain_part = line_sum(
            "back", 3, lines, normed_share, tokens_own, d_hidden_own, gains[0:1],
        )
        down_part = rows_dot(normed, d_latent_low)
        down_part = down_part[:, :rank] + down_part[:, third : third + rank]
        over_all = jnp.concatenate(
            [
                by_owner(jnp.sum(mixer_gain_part, axis=0)),
                by_owner(jnp.sum(feed_gain_part, axis=0)),
                by_owner(jnp.sum(head_gain_part, axis=0)),
                by_owner(down_part),
            ],
            axis=1,
        )
        over_owners = jnp.concatenate([by_owner(up_part), by_owner(bias_part[0])], axis=1)
        summed, small = small_sum(over_all, over_owners, groups, lines, 5)
        mixer_sum = summed[:per]
        feed_sum = summed[per : 2 * per]
        head_sum = summed[2 * per : 2 * per + head_per]
        down_sum = summed[2 * per + head_per :].reshape(per, rank)
        up_sum = small[:up_per]
        bias_sum = small[up_per:]

    def halves(row_block, dims):
        split = row_block.reshape(row_block.shape[0], groups // 2, 2, dims // groups)
        keep = lax.dynamic_index_in_dim(split, parity, 2, keepdims=False)
        send = lax.dynamic_index_in_dim(split, 1 - parity, 2, keepdims=False)
        got = lax.ppermute(send, "dp", pairs)
        shape = (row_block.shape[0], dims // 2)
        return keep.reshape(shape), got.reshape(shape)

    def partner(row_block):
        return row_block, lax.ppermute(row_block, "dp", pairs)

    def summed_share(left, right):
        share = (rows_dot(left[0], right[0]) + rows_dot(left[1], right[1])).astype(bf16)
        rows = share.shape[0] // (groups // 2)
        blocks = share.reshape(groups // 2, rows, share.shape[1])
        moved = lax.all_to_all(
            blocks, "dp", split_axis=0, concat_axis=0, tiled=True, axis_index_groups=same_parity
        )
        return jnp.sum(moved.astype(f32), axis=0)

    if not fused:
        grad_feed_down = summed_share(halves(active, active.shape[1]), partner(cotangent))[None]
        feed_halves = halves(feed_normed, width)
        normed_halves = halves(normed, width)
        grad_feed_gate = summed_share(feed_halves, partner(d_gate_hidden))
        grad_feed_up = summed_share(feed_halves, partner(d_up_hidden))
        grad_out = summed_share(halves(gated, dv), partner(d_mixed))[None]
        grad_query = summed_share(normed_halves, partner(d_query_low))
        grad_key = summed_share(normed_halves, partner(d_key_low))
        grad_value = summed_share(normed_halves, partner(d_value_low))
        grad_gate = summed_share(normed_halves, partner(d_gate_low))

    return (
        layer_out,
        token_grad,
        mixer_sum,
        grad_query,
        grad_key,
        grad_value,
        grad_gate,
        down_sum,
        up_sum.reshape(1, dk // groups, rank),
        bias_sum.reshape(1, dk // groups),
        head_sum,
        grad_out,
        feed_sum,
        grad_feed_gate,
        grad_feed_up,
        grad_feed_down,
    )


def solution(mesh):
    placed = (
        P("dp", None),
        P("dp", None),
        P(),
        P("dp", None),
        P(),
        P(None, "tensor"),
        P(None, "tensor"),
        P(None, "tensor"),
        P(None, "tensor"),
        P(),
        P("tensor", None),
        P("tensor"),
        P(),
        P("tensor", None),
        P(),
        P(None, "tensor"),
        P(None, "tensor"),
        P("tensor", None),
    )
    return jax.shard_map(
        per_device,
        mesh=mesh,
        in_specs=placed,
        out_specs=(
            P("dp", None),
            P("dp", None),
            P("dp"),
            P("dp", "tensor"),
            P("dp", "tensor"),
            P("dp", "tensor"),
            P("dp", "tensor"),
            P("dp", None),
            P("tensor", "dp", None),
            P("tensor", "dp"),
            P("dp"),
            P("tensor", "dp", None),
            P("dp"),
            P("dp", "tensor"),
            P("dp", "tensor"),
            P("tensor", "dp", None),
        ),
        check_vma=False,
    )
```

```python
import functools

import jax
import jax.numpy as jnp
from jax import lax
from jax.experimental import pallas as pl
from jax.experimental.pallas import tpu as pltpu
from jax.sharding import PartitionSpec as P

OWN_CAP = 1024
SPAN = 128
LANES = 128
epsilon = 1e-06
head_floor = 1.0

f32 = jnp.float32
bf16 = jnp.bfloat16
MESH = pl.DeviceIdType.MESH


def rows_dot(left, right):
    return lax.dot_general(left, right, (((0,), (0,)), ((), ())), preferred_element_type=f32)


def dot_t(left, right):
    return lax.dot_general(left, right, (((1,), (1,)), ((), ())), preferred_element_type=f32)


def dot(left, right):
    return jnp.dot(left, right, preferred_element_type=f32)


def span_terms(first, ends, logits):
    rows = logits.shape[0]

    def label(position):
        count = jnp.zeros_like(position)
        for end in ends:
            count = count + (position >= end).astype(jnp.int32)
        return count

    log_decay = jax.nn.log_sigmoid(logits) * (1.0 / 16.0)
    row = lax.broadcasted_iota(jnp.int32, (rows, rows), 0)
    column = lax.broadcasted_iota(jnp.int32, (rows, rows), 1)
    lower = (row >= column).astype(f32)
    cumulative = jnp.dot(
        lower, log_decay, precision=lax.Precision.HIGHEST, preferred_element_type=f32
    )
    total = cumulative[rows - 1 :, :]
    middle = cumulative[rows // 2 - 1 : rows // 2, :]
    label_column = label(first + lax.broadcasted_iota(jnp.int32, (rows, 1), 0))
    label_row = label(first + lax.broadcasted_iota(jnp.int32, (1, rows), 1))
    before = jnp.where(first > 0, label(first - 1), -1)
    last = label(first + rows - 1)
    carried = (label_column == before).astype(f32)
    tail = (label_column == last).astype(f32)
    keep = (before == last).astype(f32)
    allowed = (row >= column) & (label_column == label_row)
    return log_decay, cumulative, total, middle, carried, tail, keep, allowed


def span_forward(dk, dv, step, ends, held_ref, up_ref, bias_ref, state, states_ref, result):
    first = step * SPAN
    at = pl.ds(pl.multiple_of(first, SPAN), SPAN)
    queries = held_ref[at, :dk].astype(f32) * (float(dk) ** -0.5)
    keys = held_ref[at, dk : 2 * dk].astype(f32)
    values = held_ref[at, 2 * dk : 2 * dk + dv]
    logits = dot(held_ref[at, 2 * dk + dv :], up_ref[...]) + bias_ref[...]
    _, cumulative, total, middle, carried, tail, keep, allowed = span_terms(first, ends, logits)
    query_mid = (queries * jnp.exp(cumulative - middle)).astype(bf16)
    key_mid = (keys * jnp.exp(middle - cumulative)).astype(bf16)
    query_start = (queries * jnp.exp(cumulative) * carried).astype(bf16)
    key_end = (keys * jnp.exp(total - cumulative) * tail).astype(bf16)
    scores = jnp.where(allowed, dot_t(query_mid, key_mid), 0.0).astype(bf16)
    entering = state[...]
    entering_low = entering.astype(bf16)
    states_ref[step] = entering_low
    attended = dot(scores, values) + dot(query_start, entering_low)
    result[at, :] = attended.astype(bf16)
    decay_column = jnp.transpose(jnp.broadcast_to(keep * jnp.exp(total), (8, dk)))[:, :1]
    state[...] = decay_column * entering + rows_dot(key_end, values)


def span_backward(
    dk, dv, step, ends, d_out, held_ref, entering, up_ref, bias_ref, down_ref, d_state, result,
    grad_up_ref, grad_bias_ref,
):
    first = step * SPAN
    at = pl.ds(pl.multiple_of(first, SPAN), SPAN)
    scale = float(dk) ** -0.5
    queries = held_ref[at, :dk].astype(f32) * scale
    keys = held_ref[at, dk : 2 * dk].astype(f32)
    values = held_ref[at, 2 * dk : 2 * dk + dv]
    latent = held_ref[at, 2 * dk + dv :]
    logits = dot(latent, up_ref[...]) + bias_ref[...]
    _, cumulative, total, middle, carried, tail, keep, allowed = span_terms(first, ends, logits)
    grow_query = jnp.exp(cumulative - middle)
    grow_key = jnp.exp(middle - cumulative)
    start_decay = jnp.exp(cumulative) * carried
    end_decay = jnp.exp(total - cumulative) * tail
    query_mid = (queries * grow_query).astype(bf16)
    key_mid = (keys * grow_key).astype(bf16)
    query_start = (queries * start_decay).astype(bf16)
    key_end = (keys * end_decay).astype(bf16)
    scores = jnp.where(allowed, dot_t(query_mid, key_mid), 0.0).astype(bf16)
    d_scores = jnp.where(allowed, dot_t(d_out, values), 0.0).astype(bf16)
    leaving = d_state[...]
    leaving_low = leaving.astype(bf16)
    d_values = rows_dot(scores, d_out) + dot(key_end, leaving_low)
    d_queries = dot(d_scores, key_mid) * grow_query + dot_t(d_out, entering) * start_decay
    d_key_end = dot_t(values, leaving_low) * end_decay
    d_keys = rows_dot(d_scores, query_mid) * grow_key + d_key_end
    kept = keep * jnp.exp(total)
    state_pair = jnp.sum(entering.astype(f32) * leaving, axis=1, keepdims=True)
    state_row = jnp.transpose(jnp.broadcast_to(state_pair, (dk, LANES)))[:1, :]
    d_total = jnp.sum(keys * d_key_end, axis=0, keepdims=True) + kept * state_row
    d_cumulative = queries * d_queries - keys * d_keys
    row = lax.broadcasted_iota(jnp.int32, (SPAN, SPAN), 0)
    column = lax.broadcasted_iota(jnp.int32, (SPAN, SPAN), 1)
    upper = (row <= column).astype(f32)
    d_log_decay = (
        jnp.dot(upper, d_cumulative, precision=lax.Precision.HIGHEST, preferred_element_type=f32)
        + d_total
    )
    d_logits = d_log_decay * (1.0 / 16.0) * jax.nn.sigmoid(-logits)
    grad_bias_ref[...] += jnp.broadcast_to(jnp.sum(d_logits, axis=0, keepdims=True), (8, dk))
    d_logits_high = d_logits.astype(bf16)
    d_logits_low = (d_logits - d_logits_high.astype(f32)).astype(bf16)
    grad_up_ref[...] += rows_dot(d_logits_high, latent) + rows_dot(d_logits_low, latent)
    d_latent = dot_t(d_logits_high, down_ref[...]) + dot_t(d_logits_low, down_ref[...])
    high = d_latent.astype(bf16).astype(f32)
    lane = lax.broadcasted_iota(jnp.int32, d_latent.shape, 1)
    d_latent_packed = jnp.where(lane < LANES // 4, high, d_latent - high)
    result[at, :dk] = (d_queries * scale).astype(bf16)
    result[at, dk : 2 * dk] = d_keys.astype(bf16)
    result[at, 2 * dk : 2 * dk + dv] = d_values.astype(bf16)
    result[at, 2 * dk + dv :] = d_latent_packed.astype(bf16)
    kept_column = jnp.transpose(jnp.broadcast_to(kept, (8, dk)))[:, :1]
    d_state[...] = kept_column * leaving + rows_dot(query_start, d_out)


FINE = 16
SKEW = 3


class Line:
    def __init__(self, n, share_ref, up_in, down_in, out_ref, sems, finish):
        self.n, self.me = n, lax.axis_index("tensor")
        self.share, self.up_in, self.down_in, self.out = share_ref, up_in, down_in, out_ref
        self.sems, self.finish = sems, finish
        self.half = up_in.shape[0]
        self.block = self.half // 2
        self.count = self.half // FINE
        self.second = self.count + 2
        self.steps = self.second + self.count + SKEW * (n - 2)

    @staticmethod
    def scratch(half, width):
        return [pltpu.VMEM((half, width), bf16), pltpu.VMEM((half, width), bf16)]

    @staticmethod
    def semaphores(half):
        return pltpu.SemaphoreType.DMA((8, half // FINE))

    def own_copies(self, source, target, sems):
        block = self.block
        return [
            pltpu.make_async_copy(
                source.at[
                    pl.ds(
                        pl.multiple_of(2 * i * block + jnp.where(self.me == 0, block, 0), block),
                        block,
                    ),
                    :,
                ],
                target.at[pl.ds(i * block, block), :],
                sems[i],
            )
            for i in range(2)
        ]

    def greet(self, barrier, others):
        n, me = self.n, self.me

        @pl.when(me > 0)
        def _():
            pl.semaphore_signal(barrier, inc=1, device_id={"tensor": me - 1}, device_id_type=MESH)

        @pl.when(me < n - 1)
        def _():
            pl.semaphore_signal(barrier, inc=1, device_id={"tensor": me + 1}, device_id_type=MESH)

        inside = (me > 0) & (me < n - 1)

        @pl.when(inside)
        def _():
            pl.semaphore_wait(barrier, others + 2)

        @pl.when(jnp.logical_not(inside))
        def _():
            pl.semaphore_wait(barrier, others + 1)

    def greet_all(self, barrier, others):
        n, me = self.n, self.me

        @pl.when(me > 0)
        def _():
            pl.semaphore_signal(barrier, inc=1, device_id={"tensor": me - 1}, device_id_type=MESH)

        @pl.when(me < n - 1)
        def _():
            pl.semaphore_signal(barrier, inc=1, device_id={"tensor": me + 1}, device_id_type=MESH)

        pl.semaphore_wait(barrier, others + n - 1)

    def own(self, g):
        return pl.ds(pl.multiple_of(g * FINE, FINE), FINE)

    def at(self, g):
        per = self.block // FINE
        return pl.ds(
            pl.multiple_of((g // per) * 2 * self.block + lax.rem(g, per) * FINE, FINE), FINE
        )

    def low(self, g):
        per = self.block // FINE
        start = (g // per) * 2 * self.block + self.block + lax.rem(g, per) * FINE
        return pl.ds(pl.multiple_of(start, FINE), FINE)

    def right(self, source, target, lane, g):
        return pltpu.make_async_remote_copy(
            source, target, self.sems.at[2 * lane, g], self.sems.at[2 * lane + 1, g],
            device_id={"tensor": jnp.minimum(self.me + 1, self.n - 1)}, device_id_type=MESH,
        )

    def left(self, source, target, lane, g):
        return pltpu.make_async_remote_copy(
            source, target, self.sems.at[2 * lane, g], self.sems.at[2 * lane + 1, g],
            device_id={"tensor": jnp.maximum(self.me - 1, 0)}, device_id_type=MESH,
        )

    def up_copy(self, g):
        rows = self.up_in.at[self.own(g), :]
        return self.right(rows, rows, 0, g)

    def down_copy(self, g):
        rows = self.down_in.at[self.own(g), :]
        return self.left(rows, rows, 1, g)

    def up_back_copy(self, g):
        rows = self.out.at[self.at(g), :]
        return self.left(rows, rows, 2, g)

    def down_back_copy(self, g):
        rows = self.out.at[self.low(g), :]
        return self.right(rows, rows, 3, g)

    def prime(self, block=None):
        first, last = (0, self.count)
        if block is not None:
            per = self.block // FINE
            first, last = block * per, block * per + per

        @pl.when(self.me == 0)
        def _():
            @pl.loop(first, last)
            def _(g):
                self.right(
                    self.share.at[self.at(g), :], self.up_in.at[self.own(g), :], 0, g
                ).start()

        @pl.when(self.me == self.n - 1)
        def _():
            @pl.loop(first, last)
            def _(g):
                self.left(
                    self.share.at[self.low(g), :], self.down_in.at[self.own(g), :], 1, g
                ).start()

    def step(self, step):
        n, me, count = self.n, self.me, self.count
        at, low, own = self.at, self.low, self.own
        g_up = step - SKEW * (me - 1)

        @pl.when((me > 0) & (g_up >= 0) & (g_up < count))
        def _():
            self.up_copy(g_up).wait_recv()
            total = self.up_in[own(g_up), :].astype(f32) + self.share[at(g_up), :].astype(f32)

            @pl.when(me < n - 1)
            def _():
                self.up_in[own(g_up), :] = total.astype(bf16)
                self.up_copy(g_up).start()

            @pl.when(me == n - 1)
            def _():
                self.finish(total, own(g_up), at(g_up))
                self.up_back_copy(g_up).start()

        g_down = step - SKEW * (n - 2 - me)

        @pl.when((me < n - 1) & (g_down >= 0) & (g_down < count))
        def _():
            self.down_copy(g_down).wait_recv()
            total = self.down_in[own(g_down), :].astype(f32) + (
                self.share[low(g_down), :].astype(f32)
            )

            @pl.when(me > 0)
            def _():
                self.down_in[own(g_down), :] = total.astype(bf16)
                self.down_copy(g_down).start()

            @pl.when(me == 0)
            def _():
                self.finish(total, own(g_down), low(g_down))
                self.down_back_copy(g_down).start()

        g_up_back = step - self.second - SKEW * (n - 2 - me)

        @pl.when((me < n - 1) & (g_up_back >= 0) & (g_up_back < count))
        def _():
            self.up_back_copy(g_up_back).wait_recv()

            @pl.when(me > 0)
            def _():
                self.up_back_copy(g_up_back).start()

        g_down_back = step - self.second - SKEW * (me - 1)

        @pl.when((me > 0) & (g_down_back >= 0) & (g_down_back < count))
        def _():
            self.down_back_copy(g_down_back).wait_recv()

            @pl.when(me < n - 1)
            def _():
                self.down_back_copy(g_down_back).start()

    def run(self, first, last):
        @pl.loop(first, last)
        def _(step):
            self.step(step)

    def drain(self):
        n, me = self.n, self.me

        @pl.loop(0, self.count)
        def _(g):
            @pl.when(me < n - 1)
            def _():
                self.up_copy(g).wait_send()
                self.down_back_copy(g).wait_send()

            @pl.when(me > 0)
            def _():
                self.down_copy(g).wait_send()
                self.up_back_copy(g).wait_send()


def norm_back(x_ref, base, gain, out_ref, kept_ref, gain_grad_ref):
    gain_grad_ref[...] = jnp.zeros_like(gain_grad_ref)

    def finish(total, own, place):
        rows = x_ref[own, :].astype(f32)
        scaling = lax.rsqrt(jnp.mean(rows * rows, axis=1, keepdims=True) + epsilon)
        unit = rows * scaling
        gained = gain() * total
        grad = base(own, place).astype(f32) + scaling * (
            gained - unit * jnp.mean(gained * unit, axis=1, keepdims=True)
        )
        if kept_ref is not None:
            kept_ref[own, :] = grad
        out_ref[place, :] = grad.astype(out_ref.dtype)
        term = total * unit
        part = term[0:8, :]
        for i in range(1, FINE // 8):
            part = part + term[8 * i : 8 * i + 8, :]
        gain_grad_ref[...] += part

    return finish


def norm_forward(base, gain, out_ref, kept_ref):
    def finish(total, own, place):
        hidden = base(own, place).astype(f32) + total
        kept_ref[own, :] = hidden
        scaling = lax.rsqrt(jnp.mean(hidden * hidden, axis=1, keepdims=True) + epsilon)
        out_ref[place, :] = (hidden * scaling * gain()).astype(bf16)

    return finish


def line_kernel(mode, n, *refs):
    share_ref, x_ref, base_ref, gain_ref, out_ref, kept_ref, gain_grad_ref = refs[:7]
    up_in, down_in, sems = refs[7:]

    def base(own, place):
        return base_ref[own, :]

    def gain():
        return gain_ref[...]

    gain_grad_ref[...] = jnp.zeros_like(gain_grad_ref)
    if mode == "norm":
        finish = norm_forward(base, gain, out_ref, kept_ref)
    else:
        finish = norm_back(x_ref, base, gain, out_ref, kept_ref, gain_grad_ref)
    line = Line(n, share_ref, up_in, down_in, out_ref, sems, finish)
    line.greet(pltpu.get_barrier_semaphore(), 0)
    line.prime()
    line.run(0, line.steps)
    line.drain()


def line_sum(mode, call, n, share, x_own, base_own, gain):
    rows, width = share.shape
    half = rows // 2
    vmem = pl.BlockSpec(memory_space=pltpu.VMEM)
    return pl.pallas_call(
        functools.partial(line_kernel, mode, n),
        in_specs=[vmem] * 4,
        out_specs=[vmem] * 3,
        out_shape=[
            jax.ShapeDtypeStruct((rows, width), bf16),
            jax.ShapeDtypeStruct((half, width), f32),
            jax.ShapeDtypeStruct((8, width), f32),
        ],
        scratch_shapes=Line.scratch(half, width) + [Line.semaphores(half)],
        compiler_params=pltpu.CompilerParams(
            collective_id=call, has_side_effects=True, vmem_limit_bytes=40 << 20
        ),
        name="line_" + mode,
    )(share, x_own, base_own, gain)


def partner_of(index):
    return index + 1 - 2 * lax.rem(index, 2)


def to_dp(source, target, send, recv, device):
    return pltpu.make_async_remote_copy(
        source, target, send, recv, device_id={"dp": device}, device_id_type=MESH
    )


def greet_dp(barrier, groups):
    member = lax.axis_index("dp")

    @pl.loop(1, groups)
    def _(k):
        pl.semaphore_signal(
            barrier, inc=1, device_id={"dp": lax.rem(member + k, groups)}, device_id_type=MESH
        )


class ColGrad:
    TILE = 256

    def __init__(self, groups, left, right, first, recv, refs):
        (
            self.left, self.right, self.left_in, self.right_in, self.send,
            self.load_sems, self.pair_sems, self.sems,
        ) = refs
        self.left_far, self.right_far, self.recv, self.groups = left, right, recv, groups
        self.member = lax.axis_index("dp")
        self.parity = lax.rem(self.member, 2)
        self.half = right.shape[1] // 2
        self.first, self.wide = first, self.right_in.shape[1]
        self.size = self.send.shape[0] // groups
        self.items = self.wide // self.TILE

    @staticmethod
    def scratch(groups, count, rows, wide):
        return [
            pltpu.VMEM((count, rows), bf16),
            pltpu.VMEM((count, wide), bf16),
            pltpu.VMEM((count, rows), bf16),
            pltpu.VMEM((count, wide), bf16),
            pltpu.VMEM((rows, wide), bf16),
            pltpu.SemaphoreType.DMA((3,)),
            pltpu.SemaphoreType.DMA((2, 2)),
            pltpu.SemaphoreType.DMA((2, groups)),
        ]

    def halves(self, parity):
        start = pl.multiple_of(parity * self.half + self.first, self.TILE)
        return self.right_far.at[:, pl.ds(start, self.wide)]

    def loads(self):
        return (
            pltpu.make_async_copy(self.left_far, self.left, self.load_sems.at[0]),
            pltpu.make_async_copy(self.halves(self.parity), self.right, self.load_sems.at[1]),
        )

    def pair_copies(self):
        partner = partner_of(self.member)
        sems = self.pair_sems
        return (
            to_dp(self.left_far, self.left_in, sems.at[0, 0], sems.at[1, 0], partner),
            to_dp(
                self.halves(1 - self.parity), self.right_in, sems.at[0, 1], sems.at[1, 1], partner
            ),
        )

    def start(self):
        for c in self.pair_copies() + self.loads():
            c.start()

    def ready(self):
        for c in self.loads():
            c.wait()
        for c in self.pair_copies():
            c.wait_recv()

    def item(self, t):
        span = pl.ds(pl.multiple_of(t * self.TILE, self.TILE), self.TILE)
        product = rows_dot(self.left[...], self.right[:, span]) + rows_dot(
            self.left_in[...], self.right_in[:, span]
        )
        self.send[:, span] = product.astype(bf16)

    def copy(self, to, source):
        rows = pl.ds(pl.multiple_of(to * self.size, 16), self.size)
        return to_dp(
            self.send.at[rows, :], self.recv.at[source], self.sems.at[0, to],
            self.sems.at[1, source], to,
        )

    def send_all(self):
        @pl.loop(1, self.groups)
        def _(k):
            self.copy(lax.rem(self.member + k, self.groups), self.member).start()

        self.keep().start()

    def keep(self):
        own = pl.ds(pl.multiple_of(self.member * self.size, 16), self.size)
        return pltpu.make_async_copy(
            self.send.at[own, :], self.recv.at[self.member], self.load_sems.at[2]
        )

    def receive(self):
        self.keep().wait()

        @pl.loop(1, self.groups)
        def _(k):
            self.copy(0, lax.rem(self.member + k, self.groups)).wait_recv()

    def drain(self):
        for c in self.pair_copies():
            c.wait_send()

        @pl.loop(1, self.groups)
        def _(k):
            self.copy(lax.rem(self.member + k, self.groups), self.member).wait_send()


class RowGrads:
    def __init__(self, groups, left, tiles, recv, refs, deferred=0):
        (
            self.left, self.all, self.left_in, self.all_in, self.send,
            self.load_sems, self.left_sems, self.piece_sems, self.sems, self.keep_sems,
        ) = refs
        self.left_far, self.tiles, self.recv = left, tiles, recv
        self.live = len(tiles) - deferred
        if left is None:
            self.left_far = self.left
        self.member = lax.axis_index("dp")
        self.parity = lax.rem(self.member, 2)
        self.mine = self.member // 2
        self.team = groups // 2
        self.block = self.left.shape[1] // groups
        self.items = self.team * len(tiles)

    @staticmethod
    def scratch(groups, count, width, total, pieces, tiles):
        team = groups // 2
        return [
            pltpu.VMEM((count, width), bf16),
            pltpu.VMEM((count, total), bf16),
            pltpu.VMEM((count, width // 2), bf16),
            pltpu.VMEM((count, total), bf16),
            pltpu.VMEM((team, width // groups, total), bf16),
            pltpu.SemaphoreType.DMA((1 + pieces,)),
            pltpu.SemaphoreType.DMA((2, team)),
            pltpu.SemaphoreType.DMA((2, pieces)),
            pltpu.SemaphoreType.DMA((2, tiles, team)),
            pltpu.SemaphoreType.DMA((tiles,)),
        ]

    def columns(self, j):
        return pl.ds(pl.multiple_of(j * self.block, self.block), self.block)

    def left_load(self):
        return pltpu.make_async_copy(self.left_far, self.left, self.load_sems.at[0])

    def piece_load(self, p, source, span):
        return pltpu.make_async_copy(source, self.all.at[:, span], self.load_sems.at[1 + p])

    def left_copy(self, q):
        return to_dp(
            self.left_far.at[:, self.columns(2 * q + 1 - self.parity)],
            self.left_in.at[:, self.columns(q)],
            self.left_sems.at[0, q], self.left_sems.at[1, q], partner_of(self.member),
        )

    def piece_copy(self, p, source, span, rows=slice(None)):
        return to_dp(
            source, self.all_in.at[rows, span], self.piece_sems.at[0, p], self.piece_sems.at[1, p],
            partner_of(self.member),
        )

    def start_left(self):
        @pl.loop(0, self.team)
        def _(q):
            self.left_copy(q).start()

        self.left_load().start()

    def ready_left(self):
        self.left_load().wait()

        @pl.loop(0, self.team)
        def _(q):
            self.left_copy(q).wait_recv()

    def copy(self, t, to, source):
        start, wide = self.tiles[t]
        span = pl.ds(start, wide)
        return to_dp(
            self.send.at[to, :, span], self.recv.at[source, :, span],
            self.sems.at[0, t, to], self.sems.at[1, t, source], 2 * to + self.parity,
        )

    def item(self, w):
        count = len(self.tiles)
        k = w // count
        to = lax.rem(self.mine + 1 + k, self.team)
        for t in range(count):
            start, wide = self.tiles[t]

            @pl.when((w >= 0) & (w < self.items) & (lax.rem(w, count) == t))
            def _():
                span = pl.ds(start, wide)
                product = rows_dot(
                    self.left[:, self.columns(2 * to + self.parity)], self.all[:, span]
                ) + rows_dot(self.left_in[:, self.columns(to)], self.all_in[:, span])
                self.send[to, :, span] = product.astype(bf16)

                if t < self.live:
                    @pl.when(k < self.team - 1)
                    def _():
                        self.copy(t, to, self.mine).start()

                    @pl.when(k == self.team - 1)
                    def _():
                        self.keep(t).start()

    def keep(self, t):
        start, wide = self.tiles[t]
        span = pl.ds(start, wide)
        return pltpu.make_async_copy(
            self.send.at[self.mine, :, span], self.recv.at[self.mine, :, span], self.keep_sems.at[t]
        )

    def receive(self):
        for t in range(self.live):
            self.keep(t).wait()

            @pl.loop(1, self.team)
            def _(k):
                self.copy(t, 0, lax.rem(self.mine + k, self.team)).wait_recv()

    def drain(self):
        @pl.loop(0, self.team)
        def _(q):
            self.left_copy(q).wait_send()

        for t in range(self.live):
            @pl.loop(1, self.team)
            def _(k):
                self.copy(t, lax.rem(self.mine + k, self.team), self.mine).wait_send()


def splitter(refs):
    refs = list(refs)

    def take(k):
        out = refs[:k]
        del refs[:k]
        return out

    return take


def one_hot(index, base, shape, dim):
    return (index == base + lax.broadcasted_iota(jnp.int32, shape, dim)).astype(f32).astype(bf16)


def thirds(source, terms, target):
    third = LANES // 4
    size = source.shape[0]
    target[...] = jnp.zeros_like(target)
    for i in range(terms):
        target[i * third : i * third + size, :] = source[...]


class Exchange:
    def __init__(self, groups, cuts, sent, came, sems):
        self.groups, self.sent, self.came, self.sems = groups, sent, came, sems
        self.spans = [pl.ds(a, b - a) for a, b in zip((0,) + cuts, cuts + (sent.shape[1],))]
        self.member = lax.axis_index("dp")
        self.cap = sent.shape[0] // groups

    @staticmethod
    def scratch(groups, slots, width, pieces):
        return [
            pltpu.VMEM((slots, width), bf16),
            pltpu.VMEM((slots, width), bf16),
            pltpu.SemaphoreType.DMA((2, pieces, groups)),
        ]

    def part(self, j):
        return pl.ds(pl.multiple_of(j * self.cap, self.cap), self.cap)

    def copy(self, p, to, source):
        span = self.spans[p]
        return to_dp(
            self.sent.at[self.part(to), span], self.came.at[self.part(source), span],
            self.sems.at[0, p, to], self.sems.at[1, p, source], to,
        )

    def send(self, p, index_ref, dim, source, between=None):
        span = self.spans[p]
        groups, count = self.groups, source.shape[0]
        rows = self.sent.shape[0] // 2

        @pl.loop(0, 2)
        def _(h):
            at = pl.ds(pl.multiple_of(h * rows, rows), rows)
            if dim == 0:
                pick = one_hot(index_ref[...], h * rows, (rows, count), 0)
            else:
                pick = one_hot(index_ref[at, :], 0, (rows, count), 1)
            self.sent[at, span] = dot(pick, source[:, span]).astype(bf16)

            @pl.loop(0, groups // 2)
            def _(k):
                to = h * (groups // 2) + lax.rem(self.member + k, groups // 2)

                @pl.when(to != self.member)
                def _():
                    self.copy(p, to, self.member).start()

            if between is not None:
                between(h)

        own = self.part(self.member)
        self.came[own, span] = self.sent[own, span]

    def receive(self, p):
        @pl.loop(1, self.groups)
        def _(k):
            self.copy(p, 0, lax.rem(self.member + k, self.groups)).wait_recv()

    def drain(self):
        for p in range(len(self.spans)):
            @pl.loop(1, self.groups)
            def _(k):
                self.copy(p, lax.rem(self.member + k, self.groups), self.member).wait_send()


def place_rows(slot_row_ref, came, held, span, between=None):
    positions, slots = held.shape[0], came.shape[0]
    rows = positions // 2

    @pl.loop(0, 2)
    def _(h):
        at = pl.ds(pl.multiple_of(h * rows, rows), rows)
        pick = one_hot(slot_row_ref[...], h * rows, (rows, slots), 0)
        held[at, span] = dot(pick, came[:, span]).astype(bf16)
        if between is not None:
            between(h)


def front_kernel(groups, dk, dv, *refs):
    take = splitter(refs)
    lengths_ref, slot_rows_ref, tokens_ref, gains_ref, up_rows_ref, down_rows_ref = take(6)
    weights_far = take(3)
    gate_far, out_far = take(2)
    spilled = take(6)
    (share_ref,) = take(1)
    send_row_ref, send_column_ref, slot_row_ref, slot_column_ref = take(4)
    normed_ref, gate_ref, attended_ref, gated_ref, held_ref, states_ref = kept = take(6)
    weight_ref, gate_weight_ref, out_weight_ref = take(3)
    rows_out, state, result, rank_ref, up_ref, bias_ref, latent_ref = take(7)
    slots_ref, load_sems = take(2)
    go = Exchange(groups, (2 * dk,), *take(3))
    back = Exchange(groups, (), *take(3))
    (spill_sems,) = take(1)
    member = lax.axis_index("dp")
    count, width = tokens_ref.shape
    cap = OWN_CAP // groups
    half = count // 2
    spills = [
        pltpu.make_async_copy(kept[i], spilled[i], spill_sems.at[i]) for i in range(6)
    ]

    def spill(*which):
        for i in which:
            spills[i].start()

    end0 = lengths_ref[0, 0]
    end1 = end0 + lengths_ref[0, 1]
    ends = (end0, end1, end1 + lengths_ref[0, 2])
    third = LANES // 4

    loads = []
    offset = 0
    for i, far in enumerate(weights_far):
        wide = far.shape[1]
        loads.append(
            pltpu.make_async_copy(far, weight_ref.at[:, pl.ds(offset, wide)], load_sems.at[i])
        )
        offset += wide
    later = [
        pltpu.make_async_copy(gate_far, gate_weight_ref, load_sems.at[4]),
        pltpu.make_async_copy(out_far, out_weight_ref, load_sems.at[5]),
    ]
    for c in loads + later:
        c.start()
    barrier = pltpu.get_barrier_semaphore()
    greet_dp(barrier, groups)
    pl.semaphore_wait(barrier, groups - 1)

    pieces = count // LANES
    for i in range(pieces):
        slots_ref[:, i * LANES : (i + 1) * LANES] = slot_rows_ref[pl.ds(i, groups, stride=pieces), :]
    owners = slots_ref[...] // OWN_CAP
    mine = owners == member
    my_slots = slots_ref[pl.ds(member, 1), :]
    my_owner = my_slots // OWN_CAP
    device = lax.broadcasted_iota(jnp.int32, (groups, count), 0)
    chosen = (my_owner == device).astype(f32)
    before = (
        lax.broadcasted_iota(jnp.int32, (count, count), 0)
        < lax.broadcasted_iota(jnp.int32, (count, count), 1)
    ).astype(f32).astype(bf16)
    send_rank = jnp.sum(chosen * dot(chosen.astype(bf16), before), axis=0, keepdims=True)
    send_row = my_owner * cap + send_rank.astype(jnp.int32)
    send_row_ref[...] = send_row
    send_column_ref[...] = jnp.transpose(
        jnp.broadcast_to(send_row.astype(f32), (8, count))
    )[:, :1].astype(jnp.int32)
    rank_ref[...] = jnp.where(mine, dot(mine.astype(f32).astype(bf16), before), -1.0)

    bias_ref[...] = gains_ref[2:3, dv : dv + dk]
    thirds(up_rows_ref, 3, up_ref)
    thirds(down_rows_ref, 3, latent_ref)

    tile = count // 5

    @pl.loop(0, 5)
    def _(i):
        at = pl.ds(pl.multiple_of(i * tile, tile), tile)
        rows = tokens_ref[at, :].astype(f32)
        scaling = lax.rsqrt(jnp.mean(rows * rows, axis=1, keepdims=True) + epsilon)
        normed_ref[at, :] = (rows * scaling * gains_ref[0:1, :]).astype(bf16)

    for c in loads[:2]:
        c.wait()
    body = 2 * dk + dv

    spill(0)

    def project(first, last):
        @pl.loop(first // 256, last // 256)
        def _(i):
            to = pl.ds(pl.multiple_of(i * 256, 256), 256)
            rows_out[:, to] = dot(normed_ref[...], weight_ref[:, to]).astype(bf16)

    project(0, 2 * dk)
    go.send(0, send_row_ref, 0, rows_out)
    for c in loads[2:]:
        c.wait()
    project(2 * dk, body)
    latent = dot_t(normed_ref[...], latent_ref[...])
    high = latent.astype(bf16).astype(f32)
    middle = (latent - high).astype(bf16).astype(f32)
    lane = lax.broadcasted_iota(jnp.int32, latent.shape, 1)
    rows_out[:, body:] = jnp.where(
        lane < third, high, jnp.where(lane < 2 * third, middle, latent - high - middle)
    ).astype(bf16)
    go.send(1, send_row_ref, 0, rows_out)

    for c in later:
        c.wait()

    @pl.loop(0, dv // 256)
    def _(i):
        to = pl.ds(pl.multiple_of(i * 256, 256), 256)
        gate_ref[:, to] = dot(normed_ref[...], gate_weight_ref[:, to])

    spill(1)

    @pl.loop(0, groups)
    def _(j):
        rank = rank_ref[pl.ds(j, 1), :]
        local = (lax.rem(slots_ref[pl.ds(j, 1), :], OWN_CAP) - OWN_CAP).astype(f32)
        wanted = lax.broadcasted_iota(jnp.int32, (cap, count), 0).astype(f32)
        at = jnp.sum(jnp.where(rank == wanted, local, 0.0), axis=1, keepdims=True)
        slot_column_ref[go.part(j), :] = at.astype(jnp.int32) + OWN_CAP

    slots = slot_row_ref.shape[1]
    slot_row_ref[...] = jnp.transpose(
        jnp.broadcast_to(slot_column_ref[...].astype(f32), (slots, LANES))
    )[:1, :].astype(jnp.int32)
    state[...] = jnp.zeros_like(state)
    for p in range(2):
        go.receive(p)
        place_rows(slot_row_ref, go.came, held_ref, go.spans[p])

    @pl.loop(0, held_ref.shape[0] // SPAN)
    def _(step):
        span_forward(dk, dv, step, ends, held_ref, up_ref, bias_ref, state, states_ref, result)

    back.send(0, slot_column_ref, 1, result)
    spill(4, 5)
    back.receive(0)

    def head_rows(at):
        pick = one_hot(send_column_ref[at, :], 0, (half, slots), 1)
        attended = dot(pick, back.came[...])
        attended_ref[at, :] = attended.astype(bf16)
        gate = gate_ref[at, :]
        scaling = lax.rsqrt(jnp.mean(attended * attended, axis=1, keepdims=True) + head_floor)
        gated = attended * scaling * gains_ref[2:3, :dv] * (gate * jax.nn.sigmoid(gate))
        gated_ref[at, :] = gated.astype(bf16)

        @pl.loop(0, width // 512)
        def _(i):
            to = pl.ds(pl.multiple_of(i * 512, 512), 512)
            share_ref[at, to] = dot(gated_ref[at, :], out_weight_ref[:, to]).astype(bf16)

    @pl.loop(0, 2)
    def _(i):
        head_rows(pl.ds(pl.multiple_of(i * half, half), half))

    spill(2, 3)
    go.drain()
    back.drain()
    for c in spills:
        c.wait()


def front(
    call, groups, lengths, slots, tokens, gains, up_rows, down_rows, weights, gate_weight,
    out_weight,
):
    count, width = tokens.shape
    dk, dv = weights[0].shape[1], weights[2].shape[1]
    body = 2 * dk + dv
    wide = body + LANES
    spans = OWN_CAP // SPAN
    vmem = pl.BlockSpec(memory_space=pltpu.VMEM)
    far = pl.BlockSpec(memory_space=pl.ANY)
    smem = pl.BlockSpec(memory_space=pltpu.SMEM)
    shape = jax.ShapeDtypeStruct
    saved = [
        shape((count, width), bf16),
        shape((count, dv), f32),
        shape((count, dv), bf16),
        shape((count, dv), bf16),
        shape((OWN_CAP, wide), bf16),
        shape((spans, dk, dv), bf16),
    ]
    return pl.pallas_call(
        functools.partial(front_kernel, groups, dk, dv),
        in_specs=[smem] + [vmem] * 5 + [far] * 5,
        out_specs=[far] * 6 + [vmem] * 5,
        out_shape=[
            *saved,
            shape((count, width), bf16),
            shape((1, count), jnp.int32),
            shape((count, 1), jnp.int32),
            shape((1, OWN_CAP), jnp.int32),
            shape((OWN_CAP, 1), jnp.int32),
        ],
        scratch_shapes=[pltpu.VMEM(a.shape, a.dtype) for a in saved]
        + [
            pltpu.VMEM((width, body), bf16),
            pltpu.VMEM((width, dv), bf16),
            pltpu.VMEM((dv, width), bf16),
            pltpu.VMEM((count, wide), bf16),
            pltpu.VMEM((dk, dv), f32),
            pltpu.VMEM((OWN_CAP, dv), bf16),
            pltpu.VMEM((groups, count), f32),
            pltpu.VMEM((LANES, dk), bf16),
            pltpu.VMEM((1, dk), f32),
            pltpu.VMEM((LANES, width), bf16),
            pltpu.VMEM((groups, count), jnp.int32),
            pltpu.SemaphoreType.DMA((8,)),
        ]
        + Exchange.scratch(groups, OWN_CAP, wide, 2)
        + Exchange.scratch(groups, OWN_CAP, dv, 1)
        + [pltpu.SemaphoreType.DMA((6,))],
        compiler_params=pltpu.CompilerParams(
            collective_id=call, has_side_effects=True, vmem_limit_bytes=60 << 20
        ),
        cost_estimate=pl.CostEstimate(
            flops=12_000_000_000, bytes_accessed=200_000_000, transcendentals=4_000_000
        ),
        name="front",
    )(
        lengths, slots, tokens, gains, up_rows, down_rows, *weights, gate_weight, out_weight,
    )


def back_feed_kernel(n, groups, tiles, *refs):
    take = splitter(refs)
    gains_ref, first_share_ref, tokens_far, cotangent_far, gate_far, up_far, down_far = take(7)
    out_ref, kept_ref, gain_grad_ref = take(3)
    recv, more_far, active_far, layer_far, hidden_far = take(5)
    active_ref, layer_ref, first_up, first_down, up_in, down_in = take(6)
    hidden_ref, tokens_ref, cotangent_ref, share_ref, weight_ref, d_active_ref = take(6)
    load_sems, weight_sems, first_sems, sems = take(4)
    rows = RowGrads(groups, None, tiles, recv, take(10), deferred=1)
    feed_ref = rows.left
    count, width = share_ref.shape
    wide = active_ref.shape[1]
    full, rest = wide // 256, wide % 256
    pieces = full + (rest > 0)
    half = count // 2
    first_line = Line(
        n, first_share_ref, first_up, first_down, feed_ref, first_sems,
        norm_forward(
            lambda own, place: tokens_ref[own, :], lambda: gains_ref[1:2, :], feed_ref, hidden_ref
        ),
    )
    line = Line(
        n, share_ref, up_in, down_in, out_ref, sems,
        norm_back(
            hidden_ref, lambda own, place: cotangent_ref[place, :], lambda: gains_ref[1:2, :],
            out_ref, kept_ref, gain_grad_ref,
        ),
    )
    token_loads = first_line.own_copies(tokens_far, tokens_ref, [load_sems.at[0], load_sems.at[1]])
    cotangent_load = pltpu.make_async_copy(cotangent_far, cotangent_ref, load_sems.at[2])
    down_load = pltpu.make_async_copy(
        down_far, weight_ref.at[pl.ds(0, wide), pl.ds(0, width)], load_sems.at[3]
    )
    active_spill = pltpu.make_async_copy(active_ref, active_far, load_sems.at[4])
    layer_spill = pltpu.make_async_copy(layer_ref, layer_far, load_sems.at[5])
    hidden_spill = pltpu.make_async_copy(hidden_ref, hidden_far, load_sems.at[6])
    more_start, more_wide = tiles[-1]
    more_spill = pltpu.make_async_copy(
        rows.send.at[:, :, pl.ds(more_start, more_wide)], more_far, load_sems.at[7]
    )

    def spans(i, size):
        start = pl.multiple_of(i * 256, 256)
        return pl.ds(start, size), pl.ds(pl.multiple_of(wide + start, LANES), size)

    def weight_loads(i, size):
        gate_span, up_span = spans(i, size)
        return (
            pltpu.make_async_copy(
                gate_far.at[:, gate_span], weight_ref.at[:, gate_span], weight_sems.at[0, i]
            ),
            pltpu.make_async_copy(
                up_far.at[:, gate_span], weight_ref.at[:, up_span], weight_sems.at[1, i]
            ),
        )

    def block_rows(b):
        return pl.ds(b * half, half)

    def piece_copies(b, i, size):
        gate_span, up_span = spans(i, size)
        at = block_rows(b)
        return tuple(
            rows.piece_copy(2 * (b * pieces + i) + j, rows.all.at[at, span], span, at)
            for j, span in enumerate((gate_span, up_span))
        )

    def each(action):
        @pl.loop(0, full)
        def _(i):
            action(i, 256)

        if rest:
            action(full, rest)

    def at_item(w, action):
        @pl.when((w >= 0) & (w < full))
        def _():
            action(w, 256)

        if rest:
            @pl.when(w == full)
            def _():
                action(full, rest)

    down_load.start()
    cotangent_load.start()
    for c in token_loads:
        c.start()
    barrier = pltpu.get_barrier_semaphore()
    greet_dp(barrier, groups)
    line.greet(barrier, groups - 1)
    first_line.prime()
    for c in token_loads:
        c.wait()

    def make_d_active(i, size):
        span, _ = spans(i, size)
        d_active_ref[:, span] = dot_t(
            cotangent_ref[...], weight_ref[span, pl.ds(0, width)]
        ).astype(bf16)

    def start_weights(i, size):
        for c in weight_loads(i, size):
            c.start()

    def hidden_units(b, i, size):
        if b == 0:
            for c in weight_loads(i, size):
                c.wait()
        gate_span, up_span = spans(i, size)
        at = block_rows(b)
        gate = dot(feed_ref[at, :], weight_ref[:, gate_span])
        up = dot(feed_ref[at, :], weight_ref[:, up_span])
        d_active = d_active_ref[at, gate_span].astype(f32)
        sigmoid = jax.nn.sigmoid(gate)
        swish = gate * sigmoid
        active_ref[at, gate_span] = (swish * up).astype(bf16)
        rows.all[at, gate_span] = (
            d_active * up * sigmoid * (1.0 + gate * (1.0 - sigmoid))
        ).astype(bf16)
        rows.all[at, up_span] = (d_active * swish).astype(bf16)
        for c in piece_copies(b, i, size):
            c.start()

    share_items = width // 256

    def make_share(b, w):
        @pl.when((w >= 0) & (w < share_items))
        def _():
            to = pl.ds(pl.multiple_of(w * 256, 256), 256)
            at = block_rows(b)
            share_ref[at, to] = dot_t(rows.all[at, :], weight_ref[to, :]).astype(bf16)

    per = first_line.block // FINE
    arrived = first_line.second + SKEW * (n - 2) + per
    d_first = 3

    @pl.loop(0, first_line.steps)
    def _(step):
        first_line.step(step)

        @pl.when(step == d_first)
        def _():
            down_load.wait()
            cotangent_load.wait()

        at_item(step - d_first, make_d_active)

        @pl.when(step == d_first + pieces)
        def _():
            each(start_weights)

        at_item(step - arrived, lambda i, size: hidden_units(0, i, size))
        w = 2 * (step - arrived - pieces)
        make_share(0, w)
        make_share(0, w + 1)

    done_share = 2 * (first_line.steps - arrived - pieces)

    @pl.loop(done_share, max(share_items, done_share))
    def _(w):
        make_share(0, w)

    line.prime(0)
    hidden_spill.start()

    @pl.loop(0, rows.team)
    def _(q):
        rows.left_copy(q).start()

    layer_items = width // 512
    first_work = 8
    if 2 * (per - pieces) < share_items:
        raise ValueError("shares late")

    @pl.loop(0, line.steps)
    def _(step):
        @pl.when(step == per)
        def _():
            line.prime(1)
            active_spill.start()
            down_load.start()

        line.step(step)
        at_item(step, lambda i, size: hidden_units(1, i, size))
        w = 2 * (step - pieces)
        make_share(1, w)
        make_share(1, w + 1)
        w = step - first_work

        @pl.when(w == 0)
        def _():
            @pl.loop(0, rows.team)
            def _(q):
                rows.left_copy(q).wait_recv()

            for b in range(2):
                def arrive(i, size, b=b):
                    for c in piece_copies(b, i, size):
                        c.wait_recv()

                each(arrive)

        rows.item(w)

        @pl.when(w == rows.items)
        def _():
            more_spill.start()
            down_load.wait()

        layer_item = w - rows.items

        @pl.when((layer_item >= 0) & (layer_item < layer_items))
        def _():
            to = pl.ds(pl.multiple_of(layer_item * 512, 512), 512)
            layer_ref[:, to] = dot(active_ref[...], weight_ref[pl.ds(0, wide), to]).astype(bf16)

        @pl.when(layer_item == layer_items)
        def _():
            layer_spill.start()

    rows.receive()
    first_line.drain()
    line.drain()
    rows.drain()
    for c in (active_spill, layer_spill, hidden_spill, more_spill):
        c.wait()
    for b in range(2):
        def sent(i, size, b=b):
            for c in piece_copies(b, i, size):
                c.wait_send()

        each(sent)


def back_feed(call, n, groups, gains, share, tokens, cotangent, feed_gate, feed_up, feed_down):
    count, width = share.shape
    half = count // 2
    wide = feed_gate.shape[1]
    pieces = (wide + 255) // 256
    cut = (wide // 2 + LANES - 1) // LANES * LANES
    tiles = [(0, cut), (cut, wide - cut), (wide, cut), (wide + cut, wide - cut)]
    team, per = groups // 2, width // groups
    vmem = pl.BlockSpec(memory_space=pltpu.VMEM)
    far = pl.BlockSpec(memory_space=pl.ANY)
    shape = jax.ShapeDtypeStruct
    return pl.pallas_call(
        functools.partial(back_feed_kernel, n, groups, tiles),
        in_specs=[vmem] * 2 + [far] * 5,
        out_specs=[vmem] * 3 + [far] * 5,
        out_shape=[
            shape((count, width), bf16),
            shape((half, width), f32),
            shape((8, width), f32),
            shape((team, per, wide + cut), bf16),
            shape((team, per, wide - cut), bf16),
            shape((count, wide), bf16),
            shape((count, width), bf16),
            shape((half, width), f32),
        ],
        scratch_shapes=[pltpu.VMEM((count, wide), bf16), pltpu.VMEM((count, width), bf16)]
        + Line.scratch(half, width)
        + Line.scratch(half, width)
        + [
            pltpu.VMEM((half, width), f32),
            pltpu.VMEM((half, width), bf16),
            pltpu.VMEM((count, width), bf16),
            pltpu.VMEM((count, width), bf16),
            pltpu.VMEM((width, 2 * wide), bf16),
            pltpu.VMEM((count, wide), bf16),
            pltpu.SemaphoreType.DMA((8,)),
            pltpu.SemaphoreType.DMA((2, pieces)),
            Line.semaphores(half),
            Line.semaphores(half),
        ]
        + RowGrads.scratch(groups, count, width, 2 * wide, 4 * pieces, len(tiles)),
        compiler_params=pltpu.CompilerParams(
            collective_id=call, has_side_effects=True, vmem_limit_bytes=61 << 20
        ),
        cost_estimate=pl.CostEstimate(
            flops=30_000_000_000, bytes_accessed=200_000_000, transcendentals=0
        ),
        name="back_feed",
    )(gains, share, tokens, cotangent, feed_gate, feed_up, feed_down)


class SmallSum:
    def __init__(self, n, groups, wide, near, near_all, wide_out, near_out, refs):
        (
            self.wide_in, self.near_in, self.wide_line, self.near_line, self.sems, self.line_sems,
        ) = refs
        self.n, self.groups, self.near_all = n, groups, near_all
        self.wide, self.near, self.wide_out, self.near_out = wide, near, wide_out, near_out
        self.member, self.place = lax.axis_index("dp"), lax.axis_index("tensor")
        self.block = wide.shape[1] // groups

    @staticmethod
    def scratch(n, groups, wide, near):
        block = wide[1] // groups
        return [
            pltpu.VMEM((groups, wide[0], block), f32),
            pltpu.VMEM(near, f32),
            pltpu.VMEM((n, wide[0], block), f32),
            pltpu.VMEM((n,) + near[1:], f32),
            pltpu.SemaphoreType.DMA((2, 2, groups)),
            pltpu.SemaphoreType.DMA((2, 2, n)),
        ]

    def greet(self, barrier):
        n, place = self.n, self.place
        for k in range(2, n):
            @pl.when(place + k < n)
            def _():
                pl.semaphore_signal(
                    barrier, inc=1, device_id={"tensor": place + k}, device_id_type=MESH
                )

            @pl.when(place - k >= 0)
            def _():
                pl.semaphore_signal(
                    barrier, inc=1, device_id={"tensor": place - k}, device_id_type=MESH
                )

    def cut(self, j):
        return pl.ds(pl.multiple_of(j * self.block, self.block), self.block)

    def copies(self, to, source):
        return (
            to_dp(
                self.wide.at[:, self.cut(to)], self.wide_in.at[source],
                self.sems.at[0, 0, to], self.sems.at[1, 0, source], to,
            ),
            to_dp(
                self.near.at[to], self.near_in.at[source],
                self.sems.at[0, 1, to], self.sems.at[1, 1, source], to,
            ),
        )

    def line_copies(self, to, source):
        return tuple(
            pltpu.make_async_remote_copy(
                line.at[self.place], line.at[source], self.line_sems.at[0, i, to],
                self.line_sems.at[1, i, source], device_id={"tensor": to}, device_id_type=MESH,
            )
            for i, line in enumerate((self.wide_line, self.near_line))
        )

    def send(self):
        @pl.loop(1, self.groups)
        def _(k):
            for c in self.copies(lax.rem(self.member + k, self.groups), self.member):
                c.start()

        self.wide_in[pl.ds(self.member, 1)] = self.wide[:, self.cut(self.member)][None]
        self.near_in[pl.ds(self.member, 1)] = self.near[pl.ds(self.member, 1)]

    def forward(self):
        @pl.loop(1, self.groups)
        def _(k):
            for c in self.copies(0, lax.rem(self.member + k, self.groups)):
                c.wait_recv()

        for came, line in ((self.wide_in, self.wide_line), (self.near_in, self.near_line)):
            total = came[0]
            for j in range(1, self.groups):
                total = total + came[j]
            line[pl.ds(self.place, 1)] = total[None]

        @pl.loop(1, self.n)
        def _(k):
            for c in self.line_copies(lax.rem(self.place + k, self.n), self.place):
                c.start()

    def receive(self):
        @pl.loop(1, self.n)
        def _(k):
            for c in self.line_copies(0, lax.rem(self.place + k, self.n)):
                c.wait_recv()

        total = self.wide_line[0]
        for j in range(1, self.n):
            total = total + self.wide_line[j]
        self.wide_out[...] = total
        own = self.near_line[pl.ds(self.place, 1)][0]
        total = self.near_line[0]
        for j in range(1, self.n):
            total = total + self.near_line[j]
        row = lax.broadcasted_iota(jnp.int32, own.shape, 0)
        self.near_out[...] = jnp.where(row < self.near_all, total, own)

    def drain(self):
        @pl.loop(1, self.groups)
        def _(k):
            for c in self.copies(lax.rem(self.member + k, self.groups), self.member):
                c.wait_send()

        @pl.loop(1, self.n)
        def _(k):
            for c in self.line_copies(lax.rem(self.place + k, self.n), self.place):
                c.wait_send()


def back_mixer_kernel(n, groups, widths, near_all, tiles, *refs):
    take = splitter(refs)
    gains_ref, near_ref, down_rows_ref, x_far, base_far, left_far = take(6)
    parts = take(2)
    col_left, col_right, more_far = take(3)
    weights = take(len(widths))
    out_ref, wide_out, near_out, recv, col_recv, more_recv = take(6)
    more_ref, more_sems, more_load_sems = take(3)
    up_in, down_in, x_ref, base_ref, share_ref, wide_ref, gain_grad_ref = take(7)
    weight_ref, latent_ref, load_sems, sems = take(4)
    rows = RowGrads(groups, left_far, tiles, recv, take(10))
    part_spans = [
        pl.ds(0, parts[0].shape[1]), pl.ds(parts[0].shape[1], parts[1].shape[1])
    ]
    part_loads = [rows.piece_load(i, parts[i], part_spans[i]) for i in range(2)]
    part_copies = [rows.piece_copy(i, parts[i], part_spans[i]) for i in range(2)]
    cols = ColGrad(groups, col_left, col_right, 0, col_recv, take(8))
    small = SmallSum(n, groups, wide_ref, near_ref, near_all, wide_out, near_out, take(6))
    finish = norm_back(
        x_ref, lambda own, place: base_ref[own, :], lambda: gains_ref[0:1, :], out_ref, None,
        gain_grad_ref,
    )
    line = Line(n, share_ref, up_in, down_in, out_ref, sems, finish)
    loads = line.own_copies(x_far, x_ref, [load_sems.at[0], more_load_sems.at[0]])
    loads.append(pltpu.make_async_copy(base_far, base_ref, load_sems.at[1]))
    more_load = pltpu.make_async_copy(more_far, more_ref, more_load_sems.at[1])

    def more_copy(to, source):
        return to_dp(
            more_ref.at[to], more_recv.at[source], more_sems.at[0, to], more_sems.at[1, source],
            2 * to + rows.parity,
        )

    more_keep = pltpu.make_async_copy(
        more_ref.at[rows.mine], more_recv.at[rows.mine], more_load_sems.at[2]
    )
    more_load.start()
    weight_loads = []
    offset = 0
    for i, wide in enumerate(widths):
        if i == len(widths) - 1:
            latent_at = offset
            offset += LANES
        weight_loads.append(
            pltpu.make_async_copy(
                weights[i], weight_ref.at[:, pl.ds(offset, wide)], load_sems.at[2 + i]
            )
        )
        offset += wide
    for c in part_loads + weight_loads:
        c.start()
    thirds(down_rows_ref, 2, latent_ref)
    weight_ref[:, pl.ds(latent_at, LANES)] = jnp.transpose(latent_ref[...].astype(f32)).astype(bf16)
    barrier = pltpu.get_barrier_semaphore()
    greet_dp(barrier, groups)
    small.greet(barrier)
    line.greet_all(barrier, groups - 1)
    rows.start_left()
    for c in part_copies:
        c.start()
    cols.start()
    for c in loads:
        c.start()
    more_load.wait()
    more_keep.start()

    @pl.loop(1, rows.team)
    def _(k):
        more_copy(lax.rem(rows.mine + k, rows.team), rows.mine).start()

    for c in part_loads + weight_loads:
        c.wait()

    count, width = share_ref.shape
    tile_rows, tile_columns = count // 2, 512
    across = width // tile_columns

    for c in loads:
        c.wait()
    for b in range(2):
        at = pl.ds(b * tile_rows, tile_rows)

        @pl.loop(0, across)
        def _(i):
            to = pl.ds(pl.multiple_of(i * tile_columns, tile_columns), tile_columns)
            share_ref[at, to] = dot_t(rows.all[at, :], weight_ref[to, :]).astype(bf16)

        line.prime(b)

    third = LANES // 4
    first_cols = rows.items
    last_item = first_cols + cols.items

    @pl.loop(0, line.steps)
    def _(step):
        line.step(step)

        @pl.when(step == 0)
        def _():
            rows.ready_left()
            for c in part_copies:
                c.wait_recv()

        rows.item(step)

        @pl.when(step == first_cols)
        def _():
            cols.ready()

        @pl.when((step >= first_cols) & (step < last_item))
        def _():
            cols.item(step - first_cols)

        @pl.when(step == last_item)
        def _():
            cols.send_all()
            product = rows_dot(rows.all[:, pl.ds(latent_at, LANES)], rows.left[...])
            wide_ref[:16, :] = product[:16, :] + product[third : third + 16, :]

        @pl.when(step == line.count + SKEW * (n - 2) + 2)
        def _():
            wide_ref[16:, :] = gain_grad_ref[...]
            small.send()

        @pl.when(step == line.second + 14)
        def _():
            small.forward()

    more_keep.wait()

    @pl.loop(1, rows.team)
    def _(k):
        more_copy(0, lax.rem(rows.mine + k, rows.team)).wait_recv()
        more_copy(lax.rem(rows.mine + k, rows.team), rows.mine).wait_send()

    rows.receive()
    cols.receive()
    small.receive()
    line.drain()
    rows.drain()
    for c in part_copies:
        c.wait_send()
    cols.drain()
    small.drain()


def back_mixer(
    call, n, groups, gains, near, near_all, down_rows, x, base_own, left, parts, pair, weights
):
    count, width = left.shape
    half = count // 2
    widths = [w.shape[1] for w in weights]
    total = sum(part.shape[1] for part in parts)
    start = parts[0].shape[1]
    tiles = [(0, 512), (512, 512), (start, parts[1].shape[1])]
    col_rows = pair[0].shape[1]
    vmem = pl.BlockSpec(memory_space=pltpu.VMEM)
    far = pl.BlockSpec(memory_space=pl.ANY)
    wide_shape = (24, width)
    return pl.pallas_call(
        functools.partial(back_mixer_kernel, n, groups, widths, near_all, tiles),
        in_specs=[vmem] * 3 + [far] * (8 + len(weights)),
        out_specs=[vmem] * 3 + [far] * 3,
        out_shape=[
            jax.ShapeDtypeStruct((count, width), bf16),
            jax.ShapeDtypeStruct((24, width // groups), f32),
            jax.ShapeDtypeStruct(near.shape[1:], f32),
            jax.ShapeDtypeStruct((groups // 2, width // groups, total), bf16),
            jax.ShapeDtypeStruct((groups, col_rows // groups, width // 2), bf16),
            jax.ShapeDtypeStruct(pair[2].shape, bf16),
        ],
        scratch_shapes=[
            pltpu.VMEM(pair[2].shape, bf16),
            pltpu.SemaphoreType.DMA((2, groups // 2)),
            pltpu.SemaphoreType.DMA((3,)),
        ]
        + Line.scratch(half, width)
        + [
            pltpu.VMEM((half, width), x.dtype),
            pltpu.VMEM((half, width), base_own.dtype),
            pltpu.VMEM((count, width), bf16),
            pltpu.VMEM(wide_shape, f32),
            pltpu.VMEM((8, width), f32),
            pltpu.VMEM((width, total), bf16),
            pltpu.VMEM((LANES, width), bf16),
            pltpu.SemaphoreType.DMA((2 + len(weights),)),
            Line.semaphores(half),
        ]
        + RowGrads.scratch(groups, count, width, total, 2, len(tiles))
        + ColGrad.scratch(groups, count, col_rows, width // 2)
        + SmallSum.scratch(n, groups, wide_shape, near.shape),
        compiler_params=pltpu.CompilerParams(
            collective_id=call, has_side_effects=True, vmem_limit_bytes=61 << 20
        ),
        cost_estimate=pl.CostEstimate(
            flops=12_000_000_000, bytes_accessed=200_000_000, transcendentals=0
        ),
        name="back_mixer",
    )(gains, near, down_rows, x, base_own, left, *parts, *pair, *weights)


def outputs_kernel(dk, dv, rank, near_all, *refs):
    take = splitter(refs)
    feed_ref, feed_more_ref, rows_ref, down_ref, out_ref = take(5)
    wide_ref, near_ref, token_ref, layer_ref = take(4)
    token_out, layer_out, query_out, key_out, value_out, gate_out = take(6)
    feed_gate_out, feed_up_out, feed_down_out, out_out, decay_out, vector_out = take(6)
    step = pl.program_id(0)

    def total(ref, start, wide):
        span = pl.ds(start, wide)
        result = ref[0, :, span].astype(f32)
        for q in range(1, ref.shape[0]):
            result = result + ref[q, :, span].astype(f32)
        return result

    wide = feed_gate_out.shape[1]
    feed_gate_out[...] = total(feed_ref, 0, wide)
    there = feed_ref.shape[2] - wide
    feed_up_out[:, :there] = total(feed_ref, wide, there)
    feed_up_out[:, there:] = total(feed_more_ref, 0, wide - there)
    query_out[...] = total(rows_ref, 0, dk)
    key_out[...] = total(rows_ref, dk, dk)
    value_out[...] = total(rows_ref, 2 * dk, dv)
    gate_out[...] = total(rows_ref, 2 * dk + dv + LANES, dv)
    token_out[...] = token_ref[...]
    layer_out[...] = layer_ref[...]

    @pl.when(lax.rem(step, pl.num_programs(0) // 2) == 0)
    def _():
        half = out_out.shape[2] // 2
        for ref, out in ((down_ref, feed_down_out), (out_ref, out_out)):
            for b in range(2):
                result = ref[b].astype(f32)
                for q in range(1, ref.shape[0] // 2):
                    result = result + ref[2 * q + b].astype(f32)
                out[0, :, b * half : (b + 1) * half] = result

    @pl.when(step == 0)
    def _():
        decay_out[...] = wide_ref[:rank, :]
        vector_out[...] = jnp.sum(wide_ref[rank:, :], axis=0, keepdims=True)


def outputs(
    groups, dk, dv, rank, near_all, feed, feed_more, rows, down, out, wide_sum, near_sum, token,
    layer,
):
    steps = 4
    count, width = token.shape
    wide = (feed.shape[2] + feed_more.shape[2]) // 2
    per = width // groups
    block = per // steps
    shape = jax.ShapeDtypeStruct

    def rows_of(columns):
        return pl.BlockSpec((block, columns), lambda i: (i, 0))

    def fixed(array):
        return pl.BlockSpec(array.shape, lambda i: (0,) * array.ndim)

    def recv(array):
        return pl.BlockSpec((array.shape[0], block, array.shape[2]), lambda i: (0, i, 0))

    def recv_half(array):
        return pl.BlockSpec(
            (array.shape[0], array.shape[1] // 2, array.shape[2]), lambda i: (0, i // (steps // 2), 0)
        )

    def out_half(array):
        return pl.BlockSpec((1, array.shape[1] // 2, width), lambda i: (0, i // (steps // 2), 0))

    tokens_block = pl.BlockSpec((count // steps, width), lambda i: (i, 0))
    return pl.pallas_call(
        functools.partial(outputs_kernel, dk, dv, rank, near_all),
        grid=(steps,),
        in_specs=[
            recv(feed), recv(feed_more), recv(rows), recv_half(down), recv_half(out), fixed(wide_sum),
            fixed(near_sum), tokens_block, tokens_block,
        ],
        out_specs=[
            tokens_block, tokens_block, rows_of(dk), rows_of(dk), rows_of(dv), rows_of(dv),
            rows_of(wide), rows_of(wide), out_half(down), out_half(out),
            pl.BlockSpec((rank, per), lambda i: (0, 0)),
            pl.BlockSpec((1, per), lambda i: (0, 0)),
        ],
        out_shape=[
            shape((count, width), bf16),
            shape((count, width), bf16),
            shape((per, dk), f32),
            shape((per, dk), f32),
            shape((per, dv), f32),
            shape((per, dv), f32),
            shape((per, wide), f32),
            shape((per, wide), f32),
            shape((1, down.shape[1], width), f32),
            shape((1, out.shape[1], width), f32),
            shape((rank, per), f32),
            shape((1, per), f32),
        ],
        compiler_params=pltpu.CompilerParams(vmem_limit_bytes=60 << 20),
        name="outputs",
    )(feed, feed_more, rows, down, out, wide_sum, near_sum, token, layer)


def recur_back_kernel(n, groups, dk, dv, beside, *refs):
    (
        lengths_ref, send_row_ref, send_column_ref, slot_row_ref, slot_column_ref,
        d_mixed_ref, out_weight_ref, attended_ref, gate_ref, gains_ref, up_rows_ref,
        share_ref, held_far, states_far, hidden_far, active_far, cotangent_far,
        d_rows_ref, d_gate_ref, head_gain_ref, grad_up_ref, grad_bias_ref, layer_ref, grad_down_ref,
        up_in, down_in, d_attended, d_placed, d_state, result,
        held_ref, states_ref, hidden_ref, up_ref, down_ref, bias_ref, load_sems, sems,
    ) = refs[:38]
    go = Exchange(groups, (), *refs[38:41])
    back = Exchange(groups, (2 * dk,), *refs[41:44])
    cols = None
    if beside:
        cols = ColGrad(groups, active_far, cotangent_far, 0, grad_down_ref, refs[44:])
    count = d_mixed_ref.shape[0]
    slots = slot_row_ref.shape[1]
    end0 = lengths_ref[0, 0]
    end1 = end0 + lengths_ref[0, 1]
    ends = (end0, end1, end1 + lengths_ref[0, 2])

    def finish(total, own, place):
        layer_ref[place, :] = (hidden_ref[own, :] + total).astype(layer_ref.dtype)

    line = Line(n, share_ref, up_in, down_in, layer_ref, sems, finish)
    loads = (
        pltpu.make_async_copy(hidden_far, hidden_ref, load_sems.at[0]),
        pltpu.make_async_copy(held_far, held_ref, load_sems.at[1]),
        pltpu.make_async_copy(states_far, states_ref, load_sems.at[2]),
    )
    barrier = pltpu.get_barrier_semaphore()
    greet_dp(barrier, groups)
    line.greet(barrier, groups - 1)
    line.prime()
    for c in loads:
        c.start()
    if beside:
        cols.start()
    loads[0].wait()

    bias_ref[...] = gains_ref[2:3, dv : dv + dk]
    thirds(up_rows_ref, 3, up_ref)
    thirds(up_rows_ref, 2, down_ref)

    head_gain_ref[...] = jnp.zeros_like(head_gain_ref)
    tile = count // 2

    @pl.loop(0, 2)
    def _(i):
        rows = pl.ds(pl.multiple_of(i * tile, tile), tile)
        d_gated = dot_t(d_mixed_ref[rows, :], out_weight_ref[...])
        attended = attended_ref[rows, :].astype(f32)
        gate = gate_ref[rows, :]
        scaling = lax.rsqrt(jnp.mean(attended * attended, axis=1, keepdims=True) + head_floor)
        unit = attended * scaling
        sigmoid = jax.nn.sigmoid(gate)
        swish = gate * sigmoid
        gained = d_gated * gains_ref[2:3, :dv]
        d_gate_ref[rows, :] = (
            gained * unit * sigmoid * (1.0 + gate * (1.0 - sigmoid))
        ).astype(bf16)
        d_unit = gained * swish
        d_attended[rows, :] = (
            scaling * (d_unit - unit * jnp.mean(d_unit * unit, axis=1, keepdims=True))
        ).astype(bf16)
        term = d_gated * unit * swish
        piece = term[0:8, :]
        for r in range(1, tile // 8):
            piece = piece + term[8 * r : 8 * r + 8, :]
        head_gain_ref[...] += piece
        line.step(2 * i)
        line.step(2 * i + 1)

    go.send(0, send_row_ref, 0, d_attended, lambda h: line.step(4 + h))
    d_state[...] = jnp.zeros_like(d_state)
    grad_up_ref[...] = jnp.zeros_like(grad_up_ref)
    grad_bias_ref[...] = jnp.zeros_like(grad_bias_ref)
    done = 14
    if beside:
        cols.ready()

        @pl.loop(0, cols.items)
        def _(i):
            cols.item(i)
            line.step(6 + 2 * i)
            line.step(7 + 2 * i)

        done = 6 + 2 * cols.items
        cols.send_all()
    else:
        line.run(6, done)
    for c in loads[1:]:
        c.wait()

    go.receive(0)
    place_rows(slot_row_ref, go.came, d_placed, go.spans[0], lambda h: line.step(done + h))
    spanned = done + 2
    spans = held_ref.shape[0] // SPAN

    @pl.loop(0, spans)
    def _(i):
        step = spans - 1 - i
        d_out = d_placed[pl.ds(pl.multiple_of(step * SPAN, SPAN), SPAN), :]
        span_backward(
            dk, dv, step, ends, d_out, held_ref, states_ref[step], up_ref, bias_ref, down_ref,
            d_state, result, grad_up_ref, grad_bias_ref,
        )
        line.step(spanned + 2 * i)
        line.step(spanned + 1 + 2 * i)

    sent = spanned + 2 * spans
    for p in range(2):
        back.send(
            p, slot_column_ref, 1, result, lambda h, p=p: line.step(sent + 2 * p + h)
        )
    last_steps = (sent + 4, sent + 4 + (line.steps - sent - 4) * 2 // 3, line.steps)
    for p in range(2):
        line.run(last_steps[p], last_steps[p + 1])
        if beside and p:
            cols.receive()
        back.receive(p)
        span = back.spans[p]

        @pl.loop(0, 2)
        def _(i):
            rows = pl.ds(pl.multiple_of(i * tile, tile), tile)
            pick = one_hot(send_column_ref[rows, :], 0, (tile, slots), 1)
            d_rows_ref[rows, span] = dot(pick, back.came[:, span]).astype(bf16)

    line.drain()
    if beside:
        cols.drain()
    go.drain()
    back.drain()


def recur_back(
    call, n, groups, dk, dv, beside, lengths, send_row, send_column, slot_row, slot_column, d_mixed, out_weight, attended, gate_pre,
    gains, up_rows, share, held, states, hidden_own, active, cotangent,
):
    count, width = d_mixed.shape
    slots, wide = held.shape
    half = count // 2
    vmem = pl.BlockSpec(memory_space=pltpu.VMEM)
    operands = [
        lengths, send_row, send_column, slot_row, slot_column, d_mixed, out_weight, attended, gate_pre, gains, up_rows, share, held, states, hidden_own, active, cotangent,
    ]
    far = pl.BlockSpec(memory_space=pl.ANY)
    return pl.pallas_call(
        functools.partial(recur_back_kernel, n, groups, dk, dv, beside),
        in_specs=[pl.BlockSpec(memory_space=pltpu.SMEM)] + [vmem] * (len(operands) - 6) + [far] * 5,
        out_specs=[vmem] * 6 + [far],
        out_shape=[
            jax.ShapeDtypeStruct((count, wide), bf16),
            jax.ShapeDtypeStruct((count, dv), bf16),
            jax.ShapeDtypeStruct((8, dv), f32),
            jax.ShapeDtypeStruct((dk, LANES), f32),
            jax.ShapeDtypeStruct((8, dk), f32),
            jax.ShapeDtypeStruct((count, width), bf16),
            jax.ShapeDtypeStruct(
                (groups, active.shape[1] // groups if beside else 8, width // 2), bf16
            ),
        ],
        scratch_shapes=Line.scratch(half, width)
        + [
            pltpu.VMEM((count, dv), bf16),
            pltpu.VMEM((slots, dv), bf16),
            pltpu.VMEM((dk, dv), f32),
            pltpu.VMEM((slots, wide), bf16),
            pltpu.VMEM(held.shape, bf16),
            pltpu.VMEM(states.shape, bf16),
            pltpu.VMEM((half, width), f32),
            pltpu.VMEM((LANES, dk), bf16),
            pltpu.VMEM((LANES, dk), bf16),
            pltpu.VMEM((1, dk), f32),
            pltpu.SemaphoreType.DMA((3,)),
            Line.semaphores(half),
        ]
        + Exchange.scratch(groups, slots, dv, 1)
        + Exchange.scratch(groups, slots, wide, 2)
        + (ColGrad.scratch(groups, count, active.shape[1], width // 2) if beside else []),
        compiler_params=pltpu.CompilerParams(
            collective_id=call, has_side_effects=True, vmem_limit_bytes=60 << 20
        ),
        cost_estimate=pl.CostEstimate(
            flops=12_000_000_000, bytes_accessed=200_000_000, transcendentals=4_000_000
        ),
        name="recur_back",
    )(*operands)


def small_sum_kernel(groups, n, rows_all, part_ref, out_ref, held, line, line_in, sems, line_sems):
    me = lax.axis_index("dp")
    place = lax.axis_index("tensor")
    barrier = pltpu.get_barrier_semaphore()

    def peer(k):
        return lax.rem(me + k, groups)

    def mate(k):
        return lax.rem(place + k, n)

    @pl.loop(1, groups)
    def _(k):
        pl.semaphore_signal(barrier, inc=1, device_id={"dp": peer(k)}, device_id_type=MESH)

    @pl.loop(1, n)
    def _(k):
        pl.semaphore_signal(barrier, inc=1, device_id={"tensor": mate(k)}, device_id_type=MESH)

    pl.semaphore_wait(barrier, groups + n - 2)

    def copy(k, source):
        return pltpu.make_async_remote_copy(
            part_ref.at[peer(k)], held.at[source], sems.at[0, k], sems.at[1, source],
            device_id={"dp": peer(k)}, device_id_type=MESH,
        )

    def line_copy(k, source):
        return pltpu.make_async_remote_copy(
            line, line_in.at[source], line_sems.at[0, k], line_sems.at[1, source],
            device_id={"tensor": mate(k)}, device_id_type=MESH,
        )

    @pl.loop(1, groups)
    def _(k):
        copy(k, me).start()

    held[pl.ds(me, 1)] = part_ref[pl.ds(me, 1)]

    @pl.loop(1, groups)
    def _(k):
        copy(k, peer(k)).wait_recv()

    total = held[0]
    for i in range(1, groups):
        total = total + held[i]
    line[...] = total[:rows_all]
    out_ref[...] = total

    @pl.loop(1, n)
    def _(k):
        line_copy(k, place).start()

    line_in[pl.ds(place, 1)] = total[None, :rows_all]

    @pl.loop(1, n)
    def _(k):
        line_copy(k, mate(k)).wait_recv()

    total = line_in[0]
    for i in range(1, n):
        total = total + line_in[i]
    out_ref[:rows_all] = total

    @pl.loop(1, groups)
    def _(k):
        copy(k, me).wait_send()

    @pl.loop(1, n)
    def _(k):
        line_copy(k, place).wait_send()


def small_sum(over_all, over_owners, groups, n, call):
    def tiles(blocks):
        short = -blocks.shape[1] % (8 * LANES)
        return jnp.pad(blocks, ((0, 0), (0, short))).reshape(groups, -1, LANES)

    first, second = tiles(over_all), tiles(over_owners)
    rows_all = first.shape[1]
    part = jnp.concatenate([first, second], axis=1)
    vmem = pl.BlockSpec(memory_space=pltpu.VMEM)
    total = pl.pallas_call(
        functools.partial(small_sum_kernel, groups, n, rows_all),
        in_specs=[vmem],
        out_specs=vmem,
        out_shape=jax.ShapeDtypeStruct(part.shape[1:], f32),
        scratch_shapes=[
            pltpu.VMEM(part.shape, f32),
            pltpu.VMEM((rows_all, LANES), f32),
            pltpu.VMEM((n, rows_all, LANES), f32),
            pltpu.SemaphoreType.DMA((2, groups)),
            pltpu.SemaphoreType.DMA((2, n)),
        ],
        compiler_params=pltpu.CompilerParams(collective_id=call, has_side_effects=True),
        name="small_sum",
    )(part)
    return (
        total[:rows_all].reshape(-1)[: over_all.shape[1]],
        total[rows_all:].reshape(-1)[: over_owners.shape[1]],
    )


def per_device(
    tokens,
    cotangent,
    token_slots,
    lengths,
    mixer_gain,
    query_weight,
    key_weight,
    value_weight,
    gate_weight,
    decay_down,
    decay_up,
    decay_bias,
    head_gain,
    out_weight,
    feed_gain,
    feed_gate,
    feed_up,
    feed_down,
):
    groups = lax.axis_size("dp")
    lines = lax.axis_size("tensor")
    member = lax.axis_index("dp")
    place = lax.axis_index("tensor")
    count, width = tokens.shape
    dk = query_weight.shape[1]
    dv = value_weight.shape[1]
    rank = decay_up.shape[1]
    parity = lax.rem(member, 2)
    pairs = [(i, i ^ 1) for i in range(groups)]
    same_parity = [[i for i in range(groups) if i % 2 == b] for b in range(2)]

    fused = (width // groups) % LANES == 0
    third = LANES // 4
    down_rows = decay_down.T
    up_rows = decay_up.T
    last = jnp.pad(jnp.concatenate([head_gain, decay_bias]), (0, width - dv - dk))
    gains = jnp.stack([mixer_gain, feed_gain, last]).astype(f32)
    (
        normed, gate_pre, attended, gated, held, states, mixer_share, send_row, send_column, slot_row,
        slot_column,
    ) = front(
        1, groups, lengths, token_slots.reshape(-1, LANES), tokens, gains, up_rows,
        down_rows, [query_weight, key_weight, value_weight], gate_weight, out_weight,
    )

    if fused:
        (
            d_mixed, d_hidden_own, feed_gain_part, feed_recv, feed_more, active, layer_share,
            hidden_own,
        ) = back_feed(
            2, lines, groups, gains, mixer_share, tokens, cotangent, feed_gate, feed_up, feed_down
        )
    else:
        quarter = count // 4

        def own_rows(rows):
            blocks = rows.reshape(2, 2, quarter, width)
            return jnp.where(place == 0, blocks[:, 1], blocks[:, 0]).reshape(2 * quarter, width)

        tokens_own, cotangent_own = own_rows(tokens), own_rows(cotangent)
        feed_normed, hidden_own, _ = line_sum(
            "norm", 5, lines, mixer_share, tokens_own, tokens_own, gains[1:2]
        )
        d_active = dot_t(cotangent, feed_down).astype(bf16)
        gate_hidden = dot(feed_normed, feed_gate)
        up_hidden = dot(feed_normed, feed_up)
        d_active = d_active.astype(f32)
        sigmoid_gate = jax.nn.sigmoid(gate_hidden)
        swish_gate = gate_hidden * sigmoid_gate
        active = (swish_gate * up_hidden).astype(bf16)
        d_gate_hidden = (
            d_active * up_hidden * sigmoid_gate * (1.0 + gate_hidden * (1.0 - sigmoid_gate))
        ).astype(bf16)
        d_up_hidden = (d_active * swish_gate).astype(bf16)
        feed_share = (dot_t(d_gate_hidden, feed_gate) + dot_t(d_up_hidden, feed_up)).astype(bf16)
        d_mixed, d_hidden_own, feed_gain_part = line_sum(
            "back", 2, lines, feed_share, hidden_own, cotangent_own, gains[1:2]
        )
        layer_share = dot(active, feed_down).astype(bf16)

    d_rows, d_gate_low, head_gain_part, up_part, bias_part, layer_out, down_recv = recur_back(
        4, lines, groups, dk, dv, fused, lengths, send_row, send_column, slot_row, slot_column, d_mixed,
        out_weight, attended, gate_pre, gains, up_rows, layer_share, held, states, hidden_own, active,
        cotangent,
    )
    up_part = up_part[:, :rank] + up_part[:, third : third + rank] + (
        up_part[:, 2 * third : 2 * third + rank]
    )

    def by_owner(vector):
        return vector.reshape(groups, -1)

    per = width // groups
    head_per = dv // groups
    up_per = dk // groups * rank
    if fused:
        near = [
            by_owner(jnp.sum(feed_gain_part, axis=0)),
            jnp.pad(by_owner(jnp.sum(head_gain_part, axis=0)), ((0, 0), (0, -head_per % LANES))),
            by_owner(up_part),
            jnp.pad(by_owner(bias_part[0]), ((0, 0), (0, -(dk // groups) % LANES))),
        ]
        near_all = (per + head_per + LANES - 1) // LANES
        near = jnp.concatenate(near, axis=1)
        near = jnp.pad(near, ((0, 0), (0, -near.shape[1] % (8 * LANES))))
        token_grad, wide_sum, near_sum, rows_recv, out_recv, feed_more = back_mixer(
            3, lines, groups, gains, near.reshape(groups, -1, LANES), near_all, down_rows, tokens,
            d_hidden_own, normed, [d_rows, d_gate_low], (gated, d_mixed, feed_more),
            [query_weight, key_weight, value_weight, gate_weight],
        )
        (
            token_grad, layer_out, grad_query, grad_key, grad_value, grad_gate, grad_feed_gate,
            grad_feed_up, grad_feed_down, grad_out, down_sum, mixer_sum,
        ) = outputs(
            groups, dk, dv, rank, near_all, feed_recv, feed_more, rows_recv, down_recv, out_recv,
            wide_sum, near_sum, token_grad, layer_out,
        )
        near_sum = near_sum.reshape(-1)
        mixer_sum = mixer_sum.reshape(-1)
        down_sum = down_sum.T
        feed_sum = near_sum[:per]
        head_sum = near_sum[per : per + head_per]
        up_sum = near_sum[near_all * LANES : near_all * LANES + up_per]
        bias_sum = near_sum[near_all * LANES + up_per :][: dk // groups]
    else:
        down_pad = jnp.pad(decay_down, ((0, 0), (0, third - rank)))
        down_none = jnp.zeros_like(down_pad)
        down_both = jnp.concatenate([down_pad, down_pad, down_none, down_none], axis=1)
        d_query_low = d_rows[:, :dk]
        d_key_low = d_rows[:, dk : 2 * dk]
        d_value_low = d_rows[:, 2 * dk : 2 * dk + dv]
        d_latent_low = d_rows[:, 2 * dk + dv :]
        normed_share = (
            dot_t(d_query_low, query_weight)
            + dot_t(d_key_low, key_weight)
            + dot_t(d_value_low, value_weight)
            + dot_t(d_gate_low, gate_weight)
            + dot_t(d_latent_low, down_both)
        ).astype(bf16)
        token_grad, _, mixer_gain_part = line_sum(
            "back", 3, lines, normed_share, tokens_own, d_hidden_own, gains[0:1],
        )
        down_part = rows_dot(normed, d_latent_low)
        down_part = down_part[:, :rank] + down_part[:, third : third + rank]
        over_all = jnp.concatenate(
            [
                by_owner(jnp.sum(mixer_gain_part, axis=0)),
                by_owner(jnp.sum(feed_gain_part, axis=0)),
                by_owner(jnp.sum(head_gain_part, axis=0)),
                by_owner(down_part),
            ],
            axis=1,
        )
        over_owners = jnp.concatenate([by_owner(up_part), by_owner(bias_part[0])], axis=1)
        summed, small = small_sum(over_all, over_owners, groups, lines, 5)
        mixer_sum = summed[:per]
        feed_sum = summed[per : 2 * per]
        head_sum = summed[2 * per : 2 * per + head_per]
        down_sum = summed[2 * per + head_per :].reshape(per, rank)
        up_sum = small[:up_per]
        bias_sum = small[up_per:]

    def halves(row_block, dims):
        split = row_block.reshape(row_block.shape[0], groups // 2, 2, dims // groups)
        keep = lax.dynamic_index_in_dim(split, parity, 2, keepdims=False)
        send = lax.dynamic_index_in_dim(split, 1 - parity, 2, keepdims=False)
        got = lax.ppermute(send, "dp", pairs)
        shape = (row_block.shape[0], dims // 2)
        return keep.reshape(shape), got.reshape(shape)

    def partner(row_block):
        return row_block, lax.ppermute(row_block, "dp", pairs)

    def summed_share(left, right):
        share = (rows_dot(left[0], right[0]) + rows_dot(left[1], right[1])).astype(bf16)
        rows = share.shape[0] // (groups // 2)
        blocks = share.reshape(groups // 2, rows, share.shape[1])
        moved = lax.all_to_all(
            blocks, "dp", split_axis=0, concat_axis=0, tiled=True, axis_index_groups=same_parity
        )
        return jnp.sum(moved.astype(f32), axis=0)

    if not fused:
        grad_feed_down = summed_share(halves(active, active.shape[1]), partner(cotangent))[None]
        feed_halves = halves(feed_normed, width)
        normed_halves = halves(normed, width)
        grad_feed_gate = summed_share(feed_halves, partner(d_gate_hidden))
        grad_feed_up = summed_share(feed_halves, partner(d_up_hidden))
        grad_out = summed_share(halves(gated, dv), partner(d_mixed))[None]
        grad_query = summed_share(normed_halves, partner(d_query_low))
        grad_key = summed_share(normed_halves, partner(d_key_low))
        grad_value = summed_share(normed_halves, partner(d_value_low))
        grad_gate = summed_share(normed_halves, partner(d_gate_low))

    return (
        layer_out,
        token_grad,
        mixer_sum,
        grad_query,
        grad_key,
        grad_value,
        grad_gate,
        down_sum,
        up_sum.reshape(1, dk // groups, rank),
        bias_sum.reshape(1, dk // groups),
        head_sum,
        grad_out,
        feed_sum,
        grad_feed_gate,
        grad_feed_up,
        grad_feed_down,
    )


def solution(mesh):
    placed = (
        P("dp", None),
        P("dp", None),
        P(),
        P("dp", None),
        P(),
        P(None, "tensor"),
        P(None, "tensor"),
        P(None, "tensor"),
        P(None, "tensor"),
        P(),
        P("tensor", None),
        P("tensor"),
        P(),
        P("tensor", None),
        P(),
        P(None, "tensor"),
        P(None, "tensor"),
        P("tensor", None),
    )
    return jax.shard_map(
        per_device,
        mesh=mesh,
        in_specs=placed,
        out_specs=(
            P("dp", None),
            P("dp", None),
            P("dp"),
            P("dp", "tensor"),
            P("dp", "tensor"),
            P("dp", "tensor"),
            P("dp", "tensor"),
            P("dp", None),
            P("tensor", "dp", None),
            P("tensor", "dp"),
            P("dp"),
            P("tensor", "dp", None),
            P("dp"),
            P("dp", "tensor"),
            P("dp", "tensor"),
            P("tensor", "dp", None),
        ),
        check_vma=False,
    )
```

```python
import functools

import jax
import jax.numpy as jnp
from jax import lax
from jax.experimental import pallas as pl
from jax.experimental.pallas import tpu as pltpu
from jax.sharding import PartitionSpec as P

OWN_CAP = 1024
SPAN = 128
LANES = 128
epsilon = 1e-06
head_floor = 1.0

f32 = jnp.float32
bf16 = jnp.bfloat16
MESH = pl.DeviceIdType.MESH


def rows_dot(left, right):
    return lax.dot_general(left, right, (((0,), (0,)), ((), ())), preferred_element_type=f32)


def dot_t(left, right):
    return lax.dot_general(left, right, (((1,), (1,)), ((), ())), preferred_element_type=f32)


def dot(left, right):
    return jnp.dot(left, right, preferred_element_type=f32)


def span_terms(first, ends, logits):
    rows = logits.shape[0]

    def label(position):
        count = jnp.zeros_like(position)
        for end in ends:
            count = count + (position >= end).astype(jnp.int32)
        return count

    log_decay = jax.nn.log_sigmoid(logits) * (1.0 / 16.0)
    row = lax.broadcasted_iota(jnp.int32, (rows, rows), 0)
    column = lax.broadcasted_iota(jnp.int32, (rows, rows), 1)
    lower = (row >= column).astype(f32)
    cumulative = jnp.dot(
        lower, log_decay, precision=lax.Precision.HIGHEST, preferred_element_type=f32
    )
    total = cumulative[rows - 1 :, :]
    middle = cumulative[rows // 2 - 1 : rows // 2, :]
    label_column = label(first + lax.broadcasted_iota(jnp.int32, (rows, 1), 0))
    label_row = label(first + lax.broadcasted_iota(jnp.int32, (1, rows), 1))
    before = jnp.where(first > 0, label(first - 1), -1)
    last = label(first + rows - 1)
    carried = (label_column == before).astype(f32)
    tail = (label_column == last).astype(f32)
    keep = (before == last).astype(f32)
    allowed = (row >= column) & (label_column == label_row)
    return log_decay, cumulative, total, middle, carried, tail, keep, allowed


def span_forward(dk, dv, step, ends, held_ref, up_ref, bias_ref, state, states_ref, result):
    first = step * SPAN
    at = pl.ds(pl.multiple_of(first, SPAN), SPAN)
    queries = held_ref[at, :dk].astype(f32) * (float(dk) ** -0.5)
    keys = held_ref[at, dk : 2 * dk].astype(f32)
    values = held_ref[at, 2 * dk : 2 * dk + dv]
    logits = dot(held_ref[at, 2 * dk + dv :], up_ref[...]) + bias_ref[...]
    _, cumulative, total, middle, carried, tail, keep, allowed = span_terms(first, ends, logits)
    query_mid = (queries * jnp.exp(cumulative - middle)).astype(bf16)
    key_mid = (keys * jnp.exp(middle - cumulative)).astype(bf16)
    query_start = (queries * jnp.exp(cumulative) * carried).astype(bf16)
    key_end = (keys * jnp.exp(total - cumulative) * tail).astype(bf16)
    scores = jnp.where(allowed, dot_t(query_mid, key_mid), 0.0).astype(bf16)
    entering = state[...]
    entering_low = entering.astype(bf16)
    states_ref[step] = entering_low
    attended = dot(scores, values) + dot(query_start, entering_low)
    result[at, :] = attended.astype(bf16)
    decay_column = jnp.transpose(jnp.broadcast_to(keep * jnp.exp(total), (8, dk)))[:, :1]
    state[...] = decay_column * entering + rows_dot(key_end, values)


def span_backward(
    dk, dv, step, ends, d_out, held_ref, entering, up_ref, bias_ref, down_ref, d_state, result,
    grad_up_ref, grad_bias_ref,
):
    first = step * SPAN
    at = pl.ds(pl.multiple_of(first, SPAN), SPAN)
    scale = float(dk) ** -0.5
    queries = held_ref[at, :dk].astype(f32) * scale
    keys = held_ref[at, dk : 2 * dk].astype(f32)
    values = held_ref[at, 2 * dk : 2 * dk + dv]
    latent = held_ref[at, 2 * dk + dv :]
    logits = dot(latent, up_ref[...]) + bias_ref[...]
    _, cumulative, total, middle, carried, tail, keep, allowed = span_terms(first, ends, logits)
    grow_query = jnp.exp(cumulative - middle)
    grow_key = jnp.exp(middle - cumulative)
    start_decay = jnp.exp(cumulative) * carried
    end_decay = jnp.exp(total - cumulative) * tail
    query_mid = (queries * grow_query).astype(bf16)
    key_mid = (keys * grow_key).astype(bf16)
    query_start = (queries * start_decay).astype(bf16)
    key_end = (keys * end_decay).astype(bf16)
    scores = jnp.where(allowed, dot_t(query_mid, key_mid), 0.0).astype(bf16)
    d_scores = jnp.where(allowed, dot_t(d_out, values), 0.0).astype(bf16)
    leaving = d_state[...]
    leaving_low = leaving.astype(bf16)
    d_values = rows_dot(scores, d_out) + dot(key_end, leaving_low)
    d_queries = dot(d_scores, key_mid) * grow_query + dot_t(d_out, entering) * start_decay
    d_key_end = dot_t(values, leaving_low) * end_decay
    d_keys = rows_dot(d_scores, query_mid) * grow_key + d_key_end
    kept = keep * jnp.exp(total)
    state_pair = jnp.sum(entering.astype(f32) * leaving, axis=1, keepdims=True)
    state_row = jnp.transpose(jnp.broadcast_to(state_pair, (dk, LANES)))[:1, :]
    d_total = jnp.sum(keys * d_key_end, axis=0, keepdims=True) + kept * state_row
    d_cumulative = queries * d_queries - keys * d_keys
    row = lax.broadcasted_iota(jnp.int32, (SPAN, SPAN), 0)
    column = lax.broadcasted_iota(jnp.int32, (SPAN, SPAN), 1)
    upper = (row <= column).astype(f32)
    d_log_decay = (
        jnp.dot(upper, d_cumulative, precision=lax.Precision.HIGHEST, preferred_element_type=f32)
        + d_total
    )
    d_logits = d_log_decay * (1.0 / 16.0) * jax.nn.sigmoid(-logits)
    grad_bias_ref[...] += jnp.broadcast_to(jnp.sum(d_logits, axis=0, keepdims=True), (8, dk))
    d_logits_high = d_logits.astype(bf16)
    d_logits_low = (d_logits - d_logits_high.astype(f32)).astype(bf16)
    grad_up_ref[...] += rows_dot(d_logits_high, latent) + rows_dot(d_logits_low, latent)
    d_latent = dot_t(d_logits_high, down_ref[...]) + dot_t(d_logits_low, down_ref[...])
    high = d_latent.astype(bf16).astype(f32)
    lane = lax.broadcasted_iota(jnp.int32, d_latent.shape, 1)
    d_latent_packed = jnp.where(lane < LANES // 4, high, d_latent - high)
    result[at, :dk] = (d_queries * scale).astype(bf16)
    result[at, dk : 2 * dk] = d_keys.astype(bf16)
    result[at, 2 * dk : 2 * dk + dv] = d_values.astype(bf16)
    result[at, 2 * dk + dv :] = d_latent_packed.astype(bf16)
    kept_column = jnp.transpose(jnp.broadcast_to(kept, (8, dk)))[:, :1]
    d_state[...] = kept_column * leaving + rows_dot(query_start, d_out)


FINE = 16
SKEW = 3


class Line:
    def __init__(self, n, share_ref, up_in, down_in, out_ref, sems, finish):
        self.n, self.me = n, lax.axis_index("tensor")
        self.share, self.up_in, self.down_in, self.out = share_ref, up_in, down_in, out_ref
        self.sems, self.finish = sems, finish
        self.half = up_in.shape[0]
        self.block = self.half // 2
        self.count = self.half // FINE
        self.second = self.count + 2
        self.steps = self.second + self.count + SKEW * (n - 2)

    @staticmethod
    def scratch(half, width):
        return [pltpu.VMEM((half, width), bf16), pltpu.VMEM((half, width), bf16)]

    @staticmethod
    def semaphores(half):
        return pltpu.SemaphoreType.DMA((8, half // FINE))

    def own_copies(self, source, target, sems):
        block = self.block
        return [
            pltpu.make_async_copy(
                source.at[
                    pl.ds(
                        pl.multiple_of(2 * i * block + jnp.where(self.me == 0, block, 0), block),
                        block,
                    ),
                    :,
                ],
                target.at[pl.ds(i * block, block), :],
                sems[i],
            )
            for i in range(2)
        ]

    def greet(self, barrier, others):
        n, me = self.n, self.me

        @pl.when(me > 0)
        def _():
            pl.semaphore_signal(barrier, inc=1, device_id={"tensor": me - 1}, device_id_type=MESH)

        @pl.when(me < n - 1)
        def _():
            pl.semaphore_signal(barrier, inc=1, device_id={"tensor": me + 1}, device_id_type=MESH)

        inside = (me > 0) & (me < n - 1)

        @pl.when(inside)
        def _():
            pl.semaphore_wait(barrier, others + 2)

        @pl.when(jnp.logical_not(inside))
        def _():
            pl.semaphore_wait(barrier, others + 1)

    def greet_all(self, barrier, others):
        n, me = self.n, self.me

        @pl.when(me > 0)
        def _():
            pl.semaphore_signal(barrier, inc=1, device_id={"tensor": me - 1}, device_id_type=MESH)

        @pl.when(me < n - 1)
        def _():
            pl.semaphore_signal(barrier, inc=1, device_id={"tensor": me + 1}, device_id_type=MESH)

        pl.semaphore_wait(barrier, others + n - 1)

    def own(self, g):
        return pl.ds(pl.multiple_of(g * FINE, FINE), FINE)

    def at(self, g):
        per = self.block // FINE
        return pl.ds(
            pl.multiple_of((g // per) * 2 * self.block + lax.rem(g, per) * FINE, FINE), FINE
        )

    def low(self, g):
        per = self.block // FINE
        start = (g // per) * 2 * self.block + self.block + lax.rem(g, per) * FINE
        return pl.ds(pl.multiple_of(start, FINE), FINE)

    def right(self, source, target, lane, g):
        return pltpu.make_async_remote_copy(
            source, target, self.sems.at[2 * lane, g], self.sems.at[2 * lane + 1, g],
            device_id={"tensor": jnp.minimum(self.me + 1, self.n - 1)}, device_id_type=MESH,
        )

    def left(self, source, target, lane, g):
        return pltpu.make_async_remote_copy(
            source, target, self.sems.at[2 * lane, g], self.sems.at[2 * lane + 1, g],
            device_id={"tensor": jnp.maximum(self.me - 1, 0)}, device_id_type=MESH,
        )

    def up_copy(self, g):
        rows = self.up_in.at[self.own(g), :]
        return self.right(rows, rows, 0, g)

    def down_copy(self, g):
        rows = self.down_in.at[self.own(g), :]
        return self.left(rows, rows, 1, g)

    def up_back_copy(self, g):
        rows = self.out.at[self.at(g), :]
        return self.left(rows, rows, 2, g)

    def down_back_copy(self, g):
        rows = self.out.at[self.low(g), :]
        return self.right(rows, rows, 3, g)

    def prime(self, block=None):
        first, last = (0, self.count)
        if block is not None:
            per = self.block // FINE
            first, last = block * per, block * per + per

        @pl.when(self.me == 0)
        def _():
            @pl.loop(first, last)
            def _(g):
                self.right(
                    self.share.at[self.at(g), :], self.up_in.at[self.own(g), :], 0, g
                ).start()

        @pl.when(self.me == self.n - 1)
        def _():
            @pl.loop(first, last)
            def _(g):
                self.left(
                    self.share.at[self.low(g), :], self.down_in.at[self.own(g), :], 1, g
                ).start()

    def step(self, step):
        n, me, count = self.n, self.me, self.count
        at, low, own = self.at, self.low, self.own
        g_up = step - SKEW * (me - 1)

        @pl.when((me > 0) & (g_up >= 0) & (g_up < count))
        def _():
            self.up_copy(g_up).wait_recv()
            total = self.up_in[own(g_up), :].astype(f32) + self.share[at(g_up), :].astype(f32)

            @pl.when(me < n - 1)
            def _():
                self.up_in[own(g_up), :] = total.astype(bf16)
                self.up_copy(g_up).start()

            @pl.when(me == n - 1)
            def _():
                self.finish(total, own(g_up), at(g_up))
                self.up_back_copy(g_up).start()

        g_down = step - SKEW * (n - 2 - me)

        @pl.when((me < n - 1) & (g_down >= 0) & (g_down < count))
        def _():
            self.down_copy(g_down).wait_recv()
            total = self.down_in[own(g_down), :].astype(f32) + (
                self.share[low(g_down), :].astype(f32)
            )

            @pl.when(me > 0)
            def _():
                self.down_in[own(g_down), :] = total.astype(bf16)
                self.down_copy(g_down).start()

            @pl.when(me == 0)
            def _():
                self.finish(total, own(g_down), low(g_down))
                self.down_back_copy(g_down).start()

        g_up_back = step - self.second - SKEW * (n - 2 - me)

        @pl.when((me < n - 1) & (g_up_back >= 0) & (g_up_back < count))
        def _():
            self.up_back_copy(g_up_back).wait_recv()

            @pl.when(me > 0)
            def _():
                self.up_back_copy(g_up_back).start()

        g_down_back = step - self.second - SKEW * (me - 1)

        @pl.when((me > 0) & (g_down_back >= 0) & (g_down_back < count))
        def _():
            self.down_back_copy(g_down_back).wait_recv()

            @pl.when(me < n - 1)
            def _():
                self.down_back_copy(g_down_back).start()

    def run(self, first, last):
        @pl.loop(first, last)
        def _(step):
            self.step(step)

    def drain(self):
        n, me = self.n, self.me

        @pl.loop(0, self.count)
        def _(g):
            @pl.when(me < n - 1)
            def _():
                self.up_copy(g).wait_send()
                self.down_back_copy(g).wait_send()

            @pl.when(me > 0)
            def _():
                self.down_copy(g).wait_send()
                self.up_back_copy(g).wait_send()


def norm_back(x_ref, base, gain, out_ref, kept_ref, gain_grad_ref):
    gain_grad_ref[...] = jnp.zeros_like(gain_grad_ref)

    def finish(total, own, place):
        rows = x_ref[own, :].astype(f32)
        scaling = lax.rsqrt(jnp.mean(rows * rows, axis=1, keepdims=True) + epsilon)
        unit = rows * scaling
        gained = gain() * total
        grad = base(own, place).astype(f32) + scaling * (
            gained - unit * jnp.mean(gained * unit, axis=1, keepdims=True)
        )
        if kept_ref is not None:
            kept_ref[own, :] = grad
        out_ref[place, :] = grad.astype(out_ref.dtype)
        term = total * unit
        part = term[0:8, :]
        for i in range(1, FINE // 8):
            part = part + term[8 * i : 8 * i + 8, :]
        gain_grad_ref[...] += part

    return finish


def norm_forward(base, gain, out_ref, kept_ref):
    def finish(total, own, place):
        hidden = base(own, place).astype(f32) + total
        kept_ref[own, :] = hidden
        scaling = lax.rsqrt(jnp.mean(hidden * hidden, axis=1, keepdims=True) + epsilon)
        out_ref[place, :] = (hidden * scaling * gain()).astype(bf16)

    return finish


def line_kernel(mode, n, *refs):
    share_ref, x_ref, base_ref, gain_ref, out_ref, kept_ref, gain_grad_ref = refs[:7]
    up_in, down_in, sems = refs[7:]

    def base(own, place):
        return base_ref[own, :]

    def gain():
        return gain_ref[...]

    gain_grad_ref[...] = jnp.zeros_like(gain_grad_ref)
    if mode == "norm":
        finish = norm_forward(base, gain, out_ref, kept_ref)
    else:
        finish = norm_back(x_ref, base, gain, out_ref, kept_ref, gain_grad_ref)
    line = Line(n, share_ref, up_in, down_in, out_ref, sems, finish)
    line.greet(pltpu.get_barrier_semaphore(), 0)
    line.prime()
    line.run(0, line.steps)
    line.drain()


def line_sum(mode, call, n, share, x_own, base_own, gain):
    rows, width = share.shape
    half = rows // 2
    vmem = pl.BlockSpec(memory_space=pltpu.VMEM)
    return pl.pallas_call(
        functools.partial(line_kernel, mode, n),
        in_specs=[vmem] * 4,
        out_specs=[vmem] * 3,
        out_shape=[
            jax.ShapeDtypeStruct((rows, width), bf16),
            jax.ShapeDtypeStruct((half, width), f32),
            jax.ShapeDtypeStruct((8, width), f32),
        ],
        scratch_shapes=Line.scratch(half, width) + [Line.semaphores(half)],
        compiler_params=pltpu.CompilerParams(
            collective_id=call, has_side_effects=True, vmem_limit_bytes=40 << 20
        ),
        name="line_" + mode,
    )(share, x_own, base_own, gain)


def partner_of(index):
    return index + 1 - 2 * lax.rem(index, 2)


def to_dp(source, target, send, recv, device):
    return pltpu.make_async_remote_copy(
        source, target, send, recv, device_id={"dp": device}, device_id_type=MESH
    )


def greet_dp(barrier, groups):
    member = lax.axis_index("dp")

    @pl.loop(1, groups)
    def _(k):
        pl.semaphore_signal(
            barrier, inc=1, device_id={"dp": lax.rem(member + k, groups)}, device_id_type=MESH
        )


class ColGrad:
    def __init__(self, groups, left, right, first, tile, recv, refs):
        self.tile = tile
        (
            self.left, self.right, self.left_in, self.right_in, self.send,
            self.load_sems, self.pair_sems, self.sems,
        ) = refs
        self.left_far, self.right_far, self.recv, self.groups = left, right, recv, groups
        self.member = lax.axis_index("dp")
        self.parity = lax.rem(self.member, 2)
        self.half = right.shape[1] // 2
        self.first, self.wide = first, self.right_in.shape[1]
        self.size = self.send.shape[0] // groups
        self.items = self.wide // self.tile

    @staticmethod
    def scratch(groups, count, rows, wide):
        return [
            pltpu.VMEM((count, rows), bf16),
            pltpu.VMEM((count, wide), bf16),
            pltpu.VMEM((count, rows), bf16),
            pltpu.VMEM((count, wide), bf16),
            pltpu.VMEM((rows, wide), bf16),
            pltpu.SemaphoreType.DMA((3,)),
            pltpu.SemaphoreType.DMA((2, 2)),
            pltpu.SemaphoreType.DMA((2, groups)),
        ]

    def halves(self, parity):
        start = pl.multiple_of(parity * self.half + self.first, self.tile)
        return self.right_far.at[:, pl.ds(start, self.wide)]

    def loads(self):
        return (
            pltpu.make_async_copy(self.left_far, self.left, self.load_sems.at[0]),
            pltpu.make_async_copy(self.halves(self.parity), self.right, self.load_sems.at[1]),
        )

    def pair_copies(self):
        partner = partner_of(self.member)
        sems = self.pair_sems
        return (
            to_dp(self.left_far, self.left_in, sems.at[0, 0], sems.at[1, 0], partner),
            to_dp(
                self.halves(1 - self.parity), self.right_in, sems.at[0, 1], sems.at[1, 1], partner
            ),
        )

    def start(self):
        for c in self.pair_copies() + self.loads():
            c.start()

    def ready(self):
        for c in self.loads():
            c.wait()
        for c in self.pair_copies():
            c.wait_recv()

    def item(self, t):
        span = pl.ds(pl.multiple_of(t * self.tile, self.tile), self.tile)
        product = rows_dot(self.left[...], self.right[:, span]) + rows_dot(
            self.left_in[...], self.right_in[:, span]
        )
        self.send[:, span] = product.astype(bf16)

    def copy(self, to, source):
        rows = pl.ds(pl.multiple_of(to * self.size, 16), self.size)
        return to_dp(
            self.send.at[rows, :], self.recv.at[source], self.sems.at[0, to],
            self.sems.at[1, source], to,
        )

    def send_all(self):
        @pl.loop(1, self.groups)
        def _(k):
            self.copy(lax.rem(self.member + k, self.groups), self.member).start()

        self.keep().start()

    def keep(self):
        own = pl.ds(pl.multiple_of(self.member * self.size, 16), self.size)
        return pltpu.make_async_copy(
            self.send.at[own, :], self.recv.at[self.member], self.load_sems.at[2]
        )

    def receive(self):
        self.keep().wait()

        @pl.loop(1, self.groups)
        def _(k):
            self.copy(0, lax.rem(self.member + k, self.groups)).wait_recv()

    def drain(self):
        for c in self.pair_copies():
            c.wait_send()

        @pl.loop(1, self.groups)
        def _(k):
            self.copy(lax.rem(self.member + k, self.groups), self.member).wait_send()


class RowGrads:
    def __init__(self, groups, left, tiles, recv, refs, deferred=0):
        (
            self.left, self.all, self.left_in, self.all_in, self.send,
            self.load_sems, self.left_sems, self.piece_sems, self.sems, self.keep_sems,
        ) = refs
        self.left_far, self.tiles, self.recv = left, tiles, recv
        self.live = len(tiles) - deferred
        if left is None:
            self.left_far = self.left
        self.member = lax.axis_index("dp")
        self.parity = lax.rem(self.member, 2)
        self.mine = self.member // 2
        self.team = groups // 2
        self.block = self.left.shape[1] // groups
        self.items = self.team * len(tiles)

    @staticmethod
    def scratch(groups, count, width, total, pieces, tiles):
        team = groups // 2
        return [
            pltpu.VMEM((count, width), bf16),
            pltpu.VMEM((count, total), bf16),
            pltpu.VMEM((count, width // 2), bf16),
            pltpu.VMEM((count, total), bf16),
            pltpu.VMEM((team, width // groups, total), bf16),
            pltpu.SemaphoreType.DMA((1 + pieces,)),
            pltpu.SemaphoreType.DMA((2, team)),
            pltpu.SemaphoreType.DMA((2, pieces)),
            pltpu.SemaphoreType.DMA((2, tiles, team)),
            pltpu.SemaphoreType.DMA((tiles,)),
        ]

    def columns(self, j):
        return pl.ds(pl.multiple_of(j * self.block, self.block), self.block)

    def left_load(self):
        return pltpu.make_async_copy(self.left_far, self.left, self.load_sems.at[0])

    def piece_load(self, p, source, span):
        return pltpu.make_async_copy(source, self.all.at[:, span], self.load_sems.at[1 + p])

    def left_copy(self, q):
        return to_dp(
            self.left_far.at[:, self.columns(2 * q + 1 - self.parity)],
            self.left_in.at[:, self.columns(q)],
            self.left_sems.at[0, q], self.left_sems.at[1, q], partner_of(self.member),
        )

    def piece_copy(self, p, source, span, rows=slice(None)):
        return to_dp(
            source, self.all_in.at[rows, span], self.piece_sems.at[0, p], self.piece_sems.at[1, p],
            partner_of(self.member),
        )

    def start_left(self):
        @pl.loop(0, self.team)
        def _(q):
            self.left_copy(q).start()

        self.left_load().start()

    def ready_left(self):
        self.left_load().wait()

        @pl.loop(0, self.team)
        def _(q):
            self.left_copy(q).wait_recv()

    def copy(self, t, to, source):
        start, wide = self.tiles[t]
        span = pl.ds(start, wide)
        return to_dp(
            self.send.at[to, :, span], self.recv.at[source, :, span],
            self.sems.at[0, t, to], self.sems.at[1, t, source], 2 * to + self.parity,
        )

    def item(self, w):
        count = len(self.tiles)
        k = w // count
        to = lax.rem(self.mine + 1 + k, self.team)
        for t in range(count):
            start, wide = self.tiles[t]

            @pl.when((w >= 0) & (w < self.items) & (lax.rem(w, count) == t))
            def _():
                span = pl.ds(start, wide)
                product = rows_dot(
                    self.left[:, self.columns(2 * to + self.parity)], self.all[:, span]
                ) + rows_dot(self.left_in[:, self.columns(to)], self.all_in[:, span])
                self.send[to, :, span] = product.astype(bf16)

                if t < self.live:
                    @pl.when(k < self.team - 1)
                    def _():
                        self.copy(t, to, self.mine).start()

                    @pl.when(k == self.team - 1)
                    def _():
                        self.keep(t).start()

    def keep(self, t):
        start, wide = self.tiles[t]
        span = pl.ds(start, wide)
        return pltpu.make_async_copy(
            self.send.at[self.mine, :, span], self.recv.at[self.mine, :, span], self.keep_sems.at[t]
        )

    def receive(self):
        for t in range(self.live):
            self.keep(t).wait()

            @pl.loop(1, self.team)
            def _(k):
                self.copy(t, 0, lax.rem(self.mine + k, self.team)).wait_recv()

    def drain(self):
        @pl.loop(0, self.team)
        def _(q):
            self.left_copy(q).wait_send()

        for t in range(self.live):
            @pl.loop(1, self.team)
            def _(k):
                self.copy(t, lax.rem(self.mine + k, self.team), self.mine).wait_send()


def splitter(refs):
    refs = list(refs)

    def take(k):
        out = refs[:k]
        del refs[:k]
        return out

    return take


def one_hot(index, base, shape, dim):
    return (index == base + lax.broadcasted_iota(jnp.int32, shape, dim)).astype(f32).astype(bf16)


def thirds(source, terms, target):
    third = LANES // 4
    size = source.shape[0]
    target[...] = jnp.zeros_like(target)
    for i in range(terms):
        target[i * third : i * third + size, :] = source[...]


class Exchange:
    def __init__(self, groups, cuts, sent, came, sems):
        self.groups, self.sent, self.came, self.sems = groups, sent, came, sems
        self.spans = [pl.ds(a, b - a) for a, b in zip((0,) + cuts, cuts + (sent.shape[1],))]
        self.member = lax.axis_index("dp")
        self.cap = sent.shape[0] // groups

    @staticmethod
    def scratch(groups, slots, width, pieces):
        return [
            pltpu.VMEM((slots, width), bf16),
            pltpu.VMEM((slots, width), bf16),
            pltpu.SemaphoreType.DMA((2, pieces, groups)),
        ]

    def part(self, j):
        return pl.ds(pl.multiple_of(j * self.cap, self.cap), self.cap)

    def copy(self, p, to, source):
        span = self.spans[p]
        return to_dp(
            self.sent.at[self.part(to), span], self.came.at[self.part(source), span],
            self.sems.at[0, p, to], self.sems.at[1, p, source], to,
        )

    def send(self, p, index_ref, dim, source, between=None):
        span = self.spans[p]
        groups, count = self.groups, source.shape[0]
        rows = self.sent.shape[0] // 2

        @pl.loop(0, 2)
        def _(h):
            at = pl.ds(pl.multiple_of(h * rows, rows), rows)
            if dim == 0:
                pick = one_hot(index_ref[...], h * rows, (rows, count), 0)
            else:
                pick = one_hot(index_ref[at, :], 0, (rows, count), 1)
            self.sent[at, span] = dot(pick, source[:, span]).astype(bf16)

            @pl.loop(0, groups // 2)
            def _(k):
                to = h * (groups // 2) + lax.rem(self.member + k, groups // 2)

                @pl.when(to != self.member)
                def _():
                    self.copy(p, to, self.member).start()

            if between is not None:
                between(h)

        own = self.part(self.member)
        self.came[own, span] = self.sent[own, span]

    def receive(self, p):
        @pl.loop(1, self.groups)
        def _(k):
            self.copy(p, 0, lax.rem(self.member + k, self.groups)).wait_recv()

    def drain(self):
        for p in range(len(self.spans)):
            @pl.loop(1, self.groups)
            def _(k):
                self.copy(p, lax.rem(self.member + k, self.groups), self.member).wait_send()


def place_rows(slot_row_ref, came, held, span, between=None):
    positions, slots = held.shape[0], came.shape[0]
    rows = positions // 2

    @pl.loop(0, 2)
    def _(h):
        at = pl.ds(pl.multiple_of(h * rows, rows), rows)
        pick = one_hot(slot_row_ref[...], h * rows, (rows, slots), 0)
        held[at, span] = dot(pick, came[:, span]).astype(bf16)
        if between is not None:
            between(h)


def front_kernel(groups, dk, dv, *refs):
    take = splitter(refs)
    lengths_ref, slot_rows_ref, tokens_ref, gains_ref, up_rows_ref, down_rows_ref = take(6)
    weights_far = take(3)
    gate_far, out_far = take(2)
    spilled = take(6)
    (share_ref,) = take(1)
    send_row_ref, send_column_ref, slot_row_ref, slot_column_ref = take(4)
    normed_ref, gate_ref, attended_ref, gated_ref, held_ref, states_ref = kept = take(6)
    weight_ref, gate_weight_ref, out_weight_ref = take(3)
    rows_out, state, result, rank_ref, up_ref, bias_ref, latent_ref = take(7)
    slots_ref, load_sems = take(2)
    go = Exchange(groups, (2 * dk,), *take(3))
    back = Exchange(groups, (), *take(3))
    (spill_sems,) = take(1)
    member = lax.axis_index("dp")
    count, width = tokens_ref.shape
    cap = OWN_CAP // groups
    half = count // 2
    spills = [
        pltpu.make_async_copy(kept[i], spilled[i], spill_sems.at[i]) for i in range(6)
    ]

    def spill(*which):
        for i in which:
            spills[i].start()

    end0 = lengths_ref[0, 0]
    end1 = end0 + lengths_ref[0, 1]
    ends = (end0, end1, end1 + lengths_ref[0, 2])
    third = LANES // 4

    loads = []
    offset = 0
    for i, far in enumerate(weights_far):
        wide = far.shape[1]
        loads.append(
            pltpu.make_async_copy(far, weight_ref.at[:, pl.ds(offset, wide)], load_sems.at[i])
        )
        offset += wide
    later = [
        pltpu.make_async_copy(gate_far, gate_weight_ref, load_sems.at[4]),
        pltpu.make_async_copy(out_far, out_weight_ref, load_sems.at[5]),
    ]
    for c in loads + later:
        c.start()
    barrier = pltpu.get_barrier_semaphore()
    greet_dp(barrier, groups)
    pl.semaphore_wait(barrier, groups - 1)

    pieces = count // LANES
    for i in range(pieces):
        slots_ref[:, i * LANES : (i + 1) * LANES] = slot_rows_ref[pl.ds(i, groups, stride=pieces), :]
    owners = slots_ref[...] // OWN_CAP
    mine = owners == member
    my_slots = slots_ref[pl.ds(member, 1), :]
    my_owner = my_slots // OWN_CAP
    device = lax.broadcasted_iota(jnp.int32, (groups, count), 0)
    chosen = (my_owner == device).astype(f32)
    before = (
        lax.broadcasted_iota(jnp.int32, (count, count), 0)
        < lax.broadcasted_iota(jnp.int32, (count, count), 1)
    ).astype(f32).astype(bf16)
    send_rank = jnp.sum(chosen * dot(chosen.astype(bf16), before), axis=0, keepdims=True)
    send_row = my_owner * cap + send_rank.astype(jnp.int32)
    send_row_ref[...] = send_row
    send_column_ref[...] = jnp.transpose(
        jnp.broadcast_to(send_row.astype(f32), (8, count))
    )[:, :1].astype(jnp.int32)
    rank_ref[...] = jnp.where(mine, dot(mine.astype(f32).astype(bf16), before), -1.0)

    bias_ref[...] = gains_ref[2:3, dv : dv + dk]
    thirds(up_rows_ref, 3, up_ref)
    thirds(down_rows_ref, 3, latent_ref)

    tile = count // 5

    @pl.loop(0, 5)
    def _(i):
        at = pl.ds(pl.multiple_of(i * tile, tile), tile)
        rows = tokens_ref[at, :].astype(f32)
        scaling = lax.rsqrt(jnp.mean(rows * rows, axis=1, keepdims=True) + epsilon)
        normed_ref[at, :] = (rows * scaling * gains_ref[0:1, :]).astype(bf16)

    for c in loads[:2]:
        c.wait()
    body = 2 * dk + dv

    spill(0)

    def project(first, last):
        @pl.loop(first // 256, last // 256)
        def _(i):
            to = pl.ds(pl.multiple_of(i * 256, 256), 256)
            rows_out[:, to] = dot(normed_ref[...], weight_ref[:, to]).astype(bf16)

    project(0, 2 * dk)
    go.send(0, send_row_ref, 0, rows_out)
    for c in loads[2:]:
        c.wait()
    project(2 * dk, body)
    latent = dot_t(normed_ref[...], latent_ref[...])
    high = latent.astype(bf16).astype(f32)
    middle = (latent - high).astype(bf16).astype(f32)
    lane = lax.broadcasted_iota(jnp.int32, latent.shape, 1)
    rows_out[:, body:] = jnp.where(
        lane < third, high, jnp.where(lane < 2 * third, middle, latent - high - middle)
    ).astype(bf16)
    go.send(1, send_row_ref, 0, rows_out)

    for c in later:
        c.wait()

    @pl.loop(0, dv // 256)
    def _(i):
        to = pl.ds(pl.multiple_of(i * 256, 256), 256)
        gate_ref[:, to] = dot(normed_ref[...], gate_weight_ref[:, to])

    spill(1)

    @pl.loop(0, groups)
    def _(j):
        rank = rank_ref[pl.ds(j, 1), :]
        local = (lax.rem(slots_ref[pl.ds(j, 1), :], OWN_CAP) - OWN_CAP).astype(f32)
        wanted = lax.broadcasted_iota(jnp.int32, (cap, count), 0).astype(f32)
        at = jnp.sum(jnp.where(rank == wanted, local, 0.0), axis=1, keepdims=True)
        slot_column_ref[go.part(j), :] = at.astype(jnp.int32) + OWN_CAP

    slots = slot_row_ref.shape[1]
    slot_row_ref[...] = jnp.transpose(
        jnp.broadcast_to(slot_column_ref[...].astype(f32), (slots, LANES))
    )[:1, :].astype(jnp.int32)
    state[...] = jnp.zeros_like(state)
    for p in range(2):
        go.receive(p)
        place_rows(slot_row_ref, go.came, held_ref, go.spans[p])

    @pl.loop(0, held_ref.shape[0] // SPAN)
    def _(step):
        span_forward(dk, dv, step, ends, held_ref, up_ref, bias_ref, state, states_ref, result)

    back.send(0, slot_column_ref, 1, result)
    spill(4, 5)
    back.receive(0)

    def head_rows(at):
        pick = one_hot(send_column_ref[at, :], 0, (half, slots), 1)
        attended = dot(pick, back.came[...])
        attended_ref[at, :] = attended.astype(bf16)
        gate = gate_ref[at, :]
        scaling = lax.rsqrt(jnp.mean(attended * attended, axis=1, keepdims=True) + head_floor)
        gated = attended * scaling * gains_ref[2:3, :dv] * (gate * jax.nn.sigmoid(gate))
        gated_ref[at, :] = gated.astype(bf16)

        @pl.loop(0, width // 512)
        def _(i):
            to = pl.ds(pl.multiple_of(i * 512, 512), 512)
            share_ref[at, to] = dot(gated_ref[at, :], out_weight_ref[:, to]).astype(bf16)

    @pl.loop(0, 2)
    def _(i):
        head_rows(pl.ds(pl.multiple_of(i * half, half), half))

    spill(2, 3)
    go.drain()
    back.drain()
    for c in spills:
        c.wait()


def front(
    call, groups, lengths, slots, tokens, gains, up_rows, down_rows, weights, gate_weight,
    out_weight,
):
    count, width = tokens.shape
    dk, dv = weights[0].shape[1], weights[2].shape[1]
    body = 2 * dk + dv
    wide = body + LANES
    spans = OWN_CAP // SPAN
    vmem = pl.BlockSpec(memory_space=pltpu.VMEM)
    far = pl.BlockSpec(memory_space=pl.ANY)
    smem = pl.BlockSpec(memory_space=pltpu.SMEM)
    shape = jax.ShapeDtypeStruct
    saved = [
        shape((count, width), bf16),
        shape((count, dv), f32),
        shape((count, dv), bf16),
        shape((count, dv), bf16),
        shape((OWN_CAP, wide), bf16),
        shape((spans, dk, dv), bf16),
    ]
    return pl.pallas_call(
        functools.partial(front_kernel, groups, dk, dv),
        in_specs=[smem] + [vmem] * 5 + [far] * 5,
        out_specs=[far] * 6 + [vmem] * 5,
        out_shape=[
            *saved,
            shape((count, width), bf16),
            shape((1, count), jnp.int32),
            shape((count, 1), jnp.int32),
            shape((1, OWN_CAP), jnp.int32),
            shape((OWN_CAP, 1), jnp.int32),
        ],
        scratch_shapes=[pltpu.VMEM(a.shape, a.dtype) for a in saved]
        + [
            pltpu.VMEM((width, body), bf16),
            pltpu.VMEM((width, dv), bf16),
            pltpu.VMEM((dv, width), bf16),
            pltpu.VMEM((count, wide), bf16),
            pltpu.VMEM((dk, dv), f32),
            pltpu.VMEM((OWN_CAP, dv), bf16),
            pltpu.VMEM((groups, count), f32),
            pltpu.VMEM((LANES, dk), bf16),
            pltpu.VMEM((1, dk), f32),
            pltpu.VMEM((LANES, width), bf16),
            pltpu.VMEM((groups, count), jnp.int32),
            pltpu.SemaphoreType.DMA((8,)),
        ]
        + Exchange.scratch(groups, OWN_CAP, wide, 2)
        + Exchange.scratch(groups, OWN_CAP, dv, 1)
        + [pltpu.SemaphoreType.DMA((6,))],
        compiler_params=pltpu.CompilerParams(
            collective_id=call, has_side_effects=True, vmem_limit_bytes=60 << 20
        ),
        cost_estimate=pl.CostEstimate(
            flops=12_000_000_000, bytes_accessed=200_000_000, transcendentals=4_000_000
        ),
        name="front",
    )(
        lengths, slots, tokens, gains, up_rows, down_rows, *weights, gate_weight, out_weight,
    )


def back_feed_kernel(n, groups, tiles, *refs):
    take = splitter(refs)
    gains_ref, first_share_ref, tokens_far, cotangent_far, gate_far, up_far, down_far = take(7)
    out_ref, kept_ref, gain_grad_ref = take(3)
    recv, more_far, active_far, layer_far, hidden_far = take(5)
    active_ref, layer_ref, first_up, first_down, up_in, down_in = take(6)
    hidden_ref, tokens_ref, cotangent_ref, share_ref, weight_ref, d_active_ref = take(6)
    load_sems, weight_sems, first_sems, sems = take(4)
    rows = RowGrads(groups, None, tiles, recv, take(10), deferred=1)
    feed_ref = rows.left
    count, width = share_ref.shape
    wide = active_ref.shape[1]
    full, rest = wide // 256, wide % 256
    pieces = full + (rest > 0)
    half = count // 2
    first_line = Line(
        n, first_share_ref, first_up, first_down, feed_ref, first_sems,
        norm_forward(
            lambda own, place: tokens_ref[own, :], lambda: gains_ref[1:2, :], feed_ref, hidden_ref
        ),
    )
    line = Line(
        n, share_ref, up_in, down_in, out_ref, sems,
        norm_back(
            hidden_ref, lambda own, place: cotangent_ref[place, :], lambda: gains_ref[1:2, :],
            out_ref, kept_ref, gain_grad_ref,
        ),
    )
    token_loads = first_line.own_copies(tokens_far, tokens_ref, [load_sems.at[0], load_sems.at[1]])
    cotangent_load = pltpu.make_async_copy(cotangent_far, cotangent_ref, load_sems.at[2])
    down_load = pltpu.make_async_copy(
        down_far, weight_ref.at[pl.ds(0, wide), pl.ds(0, width)], load_sems.at[3]
    )
    active_spill = pltpu.make_async_copy(active_ref, active_far, load_sems.at[4])
    layer_spill = pltpu.make_async_copy(layer_ref, layer_far, load_sems.at[5])
    hidden_spill = pltpu.make_async_copy(hidden_ref, hidden_far, load_sems.at[6])
    more_start, more_wide = tiles[-1]
    more_spill = pltpu.make_async_copy(
        rows.send.at[:, :, pl.ds(more_start, more_wide)], more_far, load_sems.at[7]
    )

    def spans(i, size):
        start = pl.multiple_of(i * 256, 256)
        return pl.ds(start, size), pl.ds(pl.multiple_of(wide + start, LANES), size)

    def weight_loads(i, size):
        gate_span, up_span = spans(i, size)
        return (
            pltpu.make_async_copy(
                gate_far.at[:, gate_span], weight_ref.at[:, gate_span], weight_sems.at[0, i]
            ),
            pltpu.make_async_copy(
                up_far.at[:, gate_span], weight_ref.at[:, up_span], weight_sems.at[1, i]
            ),
        )

    def block_rows(b):
        return pl.ds(b * half, half)

    def piece_copies(b, i, size):
        gate_span, up_span = spans(i, size)
        at = block_rows(b)
        return tuple(
            rows.piece_copy(2 * (b * pieces + i) + j, rows.all.at[at, span], span, at)
            for j, span in enumerate((gate_span, up_span))
        )

    def each(action):
        @pl.loop(0, full)
        def _(i):
            action(i, 256)

        if rest:
            action(full, rest)

    def at_item(w, action):
        @pl.when((w >= 0) & (w < full))
        def _():
            action(w, 256)

        if rest:
            @pl.when(w == full)
            def _():
                action(full, rest)

    down_load.start()
    cotangent_load.start()
    for c in token_loads:
        c.start()
    barrier = pltpu.get_barrier_semaphore()
    greet_dp(barrier, groups)
    line.greet(barrier, groups - 1)
    first_line.prime()
    for c in token_loads:
        c.wait()

    def make_d_active(i, size):
        span, _ = spans(i, size)
        d_active_ref[:, span] = dot_t(
            cotangent_ref[...], weight_ref[span, pl.ds(0, width)]
        ).astype(bf16)

    def start_weights(i, size):
        for c in weight_loads(i, size):
            c.start()

    def hidden_units(b, i, size):
        if b == 0:
            for c in weight_loads(i, size):
                c.wait()
        gate_span, up_span = spans(i, size)
        at = block_rows(b)
        gate = dot(feed_ref[at, :], weight_ref[:, gate_span])
        up = dot(feed_ref[at, :], weight_ref[:, up_span])
        d_active = d_active_ref[at, gate_span].astype(f32)
        sigmoid = jax.nn.sigmoid(gate)
        swish = gate * sigmoid
        active_ref[at, gate_span] = (swish * up).astype(bf16)
        rows.all[at, gate_span] = (
            d_active * up * sigmoid * (1.0 + gate * (1.0 - sigmoid))
        ).astype(bf16)
        rows.all[at, up_span] = (d_active * swish).astype(bf16)
        for c in piece_copies(b, i, size):
            c.start()

    share_items = width // 256

    def make_share(b, w):
        @pl.when((w >= 0) & (w < share_items))
        def _():
            to = pl.ds(pl.multiple_of(w * 256, 256), 256)
            at = block_rows(b)
            share_ref[at, to] = dot_t(rows.all[at, :], weight_ref[to, :]).astype(bf16)

    per = first_line.block // FINE
    arrived = first_line.second + SKEW * (n - 2) + per
    d_first = 10

    @pl.loop(0, first_line.steps)
    def _(step):
        first_line.step(step)

        @pl.when(step == d_first)
        def _():
            down_load.wait()
            cotangent_load.wait()

        at_item(step - d_first, make_d_active)

        @pl.when(step == d_first + pieces)
        def _():
            each(start_weights)

        at_item(step - arrived, lambda i, size: hidden_units(0, i, size))
        w = 2 * (step - arrived - pieces)
        make_share(0, w)
        make_share(0, w + 1)

    done_share = 2 * (first_line.steps - arrived - pieces)

    @pl.loop(done_share, max(share_items, done_share))
    def _(w):
        make_share(0, w)

    line.prime(0)
    hidden_spill.start()

    @pl.loop(0, rows.team)
    def _(q):
        rows.left_copy(q).start()

    layer_items = width // 512
    first_work = 8
    if 2 * (per - pieces) < share_items:
        raise ValueError("shares late")

    @pl.loop(0, line.steps)
    def _(step):
        @pl.when(step == per)
        def _():
            line.prime(1)
            active_spill.start()
            down_load.start()

        line.step(step)
        at_item(step, lambda i, size: hidden_units(1, i, size))
        w = 2 * (step - pieces)
        make_share(1, w)
        make_share(1, w + 1)
        w = step - first_work

        @pl.when(w == 0)
        def _():
            @pl.loop(0, rows.team)
            def _(q):
                rows.left_copy(q).wait_recv()

            for b in range(2):
                def arrive(i, size, b=b):
                    for c in piece_copies(b, i, size):
                        c.wait_recv()

                each(arrive)

        rows.item(w)

        @pl.when(w == rows.items)
        def _():
            more_spill.start()
            down_load.wait()

        layer_item = w - rows.items

        @pl.when((layer_item >= 0) & (layer_item < layer_items))
        def _():
            to = pl.ds(pl.multiple_of(layer_item * 512, 512), 512)
            layer_ref[:, to] = dot(active_ref[...], weight_ref[pl.ds(0, wide), to]).astype(bf16)

        @pl.when(layer_item == layer_items)
        def _():
            layer_spill.start()

    rows.receive()
    first_line.drain()
    line.drain()
    rows.drain()
    for c in (active_spill, layer_spill, hidden_spill, more_spill):
        c.wait()
    for b in range(2):
        def sent(i, size, b=b):
            for c in piece_copies(b, i, size):
                c.wait_send()

        each(sent)


def back_feed(call, n, groups, gains, share, tokens, cotangent, feed_gate, feed_up, feed_down):
    count, width = share.shape
    half = count // 2
    wide = feed_gate.shape[1]
    pieces = (wide + 255) // 256
    cut = (wide // 2 + LANES - 1) // LANES * LANES
    tiles = [(0, cut), (cut, wide - cut), (wide, cut), (wide + cut, wide - cut)]
    team, per = groups // 2, width // groups
    vmem = pl.BlockSpec(memory_space=pltpu.VMEM)
    far = pl.BlockSpec(memory_space=pl.ANY)
    shape = jax.ShapeDtypeStruct
    return pl.pallas_call(
        functools.partial(back_feed_kernel, n, groups, tiles),
        in_specs=[vmem] * 2 + [far] * 5,
        out_specs=[vmem] * 3 + [far] * 5,
        out_shape=[
            shape((count, width), bf16),
            shape((half, width), f32),
            shape((8, width), f32),
            shape((team, per, wide + cut), bf16),
            shape((team, per, wide - cut), bf16),
            shape((count, wide), bf16),
            shape((count, width), bf16),
            shape((half, width), f32),
        ],
        scratch_shapes=[pltpu.VMEM((count, wide), bf16), pltpu.VMEM((count, width), bf16)]
        + Line.scratch(half, width)
        + Line.scratch(half, width)
        + [
            pltpu.VMEM((half, width), f32),
            pltpu.VMEM((half, width), bf16),
            pltpu.VMEM((count, width), bf16),
            pltpu.VMEM((count, width), bf16),
            pltpu.VMEM((width, 2 * wide), bf16),
            pltpu.VMEM((count, wide), bf16),
            pltpu.SemaphoreType.DMA((8,)),
            pltpu.SemaphoreType.DMA((2, pieces)),
            Line.semaphores(half),
            Line.semaphores(half),
        ]
        + RowGrads.scratch(groups, count, width, 2 * wide, 4 * pieces, len(tiles)),
        compiler_params=pltpu.CompilerParams(
            collective_id=call, has_side_effects=True, vmem_limit_bytes=61 << 20
        ),
        cost_estimate=pl.CostEstimate(
            flops=30_000_000_000, bytes_accessed=200_000_000, transcendentals=0
        ),
        name="back_feed",
    )(gains, share, tokens, cotangent, feed_gate, feed_up, feed_down)


class SmallSum:
    def __init__(self, n, groups, wide, near, near_all, wide_out, near_out, refs):
        (
            self.wide_in, self.near_in, self.wide_line, self.near_line, self.sems, self.line_sems,
        ) = refs
        self.n, self.groups, self.near_all = n, groups, near_all
        self.wide, self.near, self.wide_out, self.near_out = wide, near, wide_out, near_out
        self.member, self.place = lax.axis_index("dp"), lax.axis_index("tensor")
        self.block = wide.shape[1] // groups

    @staticmethod
    def scratch(n, groups, wide, near):
        block = wide[1] // groups
        return [
            pltpu.VMEM((groups, wide[0], block), f32),
            pltpu.VMEM(near, f32),
            pltpu.VMEM((n, wide[0], block), f32),
            pltpu.VMEM((n,) + near[1:], f32),
            pltpu.SemaphoreType.DMA((2, 2, groups)),
            pltpu.SemaphoreType.DMA((2, 2, n)),
        ]

    def greet(self, barrier):
        n, place = self.n, self.place
        for k in range(2, n):
            @pl.when(place + k < n)
            def _():
                pl.semaphore_signal(
                    barrier, inc=1, device_id={"tensor": place + k}, device_id_type=MESH
                )

            @pl.when(place - k >= 0)
            def _():
                pl.semaphore_signal(
                    barrier, inc=1, device_id={"tensor": place - k}, device_id_type=MESH
                )

    def cut(self, j):
        return pl.ds(pl.multiple_of(j * self.block, self.block), self.block)

    def copies(self, to, source):
        return (
            to_dp(
                self.wide.at[:, self.cut(to)], self.wide_in.at[source],
                self.sems.at[0, 0, to], self.sems.at[1, 0, source], to,
            ),
            to_dp(
                self.near.at[to], self.near_in.at[source],
                self.sems.at[0, 1, to], self.sems.at[1, 1, source], to,
            ),
        )

    def line_copies(self, to, source):
        return tuple(
            pltpu.make_async_remote_copy(
                line.at[self.place], line.at[source], self.line_sems.at[0, i, to],
                self.line_sems.at[1, i, source], device_id={"tensor": to}, device_id_type=MESH,
            )
            for i, line in enumerate((self.wide_line, self.near_line))
        )

    def send(self):
        @pl.loop(1, self.groups)
        def _(k):
            for c in self.copies(lax.rem(self.member + k, self.groups), self.member):
                c.start()

        self.wide_in[pl.ds(self.member, 1)] = self.wide[:, self.cut(self.member)][None]
        self.near_in[pl.ds(self.member, 1)] = self.near[pl.ds(self.member, 1)]

    def forward(self):
        @pl.loop(1, self.groups)
        def _(k):
            for c in self.copies(0, lax.rem(self.member + k, self.groups)):
                c.wait_recv()

        for came, line in ((self.wide_in, self.wide_line), (self.near_in, self.near_line)):
            total = came[0]
            for j in range(1, self.groups):
                total = total + came[j]
            line[pl.ds(self.place, 1)] = total[None]

        @pl.loop(1, self.n)
        def _(k):
            for c in self.line_copies(lax.rem(self.place + k, self.n), self.place):
                c.start()

    def receive(self):
        @pl.loop(1, self.n)
        def _(k):
            for c in self.line_copies(0, lax.rem(self.place + k, self.n)):
                c.wait_recv()

        total = self.wide_line[0]
        for j in range(1, self.n):
            total = total + self.wide_line[j]
        self.wide_out[...] = total
        own = self.near_line[pl.ds(self.place, 1)][0]
        total = self.near_line[0]
        for j in range(1, self.n):
            total = total + self.near_line[j]
        row = lax.broadcasted_iota(jnp.int32, own.shape, 0)
        self.near_out[...] = jnp.where(row < self.near_all, total, own)

    def drain(self):
        @pl.loop(1, self.groups)
        def _(k):
            for c in self.copies(lax.rem(self.member + k, self.groups), self.member):
                c.wait_send()

        @pl.loop(1, self.n)
        def _(k):
            for c in self.line_copies(lax.rem(self.place + k, self.n), self.place):
                c.wait_send()


def back_mixer_kernel(n, groups, widths, near_all, tiles, *refs):
    take = splitter(refs)
    gains_ref, near_ref, down_rows_ref, x_far, base_far, left_far = take(6)
    parts = take(2)
    col_left, col_right, more_far = take(3)
    weights = take(len(widths))
    out_ref, wide_out, near_out, recv, col_recv, more_recv = take(6)
    more_ref, more_sems, more_load_sems = take(3)
    up_in, down_in, x_ref, base_ref, share_ref, wide_ref, gain_grad_ref = take(7)
    weight_ref, latent_ref, load_sems, sems = take(4)
    rows = RowGrads(groups, left_far, tiles, recv, take(10))
    part_spans = [
        pl.ds(0, parts[0].shape[1]), pl.ds(parts[0].shape[1], parts[1].shape[1])
    ]
    part_loads = [rows.piece_load(i, parts[i], part_spans[i]) for i in range(2)]
    part_copies = [rows.piece_copy(i, parts[i], part_spans[i]) for i in range(2)]
    cols = ColGrad(groups, col_left, col_right, 0, 256, col_recv, take(8))
    small = SmallSum(n, groups, wide_ref, near_ref, near_all, wide_out, near_out, take(6))
    finish = norm_back(
        x_ref, lambda own, place: base_ref[own, :], lambda: gains_ref[0:1, :], out_ref, None,
        gain_grad_ref,
    )
    line = Line(n, share_ref, up_in, down_in, out_ref, sems, finish)
    loads = line.own_copies(x_far, x_ref, [load_sems.at[0], more_load_sems.at[0]])
    loads.append(pltpu.make_async_copy(base_far, base_ref, load_sems.at[1]))
    more_load = pltpu.make_async_copy(more_far, more_ref, more_load_sems.at[1])

    def more_copy(to, source):
        return to_dp(
            more_ref.at[to], more_recv.at[source], more_sems.at[0, to], more_sems.at[1, source],
            2 * to + rows.parity,
        )

    more_keep = pltpu.make_async_copy(
        more_ref.at[rows.mine], more_recv.at[rows.mine], more_load_sems.at[2]
    )
    more_load.start()
    weight_loads = []
    offset = 0
    for i, wide in enumerate(widths):
        if i == len(widths) - 1:
            latent_at = offset
            offset += LANES
        weight_loads.append(
            pltpu.make_async_copy(
                weights[i], weight_ref.at[:, pl.ds(offset, wide)], load_sems.at[2 + i]
            )
        )
        offset += wide
    for c in part_loads + weight_loads:
        c.start()
    thirds(down_rows_ref, 2, latent_ref)
    weight_ref[:, pl.ds(latent_at, LANES)] = jnp.transpose(latent_ref[...].astype(f32)).astype(bf16)
    barrier = pltpu.get_barrier_semaphore()
    greet_dp(barrier, groups)
    small.greet(barrier)
    line.greet_all(barrier, groups - 1)
    rows.start_left()
    for c in part_copies:
        c.start()
    cols.start()
    for c in loads:
        c.start()
    more_load.wait()
    more_keep.start()

    @pl.loop(1, rows.team)
    def _(k):
        more_copy(lax.rem(rows.mine + k, rows.team), rows.mine).start()

    for c in part_loads + weight_loads:
        c.wait()

    count, width = share_ref.shape
    tile_rows, tile_columns = count // 2, 512
    across = width // tile_columns

    for c in loads:
        c.wait()
    for b in range(2):
        at = pl.ds(b * tile_rows, tile_rows)

        @pl.loop(0, across)
        def _(i):
            to = pl.ds(pl.multiple_of(i * tile_columns, tile_columns), tile_columns)
            share_ref[at, to] = dot_t(rows.all[at, :], weight_ref[to, :]).astype(bf16)

        line.prime(b)

    third = LANES // 4
    first_cols = rows.items
    last_item = first_cols + cols.items

    @pl.loop(0, line.steps)
    def _(step):
        line.step(step)

        @pl.when(step == 0)
        def _():
            rows.ready_left()
            for c in part_copies:
                c.wait_recv()

        rows.item(step)

        @pl.when(step == first_cols)
        def _():
            cols.ready()

        @pl.when((step >= first_cols) & (step < last_item))
        def _():
            cols.item(step - first_cols)

        @pl.when(step == last_item)
        def _():
            cols.send_all()
            product = rows_dot(rows.all[:, pl.ds(latent_at, LANES)], rows.left[...])
            wide_ref[:16, :] = product[:16, :] + product[third : third + 16, :]

        @pl.when(step == line.count + SKEW * (n - 2) + 2)
        def _():
            wide_ref[16:, :] = gain_grad_ref[...]
            small.send()

        @pl.when(step == line.second + 14)
        def _():
            small.forward()

    more_keep.wait()

    @pl.loop(1, rows.team)
    def _(k):
        more_copy(0, lax.rem(rows.mine + k, rows.team)).wait_recv()
        more_copy(lax.rem(rows.mine + k, rows.team), rows.mine).wait_send()

    rows.receive()
    cols.receive()
    small.receive()
    line.drain()
    rows.drain()
    for c in part_copies:
        c.wait_send()
    cols.drain()
    small.drain()


def back_mixer(
    call, n, groups, gains, near, near_all, down_rows, x, base_own, left, parts, pair, weights
):
    count, width = left.shape
    half = count // 2
    widths = [w.shape[1] for w in weights]
    total = sum(part.shape[1] for part in parts)
    start = parts[0].shape[1]
    tiles = [(0, 512), (512, 512), (start, parts[1].shape[1])]
    col_rows = pair[0].shape[1]
    vmem = pl.BlockSpec(memory_space=pltpu.VMEM)
    far = pl.BlockSpec(memory_space=pl.ANY)
    wide_shape = (24, width)
    return pl.pallas_call(
        functools.partial(back_mixer_kernel, n, groups, widths, near_all, tiles),
        in_specs=[vmem] * 3 + [far] * (8 + len(weights)),
        out_specs=[vmem] * 3 + [far] * 3,
        out_shape=[
            jax.ShapeDtypeStruct((count, width), bf16),
            jax.ShapeDtypeStruct((24, width // groups), f32),
            jax.ShapeDtypeStruct(near.shape[1:], f32),
            jax.ShapeDtypeStruct((groups // 2, width // groups, total), bf16),
            jax.ShapeDtypeStruct((groups, col_rows // groups, width // 2), bf16),
            jax.ShapeDtypeStruct(pair[2].shape, bf16),
        ],
        scratch_shapes=[
            pltpu.VMEM(pair[2].shape, bf16),
            pltpu.SemaphoreType.DMA((2, groups // 2)),
            pltpu.SemaphoreType.DMA((3,)),
        ]
        + Line.scratch(half, width)
        + [
            pltpu.VMEM((half, width), x.dtype),
            pltpu.VMEM((half, width), base_own.dtype),
            pltpu.VMEM((count, width), bf16),
            pltpu.VMEM(wide_shape, f32),
            pltpu.VMEM((8, width), f32),
            pltpu.VMEM((width, total), bf16),
            pltpu.VMEM((LANES, width), bf16),
            pltpu.SemaphoreType.DMA((2 + len(weights),)),
            Line.semaphores(half),
        ]
        + RowGrads.scratch(groups, count, width, total, 2, len(tiles))
        + ColGrad.scratch(groups, count, col_rows, width // 2)
        + SmallSum.scratch(n, groups, wide_shape, near.shape),
        compiler_params=pltpu.CompilerParams(
            collective_id=call, has_side_effects=True, vmem_limit_bytes=61 << 20
        ),
        cost_estimate=pl.CostEstimate(
            flops=12_000_000_000, bytes_accessed=200_000_000, transcendentals=0
        ),
        name="back_mixer",
    )(gains, near, down_rows, x, base_own, left, *parts, *pair, *weights)


def outputs_kernel(dk, dv, rank, near_all, *refs):
    take = splitter(refs)
    feed_ref, feed_more_ref, rows_ref, down_ref, out_ref = take(5)
    wide_ref, near_ref, token_ref, layer_ref = take(4)
    token_out, layer_out, query_out, key_out, value_out, gate_out = take(6)
    feed_gate_out, feed_up_out, feed_down_out, out_out, decay_out, vector_out = take(6)
    step = pl.program_id(0)

    def total(ref, start, wide):
        span = pl.ds(start, wide)
        result = ref[0, :, span].astype(f32)
        for q in range(1, ref.shape[0]):
            result = result + ref[q, :, span].astype(f32)
        return result

    wide = feed_gate_out.shape[1]
    feed_gate_out[...] = total(feed_ref, 0, wide)
    there = feed_ref.shape[2] - wide
    feed_up_out[:, :there] = total(feed_ref, wide, there)
    feed_up_out[:, there:] = total(feed_more_ref, 0, wide - there)
    query_out[...] = total(rows_ref, 0, dk)
    key_out[...] = total(rows_ref, dk, dk)
    value_out[...] = total(rows_ref, 2 * dk, dv)
    gate_out[...] = total(rows_ref, 2 * dk + dv + LANES, dv)
    token_out[...] = token_ref[...]
    layer_out[...] = layer_ref[...]

    @pl.when(lax.rem(step, pl.num_programs(0) // 2) == 0)
    def _():
        half = out_out.shape[2] // 2
        for ref, out in ((down_ref, feed_down_out), (out_ref, out_out)):
            for b in range(2):
                result = ref[b].astype(f32)
                for q in range(1, ref.shape[0] // 2):
                    result = result + ref[2 * q + b].astype(f32)
                out[0, :, b * half : (b + 1) * half] = result

    @pl.when(step == 0)
    def _():
        decay_out[...] = wide_ref[:rank, :]
        vector_out[...] = jnp.sum(wide_ref[rank:, :], axis=0, keepdims=True)


def outputs(
    groups, dk, dv, rank, near_all, feed, feed_more, rows, down, out, wide_sum, near_sum, token,
    layer,
):
    steps = 4
    count, width = token.shape
    wide = (feed.shape[2] + feed_more.shape[2]) // 2
    per = width // groups
    block = per // steps
    shape = jax.ShapeDtypeStruct

    def rows_of(columns):
        return pl.BlockSpec((block, columns), lambda i: (i, 0))

    def fixed(array):
        return pl.BlockSpec(array.shape, lambda i: (0,) * array.ndim)

    def recv(array):
        return pl.BlockSpec((array.shape[0], block, array.shape[2]), lambda i: (0, i, 0))

    def recv_half(array):
        return pl.BlockSpec(
            (array.shape[0], array.shape[1] // 2, array.shape[2]), lambda i: (0, i // (steps // 2), 0)
        )

    def out_half(array):
        return pl.BlockSpec((1, array.shape[1] // 2, width), lambda i: (0, i // (steps // 2), 0))

    tokens_block = pl.BlockSpec((count // steps, width), lambda i: (i, 0))
    return pl.pallas_call(
        functools.partial(outputs_kernel, dk, dv, rank, near_all),
        grid=(steps,),
        in_specs=[
            recv(feed), recv(feed_more), recv(rows), recv_half(down), recv_half(out), fixed(wide_sum),
            fixed(near_sum), tokens_block, tokens_block,
        ],
        out_specs=[
            tokens_block, tokens_block, rows_of(dk), rows_of(dk), rows_of(dv), rows_of(dv),
            rows_of(wide), rows_of(wide), out_half(down), out_half(out),
            pl.BlockSpec((rank, per), lambda i: (0, 0)),
            pl.BlockSpec((1, per), lambda i: (0, 0)),
        ],
        out_shape=[
            shape((count, width), bf16),
            shape((count, width), bf16),
            shape((per, dk), f32),
            shape((per, dk), f32),
            shape((per, dv), f32),
            shape((per, dv), f32),
            shape((per, wide), f32),
            shape((per, wide), f32),
            shape((1, down.shape[1], width), f32),
            shape((1, out.shape[1], width), f32),
            shape((rank, per), f32),
            shape((1, per), f32),
        ],
        compiler_params=pltpu.CompilerParams(vmem_limit_bytes=60 << 20),
        name="outputs",
    )(feed, feed_more, rows, down, out, wide_sum, near_sum, token, layer)


def recur_back_kernel(n, groups, dk, dv, beside, *refs):
    (
        lengths_ref, send_row_ref, send_column_ref, slot_row_ref, slot_column_ref,
        d_mixed_far, out_weight_far, attended_ref, gate_ref, gains_ref, up_rows_ref,
        share_ref, held_far, states_far, hidden_far, active_far, cotangent_far,
        d_rows_ref, d_gate_ref, head_gain_ref, grad_up_ref, grad_bias_ref, layer_ref, grad_down_ref,
        up_in, down_in, d_attended, d_placed, d_state, result,
        held_ref, states_ref, hidden_ref, up_ref, down_ref, bias_ref, load_sems, sems,
        d_mixed_ref, out_weight_ref,
    ) = refs[:40]
    go = Exchange(groups, (), *refs[40:43])
    back = Exchange(groups, (2 * dk,), *refs[43:46])
    cols = None
    if beside:
        cols = ColGrad(groups, active_far, cotangent_far, 0, 512, grad_down_ref, refs[46:])
    count = d_mixed_ref.shape[0]
    slots = slot_row_ref.shape[1]
    end0 = lengths_ref[0, 0]
    end1 = end0 + lengths_ref[0, 1]
    ends = (end0, end1, end1 + lengths_ref[0, 2])

    def finish(total, own, place):
        layer_ref[place, :] = (hidden_ref[own, :] + total).astype(layer_ref.dtype)

    line = Line(n, share_ref, up_in, down_in, layer_ref, sems, finish)
    loads = (
        pltpu.make_async_copy(hidden_far, hidden_ref, load_sems.at[0]),
        pltpu.make_async_copy(held_far, held_ref, load_sems.at[1]),
        pltpu.make_async_copy(states_far, states_ref, load_sems.at[2]),
    )
    head_loads = (
        pltpu.make_async_copy(d_mixed_far, d_mixed_ref, load_sems.at[3]),
        pltpu.make_async_copy(out_weight_far, out_weight_ref, load_sems.at[4]),
    )
    for c in head_loads:
        c.start()
    barrier = pltpu.get_barrier_semaphore()
    greet_dp(barrier, groups)
    line.greet(barrier, groups - 1)
    line.prime()
    for c in loads:
        c.start()
    if beside:
        cols.start()
    loads[0].wait()

    bias_ref[...] = gains_ref[2:3, dv : dv + dk]
    thirds(up_rows_ref, 3, up_ref)
    thirds(up_rows_ref, 2, down_ref)

    head_gain_ref[...] = jnp.zeros_like(head_gain_ref)
    tile = count // 2
    for c in head_loads:
        c.wait()

    @pl.loop(0, 2)
    def _(i):
        rows = pl.ds(pl.multiple_of(i * tile, tile), tile)
        d_gated = dot_t(d_mixed_ref[rows, :], out_weight_ref[...])
        attended = attended_ref[rows, :].astype(f32)
        gate = gate_ref[rows, :]
        scaling = lax.rsqrt(jnp.mean(attended * attended, axis=1, keepdims=True) + head_floor)
        unit = attended * scaling
        sigmoid = jax.nn.sigmoid(gate)
        swish = gate * sigmoid
        gained = d_gated * gains_ref[2:3, :dv]
        d_gate_ref[rows, :] = (
            gained * unit * sigmoid * (1.0 + gate * (1.0 - sigmoid))
        ).astype(bf16)
        d_unit = gained * swish
        d_attended[rows, :] = (
            scaling * (d_unit - unit * jnp.mean(d_unit * unit, axis=1, keepdims=True))
        ).astype(bf16)
        term = d_gated * unit * swish
        piece = term[0:8, :]
        for r in range(1, tile // 8):
            piece = piece + term[8 * r : 8 * r + 8, :]
        head_gain_ref[...] += piece
        line.step(2 * i)
        line.step(2 * i + 1)

    go.send(0, send_row_ref, 0, d_attended, lambda h: line.step(4 + h))
    d_state[...] = jnp.zeros_like(d_state)
    grad_up_ref[...] = jnp.zeros_like(grad_up_ref)
    grad_bias_ref[...] = jnp.zeros_like(grad_bias_ref)
    done = 14
    if beside:
        cols.ready()

        @pl.loop(0, cols.items)
        def _(i):
            cols.item(i)
            line.step(6 + 2 * i)
            line.step(7 + 2 * i)

        done = 6 + 2 * cols.items
        cols.send_all()
    else:
        line.run(6, done)
    for c in loads[1:]:
        c.wait()

    go.receive(0)
    place_rows(slot_row_ref, go.came, d_placed, go.spans[0], lambda h: line.step(done + h))
    spanned = done + 2
    spans = held_ref.shape[0] // SPAN

    @pl.loop(0, spans)
    def _(i):
        step = spans - 1 - i
        d_out = d_placed[pl.ds(pl.multiple_of(step * SPAN, SPAN), SPAN), :]
        span_backward(
            dk, dv, step, ends, d_out, held_ref, states_ref[step], up_ref, bias_ref, down_ref,
            d_state, result, grad_up_ref, grad_bias_ref,
        )
        line.step(spanned + 2 * i)
        line.step(spanned + 1 + 2 * i)

    sent = spanned + 2 * spans
    for p in range(2):
        back.send(
            p, slot_column_ref, 1, result, lambda h, p=p: line.step(sent + 2 * p + h)
        )
    last_steps = (sent + 4, sent + 4 + (line.steps - sent - 4) * 2 // 3, line.steps)
    for p in range(2):
        line.run(last_steps[p], last_steps[p + 1])
        if beside and p:
            cols.receive()
        back.receive(p)
        span = back.spans[p]

        @pl.loop(0, 2)
        def _(i):
            rows = pl.ds(pl.multiple_of(i * tile, tile), tile)
            pick = one_hot(send_column_ref[rows, :], 0, (tile, slots), 1)
            d_rows_ref[rows, span] = dot(pick, back.came[:, span]).astype(bf16)

    line.drain()
    if beside:
        cols.drain()
    go.drain()
    back.drain()


def recur_back(
    call, n, groups, dk, dv, beside, lengths, send_row, send_column, slot_row, slot_column, d_mixed, out_weight, attended, gate_pre,
    gains, up_rows, share, held, states, hidden_own, active, cotangent,
):
    count, width = d_mixed.shape
    slots, wide = held.shape
    half = count // 2
    vmem = pl.BlockSpec(memory_space=pltpu.VMEM)
    operands = [
        lengths, send_row, send_column, slot_row, slot_column, d_mixed, out_weight, attended, gate_pre, gains, up_rows, share, held, states, hidden_own, active, cotangent,
    ]
    far = pl.BlockSpec(memory_space=pl.ANY)
    return pl.pallas_call(
        functools.partial(recur_back_kernel, n, groups, dk, dv, beside),
        in_specs=[pl.BlockSpec(memory_space=pltpu.SMEM)]
        + [vmem] * 4
        + [far] * 2
        + [vmem] * (len(operands) - 12)
        + [far] * 5,
        out_specs=[vmem] * 6 + [far],
        out_shape=[
            jax.ShapeDtypeStruct((count, wide), bf16),
            jax.ShapeDtypeStruct((count, dv), bf16),
            jax.ShapeDtypeStruct((8, dv), f32),
            jax.ShapeDtypeStruct((dk, LANES), f32),
            jax.ShapeDtypeStruct((8, dk), f32),
            jax.ShapeDtypeStruct((count, width), bf16),
            jax.ShapeDtypeStruct(
                (groups, active.shape[1] // groups if beside else 8, width // 2), bf16
            ),
        ],
        scratch_shapes=Line.scratch(half, width)
        + [
            pltpu.VMEM((count, dv), bf16),
            pltpu.VMEM((slots, dv), bf16),
            pltpu.VMEM((dk, dv), f32),
            pltpu.VMEM((slots, wide), bf16),
            pltpu.VMEM(held.shape, bf16),
            pltpu.VMEM(states.shape, bf16),
            pltpu.VMEM((half, width), f32),
            pltpu.VMEM((LANES, dk), bf16),
            pltpu.VMEM((LANES, dk), bf16),
            pltpu.VMEM((1, dk), f32),
            pltpu.SemaphoreType.DMA((5,)),
            Line.semaphores(half),
            pltpu.VMEM(d_mixed.shape, bf16),
            pltpu.VMEM(out_weight.shape, bf16),
        ]
        + Exchange.scratch(groups, slots, dv, 1)
        + Exchange.scratch(groups, slots, wide, 2)
        + (ColGrad.scratch(groups, count, active.shape[1], width // 2) if beside else []),
        compiler_params=pltpu.CompilerParams(
            collective_id=call, has_side_effects=True, vmem_limit_bytes=60 << 20
        ),
        cost_estimate=pl.CostEstimate(
            flops=12_000_000_000, bytes_accessed=200_000_000, transcendentals=4_000_000
        ),
        name="recur_back",
    )(*operands)


def small_sum_kernel(groups, n, rows_all, part_ref, out_ref, held, line, line_in, sems, line_sems):
    me = lax.axis_index("dp")
    place = lax.axis_index("tensor")
    barrier = pltpu.get_barrier_semaphore()

    def peer(k):
        return lax.rem(me + k, groups)

    def mate(k):
        return lax.rem(place + k, n)

    @pl.loop(1, groups)
    def _(k):
        pl.semaphore_signal(barrier, inc=1, device_id={"dp": peer(k)}, device_id_type=MESH)

    @pl.loop(1, n)
    def _(k):
        pl.semaphore_signal(barrier, inc=1, device_id={"tensor": mate(k)}, device_id_type=MESH)

    pl.semaphore_wait(barrier, groups + n - 2)

    def copy(k, source):
        return pltpu.make_async_remote_copy(
            part_ref.at[peer(k)], held.at[source], sems.at[0, k], sems.at[1, source],
            device_id={"dp": peer(k)}, device_id_type=MESH,
        )

    def line_copy(k, source):
        return pltpu.make_async_remote_copy(
            line, line_in.at[source], line_sems.at[0, k], line_sems.at[1, source],
            device_id={"tensor": mate(k)}, device_id_type=MESH,
        )

    @pl.loop(1, groups)
    def _(k):
        copy(k, me).start()

    held[pl.ds(me, 1)] = part_ref[pl.ds(me, 1)]

    @pl.loop(1, groups)
    def _(k):
        copy(k, peer(k)).wait_recv()

    total = held[0]
    for i in range(1, groups):
        total = total + held[i]
    line[...] = total[:rows_all]
    out_ref[...] = total

    @pl.loop(1, n)
    def _(k):
        line_copy(k, place).start()

    line_in[pl.ds(place, 1)] = total[None, :rows_all]

    @pl.loop(1, n)
    def _(k):
        line_copy(k, mate(k)).wait_recv()

    total = line_in[0]
    for i in range(1, n):
        total = total + line_in[i]
    out_ref[:rows_all] = total

    @pl.loop(1, groups)
    def _(k):
        copy(k, me).wait_send()

    @pl.loop(1, n)
    def _(k):
        line_copy(k, place).wait_send()


def small_sum(over_all, over_owners, groups, n, call):
    def tiles(blocks):
        short = -blocks.shape[1] % (8 * LANES)
        return jnp.pad(blocks, ((0, 0), (0, short))).reshape(groups, -1, LANES)

    first, second = tiles(over_all), tiles(over_owners)
    rows_all = first.shape[1]
    part = jnp.concatenate([first, second], axis=1)
    vmem = pl.BlockSpec(memory_space=pltpu.VMEM)
    total = pl.pallas_call(
        functools.partial(small_sum_kernel, groups, n, rows_all),
        in_specs=[vmem],
        out_specs=vmem,
        out_shape=jax.ShapeDtypeStruct(part.shape[1:], f32),
        scratch_shapes=[
            pltpu.VMEM(part.shape, f32),
            pltpu.VMEM((rows_all, LANES), f32),
            pltpu.VMEM((n, rows_all, LANES), f32),
            pltpu.SemaphoreType.DMA((2, groups)),
            pltpu.SemaphoreType.DMA((2, n)),
        ],
        compiler_params=pltpu.CompilerParams(collective_id=call, has_side_effects=True),
        name="small_sum",
    )(part)
    return (
        total[:rows_all].reshape(-1)[: over_all.shape[1]],
        total[rows_all:].reshape(-1)[: over_owners.shape[1]],
    )


def per_device(
    tokens,
    cotangent,
    token_slots,
    lengths,
    mixer_gain,
    query_weight,
    key_weight,
    value_weight,
    gate_weight,
    decay_down,
    decay_up,
    decay_bias,
    head_gain,
    out_weight,
    feed_gain,
    feed_gate,
    feed_up,
    feed_down,
):
    groups = lax.axis_size("dp")
    lines = lax.axis_size("tensor")
    member = lax.axis_index("dp")
    place = lax.axis_index("tensor")
    count, width = tokens.shape
    dk = query_weight.shape[1]
    dv = value_weight.shape[1]
    rank = decay_up.shape[1]
    parity = lax.rem(member, 2)
    pairs = [(i, i ^ 1) for i in range(groups)]
    same_parity = [[i for i in range(groups) if i % 2 == b] for b in range(2)]

    fused = (width // groups) % LANES == 0
    third = LANES // 4
    down_rows = decay_down.T
    up_rows = decay_up.T
    last = jnp.pad(jnp.concatenate([head_gain, decay_bias]), (0, width - dv - dk))
    gains = jnp.stack([mixer_gain, feed_gain, last]).astype(f32)
    (
        normed, gate_pre, attended, gated, held, states, mixer_share, send_row, send_column, slot_row,
        slot_column,
    ) = front(
        1, groups, lengths, token_slots.reshape(-1, LANES), tokens, gains, up_rows,
        down_rows, [query_weight, key_weight, value_weight], gate_weight, out_weight,
    )

    if fused:
        (
            d_mixed, d_hidden_own, feed_gain_part, feed_recv, feed_more, active, layer_share,
            hidden_own,
        ) = back_feed(
            2, lines, groups, gains, mixer_share, tokens, cotangent, feed_gate, feed_up, feed_down
        )
    else:
        quarter = count // 4

        def own_rows(rows):
            blocks = rows.reshape(2, 2, quarter, width)
            return jnp.where(place == 0, blocks[:, 1], blocks[:, 0]).reshape(2 * quarter, width)

        tokens_own, cotangent_own = own_rows(tokens), own_rows(cotangent)
        feed_normed, hidden_own, _ = line_sum(
            "norm", 5, lines, mixer_share, tokens_own, tokens_own, gains[1:2]
        )
        d_active = dot_t(cotangent, feed_down).astype(bf16)
        gate_hidden = dot(feed_normed, feed_gate)
        up_hidden = dot(feed_normed, feed_up)
        d_active = d_active.astype(f32)
        sigmoid_gate = jax.nn.sigmoid(gate_hidden)
        swish_gate = gate_hidden * sigmoid_gate
        active = (swish_gate * up_hidden).astype(bf16)
        d_gate_hidden = (
            d_active * up_hidden * sigmoid_gate * (1.0 + gate_hidden * (1.0 - sigmoid_gate))
        ).astype(bf16)
        d_up_hidden = (d_active * swish_gate).astype(bf16)
        feed_share = (dot_t(d_gate_hidden, feed_gate) + dot_t(d_up_hidden, feed_up)).astype(bf16)
        d_mixed, d_hidden_own, feed_gain_part = line_sum(
            "back", 2, lines, feed_share, hidden_own, cotangent_own, gains[1:2]
        )
        layer_share = dot(active, feed_down).astype(bf16)

    d_rows, d_gate_low, head_gain_part, up_part, bias_part, layer_out, down_recv = recur_back(
        4, lines, groups, dk, dv, fused, lengths, send_row, send_column, slot_row, slot_column, d_mixed,
        out_weight, attended, gate_pre, gains, up_rows, layer_share, held, states, hidden_own, active,
        cotangent,
    )
    up_part = up_part[:, :rank] + up_part[:, third : third + rank] + (
        up_part[:, 2 * third : 2 * third + rank]
    )

    def by_owner(vector):
        return vector.reshape(groups, -1)

    per = width // groups
    head_per = dv // groups
    up_per = dk // groups * rank
    if fused:
        near = [
            by_owner(jnp.sum(feed_gain_part, axis=0)),
            jnp.pad(by_owner(jnp.sum(head_gain_part, axis=0)), ((0, 0), (0, -head_per % LANES))),
            by_owner(up_part),
            jnp.pad(by_owner(bias_part[0]), ((0, 0), (0, -(dk // groups) % LANES))),
        ]
        near_all = (per + head_per + LANES - 1) // LANES
        near = jnp.concatenate(near, axis=1)
        near = jnp.pad(near, ((0, 0), (0, -near.shape[1] % (8 * LANES))))
        token_grad, wide_sum, near_sum, rows_recv, out_recv, feed_more = back_mixer(
            3, lines, groups, gains, near.reshape(groups, -1, LANES), near_all, down_rows, tokens,
            d_hidden_own, normed, [d_rows, d_gate_low], (gated, d_mixed, feed_more),
            [query_weight, key_weight, value_weight, gate_weight],
        )
        (
            token_grad, layer_out, grad_query, grad_key, grad_value, grad_gate, grad_feed_gate,
            grad_feed_up, grad_feed_down, grad_out, down_sum, mixer_sum,
        ) = outputs(
            groups, dk, dv, rank, near_all, feed_recv, feed_more, rows_recv, down_recv, out_recv,
            wide_sum, near_sum, token_grad, layer_out,
        )
        near_sum = near_sum.reshape(-1)
        mixer_sum = mixer_sum.reshape(-1)
        down_sum = down_sum.T
        feed_sum = near_sum[:per]
        head_sum = near_sum[per : per + head_per]
        up_sum = near_sum[near_all * LANES : near_all * LANES + up_per]
        bias_sum = near_sum[near_all * LANES + up_per :][: dk // groups]
    else:
        down_pad = jnp.pad(decay_down, ((0, 0), (0, third - rank)))
        down_none = jnp.zeros_like(down_pad)
        down_both = jnp.concatenate([down_pad, down_pad, down_none, down_none], axis=1)
        d_query_low = d_rows[:, :dk]
        d_key_low = d_rows[:, dk : 2 * dk]
        d_value_low = d_rows[:, 2 * dk : 2 * dk + dv]
        d_latent_low = d_rows[:, 2 * dk + dv :]
        normed_share = (
            dot_t(d_query_low, query_weight)
            + dot_t(d_key_low, key_weight)
            + dot_t(d_value_low, value_weight)
            + dot_t(d_gate_low, gate_weight)
            + dot_t(d_latent_low, down_both)
        ).astype(bf16)
        token_grad, _, mixer_gain_part = line_sum(
            "back", 3, lines, normed_share, tokens_own, d_hidden_own, gains[0:1],
        )
        down_part = rows_dot(normed, d_latent_low)
        down_part = down_part[:, :rank] + down_part[:, third : third + rank]
        over_all = jnp.concatenate(
            [
                by_owner(jnp.sum(mixer_gain_part, axis=0)),
                by_owner(jnp.sum(feed_gain_part, axis=0)),
                by_owner(jnp.sum(head_gain_part, axis=0)),
                by_owner(down_part),
            ],
            axis=1,
        )
        over_owners = jnp.concatenate([by_owner(up_part), by_owner(bias_part[0])], axis=1)
        summed, small = small_sum(over_all, over_owners, groups, lines, 5)
        mixer_sum = summed[:per]
        feed_sum = summed[per : 2 * per]
        head_sum = summed[2 * per : 2 * per + head_per]
        down_sum = summed[2 * per + head_per :].reshape(per, rank)
        up_sum = small[:up_per]
        bias_sum = small[up_per:]

    def halves(row_block, dims):
        split = row_block.reshape(row_block.shape[0], groups // 2, 2, dims // groups)
        keep = lax.dynamic_index_in_dim(split, parity, 2, keepdims=False)
        send = lax.dynamic_index_in_dim(split, 1 - parity, 2, keepdims=False)
        got = lax.ppermute(send, "dp", pairs)
        shape = (row_block.shape[0], dims // 2)
        return keep.reshape(shape), got.reshape(shape)

    def partner(row_block):
        return row_block, lax.ppermute(row_block, "dp", pairs)

    def summed_share(left, right):
        share = (rows_dot(left[0], right[0]) + rows_dot(left[1], right[1])).astype(bf16)
        rows = share.shape[0] // (groups // 2)
        blocks = share.reshape(groups // 2, rows, share.shape[1])
        moved = lax.all_to_all(
            blocks, "dp", split_axis=0, concat_axis=0, tiled=True, axis_index_groups=same_parity
        )
        return jnp.sum(moved.astype(f32), axis=0)

    if not fused:
        grad_feed_down = summed_share(halves(active, active.shape[1]), partner(cotangent))[None]
        feed_halves = halves(feed_normed, width)
        normed_halves = halves(normed, width)
        grad_feed_gate = summed_share(feed_halves, partner(d_gate_hidden))
        grad_feed_up = summed_share(feed_halves, partner(d_up_hidden))
        grad_out = summed_share(halves(gated, dv), partner(d_mixed))[None]
        grad_query = summed_share(normed_halves, partner(d_query_low))
        grad_key = summed_share(normed_halves, partner(d_key_low))
        grad_value = summed_share(normed_halves, partner(d_value_low))
        grad_gate = summed_share(normed_halves, partner(d_gate_low))

    return (
        layer_out,
        token_grad,
        mixer_sum,
        grad_query,
        grad_key,
        grad_value,
        grad_gate,
        down_sum,
        up_sum.reshape(1, dk // groups, rank),
        bias_sum.reshape(1, dk // groups),
        head_sum,
        grad_out,
        feed_sum,
        grad_feed_gate,
        grad_feed_up,
        grad_feed_down,
    )


def solution(mesh):
    placed = (
        P("dp", None),
        P("dp", None),
        P(),
        P("dp", None),
        P(),
        P(None, "tensor"),
        P(None, "tensor"),
        P(None, "tensor"),
        P(None, "tensor"),
        P(),
        P("tensor", None),
        P("tensor"),
        P(),
        P("tensor", None),
        P(),
        P(None, "tensor"),
        P(None, "tensor"),
        P("tensor", None),
    )
    return jax.shard_map(
        per_device,
        mesh=mesh,
        in_specs=placed,
        out_specs=(
            P("dp", None),
            P("dp", None),
            P("dp"),
            P("dp", "tensor"),
            P("dp", "tensor"),
            P("dp", "tensor"),
            P("dp", "tensor"),
            P("dp", None),
            P("tensor", "dp", None),
            P("tensor", "dp"),
            P("dp"),
            P("tensor", "dp", None),
            P("dp"),
            P("dp", "tensor"),
            P("dp", "tensor"),
            P("tensor", "dp", None),
        ),
        check_vma=False,
    )
```

```python
import functools

import jax
import jax.numpy as jnp
from jax import lax
from jax.experimental import pallas as pl
from jax.experimental.pallas import tpu as pltpu
from jax.sharding import PartitionSpec as P

OWN_CAP = 1024
SPAN = 128
LANES = 128
epsilon = 1e-06
head_floor = 1.0

f32 = jnp.float32
bf16 = jnp.bfloat16
MESH = pl.DeviceIdType.MESH


def rows_dot(left, right):
    return lax.dot_general(left, right, (((0,), (0,)), ((), ())), preferred_element_type=f32)


def dot_t(left, right):
    return lax.dot_general(left, right, (((1,), (1,)), ((), ())), preferred_element_type=f32)


def dot(left, right):
    return jnp.dot(left, right, preferred_element_type=f32)


def span_terms(first, ends, logits):
    rows = logits.shape[0]

    def label(position):
        count = jnp.zeros_like(position)
        for end in ends:
            count = count + (position >= end).astype(jnp.int32)
        return count

    log_decay = jax.nn.log_sigmoid(logits) * (1.0 / 16.0)
    row = lax.broadcasted_iota(jnp.int32, (rows, rows), 0)
    column = lax.broadcasted_iota(jnp.int32, (rows, rows), 1)
    lower = (row >= column).astype(f32)
    cumulative = jnp.dot(
        lower, log_decay, precision=lax.Precision.HIGHEST, preferred_element_type=f32
    )
    total = cumulative[rows - 1 :, :]
    middle = cumulative[rows // 2 - 1 : rows // 2, :]
    label_column = label(first + lax.broadcasted_iota(jnp.int32, (rows, 1), 0))
    label_row = label(first + lax.broadcasted_iota(jnp.int32, (1, rows), 1))
    before = jnp.where(first > 0, label(first - 1), -1)
    last = label(first + rows - 1)
    carried = (label_column == before).astype(f32)
    tail = (label_column == last).astype(f32)
    keep = (before == last).astype(f32)
    allowed = (row >= column) & (label_column == label_row)
    return log_decay, cumulative, total, middle, carried, tail, keep, allowed


def span_forward(dk, dv, step, ends, held_ref, up_ref, bias_ref, state, states_ref, result):
    first = step * SPAN
    at = pl.ds(pl.multiple_of(first, SPAN), SPAN)
    queries = held_ref[at, :dk].astype(f32) * (float(dk) ** -0.5)
    keys = held_ref[at, dk : 2 * dk].astype(f32)
    values = held_ref[at, 2 * dk : 2 * dk + dv]
    logits = dot(held_ref[at, 2 * dk + dv :], up_ref[...]) + bias_ref[...]
    _, cumulative, total, middle, carried, tail, keep, allowed = span_terms(first, ends, logits)
    query_mid = (queries * jnp.exp(cumulative - middle)).astype(bf16)
    key_mid = (keys * jnp.exp(middle - cumulative)).astype(bf16)
    query_start = (queries * jnp.exp(cumulative) * carried).astype(bf16)
    key_end = (keys * jnp.exp(total - cumulative) * tail).astype(bf16)
    scores = jnp.where(allowed, dot_t(query_mid, key_mid), 0.0).astype(bf16)
    entering = state[...]
    entering_low = entering.astype(bf16)
    states_ref[step] = entering_low
    attended = dot(scores, values) + dot(query_start, entering_low)
    result[at, :] = attended.astype(bf16)
    decay_column = jnp.transpose(jnp.broadcast_to(keep * jnp.exp(total), (8, dk)))[:, :1]
    state[...] = decay_column * entering + rows_dot(key_end, values)


def span_backward(
    dk, dv, step, ends, d_out, held_ref, entering, up_ref, bias_ref, down_ref, d_state, result,
    grad_up_ref, grad_bias_ref,
):
    first = step * SPAN
    at = pl.ds(pl.multiple_of(first, SPAN), SPAN)
    scale = float(dk) ** -0.5
    queries = held_ref[at, :dk].astype(f32) * scale
    keys = held_ref[at, dk : 2 * dk].astype(f32)
    values = held_ref[at, 2 * dk : 2 * dk + dv]
    latent = held_ref[at, 2 * dk + dv :]
    logits = dot(latent, up_ref[...]) + bias_ref[...]
    _, cumulative, total, middle, carried, tail, keep, allowed = span_terms(first, ends, logits)
    grow_query = jnp.exp(cumulative - middle)
    grow_key = jnp.exp(middle - cumulative)
    start_decay = jnp.exp(cumulative) * carried
    end_decay = jnp.exp(total - cumulative) * tail
    query_mid = (queries * grow_query).astype(bf16)
    key_mid = (keys * grow_key).astype(bf16)
    query_start = (queries * start_decay).astype(bf16)
    key_end = (keys * end_decay).astype(bf16)
    scores = jnp.where(allowed, dot_t(query_mid, key_mid), 0.0).astype(bf16)
    d_scores = jnp.where(allowed, dot_t(d_out, values), 0.0).astype(bf16)
    leaving = d_state[...]
    leaving_low = leaving.astype(bf16)
    d_values = rows_dot(scores, d_out) + dot(key_end, leaving_low)
    d_queries = dot(d_scores, key_mid) * grow_query + dot_t(d_out, entering) * start_decay
    d_key_end = dot_t(values, leaving_low) * end_decay
    d_keys = rows_dot(d_scores, query_mid) * grow_key + d_key_end
    kept = keep * jnp.exp(total)
    state_pair = jnp.sum(entering.astype(f32) * leaving, axis=1, keepdims=True)
    state_row = jnp.transpose(jnp.broadcast_to(state_pair, (dk, LANES)))[:1, :]
    d_total = jnp.sum(keys * d_key_end, axis=0, keepdims=True) + kept * state_row
    d_cumulative = queries * d_queries - keys * d_keys
    row = lax.broadcasted_iota(jnp.int32, (SPAN, SPAN), 0)
    column = lax.broadcasted_iota(jnp.int32, (SPAN, SPAN), 1)
    upper = (row <= column).astype(f32)
    d_log_decay = (
        jnp.dot(upper, d_cumulative, precision=lax.Precision.HIGHEST, preferred_element_type=f32)
        + d_total
    )
    d_logits = d_log_decay * (1.0 / 16.0) * jax.nn.sigmoid(-logits)
    grad_bias_ref[...] += jnp.broadcast_to(jnp.sum(d_logits, axis=0, keepdims=True), (8, dk))
    d_logits_high = d_logits.astype(bf16)
    d_logits_low = (d_logits - d_logits_high.astype(f32)).astype(bf16)
    grad_up_ref[...] += rows_dot(d_logits_high, latent) + rows_dot(d_logits_low, latent)
    d_latent = dot_t(d_logits_high, down_ref[...]) + dot_t(d_logits_low, down_ref[...])
    high = d_latent.astype(bf16).astype(f32)
    lane = lax.broadcasted_iota(jnp.int32, d_latent.shape, 1)
    d_latent_packed = jnp.where(lane < LANES // 4, high, d_latent - high)
    result[at, :dk] = (d_queries * scale).astype(bf16)
    result[at, dk : 2 * dk] = d_keys.astype(bf16)
    result[at, 2 * dk : 2 * dk + dv] = d_values.astype(bf16)
    result[at, 2 * dk + dv :] = d_latent_packed.astype(bf16)
    kept_column = jnp.transpose(jnp.broadcast_to(kept, (8, dk)))[:, :1]
    d_state[...] = kept_column * leaving + rows_dot(query_start, d_out)


FINE = 16
SKEW = 3


class Line:
    def __init__(self, n, share_ref, up_in, down_in, out_ref, sems, finish):
        self.n, self.me = n, lax.axis_index("tensor")
        self.share, self.up_in, self.down_in, self.out = share_ref, up_in, down_in, out_ref
        self.sems, self.finish = sems, finish
        self.half = up_in.shape[0]
        self.block = self.half // 2
        self.count = self.half // FINE
        self.second = self.count + 2
        self.steps = self.second + self.count + SKEW * (n - 2)

    @staticmethod
    def scratch(half, width):
        return [pltpu.VMEM((half, width), bf16), pltpu.VMEM((half, width), bf16)]

    @staticmethod
    def semaphores(half):
        return pltpu.SemaphoreType.DMA((8, half // FINE))

    def own_copies(self, source, target, sems):
        block = self.block
        return [
            pltpu.make_async_copy(
                source.at[
                    pl.ds(
                        pl.multiple_of(2 * i * block + jnp.where(self.me == 0, block, 0), block),
                        block,
                    ),
                    :,
                ],
                target.at[pl.ds(i * block, block), :],
                sems[i],
            )
            for i in range(2)
        ]

    def greet(self, barrier, others):
        n, me = self.n, self.me

        @pl.when(me > 0)
        def _():
            pl.semaphore_signal(barrier, inc=1, device_id={"tensor": me - 1}, device_id_type=MESH)

        @pl.when(me < n - 1)
        def _():
            pl.semaphore_signal(barrier, inc=1, device_id={"tensor": me + 1}, device_id_type=MESH)

        inside = (me > 0) & (me < n - 1)

        @pl.when(inside)
        def _():
            pl.semaphore_wait(barrier, others + 2)

        @pl.when(jnp.logical_not(inside))
        def _():
            pl.semaphore_wait(barrier, others + 1)

    def greet_all(self, barrier, others):
        n, me = self.n, self.me

        @pl.when(me > 0)
        def _():
            pl.semaphore_signal(barrier, inc=1, device_id={"tensor": me - 1}, device_id_type=MESH)

        @pl.when(me < n - 1)
        def _():
            pl.semaphore_signal(barrier, inc=1, device_id={"tensor": me + 1}, device_id_type=MESH)

        pl.semaphore_wait(barrier, others + n - 1)

    def own(self, g):
        return pl.ds(pl.multiple_of(g * FINE, FINE), FINE)

    def at(self, g):
        per = self.block // FINE
        return pl.ds(
            pl.multiple_of((g // per) * 2 * self.block + lax.rem(g, per) * FINE, FINE), FINE
        )

    def low(self, g):
        per = self.block // FINE
        start = (g // per) * 2 * self.block + self.block + lax.rem(g, per) * FINE
        return pl.ds(pl.multiple_of(start, FINE), FINE)

    def right(self, source, target, lane, g):
        return pltpu.make_async_remote_copy(
            source, target, self.sems.at[2 * lane, g], self.sems.at[2 * lane + 1, g],
            device_id={"tensor": jnp.minimum(self.me + 1, self.n - 1)}, device_id_type=MESH,
        )

    def left(self, source, target, lane, g):
        return pltpu.make_async_remote_copy(
            source, target, self.sems.at[2 * lane, g], self.sems.at[2 * lane + 1, g],
            device_id={"tensor": jnp.maximum(self.me - 1, 0)}, device_id_type=MESH,
        )

    def up_copy(self, g):
        rows = self.up_in.at[self.own(g), :]
        return self.right(rows, rows, 0, g)

    def down_copy(self, g):
        rows = self.down_in.at[self.own(g), :]
        return self.left(rows, rows, 1, g)

    def up_back_copy(self, g):
        rows = self.out.at[self.at(g), :]
        return self.left(rows, rows, 2, g)

    def down_back_copy(self, g):
        rows = self.out.at[self.low(g), :]
        return self.right(rows, rows, 3, g)

    def prime(self, block=None):
        first, last = (0, self.count)
        if block is not None:
            per = self.block // FINE
            first, last = block * per, block * per + per

        @pl.when(self.me == 0)
        def _():
            @pl.loop(first, last)
            def _(g):
                self.right(
                    self.share.at[self.at(g), :], self.up_in.at[self.own(g), :], 0, g
                ).start()

        @pl.when(self.me == self.n - 1)
        def _():
            @pl.loop(first, last)
            def _(g):
                self.left(
                    self.share.at[self.low(g), :], self.down_in.at[self.own(g), :], 1, g
                ).start()

    def step(self, step):
        n, me, count = self.n, self.me, self.count
        at, low, own = self.at, self.low, self.own
        g_up = step - SKEW * (me - 1)

        @pl.when((me > 0) & (g_up >= 0) & (g_up < count))
        def _():
            self.up_copy(g_up).wait_recv()
            total = self.up_in[own(g_up), :].astype(f32) + self.share[at(g_up), :].astype(f32)

            @pl.when(me < n - 1)
            def _():
                self.up_in[own(g_up), :] = total.astype(bf16)
                self.up_copy(g_up).start()

            @pl.when(me == n - 1)
            def _():
                self.finish(total, own(g_up), at(g_up))
                self.up_back_copy(g_up).start()

        g_down = step - SKEW * (n - 2 - me)

        @pl.when((me < n - 1) & (g_down >= 0) & (g_down < count))
        def _():
            self.down_copy(g_down).wait_recv()
            total = self.down_in[own(g_down), :].astype(f32) + (
                self.share[low(g_down), :].astype(f32)
            )

            @pl.when(me > 0)
            def _():
                self.down_in[own(g_down), :] = total.astype(bf16)
                self.down_copy(g_down).start()

            @pl.when(me == 0)
            def _():
                self.finish(total, own(g_down), low(g_down))
                self.down_back_copy(g_down).start()

        g_up_back = step - self.second - SKEW * (n - 2 - me)

        @pl.when((me < n - 1) & (g_up_back >= 0) & (g_up_back < count))
        def _():
            self.up_back_copy(g_up_back).wait_recv()

            @pl.when(me > 0)
            def _():
                self.up_back_copy(g_up_back).start()

        g_down_back = step - self.second - SKEW * (me - 1)

        @pl.when((me > 0) & (g_down_back >= 0) & (g_down_back < count))
        def _():
            self.down_back_copy(g_down_back).wait_recv()

            @pl.when(me < n - 1)
            def _():
                self.down_back_copy(g_down_back).start()

    def run(self, first, last):
        @pl.loop(first, last)
        def _(step):
            self.step(step)

    def drain(self):
        n, me = self.n, self.me

        @pl.loop(0, self.count)
        def _(g):
            @pl.when(me < n - 1)
            def _():
                self.up_copy(g).wait_send()
                self.down_back_copy(g).wait_send()

            @pl.when(me > 0)
            def _():
                self.down_copy(g).wait_send()
                self.up_back_copy(g).wait_send()


def norm_back(x_ref, base, gain, out_ref, kept_ref, gain_grad_ref):
    gain_grad_ref[...] = jnp.zeros_like(gain_grad_ref)

    def finish(total, own, place):
        rows = x_ref[own, :].astype(f32)
        scaling = lax.rsqrt(jnp.mean(rows * rows, axis=1, keepdims=True) + epsilon)
        unit = rows * scaling
        gained = gain() * total
        grad = base(own, place).astype(f32) + scaling * (
            gained - unit * jnp.mean(gained * unit, axis=1, keepdims=True)
        )
        if kept_ref is not None:
            kept_ref[own, :] = grad
        out_ref[place, :] = grad.astype(out_ref.dtype)
        term = total * unit
        part = term[0:8, :]
        for i in range(1, FINE // 8):
            part = part + term[8 * i : 8 * i + 8, :]
        gain_grad_ref[...] += part

    return finish


def norm_forward(base, gain, out_ref, kept_ref):
    def finish(total, own, place):
        hidden = base(own, place).astype(f32) + total
        kept_ref[own, :] = hidden
        scaling = lax.rsqrt(jnp.mean(hidden * hidden, axis=1, keepdims=True) + epsilon)
        out_ref[place, :] = (hidden * scaling * gain()).astype(bf16)

    return finish


def line_kernel(mode, n, *refs):
    share_ref, x_ref, base_ref, gain_ref, out_ref, kept_ref, gain_grad_ref = refs[:7]
    up_in, down_in, sems = refs[7:]

    def base(own, place):
        return base_ref[own, :]

    def gain():
        return gain_ref[...]

    gain_grad_ref[...] = jnp.zeros_like(gain_grad_ref)
    if mode == "norm":
        finish = norm_forward(base, gain, out_ref, kept_ref)
    else:
        finish = norm_back(x_ref, base, gain, out_ref, kept_ref, gain_grad_ref)
    line = Line(n, share_ref, up_in, down_in, out_ref, sems, finish)
    line.greet(pltpu.get_barrier_semaphore(), 0)
    line.prime()
    line.run(0, line.steps)
    line.drain()


def line_sum(mode, call, n, share, x_own, base_own, gain):
    rows, width = share.shape
    half = rows // 2
    vmem = pl.BlockSpec(memory_space=pltpu.VMEM)
    return pl.pallas_call(
        functools.partial(line_kernel, mode, n),
        in_specs=[vmem] * 4,
        out_specs=[vmem] * 3,
        out_shape=[
            jax.ShapeDtypeStruct((rows, width), bf16),
            jax.ShapeDtypeStruct((half, width), f32),
            jax.ShapeDtypeStruct((8, width), f32),
        ],
        scratch_shapes=Line.scratch(half, width) + [Line.semaphores(half)],
        compiler_params=pltpu.CompilerParams(
            collective_id=call, has_side_effects=True, vmem_limit_bytes=40 << 20
        ),
        name="line_" + mode,
    )(share, x_own, base_own, gain)


def partner_of(index):
    return index + 1 - 2 * lax.rem(index, 2)


def to_dp(source, target, send, recv, device):
    return pltpu.make_async_remote_copy(
        source, target, send, recv, device_id={"dp": device}, device_id_type=MESH
    )


def greet_dp(barrier, groups):
    member = lax.axis_index("dp")

    @pl.loop(1, groups)
    def _(k):
        pl.semaphore_signal(
            barrier, inc=1, device_id={"dp": lax.rem(member + k, groups)}, device_id_type=MESH
        )


class ColGrad:
    def __init__(self, groups, left, right, first, tile, recv, refs):
        self.tile = tile
        (
            self.left, self.right, self.left_in, self.right_in, self.send,
            self.load_sems, self.pair_sems, self.sems,
        ) = refs
        self.left_far, self.right_far, self.recv, self.groups = left, right, recv, groups
        self.member = lax.axis_index("dp")
        self.parity = lax.rem(self.member, 2)
        self.half = right.shape[1] // 2
        self.first, self.wide = first, self.right_in.shape[1]
        self.size = self.send.shape[0] // groups
        self.items = self.wide // self.tile

    @staticmethod
    def scratch(groups, count, rows, wide):
        return [
            pltpu.VMEM((count, rows), bf16),
            pltpu.VMEM((count, wide), bf16),
            pltpu.VMEM((count, rows), bf16),
            pltpu.VMEM((count, wide), bf16),
            pltpu.VMEM((rows, wide), bf16),
            pltpu.SemaphoreType.DMA((3,)),
            pltpu.SemaphoreType.DMA((2, 2)),
            pltpu.SemaphoreType.DMA((2, groups)),
        ]

    def halves(self, parity):
        start = pl.multiple_of(parity * self.half + self.first, self.tile)
        return self.right_far.at[:, pl.ds(start, self.wide)]

    def loads(self):
        return (
            pltpu.make_async_copy(self.left_far, self.left, self.load_sems.at[0]),
            pltpu.make_async_copy(self.halves(self.parity), self.right, self.load_sems.at[1]),
        )

    def pair_copies(self):
        partner = partner_of(self.member)
        sems = self.pair_sems
        return (
            to_dp(self.left_far, self.left_in, sems.at[0, 0], sems.at[1, 0], partner),
            to_dp(
                self.halves(1 - self.parity), self.right_in, sems.at[0, 1], sems.at[1, 1], partner
            ),
        )

    def start(self):
        for c in self.pair_copies() + self.loads():
            c.start()

    def ready(self):
        for c in self.loads():
            c.wait()
        for c in self.pair_copies():
            c.wait_recv()

    def item(self, t):
        span = pl.ds(pl.multiple_of(t * self.tile, self.tile), self.tile)
        product = rows_dot(self.left[...], self.right[:, span]) + rows_dot(
            self.left_in[...], self.right_in[:, span]
        )
        self.send[:, span] = product.astype(bf16)

    def copy(self, to, source):
        rows = pl.ds(pl.multiple_of(to * self.size, 16), self.size)
        return to_dp(
            self.send.at[rows, :], self.recv.at[source], self.sems.at[0, to],
            self.sems.at[1, source], to,
        )

    def send_all(self):
        @pl.loop(1, self.groups)
        def _(k):
            self.copy(lax.rem(self.member + k, self.groups), self.member).start()

        self.keep().start()

    def keep(self):
        own = pl.ds(pl.multiple_of(self.member * self.size, 16), self.size)
        return pltpu.make_async_copy(
            self.send.at[own, :], self.recv.at[self.member], self.load_sems.at[2]
        )

    def receive(self):
        self.keep().wait()

        @pl.loop(1, self.groups)
        def _(k):
            self.copy(0, lax.rem(self.member + k, self.groups)).wait_recv()

    def drain(self):
        for c in self.pair_copies():
            c.wait_send()

        @pl.loop(1, self.groups)
        def _(k):
            self.copy(lax.rem(self.member + k, self.groups), self.member).wait_send()


class RowGrads:
    def __init__(self, groups, left, tiles, recv, refs, deferred=0):
        (
            self.left, self.all, self.left_in, self.all_in, self.send,
            self.load_sems, self.left_sems, self.piece_sems, self.sems, self.keep_sems,
        ) = refs
        self.left_far, self.tiles, self.recv = left, tiles, recv
        self.live = len(tiles) - deferred
        if left is None:
            self.left_far = self.left
        self.member = lax.axis_index("dp")
        self.parity = lax.rem(self.member, 2)
        self.mine = self.member // 2
        self.team = groups // 2
        self.block = self.left.shape[1] // groups
        self.items = self.team * len(tiles)

    @staticmethod
    def scratch(groups, count, width, total, pieces, tiles):
        team = groups // 2
        return [
            pltpu.VMEM((count, width), bf16),
            pltpu.VMEM((count, total), bf16),
            pltpu.VMEM((count, width // 2), bf16),
            pltpu.VMEM((count, total), bf16),
            pltpu.VMEM((team, width // groups, total), bf16),
            pltpu.SemaphoreType.DMA((1 + pieces,)),
            pltpu.SemaphoreType.DMA((2, team)),
            pltpu.SemaphoreType.DMA((2, pieces)),
            pltpu.SemaphoreType.DMA((2, tiles, team)),
            pltpu.SemaphoreType.DMA((tiles,)),
        ]

    def columns(self, j):
        return pl.ds(pl.multiple_of(j * self.block, self.block), self.block)

    def left_load(self):
        return pltpu.make_async_copy(self.left_far, self.left, self.load_sems.at[0])

    def piece_load(self, p, source, span):
        return pltpu.make_async_copy(source, self.all.at[:, span], self.load_sems.at[1 + p])

    def left_copy(self, q):
        return to_dp(
            self.left_far.at[:, self.columns(2 * q + 1 - self.parity)],
            self.left_in.at[:, self.columns(q)],
            self.left_sems.at[0, q], self.left_sems.at[1, q], partner_of(self.member),
        )

    def piece_copy(self, p, source, span, rows=slice(None)):
        return to_dp(
            source, self.all_in.at[rows, span], self.piece_sems.at[0, p], self.piece_sems.at[1, p],
            partner_of(self.member),
        )

    def start_left(self):
        @pl.loop(0, self.team)
        def _(q):
            self.left_copy(q).start()

        self.left_load().start()

    def ready_left(self):
        self.left_load().wait()

        @pl.loop(0, self.team)
        def _(q):
            self.left_copy(q).wait_recv()

    def copy(self, t, to, source):
        start, wide = self.tiles[t]
        span = pl.ds(start, wide)
        return to_dp(
            self.send.at[to, :, span], self.recv.at[source, :, span],
            self.sems.at[0, t, to], self.sems.at[1, t, source], 2 * to + self.parity,
        )

    def item(self, w):
        count = len(self.tiles)
        k = w // count
        to = lax.rem(self.mine + 1 + k, self.team)
        for t in range(count):
            start, wide = self.tiles[t]

            @pl.when((w >= 0) & (w < self.items) & (lax.rem(w, count) == t))
            def _():
                span = pl.ds(start, wide)
                product = rows_dot(
                    self.left[:, self.columns(2 * to + self.parity)], self.all[:, span]
                ) + rows_dot(self.left_in[:, self.columns(to)], self.all_in[:, span])
                self.send[to, :, span] = product.astype(bf16)

                if t < self.live:
                    @pl.when(k < self.team - 1)
                    def _():
                        self.copy(t, to, self.mine).start()

                    @pl.when(k == self.team - 1)
                    def _():
                        self.keep(t).start()

    def keep(self, t):
        start, wide = self.tiles[t]
        span = pl.ds(start, wide)
        return pltpu.make_async_copy(
            self.send.at[self.mine, :, span], self.recv.at[self.mine, :, span], self.keep_sems.at[t]
        )

    def receive(self):
        for t in range(self.live):
            self.keep(t).wait()

            @pl.loop(1, self.team)
            def _(k):
                self.copy(t, 0, lax.rem(self.mine + k, self.team)).wait_recv()

    def drain(self):
        @pl.loop(0, self.team)
        def _(q):
            self.left_copy(q).wait_send()

        for t in range(self.live):
            @pl.loop(1, self.team)
            def _(k):
                self.copy(t, lax.rem(self.mine + k, self.team), self.mine).wait_send()


def splitter(refs):
    refs = list(refs)

    def take(k):
        out = refs[:k]
        del refs[:k]
        return out

    return take


def one_hot(index, base, shape, dim):
    return (index == base + lax.broadcasted_iota(jnp.int32, shape, dim)).astype(f32).astype(bf16)


def thirds(source, terms, target):
    third = LANES // 4
    size = source.shape[0]
    target[...] = jnp.zeros_like(target)
    for i in range(terms):
        target[i * third : i * third + size, :] = source[...]


class Exchange:
    def __init__(self, groups, cuts, sent, came, sems):
        self.groups, self.sent, self.came, self.sems = groups, sent, came, sems
        self.spans = [pl.ds(a, b - a) for a, b in zip((0,) + cuts, cuts + (sent.shape[1],))]
        self.member = lax.axis_index("dp")
        self.cap = sent.shape[0] // groups

    @staticmethod
    def scratch(groups, slots, width, pieces):
        return [
            pltpu.VMEM((slots, width), bf16),
            pltpu.VMEM((slots, width), bf16),
            pltpu.SemaphoreType.DMA((2, pieces, groups)),
        ]

    def part(self, j):
        return pl.ds(pl.multiple_of(j * self.cap, self.cap), self.cap)

    def copy(self, p, to, source):
        span = self.spans[p]
        return to_dp(
            self.sent.at[self.part(to), span], self.came.at[self.part(source), span],
            self.sems.at[0, p, to], self.sems.at[1, p, source], to,
        )

    def send(self, p, index_ref, dim, source, between=None):
        span = self.spans[p]
        groups, count = self.groups, source.shape[0]
        rows = self.sent.shape[0] // 2

        @pl.loop(0, 2)
        def _(h):
            at = pl.ds(pl.multiple_of(h * rows, rows), rows)
            if dim == 0:
                pick = one_hot(index_ref[...], h * rows, (rows, count), 0)
            else:
                pick = one_hot(index_ref[at, :], 0, (rows, count), 1)
            self.sent[at, span] = dot(pick, source[:, span]).astype(bf16)

            @pl.loop(0, groups // 2)
            def _(k):
                to = h * (groups // 2) + lax.rem(self.member + k, groups // 2)

                @pl.when(to != self.member)
                def _():
                    self.copy(p, to, self.member).start()

            if between is not None:
                between(h)

        own = self.part(self.member)
        self.came[own, span] = self.sent[own, span]

    def receive(self, p):
        @pl.loop(1, self.groups)
        def _(k):
            self.copy(p, 0, lax.rem(self.member + k, self.groups)).wait_recv()

    def drain(self):
        for p in range(len(self.spans)):
            @pl.loop(1, self.groups)
            def _(k):
                self.copy(p, lax.rem(self.member + k, self.groups), self.member).wait_send()


def place_rows(slot_row_ref, came, held, span, between=None):
    positions, slots = held.shape[0], came.shape[0]
    rows = positions // 2

    @pl.loop(0, 2)
    def _(h):
        at = pl.ds(pl.multiple_of(h * rows, rows), rows)
        pick = one_hot(slot_row_ref[...], h * rows, (rows, slots), 0)
        held[at, span] = dot(pick, came[:, span]).astype(bf16)
        if between is not None:
            between(h)


def front_kernel(groups, dk, dv, *refs):
    take = splitter(refs)
    lengths_ref, slot_rows_ref, tokens_ref, gains_ref, up_rows_ref, down_rows_ref = take(6)
    weights_far = take(3)
    gate_far, out_far = take(2)
    spilled = take(6)
    (share_ref,) = take(1)
    send_row_ref, send_column_ref, slot_row_ref, slot_column_ref = take(4)
    normed_ref, gate_ref, attended_ref, gated_ref, held_ref, states_ref = kept = take(6)
    weight_ref, gate_weight_ref, out_weight_ref = take(3)
    rows_out, state, result, rank_ref, up_ref, bias_ref, latent_ref = take(7)
    slots_ref, load_sems = take(2)
    go = Exchange(groups, (2 * dk,), *take(3))
    back = Exchange(groups, (), *take(3))
    (spill_sems,) = take(1)
    member = lax.axis_index("dp")
    count, width = tokens_ref.shape
    cap = OWN_CAP // groups
    half = count // 2
    spills = [
        pltpu.make_async_copy(kept[i], spilled[i], spill_sems.at[i]) for i in range(6)
    ]

    def spill(*which):
        for i in which:
            spills[i].start()

    end0 = lengths_ref[0, 0]
    end1 = end0 + lengths_ref[0, 1]
    ends = (end0, end1, end1 + lengths_ref[0, 2])
    third = LANES // 4

    loads = []
    offset = 0
    for i, far in enumerate(weights_far):
        wide = far.shape[1]
        loads.append(
            pltpu.make_async_copy(far, weight_ref.at[:, pl.ds(offset, wide)], load_sems.at[i])
        )
        offset += wide
    later = [
        pltpu.make_async_copy(gate_far, gate_weight_ref, load_sems.at[4]),
        pltpu.make_async_copy(out_far, out_weight_ref, load_sems.at[5]),
    ]
    for c in loads + later:
        c.start()
    barrier = pltpu.get_barrier_semaphore()
    greet_dp(barrier, groups)
    pl.semaphore_wait(barrier, groups - 1)

    pieces = count // LANES
    for i in range(pieces):
        slots_ref[:, i * LANES : (i + 1) * LANES] = slot_rows_ref[pl.ds(i, groups, stride=pieces), :]
    owners = slots_ref[...] // OWN_CAP
    mine = owners == member
    my_slots = slots_ref[pl.ds(member, 1), :]
    my_owner = my_slots // OWN_CAP
    device = lax.broadcasted_iota(jnp.int32, (groups, count), 0)
    chosen = (my_owner == device).astype(f32)
    before = (
        lax.broadcasted_iota(jnp.int32, (count, count), 0)
        < lax.broadcasted_iota(jnp.int32, (count, count), 1)
    ).astype(f32).astype(bf16)
    send_rank = jnp.sum(chosen * dot(chosen.astype(bf16), before), axis=0, keepdims=True)
    send_row = my_owner * cap + send_rank.astype(jnp.int32)
    send_row_ref[...] = send_row
    send_column_ref[...] = jnp.transpose(
        jnp.broadcast_to(send_row.astype(f32), (8, count))
    )[:, :1].astype(jnp.int32)
    rank_ref[...] = jnp.where(mine, dot(mine.astype(f32).astype(bf16), before), -1.0)

    bias_ref[...] = gains_ref[2:3, dv : dv + dk]
    thirds(up_rows_ref, 3, up_ref)
    thirds(down_rows_ref, 3, latent_ref)

    tile = count // 5

    @pl.loop(0, 5)
    def _(i):
        at = pl.ds(pl.multiple_of(i * tile, tile), tile)
        rows = tokens_ref[at, :].astype(f32)
        scaling = lax.rsqrt(jnp.mean(rows * rows, axis=1, keepdims=True) + epsilon)
        normed_ref[at, :] = (rows * scaling * gains_ref[0:1, :]).astype(bf16)

    for c in loads[:2]:
        c.wait()
    body = 2 * dk + dv

    spill(0)

    def project(first, last):
        @pl.loop(first // 256, last // 256)
        def _(i):
            to = pl.ds(pl.multiple_of(i * 256, 256), 256)
            rows_out[:, to] = dot(normed_ref[...], weight_ref[:, to]).astype(bf16)

    project(0, 2 * dk)
    go.send(0, send_row_ref, 0, rows_out)
    for c in loads[2:]:
        c.wait()
    project(2 * dk, body)
    latent = dot_t(normed_ref[...], latent_ref[...])
    high = latent.astype(bf16).astype(f32)
    middle = (latent - high).astype(bf16).astype(f32)
    lane = lax.broadcasted_iota(jnp.int32, latent.shape, 1)
    rows_out[:, body:] = jnp.where(
        lane < third, high, jnp.where(lane < 2 * third, middle, latent - high - middle)
    ).astype(bf16)
    go.send(1, send_row_ref, 0, rows_out)

    for c in later:
        c.wait()

    @pl.loop(0, dv // 256)
    def _(i):
        to = pl.ds(pl.multiple_of(i * 256, 256), 256)
        gate_ref[:, to] = dot(normed_ref[...], gate_weight_ref[:, to])

    spill(1)

    @pl.loop(0, groups)
    def _(j):
        rank = rank_ref[pl.ds(j, 1), :]
        local = (lax.rem(slots_ref[pl.ds(j, 1), :], OWN_CAP) - OWN_CAP).astype(f32)
        wanted = lax.broadcasted_iota(jnp.int32, (cap, count), 0).astype(f32)
        at = jnp.sum(jnp.where(rank == wanted, local, 0.0), axis=1, keepdims=True)
        slot_column_ref[go.part(j), :] = at.astype(jnp.int32) + OWN_CAP

    slots = slot_row_ref.shape[1]
    slot_row_ref[...] = jnp.transpose(
        jnp.broadcast_to(slot_column_ref[...].astype(f32), (slots, LANES))
    )[:1, :].astype(jnp.int32)
    state[...] = jnp.zeros_like(state)
    for p in range(2):
        go.receive(p)
        place_rows(slot_row_ref, go.came, held_ref, go.spans[p])

    @pl.loop(0, held_ref.shape[0] // SPAN, unroll=2)
    def _(step):
        span_forward(dk, dv, step, ends, held_ref, up_ref, bias_ref, state, states_ref, result)

    back.send(0, slot_column_ref, 1, result)
    spill(4, 5)
    back.receive(0)

    def head_rows(at):
        pick = one_hot(send_column_ref[at, :], 0, (half, slots), 1)
        attended = dot(pick, back.came[...])
        attended_ref[at, :] = attended.astype(bf16)
        gate = gate_ref[at, :]
        scaling = lax.rsqrt(jnp.mean(attended * attended, axis=1, keepdims=True) + head_floor)
        gated = attended * scaling * gains_ref[2:3, :dv] * (gate * jax.nn.sigmoid(gate))
        gated_ref[at, :] = gated.astype(bf16)

        @pl.loop(0, width // 512)
        def _(i):
            to = pl.ds(pl.multiple_of(i * 512, 512), 512)
            share_ref[at, to] = dot(gated_ref[at, :], out_weight_ref[:, to]).astype(bf16)

    @pl.loop(0, 2)
    def _(i):
        head_rows(pl.ds(pl.multiple_of(i * half, half), half))

    spill(2, 3)
    go.drain()
    back.drain()
    for c in spills:
        c.wait()


def front(
    call, groups, lengths, slots, tokens, gains, up_rows, down_rows, weights, gate_weight,
    out_weight,
):
    count, width = tokens.shape
    dk, dv = weights[0].shape[1], weights[2].shape[1]
    body = 2 * dk + dv
    wide = body + LANES
    spans = OWN_CAP // SPAN
    vmem = pl.BlockSpec(memory_space=pltpu.VMEM)
    far = pl.BlockSpec(memory_space=pl.ANY)
    smem = pl.BlockSpec(memory_space=pltpu.SMEM)
    shape = jax.ShapeDtypeStruct
    saved = [
        shape((count, width), bf16),
        shape((count, dv), f32),
        shape((count, dv), bf16),
        shape((count, dv), bf16),
        shape((OWN_CAP, wide), bf16),
        shape((spans, dk, dv), bf16),
    ]
    return pl.pallas_call(
        functools.partial(front_kernel, groups, dk, dv),
        in_specs=[smem] + [vmem] * 5 + [far] * 5,
        out_specs=[far] * 6 + [vmem] * 5,
        out_shape=[
            *saved,
            shape((count, width), bf16),
            shape((1, count), jnp.int32),
            shape((count, 1), jnp.int32),
            shape((1, OWN_CAP), jnp.int32),
            shape((OWN_CAP, 1), jnp.int32),
        ],
        scratch_shapes=[pltpu.VMEM(a.shape, a.dtype) for a in saved]
        + [
            pltpu.VMEM((width, body), bf16),
            pltpu.VMEM((width, dv), bf16),
            pltpu.VMEM((dv, width), bf16),
            pltpu.VMEM((count, wide), bf16),
            pltpu.VMEM((dk, dv), f32),
            pltpu.VMEM((OWN_CAP, dv), bf16),
            pltpu.VMEM((groups, count), f32),
            pltpu.VMEM((LANES, dk), bf16),
            pltpu.VMEM((1, dk), f32),
            pltpu.VMEM((LANES, width), bf16),
            pltpu.VMEM((groups, count), jnp.int32),
            pltpu.SemaphoreType.DMA((8,)),
        ]
        + Exchange.scratch(groups, OWN_CAP, wide, 2)
        + Exchange.scratch(groups, OWN_CAP, dv, 1)
        + [pltpu.SemaphoreType.DMA((6,))],
        compiler_params=pltpu.CompilerParams(
            collective_id=call, has_side_effects=True, vmem_limit_bytes=60 << 20
        ),
        cost_estimate=pl.CostEstimate(
            flops=12_000_000_000, bytes_accessed=200_000_000, transcendentals=4_000_000
        ),
        name="front",
    )(
        lengths, slots, tokens, gains, up_rows, down_rows, *weights, gate_weight, out_weight,
    )


def back_feed_kernel(n, groups, tiles, *refs):
    take = splitter(refs)
    gains_ref, first_share_ref, tokens_far, cotangent_far, gate_far, up_far, down_far = take(7)
    out_ref, kept_ref, gain_grad_ref = take(3)
    recv, more_far, active_far, layer_far, hidden_far = take(5)
    active_ref, layer_ref, first_up, first_down, up_in, down_in = take(6)
    hidden_ref, tokens_ref, cotangent_ref, share_ref, weight_ref, d_active_ref = take(6)
    load_sems, weight_sems, first_sems, sems = take(4)
    rows = RowGrads(groups, None, tiles, recv, take(10), deferred=1)
    feed_ref = rows.left
    count, width = share_ref.shape
    wide = active_ref.shape[1]
    full, rest = wide // 256, wide % 256
    pieces = full + (rest > 0)
    half = count // 2
    first_line = Line(
        n, first_share_ref, first_up, first_down, feed_ref, first_sems,
        norm_forward(
            lambda own, place: tokens_ref[own, :], lambda: gains_ref[1:2, :], feed_ref, hidden_ref
        ),
    )
    line = Line(
        n, share_ref, up_in, down_in, out_ref, sems,
        norm_back(
            hidden_ref, lambda own, place: cotangent_ref[place, :], lambda: gains_ref[1:2, :],
            out_ref, kept_ref, gain_grad_ref,
        ),
    )
    token_loads = first_line.own_copies(tokens_far, tokens_ref, [load_sems.at[0], load_sems.at[1]])
    cotangent_load = pltpu.make_async_copy(cotangent_far, cotangent_ref, load_sems.at[2])
    down_load = pltpu.make_async_copy(
        down_far, weight_ref.at[pl.ds(0, wide), pl.ds(0, width)], load_sems.at[3]
    )
    active_spill = pltpu.make_async_copy(active_ref, active_far, load_sems.at[4])
    layer_spill = pltpu.make_async_copy(layer_ref, layer_far, load_sems.at[5])
    hidden_spill = pltpu.make_async_copy(hidden_ref, hidden_far, load_sems.at[6])
    more_start, more_wide = tiles[-1]
    more_spill = pltpu.make_async_copy(
        rows.send.at[:, :, pl.ds(more_start, more_wide)], more_far, load_sems.at[7]
    )

    def spans(i, size):
        start = pl.multiple_of(i * 256, 256)
        return pl.ds(start, size), pl.ds(pl.multiple_of(wide + start, LANES), size)

    def weight_loads(i, size):
        gate_span, up_span = spans(i, size)
        return (
            pltpu.make_async_copy(
                gate_far.at[:, gate_span], weight_ref.at[:, gate_span], weight_sems.at[0, i]
            ),
            pltpu.make_async_copy(
                up_far.at[:, gate_span], weight_ref.at[:, up_span], weight_sems.at[1, i]
            ),
        )

    def block_rows(b):
        return pl.ds(b * half, half)

    def piece_copies(b, i, size):
        gate_span, up_span = spans(i, size)
        at = block_rows(b)
        return tuple(
            rows.piece_copy(2 * (b * pieces + i) + j, rows.all.at[at, span], span, at)
            for j, span in enumerate((gate_span, up_span))
        )

    def each(action):
        @pl.loop(0, full)
        def _(i):
            action(i, 256)

        if rest:
            action(full, rest)

    def at_item(w, action):
        @pl.when((w >= 0) & (w < full))
        def _():
            action(w, 256)

        if rest:
            @pl.when(w == full)
            def _():
                action(full, rest)

    down_load.start()
    cotangent_load.start()
    for c in token_loads:
        c.start()
    barrier = pltpu.get_barrier_semaphore()
    greet_dp(barrier, groups)
    line.greet(barrier, groups - 1)
    first_line.prime()
    for c in token_loads:
        c.wait()

    def make_d_active(i, size):
        span, _ = spans(i, size)
        d_active_ref[:, span] = dot_t(
            cotangent_ref[...], weight_ref[span, pl.ds(0, width)]
        ).astype(bf16)

    def start_weights(i, size):
        for c in weight_loads(i, size):
            c.start()

    def hidden_units(b, i, size):
        if b == 0:
            for c in weight_loads(i, size):
                c.wait()
        gate_span, up_span = spans(i, size)
        at = block_rows(b)
        gate = dot(feed_ref[at, :], weight_ref[:, gate_span])
        up = dot(feed_ref[at, :], weight_ref[:, up_span])
        d_active = d_active_ref[at, gate_span].astype(f32)
        sigmoid = jax.nn.sigmoid(gate)
        swish = gate * sigmoid
        active_ref[at, gate_span] = (swish * up).astype(bf16)
        rows.all[at, gate_span] = (
            d_active * up * sigmoid * (1.0 + gate * (1.0 - sigmoid))
        ).astype(bf16)
        rows.all[at, up_span] = (d_active * swish).astype(bf16)
        for c in piece_copies(b, i, size):
            c.start()

    share_items = width // 256

    def make_share(b, w):
        @pl.when((w >= 0) & (w < share_items))
        def _():
            to = pl.ds(pl.multiple_of(w * 256, 256), 256)
            at = block_rows(b)
            share_ref[at, to] = dot_t(rows.all[at, :], weight_ref[to, :]).astype(bf16)

    per = first_line.block // FINE
    arrived = first_line.second + SKEW * (n - 2) + per
    d_first = 10

    @pl.loop(0, first_line.steps)
    def _(step):
        first_line.step(step)

        @pl.when(step == d_first)
        def _():
            down_load.wait()
            cotangent_load.wait()

        at_item(step - d_first, make_d_active)

        @pl.when(step == d_first + pieces)
        def _():
            each(start_weights)

        at_item(step - arrived, lambda i, size: hidden_units(0, i, size))
        w = 2 * (step - arrived - pieces)
        make_share(0, w)
        make_share(0, w + 1)

    done_share = 2 * (first_line.steps - arrived - pieces)

    @pl.loop(done_share, max(share_items, done_share))
    def _(w):
        make_share(0, w)

    line.prime(0)
    hidden_spill.start()

    @pl.loop(0, rows.team)
    def _(q):
        rows.left_copy(q).start()

    layer_items = width // 512
    first_work = 8
    if 2 * (per - pieces) < share_items:
        raise ValueError("shares late")

    @pl.loop(0, line.steps)
    def _(step):
        @pl.when(step == per)
        def _():
            line.prime(1)
            active_spill.start()
            down_load.start()

        line.step(step)
        at_item(step, lambda i, size: hidden_units(1, i, size))
        w = 2 * (step - pieces)
        make_share(1, w)
        make_share(1, w + 1)
        w = step - first_work

        @pl.when(w == 0)
        def _():
            @pl.loop(0, rows.team)
            def _(q):
                rows.left_copy(q).wait_recv()

            for b in range(2):
                def arrive(i, size, b=b):
                    for c in piece_copies(b, i, size):
                        c.wait_recv()

                each(arrive)

        rows.item(w)

        @pl.when(w == rows.items)
        def _():
            more_spill.start()
            down_load.wait()

        layer_item = w - rows.items

        @pl.when((layer_item >= 0) & (layer_item < layer_items))
        def _():
            to = pl.ds(pl.multiple_of(layer_item * 512, 512), 512)
            layer_ref[:, to] = dot(active_ref[...], weight_ref[pl.ds(0, wide), to]).astype(bf16)

        @pl.when(layer_item == layer_items)
        def _():
            layer_spill.start()

    rows.receive()
    first_line.drain()
    line.drain()
    rows.drain()
    for c in (active_spill, layer_spill, hidden_spill, more_spill):
        c.wait()
    for b in range(2):
        def sent(i, size, b=b):
            for c in piece_copies(b, i, size):
                c.wait_send()

        each(sent)


def back_feed(call, n, groups, gains, share, tokens, cotangent, feed_gate, feed_up, feed_down):
    count, width = share.shape
    half = count // 2
    wide = feed_gate.shape[1]
    pieces = (wide + 255) // 256
    cut = (wide // 2 + LANES - 1) // LANES * LANES
    tiles = [(0, cut), (cut, wide - cut), (wide, cut), (wide + cut, wide - cut)]
    team, per = groups // 2, width // groups
    vmem = pl.BlockSpec(memory_space=pltpu.VMEM)
    far = pl.BlockSpec(memory_space=pl.ANY)
    shape = jax.ShapeDtypeStruct
    return pl.pallas_call(
        functools.partial(back_feed_kernel, n, groups, tiles),
        in_specs=[vmem] * 2 + [far] * 5,
        out_specs=[vmem] * 3 + [far] * 5,
        out_shape=[
            shape((count, width), bf16),
            shape((half, width), f32),
            shape((8, width), f32),
            shape((team, per, wide + cut), bf16),
            shape((team, per, wide - cut), bf16),
            shape((count, wide), bf16),
            shape((count, width), bf16),
            shape((half, width), f32),
        ],
        scratch_shapes=[pltpu.VMEM((count, wide), bf16), pltpu.VMEM((count, width), bf16)]
        + Line.scratch(half, width)
        + Line.scratch(half, width)
        + [
            pltpu.VMEM((half, width), f32),
            pltpu.VMEM((half, width), bf16),
            pltpu.VMEM((count, width), bf16),
            pltpu.VMEM((count, width), bf16),
            pltpu.VMEM((width, 2 * wide), bf16),
            pltpu.VMEM((count, wide), bf16),
            pltpu.SemaphoreType.DMA((8,)),
            pltpu.SemaphoreType.DMA((2, pieces)),
            Line.semaphores(half),
            Line.semaphores(half),
        ]
        + RowGrads.scratch(groups, count, width, 2 * wide, 4 * pieces, len(tiles)),
        compiler_params=pltpu.CompilerParams(
            collective_id=call, has_side_effects=True, vmem_limit_bytes=61 << 20
        ),
        cost_estimate=pl.CostEstimate(
            flops=30_000_000_000, bytes_accessed=200_000_000, transcendentals=0
        ),
        name="back_feed",
    )(gains, share, tokens, cotangent, feed_gate, feed_up, feed_down)


class SmallSum:
    def __init__(self, n, groups, wide, near, near_all, wide_out, near_out, refs):
        (
            self.wide_in, self.near_in, self.wide_line, self.near_line, self.sems, self.line_sems,
        ) = refs
        self.n, self.groups, self.near_all = n, groups, near_all
        self.wide, self.near, self.wide_out, self.near_out = wide, near, wide_out, near_out
        self.member, self.place = lax.axis_index("dp"), lax.axis_index("tensor")
        self.block = wide.shape[1] // groups

    @staticmethod
    def scratch(n, groups, wide, near):
        block = wide[1] // groups
        return [
            pltpu.VMEM((groups, wide[0], block), f32),
            pltpu.VMEM(near, f32),
            pltpu.VMEM((n, wide[0], block), f32),
            pltpu.VMEM((n,) + near[1:], f32),
            pltpu.SemaphoreType.DMA((2, 2, groups)),
            pltpu.SemaphoreType.DMA((2, 2, n)),
        ]

    def greet(self, barrier):
        n, place = self.n, self.place
        for k in range(2, n):
            @pl.when(place + k < n)
            def _():
                pl.semaphore_signal(
                    barrier, inc=1, device_id={"tensor": place + k}, device_id_type=MESH
                )

            @pl.when(place - k >= 0)
            def _():
                pl.semaphore_signal(
                    barrier, inc=1, device_id={"tensor": place - k}, device_id_type=MESH
                )

    def cut(self, j):
        return pl.ds(pl.multiple_of(j * self.block, self.block), self.block)

    def copies(self, to, source):
        return (
            to_dp(
                self.wide.at[:, self.cut(to)], self.wide_in.at[source],
                self.sems.at[0, 0, to], self.sems.at[1, 0, source], to,
            ),
            to_dp(
                self.near.at[to], self.near_in.at[source],
                self.sems.at[0, 1, to], self.sems.at[1, 1, source], to,
            ),
        )

    def line_copies(self, to, source):
        return tuple(
            pltpu.make_async_remote_copy(
                line.at[self.place], line.at[source], self.line_sems.at[0, i, to],
                self.line_sems.at[1, i, source], device_id={"tensor": to}, device_id_type=MESH,
            )
            for i, line in enumerate((self.wide_line, self.near_line))
        )

    def send(self):
        @pl.loop(1, self.groups)
        def _(k):
            for c in self.copies(lax.rem(self.member + k, self.groups), self.member):
                c.start()

        self.wide_in[pl.ds(self.member, 1)] = self.wide[:, self.cut(self.member)][None]
        self.near_in[pl.ds(self.member, 1)] = self.near[pl.ds(self.member, 1)]

    def forward(self):
        @pl.loop(1, self.groups)
        def _(k):
            for c in self.copies(0, lax.rem(self.member + k, self.groups)):
                c.wait_recv()

        for came, line in ((self.wide_in, self.wide_line), (self.near_in, self.near_line)):
            total = came[0]
            for j in range(1, self.groups):
                total = total + came[j]
            line[pl.ds(self.place, 1)] = total[None]

        @pl.loop(1, self.n)
        def _(k):
            for c in self.line_copies(lax.rem(self.place + k, self.n), self.place):
                c.start()

    def receive(self):
        @pl.loop(1, self.n)
        def _(k):
            for c in self.line_copies(0, lax.rem(self.place + k, self.n)):
                c.wait_recv()

        total = self.wide_line[0]
        for j in range(1, self.n):
            total = total + self.wide_line[j]
        self.wide_out[...] = total
        own = self.near_line[pl.ds(self.place, 1)][0]
        total = self.near_line[0]
        for j in range(1, self.n):
            total = total + self.near_line[j]
        row = lax.broadcasted_iota(jnp.int32, own.shape, 0)
        self.near_out[...] = jnp.where(row < self.near_all, total, own)

    def drain(self):
        @pl.loop(1, self.groups)
        def _(k):
            for c in self.copies(lax.rem(self.member + k, self.groups), self.member):
                c.wait_send()

        @pl.loop(1, self.n)
        def _(k):
            for c in self.line_copies(lax.rem(self.place + k, self.n), self.place):
                c.wait_send()


def back_mixer_kernel(n, groups, widths, near_all, tiles, *refs):
    take = splitter(refs)
    gains_ref, near_ref, down_rows_ref, x_far, base_far, left_far = take(6)
    parts = take(2)
    col_left, col_right, more_far = take(3)
    weights = take(len(widths))
    out_ref, wide_out, near_out, recv, col_recv, more_recv = take(6)
    more_ref, more_sems, more_load_sems = take(3)
    up_in, down_in, x_ref, base_ref, share_ref, wide_ref, gain_grad_ref = take(7)
    weight_ref, latent_ref, load_sems, sems = take(4)
    rows = RowGrads(groups, left_far, tiles, recv, take(10))
    part_spans = [
        pl.ds(0, parts[0].shape[1]), pl.ds(parts[0].shape[1], parts[1].shape[1])
    ]
    part_loads = [rows.piece_load(i, parts[i], part_spans[i]) for i in range(2)]
    part_copies = [rows.piece_copy(i, parts[i], part_spans[i]) for i in range(2)]
    cols = ColGrad(groups, col_left, col_right, 0, 256, col_recv, take(8))
    small = SmallSum(n, groups, wide_ref, near_ref, near_all, wide_out, near_out, take(6))
    finish = norm_back(
        x_ref, lambda own, place: base_ref[own, :], lambda: gains_ref[0:1, :], out_ref, None,
        gain_grad_ref,
    )
    line = Line(n, share_ref, up_in, down_in, out_ref, sems, finish)
    loads = line.own_copies(x_far, x_ref, [load_sems.at[0], more_load_sems.at[0]])
    loads.append(pltpu.make_async_copy(base_far, base_ref, load_sems.at[1]))
    more_load = pltpu.make_async_copy(more_far, more_ref, more_load_sems.at[1])

    def more_copy(to, source):
        return to_dp(
            more_ref.at[to], more_recv.at[source], more_sems.at[0, to], more_sems.at[1, source],
            2 * to + rows.parity,
        )

    more_keep = pltpu.make_async_copy(
        more_ref.at[rows.mine], more_recv.at[rows.mine], more_load_sems.at[2]
    )
    more_load.start()
    weight_loads = []
    offset = 0
    for i, wide in enumerate(widths):
        if i == len(widths) - 1:
            latent_at = offset
            offset += LANES
        weight_loads.append(
            pltpu.make_async_copy(
                weights[i], weight_ref.at[:, pl.ds(offset, wide)], load_sems.at[2 + i]
            )
        )
        offset += wide
    for c in part_loads + weight_loads:
        c.start()
    thirds(down_rows_ref, 2, latent_ref)
    weight_ref[:, pl.ds(latent_at, LANES)] = jnp.transpose(latent_ref[...].astype(f32)).astype(bf16)
    barrier = pltpu.get_barrier_semaphore()
    greet_dp(barrier, groups)
    small.greet(barrier)
    line.greet_all(barrier, groups - 1)
    rows.start_left()
    for c in part_copies:
        c.start()
    cols.start()
    for c in loads:
        c.start()
    more_load.wait()
    more_keep.start()

    @pl.loop(1, rows.team)
    def _(k):
        more_copy(lax.rem(rows.mine + k, rows.team), rows.mine).start()

    for c in part_loads + weight_loads:
        c.wait()

    count, width = share_ref.shape
    tile_rows, tile_columns = count // 2, 512
    across = width // tile_columns

    for c in loads:
        c.wait()
    for b in range(2):
        at = pl.ds(b * tile_rows, tile_rows)

        @pl.loop(0, across)
        def _(i):
            to = pl.ds(pl.multiple_of(i * tile_columns, tile_columns), tile_columns)
            share_ref[at, to] = dot_t(rows.all[at, :], weight_ref[to, :]).astype(bf16)

        line.prime(b)

    third = LANES // 4
    first_cols = rows.items
    last_item = first_cols + cols.items

    @pl.loop(0, line.steps)
    def _(step):
        line.step(step)

        @pl.when(step == 0)
        def _():
            rows.ready_left()
            for c in part_copies:
                c.wait_recv()

        rows.item(step)

        @pl.when(step == first_cols)
        def _():
            cols.ready()

        @pl.when((step >= first_cols) & (step < last_item))
        def _():
            cols.item(step - first_cols)

        @pl.when(step == last_item)
        def _():
            cols.send_all()
            product = rows_dot(rows.all[:, pl.ds(latent_at, LANES)], rows.left[...])
            wide_ref[:16, :] = product[:16, :] + product[third : third + 16, :]

        @pl.when(step == line.count + SKEW * (n - 2) + 2)
        def _():
            wide_ref[16:, :] = gain_grad_ref[...]
            small.send()

        @pl.when(step == line.second + 14)
        def _():
            small.forward()

    more_keep.wait()

    @pl.loop(1, rows.team)
    def _(k):
        more_copy(0, lax.rem(rows.mine + k, rows.team)).wait_recv()
        more_copy(lax.rem(rows.mine + k, rows.team), rows.mine).wait_send()

    rows.receive()
    cols.receive()
    small.receive()
    line.drain()
    rows.drain()
    for c in part_copies:
        c.wait_send()
    cols.drain()
    small.drain()


def back_mixer(
    call, n, groups, gains, near, near_all, down_rows, x, base_own, left, parts, pair, weights
):
    count, width = left.shape
    half = count // 2
    widths = [w.shape[1] for w in weights]
    total = sum(part.shape[1] for part in parts)
    start = parts[0].shape[1]
    tiles = [(0, 512), (512, 512), (start, parts[1].shape[1])]
    col_rows = pair[0].shape[1]
    vmem = pl.BlockSpec(memory_space=pltpu.VMEM)
    far = pl.BlockSpec(memory_space=pl.ANY)
    wide_shape = (24, width)
    return pl.pallas_call(
        functools.partial(back_mixer_kernel, n, groups, widths, near_all, tiles),
        in_specs=[vmem] * 3 + [far] * (8 + len(weights)),
        out_specs=[vmem] * 3 + [far] * 3,
        out_shape=[
            jax.ShapeDtypeStruct((count, width), bf16),
            jax.ShapeDtypeStruct((24, width // groups), f32),
            jax.ShapeDtypeStruct(near.shape[1:], f32),
            jax.ShapeDtypeStruct((groups // 2, width // groups, total), bf16),
            jax.ShapeDtypeStruct((groups, col_rows // groups, width // 2), bf16),
            jax.ShapeDtypeStruct(pair[2].shape, bf16),
        ],
        scratch_shapes=[
            pltpu.VMEM(pair[2].shape, bf16),
            pltpu.SemaphoreType.DMA((2, groups // 2)),
            pltpu.SemaphoreType.DMA((3,)),
        ]
        + Line.scratch(half, width)
        + [
            pltpu.VMEM((half, width), x.dtype),
            pltpu.VMEM((half, width), base_own.dtype),
            pltpu.VMEM((count, width), bf16),
            pltpu.VMEM(wide_shape, f32),
            pltpu.VMEM((8, width), f32),
            pltpu.VMEM((width, total), bf16),
            pltpu.VMEM((LANES, width), bf16),
            pltpu.SemaphoreType.DMA((2 + len(weights),)),
            Line.semaphores(half),
        ]
        + RowGrads.scratch(groups, count, width, total, 2, len(tiles))
        + ColGrad.scratch(groups, count, col_rows, width // 2)
        + SmallSum.scratch(n, groups, wide_shape, near.shape),
        compiler_params=pltpu.CompilerParams(
            collective_id=call, has_side_effects=True, vmem_limit_bytes=61 << 20
        ),
        cost_estimate=pl.CostEstimate(
            flops=12_000_000_000, bytes_accessed=200_000_000, transcendentals=0
        ),
        name="back_mixer",
    )(gains, near, down_rows, x, base_own, left, *parts, *pair, *weights)


def outputs_kernel(dk, dv, rank, near_all, *refs):
    take = splitter(refs)
    feed_ref, feed_more_ref, rows_ref, down_ref, out_ref = take(5)
    wide_ref, near_ref, token_ref, layer_ref = take(4)
    token_out, layer_out, query_out, key_out, value_out, gate_out = take(6)
    feed_gate_out, feed_up_out, feed_down_out, out_out, decay_out, vector_out = take(6)
    step = pl.program_id(0)

    def total(ref, start, wide):
        span = pl.ds(start, wide)
        result = ref[0, :, span].astype(f32)
        for q in range(1, ref.shape[0]):
            result = result + ref[q, :, span].astype(f32)
        return result

    wide = feed_gate_out.shape[1]
    feed_gate_out[...] = total(feed_ref, 0, wide)
    there = feed_ref.shape[2] - wide
    feed_up_out[:, :there] = total(feed_ref, wide, there)
    feed_up_out[:, there:] = total(feed_more_ref, 0, wide - there)
    query_out[...] = total(rows_ref, 0, dk)
    key_out[...] = total(rows_ref, dk, dk)
    value_out[...] = total(rows_ref, 2 * dk, dv)
    gate_out[...] = total(rows_ref, 2 * dk + dv + LANES, dv)
    token_out[...] = token_ref[...]
    layer_out[...] = layer_ref[...]

    @pl.when(lax.rem(step, pl.num_programs(0) // 2) == 0)
    def _():
        half = out_out.shape[2] // 2
        for ref, out in ((down_ref, feed_down_out), (out_ref, out_out)):
            for b in range(2):
                result = ref[b].astype(f32)
                for q in range(1, ref.shape[0] // 2):
                    result = result + ref[2 * q + b].astype(f32)
                out[0, :, b * half : (b + 1) * half] = result

    @pl.when(step == 0)
    def _():
        decay_out[...] = wide_ref[:rank, :]
        vector_out[...] = jnp.sum(wide_ref[rank:, :], axis=0, keepdims=True)


def outputs(
    groups, dk, dv, rank, near_all, feed, feed_more, rows, down, out, wide_sum, near_sum, token,
    layer,
):
    steps = 4
    count, width = token.shape
    wide = (feed.shape[2] + feed_more.shape[2]) // 2
    per = width // groups
    block = per // steps
    shape = jax.ShapeDtypeStruct

    def rows_of(columns):
        return pl.BlockSpec((block, columns), lambda i: (i, 0))

    def fixed(array):
        return pl.BlockSpec(array.shape, lambda i: (0,) * array.ndim)

    def recv(array):
        return pl.BlockSpec((array.shape[0], block, array.shape[2]), lambda i: (0, i, 0))

    def recv_half(array):
        return pl.BlockSpec(
            (array.shape[0], array.shape[1] // 2, array.shape[2]), lambda i: (0, i // (steps // 2), 0)
        )

    def out_half(array):
        return pl.BlockSpec((1, array.shape[1] // 2, width), lambda i: (0, i // (steps // 2), 0))

    tokens_block = pl.BlockSpec((count // steps, width), lambda i: (i, 0))
    return pl.pallas_call(
        functools.partial(outputs_kernel, dk, dv, rank, near_all),
        grid=(steps,),
        in_specs=[
            recv(feed), recv(feed_more), recv(rows), recv_half(down), recv_half(out), fixed(wide_sum),
            fixed(near_sum), tokens_block, tokens_block,
        ],
        out_specs=[
            tokens_block, tokens_block, rows_of(dk), rows_of(dk), rows_of(dv), rows_of(dv),
            rows_of(wide), rows_of(wide), out_half(down), out_half(out),
            pl.BlockSpec((rank, per), lambda i: (0, 0)),
            pl.BlockSpec((1, per), lambda i: (0, 0)),
        ],
        out_shape=[
            shape((count, width), bf16),
            shape((count, width), bf16),
            shape((per, dk), f32),
            shape((per, dk), f32),
            shape((per, dv), f32),
            shape((per, dv), f32),
            shape((per, wide), f32),
            shape((per, wide), f32),
            shape((1, down.shape[1], width), f32),
            shape((1, out.shape[1], width), f32),
            shape((rank, per), f32),
            shape((1, per), f32),
        ],
        compiler_params=pltpu.CompilerParams(vmem_limit_bytes=60 << 20),
        name="outputs",
    )(feed, feed_more, rows, down, out, wide_sum, near_sum, token, layer)


def recur_back_kernel(n, groups, dk, dv, beside, *refs):
    (
        lengths_ref, send_row_ref, send_column_ref, slot_row_ref, slot_column_ref,
        d_mixed_far, out_weight_far, attended_ref, gate_ref, gains_ref, up_rows_ref,
        share_ref, held_far, states_far, hidden_far, active_far, cotangent_far,
        d_rows_ref, d_gate_ref, head_gain_ref, grad_up_ref, grad_bias_ref, layer_ref, grad_down_ref,
        up_in, down_in, d_attended, d_placed, d_state, result,
        held_ref, states_ref, hidden_ref, up_ref, down_ref, bias_ref, load_sems, sems,
        d_mixed_ref, out_weight_ref,
    ) = refs[:40]
    go = Exchange(groups, (), *refs[40:43])
    back = Exchange(groups, (2 * dk,), *refs[43:46])
    cols = None
    if beside:
        cols = ColGrad(groups, active_far, cotangent_far, 0, 512, grad_down_ref, refs[46:])
    count = d_mixed_ref.shape[0]
    slots = slot_row_ref.shape[1]
    end0 = lengths_ref[0, 0]
    end1 = end0 + lengths_ref[0, 1]
    ends = (end0, end1, end1 + lengths_ref[0, 2])

    def finish(total, own, place):
        layer_ref[place, :] = (hidden_ref[own, :] + total).astype(layer_ref.dtype)

    line = Line(n, share_ref, up_in, down_in, layer_ref, sems, finish)
    loads = (
        pltpu.make_async_copy(hidden_far, hidden_ref, load_sems.at[0]),
        pltpu.make_async_copy(held_far, held_ref, load_sems.at[1]),
        pltpu.make_async_copy(states_far, states_ref, load_sems.at[2]),
    )
    head_loads = (
        pltpu.make_async_copy(d_mixed_far, d_mixed_ref, load_sems.at[3]),
        pltpu.make_async_copy(out_weight_far, out_weight_ref, load_sems.at[4]),
    )
    for c in head_loads:
        c.start()
    barrier = pltpu.get_barrier_semaphore()
    greet_dp(barrier, groups)
    line.greet(barrier, groups - 1)
    line.prime()
    for c in loads:
        c.start()
    if beside:
        cols.start()
    loads[0].wait()

    bias_ref[...] = gains_ref[2:3, dv : dv + dk]
    thirds(up_rows_ref, 3, up_ref)
    thirds(up_rows_ref, 2, down_ref)

    head_gain_ref[...] = jnp.zeros_like(head_gain_ref)
    tile = count // 2
    for c in head_loads:
        c.wait()

    @pl.loop(0, 2)
    def _(i):
        rows = pl.ds(pl.multiple_of(i * tile, tile), tile)
        d_gated = dot_t(d_mixed_ref[rows, :], out_weight_ref[...])
        attended = attended_ref[rows, :].astype(f32)
        gate = gate_ref[rows, :]
        scaling = lax.rsqrt(jnp.mean(attended * attended, axis=1, keepdims=True) + head_floor)
        unit = attended * scaling
        sigmoid = jax.nn.sigmoid(gate)
        swish = gate * sigmoid
        gained = d_gated * gains_ref[2:3, :dv]
        d_gate_ref[rows, :] = (
            gained * unit * sigmoid * (1.0 + gate * (1.0 - sigmoid))
        ).astype(bf16)
        d_unit = gained * swish
        d_attended[rows, :] = (
            scaling * (d_unit - unit * jnp.mean(d_unit * unit, axis=1, keepdims=True))
        ).astype(bf16)
        term = d_gated * unit * swish
        piece = term[0:8, :]
        for r in range(1, tile // 8):
            piece = piece + term[8 * r : 8 * r + 8, :]
        head_gain_ref[...] += piece
        line.step(2 * i)
        line.step(2 * i + 1)

    go.send(0, send_row_ref, 0, d_attended, lambda h: line.step(4 + h))
    d_state[...] = jnp.zeros_like(d_state)
    grad_up_ref[...] = jnp.zeros_like(grad_up_ref)
    grad_bias_ref[...] = jnp.zeros_like(grad_bias_ref)
    done = 14
    if beside:
        cols.ready()

        @pl.loop(0, cols.items)
        def _(i):
            cols.item(i)
            line.step(6 + 2 * i)
            line.step(7 + 2 * i)

        done = 6 + 2 * cols.items
        cols.send_all()
    else:
        line.run(6, done)
    for c in loads[1:]:
        c.wait()

    go.receive(0)
    place_rows(slot_row_ref, go.came, d_placed, go.spans[0], lambda h: line.step(done + h))
    spanned = done + 2
    spans = held_ref.shape[0] // SPAN

    @pl.loop(0, spans)
    def _(i):
        step = spans - 1 - i
        d_out = d_placed[pl.ds(pl.multiple_of(step * SPAN, SPAN), SPAN), :]
        span_backward(
            dk, dv, step, ends, d_out, held_ref, states_ref[step], up_ref, bias_ref, down_ref,
            d_state, result, grad_up_ref, grad_bias_ref,
        )
        line.step(spanned + 2 * i)
        line.step(spanned + 1 + 2 * i)

    sent = spanned + 2 * spans
    for p in range(2):
        back.send(
            p, slot_column_ref, 1, result, lambda h, p=p: line.step(sent + 2 * p + h)
        )
    last_steps = (sent + 4, sent + 4 + (line.steps - sent - 4) * 2 // 3, line.steps)
    for p in range(2):
        line.run(last_steps[p], last_steps[p + 1])
        if beside and p:
            cols.receive()
        back.receive(p)
        span = back.spans[p]

        @pl.loop(0, 2)
        def _(i):
            rows = pl.ds(pl.multiple_of(i * tile, tile), tile)
            pick = one_hot(send_column_ref[rows, :], 0, (tile, slots), 1)
            d_rows_ref[rows, span] = dot(pick, back.came[:, span]).astype(bf16)

    line.drain()
    if beside:
        cols.drain()
    go.drain()
    back.drain()


def recur_back(
    call, n, groups, dk, dv, beside, lengths, send_row, send_column, slot_row, slot_column, d_mixed, out_weight, attended, gate_pre,
    gains, up_rows, share, held, states, hidden_own, active, cotangent,
):
    count, width = d_mixed.shape
    slots, wide = held.shape
    half = count // 2
    vmem = pl.BlockSpec(memory_space=pltpu.VMEM)
    operands = [
        lengths, send_row, send_column, slot_row, slot_column, d_mixed, out_weight, attended, gate_pre, gains, up_rows, share, held, states, hidden_own, active, cotangent,
    ]
    far = pl.BlockSpec(memory_space=pl.ANY)
    return pl.pallas_call(
        functools.partial(recur_back_kernel, n, groups, dk, dv, beside),
        in_specs=[pl.BlockSpec(memory_space=pltpu.SMEM)]
        + [vmem] * 4
        + [far] * 2
        + [vmem] * (len(operands) - 12)
        + [far] * 5,
        out_specs=[vmem] * 6 + [far],
        out_shape=[
            jax.ShapeDtypeStruct((count, wide), bf16),
            jax.ShapeDtypeStruct((count, dv), bf16),
            jax.ShapeDtypeStruct((8, dv), f32),
            jax.ShapeDtypeStruct((dk, LANES), f32),
            jax.ShapeDtypeStruct((8, dk), f32),
            jax.ShapeDtypeStruct((count, width), bf16),
            jax.ShapeDtypeStruct(
                (groups, active.shape[1] // groups if beside else 8, width // 2), bf16
            ),
        ],
        scratch_shapes=Line.scratch(half, width)
        + [
            pltpu.VMEM((count, dv), bf16),
            pltpu.VMEM((slots, dv), bf16),
            pltpu.VMEM((dk, dv), f32),
            pltpu.VMEM((slots, wide), bf16),
            pltpu.VMEM(held.shape, bf16),
            pltpu.VMEM(states.shape, bf16),
            pltpu.VMEM((half, width), f32),
            pltpu.VMEM((LANES, dk), bf16),
            pltpu.VMEM((LANES, dk), bf16),
            pltpu.VMEM((1, dk), f32),
            pltpu.SemaphoreType.DMA((5,)),
            Line.semaphores(half),
            pltpu.VMEM(d_mixed.shape, bf16),
            pltpu.VMEM(out_weight.shape, bf16),
        ]
        + Exchange.scratch(groups, slots, dv, 1)
        + Exchange.scratch(groups, slots, wide, 2)
        + (ColGrad.scratch(groups, count, active.shape[1], width // 2) if beside else []),
        compiler_params=pltpu.CompilerParams(
            collective_id=call, has_side_effects=True, vmem_limit_bytes=60 << 20
        ),
        cost_estimate=pl.CostEstimate(
            flops=12_000_000_000, bytes_accessed=200_000_000, transcendentals=4_000_000
        ),
        name="recur_back",
    )(*operands)


def small_sum_kernel(groups, n, rows_all, part_ref, out_ref, held, line, line_in, sems, line_sems):
    me = lax.axis_index("dp")
    place = lax.axis_index("tensor")
    barrier = pltpu.get_barrier_semaphore()

    def peer(k):
        return lax.rem(me + k, groups)

    def mate(k):
        return lax.rem(place + k, n)

    @pl.loop(1, groups)
    def _(k):
        pl.semaphore_signal(barrier, inc=1, device_id={"dp": peer(k)}, device_id_type=MESH)

    @pl.loop(1, n)
    def _(k):
        pl.semaphore_signal(barrier, inc=1, device_id={"tensor": mate(k)}, device_id_type=MESH)

    pl.semaphore_wait(barrier, groups + n - 2)

    def copy(k, source):
        return pltpu.make_async_remote_copy(
            part_ref.at[peer(k)], held.at[source], sems.at[0, k], sems.at[1, source],
            device_id={"dp": peer(k)}, device_id_type=MESH,
        )

    def line_copy(k, source):
        return pltpu.make_async_remote_copy(
            line, line_in.at[source], line_sems.at[0, k], line_sems.at[1, source],
            device_id={"tensor": mate(k)}, device_id_type=MESH,
        )

    @pl.loop(1, groups)
    def _(k):
        copy(k, me).start()

    held[pl.ds(me, 1)] = part_ref[pl.ds(me, 1)]

    @pl.loop(1, groups)
    def _(k):
        copy(k, peer(k)).wait_recv()

    total = held[0]
    for i in range(1, groups):
        total = total + held[i]
    line[...] = total[:rows_all]
    out_ref[...] = total

    @pl.loop(1, n)
    def _(k):
        line_copy(k, place).start()

    line_in[pl.ds(place, 1)] = total[None, :rows_all]

    @pl.loop(1, n)
    def _(k):
        line_copy(k, mate(k)).wait_recv()

    total = line_in[0]
    for i in range(1, n):
        total = total + line_in[i]
    out_ref[:rows_all] = total

    @pl.loop(1, groups)
    def _(k):
        copy(k, me).wait_send()

    @pl.loop(1, n)
    def _(k):
        line_copy(k, place).wait_send()


def small_sum(over_all, over_owners, groups, n, call):
    def tiles(blocks):
        short = -blocks.shape[1] % (8 * LANES)
        return jnp.pad(blocks, ((0, 0), (0, short))).reshape(groups, -1, LANES)

    first, second = tiles(over_all), tiles(over_owners)
    rows_all = first.shape[1]
    part = jnp.concatenate([first, second], axis=1)
    vmem = pl.BlockSpec(memory_space=pltpu.VMEM)
    total = pl.pallas_call(
        functools.partial(small_sum_kernel, groups, n, rows_all),
        in_specs=[vmem],
        out_specs=vmem,
        out_shape=jax.ShapeDtypeStruct(part.shape[1:], f32),
        scratch_shapes=[
            pltpu.VMEM(part.shape, f32),
            pltpu.VMEM((rows_all, LANES), f32),
            pltpu.VMEM((n, rows_all, LANES), f32),
            pltpu.SemaphoreType.DMA((2, groups)),
            pltpu.SemaphoreType.DMA((2, n)),
        ],
        compiler_params=pltpu.CompilerParams(collective_id=call, has_side_effects=True),
        name="small_sum",
    )(part)
    return (
        total[:rows_all].reshape(-1)[: over_all.shape[1]],
        total[rows_all:].reshape(-1)[: over_owners.shape[1]],
    )


def per_device(
    tokens,
    cotangent,
    token_slots,
    lengths,
    mixer_gain,
    query_weight,
    key_weight,
    value_weight,
    gate_weight,
    decay_down,
    decay_up,
    decay_bias,
    head_gain,
    out_weight,
    feed_gain,
    feed_gate,
    feed_up,
    feed_down,
):
    groups = lax.axis_size("dp")
    lines = lax.axis_size("tensor")
    member = lax.axis_index("dp")
    place = lax.axis_index("tensor")
    count, width = tokens.shape
    dk = query_weight.shape[1]
    dv = value_weight.shape[1]
    rank = decay_up.shape[1]
    parity = lax.rem(member, 2)
    pairs = [(i, i ^ 1) for i in range(groups)]
    same_parity = [[i for i in range(groups) if i % 2 == b] for b in range(2)]

    fused = (width // groups) % LANES == 0
    third = LANES // 4
    down_rows = decay_down.T
    up_rows = decay_up.T
    last = jnp.pad(jnp.concatenate([head_gain, decay_bias]), (0, width - dv - dk))
    gains = jnp.stack([mixer_gain, feed_gain, last]).astype(f32)
    (
        normed, gate_pre, attended, gated, held, states, mixer_share, send_row, send_column, slot_row,
        slot_column,
    ) = front(
        1, groups, lengths, token_slots.reshape(-1, LANES), tokens, gains, up_rows,
        down_rows, [query_weight, key_weight, value_weight], gate_weight, out_weight,
    )

    if fused:
        (
            d_mixed, d_hidden_own, feed_gain_part, feed_recv, feed_more, active, layer_share,
            hidden_own,
        ) = back_feed(
            2, lines, groups, gains, mixer_share, tokens, cotangent, feed_gate, feed_up, feed_down
        )
    else:
        quarter = count // 4

        def own_rows(rows):
            blocks = rows.reshape(2, 2, quarter, width)
            return jnp.where(place == 0, blocks[:, 1], blocks[:, 0]).reshape(2 * quarter, width)

        tokens_own, cotangent_own = own_rows(tokens), own_rows(cotangent)
        feed_normed, hidden_own, _ = line_sum(
            "norm", 5, lines, mixer_share, tokens_own, tokens_own, gains[1:2]
        )
        d_active = dot_t(cotangent, feed_down).astype(bf16)
        gate_hidden = dot(feed_normed, feed_gate)
        up_hidden = dot(feed_normed, feed_up)
        d_active = d_active.astype(f32)
        sigmoid_gate = jax.nn.sigmoid(gate_hidden)
        swish_gate = gate_hidden * sigmoid_gate
        active = (swish_gate * up_hidden).astype(bf16)
        d_gate_hidden = (
            d_active * up_hidden * sigmoid_gate * (1.0 + gate_hidden * (1.0 - sigmoid_gate))
        ).astype(bf16)
        d_up_hidden = (d_active * swish_gate).astype(bf16)
        feed_share = (dot_t(d_gate_hidden, feed_gate) + dot_t(d_up_hidden, feed_up)).astype(bf16)
        d_mixed, d_hidden_own, feed_gain_part = line_sum(
            "back", 2, lines, feed_share, hidden_own, cotangent_own, gains[1:2]
        )
        layer_share = dot(active, feed_down).astype(bf16)

    d_rows, d_gate_low, head_gain_part, up_part, bias_part, layer_out, down_recv = recur_back(
        4, lines, groups, dk, dv, fused, lengths, send_row, send_column, slot_row, slot_column, d_mixed,
        out_weight, attended, gate_pre, gains, up_rows, layer_share, held, states, hidden_own, active,
        cotangent,
    )
    up_part = up_part[:, :rank] + up_part[:, third : third + rank] + (
        up_part[:, 2 * third : 2 * third + rank]
    )

    def by_owner(vector):
        return vector.reshape(groups, -1)

    per = width // groups
    head_per = dv // groups
    up_per = dk // groups * rank
    if fused:
        near = [
            by_owner(jnp.sum(feed_gain_part, axis=0)),
            jnp.pad(by_owner(jnp.sum(head_gain_part, axis=0)), ((0, 0), (0, -head_per % LANES))),
            by_owner(up_part),
            jnp.pad(by_owner(bias_part[0]), ((0, 0), (0, -(dk // groups) % LANES))),
        ]
        near_all = (per + head_per + LANES - 1) // LANES
        near = jnp.concatenate(near, axis=1)
        near = jnp.pad(near, ((0, 0), (0, -near.shape[1] % (8 * LANES))))
        token_grad, wide_sum, near_sum, rows_recv, out_recv, feed_more = back_mixer(
            3, lines, groups, gains, near.reshape(groups, -1, LANES), near_all, down_rows, tokens,
            d_hidden_own, normed, [d_rows, d_gate_low], (gated, d_mixed, feed_more),
            [query_weight, key_weight, value_weight, gate_weight],
        )
        (
            token_grad, layer_out, grad_query, grad_key, grad_value, grad_gate, grad_feed_gate,
            grad_feed_up, grad_feed_down, grad_out, down_sum, mixer_sum,
        ) = outputs(
            groups, dk, dv, rank, near_all, feed_recv, feed_more, rows_recv, down_recv, out_recv,
            wide_sum, near_sum, token_grad, layer_out,
        )
        near_sum = near_sum.reshape(-1)
        mixer_sum = mixer_sum.reshape(-1)
        down_sum = down_sum.T
        feed_sum = near_sum[:per]
        head_sum = near_sum[per : per + head_per]
        up_sum = near_sum[near_all * LANES : near_all * LANES + up_per]
        bias_sum = near_sum[near_all * LANES + up_per :][: dk // groups]
    else:
        down_pad = jnp.pad(decay_down, ((0, 0), (0, third - rank)))
        down_none = jnp.zeros_like(down_pad)
        down_both = jnp.concatenate([down_pad, down_pad, down_none, down_none], axis=1)
        d_query_low = d_rows[:, :dk]
        d_key_low = d_rows[:, dk : 2 * dk]
        d_value_low = d_rows[:, 2 * dk : 2 * dk + dv]
        d_latent_low = d_rows[:, 2 * dk + dv :]
        normed_share = (
            dot_t(d_query_low, query_weight)
            + dot_t(d_key_low, key_weight)
            + dot_t(d_value_low, value_weight)
            + dot_t(d_gate_low, gate_weight)
            + dot_t(d_latent_low, down_both)
        ).astype(bf16)
        token_grad, _, mixer_gain_part = line_sum(
            "back", 3, lines, normed_share, tokens_own, d_hidden_own, gains[0:1],
        )
        down_part = rows_dot(normed, d_latent_low)
        down_part = down_part[:, :rank] + down_part[:, third : third + rank]
        over_all = jnp.concatenate(
            [
                by_owner(jnp.sum(mixer_gain_part, axis=0)),
                by_owner(jnp.sum(feed_gain_part, axis=0)),
                by_owner(jnp.sum(head_gain_part, axis=0)),
                by_owner(down_part),
            ],
            axis=1,
        )
        over_owners = jnp.concatenate([by_owner(up_part), by_owner(bias_part[0])], axis=1)
        summed, small = small_sum(over_all, over_owners, groups, lines, 5)
        mixer_sum = summed[:per]
        feed_sum = summed[per : 2 * per]
        head_sum = summed[2 * per : 2 * per + head_per]
        down_sum = summed[2 * per + head_per :].reshape(per, rank)
        up_sum = small[:up_per]
        bias_sum = small[up_per:]

    def halves(row_block, dims):
        split = row_block.reshape(row_block.shape[0], groups // 2, 2, dims // groups)
        keep = lax.dynamic_index_in_dim(split, parity, 2, keepdims=False)
        send = lax.dynamic_index_in_dim(split, 1 - parity, 2, keepdims=False)
        got = lax.ppermute(send, "dp", pairs)
        shape = (row_block.shape[0], dims // 2)
        return keep.reshape(shape), got.reshape(shape)

    def partner(row_block):
        return row_block, lax.ppermute(row_block, "dp", pairs)

    def summed_share(left, right):
        share = (rows_dot(left[0], right[0]) + rows_dot(left[1], right[1])).astype(bf16)
        rows = share.shape[0] // (groups // 2)
        blocks = share.reshape(groups // 2, rows, share.shape[1])
        moved = lax.all_to_all(
            blocks, "dp", split_axis=0, concat_axis=0, tiled=True, axis_index_groups=same_parity
        )
        return jnp.sum(moved.astype(f32), axis=0)

    if not fused:
        grad_feed_down = summed_share(halves(active, active.shape[1]), partner(cotangent))[None]
        feed_halves = halves(feed_normed, width)
        normed_halves = halves(normed, width)
        grad_feed_gate = summed_share(feed_halves, partner(d_gate_hidden))
        grad_feed_up = summed_share(feed_halves, partner(d_up_hidden))
        grad_out = summed_share(halves(gated, dv), partner(d_mixed))[None]
        grad_query = summed_share(normed_halves, partner(d_query_low))
        grad_key = summed_share(normed_halves, partner(d_key_low))
        grad_value = summed_share(normed_halves, partner(d_value_low))
        grad_gate = summed_share(normed_halves, partner(d_gate_low))

    return (
        layer_out,
        token_grad,
        mixer_sum,
        grad_query,
        grad_key,
        grad_value,
        grad_gate,
        down_sum,
        up_sum.reshape(1, dk // groups, rank),
        bias_sum.reshape(1, dk // groups),
        head_sum,
        grad_out,
        feed_sum,
        grad_feed_gate,
        grad_feed_up,
        grad_feed_down,
    )


def solution(mesh):
    placed = (
        P("dp", None),
        P("dp", None),
        P(),
        P("dp", None),
        P(),
        P(None, "tensor"),
        P(None, "tensor"),
        P(None, "tensor"),
        P(None, "tensor"),
        P(),
        P("tensor", None),
        P("tensor"),
        P(),
        P("tensor", None),
        P(),
        P(None, "tensor"),
        P(None, "tensor"),
        P("tensor", None),
    )
    return jax.shard_map(
        per_device,
        mesh=mesh,
        in_specs=placed,
        out_specs=(
            P("dp", None),
            P("dp", None),
            P("dp"),
            P("dp", "tensor"),
            P("dp", "tensor"),
            P("dp", "tensor"),
            P("dp", "tensor"),
            P("dp", None),
            P("tensor", "dp", None),
            P("tensor", "dp"),
            P("dp"),
            P("tensor", "dp", None),
            P("dp"),
            P("dp", "tensor"),
            P("dp", "tensor"),
            P("tensor", "dp", None),
        ),
        check_vma=False,
    )
```
